32 devices in a mesh: exp: 4 (over y, x), seq: 8 (over z, core).
Axes of the slice: x: 2, y: 2, z: 4, core: 2. Of those that a mesh axis runs over, the one named last changes fastest.
Arguments:
- tokens: bfloat16 [4096, 2048], P(('exp', 'seq')), may hold values from -6 to 6
- routes: int32 [4096, 6], P(('exp', 'seq')), may hold values from 0 to 63, all different within a row; in each aligned block of 128 rows (0 to 127, 128 to 255, ...) at most 16 rows name the same one
- route_weights: float32 [4096, 6], P(('exp', 'seq')), may hold values from 0.2 to 1
- norm_gain: bfloat16 [2048], P(('exp', 'seq')), may hold values from 0.099609375 to 1.8984375
- w_query: bfloat16 [2048, 3072], P('exp', 'seq'), may hold values from -0.125 to 0.125
- w_kv_down: bfloat16 [2048, 576], P(('exp', 'seq')), may hold values from -0.125 to 0.125
- latent_gain: bfloat16 [512], P(('exp', 'seq')), may hold values from 0.099609375 to 1.8984375
- w_kv_up: bfloat16 [512, 4096], P('exp', 'seq'), may hold values from -0.25 to 0.25
- w_output: bfloat16 [2048, 2048], P('seq', 'exp'), may hold values from -2 to 2
- ffn_gain: bfloat16 [2048], P(('exp', 'seq')), may hold values from 0.099609375 to 1.8984375
- shared_gate: bfloat16 [2048, 2816], P('exp', 'seq'), may hold values from -0.125 to 0.125
- shared_up: bfloat16 [2048, 2816], P('exp', 'seq'), may hold values from -0.125 to 0.125
- shared_down: bfloat16 [2816, 2048], P('seq', 'exp'), may hold values from -0.109375 to 0.109375
- expert_gate: bfloat16 [64, 2048, 1408], P(('exp', 'seq')), may hold values from -0.125 to 0.125
- expert_up: bfloat16 [64, 2048, 1408], P(('exp', 'seq')), may hold values from -0.125 to 0.125
- expert_down: bfloat16 [64, 1408, 2048], P(('exp', 'seq')), may hold values from -0.15625 to 0.15625
- out_grad: bfloat16 [4096, 2048], P(('exp', 'seq')), may hold values from -6 to 6
Outputs:
- output: bfloat16 [4096, 2048], P(('exp', 'seq'))
- tokens_grad: bfloat16 [4096, 2048], P(('exp', 'seq'))
- norm_gain_grad: float32 [2048], P(('exp', 'seq'))
- w_query_grad: float32 [2048, 3072], P('exp', 'seq')
- w_kv_down_grad: float32 [2048, 576], P(('exp', 'seq'))
- latent_gain_grad: float32 [512], P(('exp', 'seq'))
- w_kv_up_grad: float32 [512, 4096], P('exp', 'seq')
- w_output_grad: float32 [2048, 2048], P('seq', 'exp')
- ffn_gain_grad: float32 [2048], P(('exp', 'seq'))
- shared_gate_grad: float32 [2048, 2816], P('exp', 'seq')
- shared_up_grad: float32 [2048, 2816], P('exp', 'seq')
- shared_down_grad: float32 [2816, 2048], P('seq', 'exp')
- expert_gate_grad: float32 [64, 2048, 1408], P(('exp', 'seq'))
- expert_up_grad: float32 [64, 2048, 1408], P(('exp', 'seq'))
- expert_down_grad: float32 [64, 1408, 2048], P(('exp', 'seq'))
The draws below stay inside these ranges and needn't reach their ends.
Inputs may be any that keep to these rules, and one draw needn't show every extreme that they name: `routes`: each token names 6 different experts. Among the 128 tokens of one device (aligned blocks of rows) no expert is named more than 16 times, a bound that some block reaches.
All inputs are finite; a program needn't handle non-finite values.
Results may differ from the reference program's by a relative error of at most 0.023.
Values may be sent and summed in bfloat16 or wider, within the bound.
No kernel may reach another device: no remote copies, remote signals or barrier semaphores. Data moves between devices by JAX's collectives and lax.ppermute only.
A program may use at most 448 MiB of HBM per device.

```python
import math
import jax
import jax.numpy as jnp
import numpy as np
from jax import lax

D = 2048
H = 16
DN = 128
DR = 64
DV = 128
R = 512
FF = 1408
SFF = 2816
EXPERTS = 64
TOP = 6
TOK_DEV = 128
LENGTH = 1024
TOKENS = 4096
CAP = 16
SPLITS = 1
FFP = 1408
EXP_ROWS = 64
N_EXP = 4


def shard_levels(stream_key, dims, cuts, smallest, largest):
    def one(dim, shards_of):
        steps = jax.random.uniform(jax.random.fold_in(jax.random.fold_in(stream_key, 6), dim), (shards_of,), jnp.float32, smallest / len(cuts), largest / len(cuts))
        return jnp.repeat(jnp.exp(steps), dims[dim] // shards_of).reshape((-1,) + (1,) * (len(dims) - dim - 1))

    gain = one(*cuts[0])
    for cut in cuts[1:]:
        gain = gain * one(*cut)
    return gain


def routed_block(own_key, own, number, rows, amount, top, most, slope):
    sequence = jax.random.permutation(own_key, amount)
    packed, common = shares(amount, rows * top, most, slope, True), shares(amount, rows * top, most, slope, False)
    places = jnp.arange(amount)

    def named(lengths, turn):
        used = int((lengths > 0).sum())
        fixed = max(1, used // 4)
        moved = fixed + (places - fixed + turn * (used - fixed)) % max(1, amount - fixed)
        return jnp.zeros((amount,), jnp.int32).at[sequence[jnp.where(places < fixed, places, moved)]].set(jnp.asarray(lengths, jnp.int32))

    lengths = jnp.where(number % 4 == 0, named(packed, number // 4), named(common, number - number // 4 - 1))
    mixed = jax.random.permutation(jax.random.fold_in(own, 3), amount)
    giver, sink = mixed[0:amount // 2 * 2:2], mixed[1:amount // 2 * 2:2]
    room = jnp.minimum(lengths[giver] - 1, most - lengths[sink]) // 2
    room = jnp.where((giver == sequence[0]) | (sink == sequence[0]) | (lengths[sink] == 0), 0, jnp.maximum(room, 0))
    moved = jax.random.randint(jax.random.fold_in(own, 4), (amount // 2,), 0, 1 << 20) % (room + 1)
    lengths = lengths.at[giver].add(-moved).at[sink].add(moved)
    items = jnp.searchsorted(jnp.cumsum(lengths), jnp.arange(rows * top), side="right").astype(jnp.int32)
    listing = items.reshape(top, rows).T
    listing = listing[jax.random.permutation(jax.random.fold_in(own, 1), rows)]
    turn = jax.random.randint(jax.random.fold_in(own, 2), (rows, 1), 0, top)
    return jnp.take_along_axis(listing, (jnp.arange(top)[None, :] + turn) % top, axis=1)


def shares(amount, total, most, skew, full):
    portions = [(1 << 20) // math.isqrt(rank ** skew) + 1 for rank in range(1, amount + 1)]
    largest = most if full else min(most, max(-(-total // amount), total * portions[0] // sum(portions)))
    least = 1 if total - largest >= amount - 1 else 0
    counts, rest = [largest] + [least] * (amount - 1), total - largest - least * (amount - 1)
    while rest > 0:
        free = [i for i in range(1, amount) if counts[i] < largest] or [i for i in range(1, amount) if counts[i] < most]
        mass, remaining = sum([portions[i] for i in free]), rest
        for i in free:
            extra = min(most - counts[i], max(1, remaining * portions[i] // mass), rest)
            counts[i] = counts[i] + extra
            rest = rest - extra
    return np.array(counts)


def scatter_about(stream_key, dims, spread, limit, pieces=(), kind=jnp.bfloat16):
    loudness = shard_levels(stream_key, dims, pieces, -0.22, 0.18) if pieces else 1.0
    entries = jax.random.normal(stream_key, dims, jnp.float32) * spread * loudness
    return jnp.minimum(jnp.maximum(entries, -limit), limit).astype(kind)


def setup_inputs(seed: int = 0) -> dict:
    streams_of = jax.random.split(jax.random.key(seed), 18)
    tokens = scatter_about(streams_of[0], (TOKENS, D), 1.0, 6.0, ((0, 32),))
    routes_keys = jax.random.split(jax.random.fold_in(streams_of[1], 1), TOKENS // TOK_DEV)
    routes_turns = jax.random.permutation(jax.random.fold_in(streams_of[1], 3), TOKENS // TOK_DEV)
    routes = jax.vmap(lambda own, number: routed_block(jax.random.fold_in(streams_of[1], 2), own, number, TOK_DEV, EXPERTS, TOP, CAP, 2))(routes_keys, routes_turns).reshape((TOKENS, TOP))
    route_weights = jnp.clip(0.2 + 0.8 * jax.random.uniform(streams_of[2], (TOKENS, TOP), jnp.float32) ** shard_levels(streams_of[2], (TOKENS, TOP), ((0, 32),), -0.2, 0.2), 0.2, 1.0)
    norm_gain = jnp.clip(1.0 + 0.18 * jax.random.normal(streams_of[3], (D,), jnp.float32), 0.099609375, 1.8984375).astype(jnp.bfloat16)
    w_query = scatter_about(streams_of[4], (D, H * (DN + DR)), D ** -0.5, 0.125, ((0, 4), (1, 8)))
    w_kv_down = scatter_about(streams_of[5], (D, R + DR), D ** -0.5, 0.125, ((0, 32),))
    latent_gain = jnp.clip(1.0 + 0.18 * jax.random.normal(streams_of[6], (R,), jnp.float32), 0.099609375, 1.8984375).astype(jnp.bfloat16)
    w_kv_up = scatter_about(streams_of[7], (R, H * (DN + DV)), R ** -0.5, 0.25, ((0, 4), (1, 8)))
    w_output = scatter_about(streams_of[8], (H * DV, D), (max(1, 4 * H * DV // LENGTH)) ** -0.5, 2.0, ((0, 8), (1, 4)))
    ffn_gain = jnp.clip(1.0 + 0.18 * jax.random.normal(streams_of[9], (D,), jnp.float32), 0.099609375, 1.8984375).astype(jnp.bfloat16)
    shared_gate = scatter_about(streams_of[10], (D, SFF), D ** -0.5, 0.125, ((0, 4), (1, 8)))
    shared_up = scatter_about(streams_of[11], (D, SFF), D ** -0.5, 0.125, ((0, 4), (1, 8)))
    shared_down = scatter_about(streams_of[12], (SFF, D), SFF ** -0.5, 0.109375, ((0, 8), (1, 4)))
    expert_gate = scatter_about(streams_of[13], (EXP_ROWS, D, FFP), D ** -0.5, 0.125, ((0, 32),))
    expert_up = scatter_about(streams_of[14], (EXP_ROWS, D, FFP), D ** -0.5, 0.125, ((0, 32),))
    expert_down = scatter_about(streams_of[15], (EXP_ROWS, FFP, D), FF ** -0.5, 0.15625, ((0, 32),))
    out_grad = scatter_about(streams_of[16], (TOKENS, D), 1.0, 6.0, ((0, 32),))
    return {"tokens": tokens, "routes": routes, "route_weights": route_weights, "norm_gain": norm_gain, "w_query": w_query, "w_kv_down": w_kv_down, "latent_gain": latent_gain, "w_kv_up": w_kv_up, "w_output": w_output, "ffn_gain": ffn_gain, "shared_gate": shared_gate, "shared_up": shared_up, "shared_down": shared_down, "expert_gate": expert_gate, "expert_up": expert_up, "expert_down": expert_down, "out_grad": out_grad}


eps_norm = 1e-06
rope_base = 50000.0

def rms_scale(values, scales):
    inverse = lax.rsqrt(lax.optimization_barrier(jnp.mean(values * values, axis=-1, keepdims=True)) + eps_norm)
    return values * inverse * scales

def rope_tables(positions, width):
    middle = width // 2
    frequency = rope_base ** (-(jnp.arange(middle, dtype=jnp.float32) * 2.0 / width))
    angles = positions.astype(jnp.float32)[:, None] * frequency[None, :]
    return (jnp.cos(angles), jnp.sin(angles))

def rotate(values, cosine_table, sine_table):
    middle = values.shape[-1] // 2
    leading = values[..., :middle]
    trailing = values[..., middle:]
    return jnp.concatenate([leading * cosine_table - trailing * sine_table, trailing * cosine_table + leading * sine_table], axis=-1)

def unrotate(values, cosine_table, sine_table):
    middle = values.shape[-1] // 2
    leading = values[..., :middle]
    trailing = values[..., middle:]
    return jnp.concatenate([leading * cosine_table + trailing * sine_table, trailing * cosine_table - leading * sine_table], axis=-1)

def silu_slope(gate_values):
    sigmoid = jax.nn.sigmoid(gate_values)
    return sigmoid * (1.0 + gate_values * (1.0 - sigmoid))

def causal_scores(query_head, key_head, factor):
    scores = jnp.dot(query_head, key_head.T, preferred_element_type=jnp.float32) * factor
    length = scores.shape[0]
    allowed = jnp.arange(length)[:, None] >= jnp.arange(length)[None, :]
    return jnp.where(allowed, scores, -1e+30)

def attend_head(query_head, key_head, value_head, factor):
    scores = causal_scores(query_head, key_head, factor)
    exponent = jnp.exp(scores)
    row_sum = lax.optimization_barrier(jnp.sum(exponent, axis=1, keepdims=True))
    weights_half = (exponent / row_sum).astype(jnp.bfloat16)
    result = jnp.dot(weights_half, value_head, preferred_element_type=jnp.float32).astype(jnp.bfloat16)
    return (result, jnp.log(row_sum)[:, 0])

def attend_back(query_head, key_head, value_head, result_head, result_grad, logsum, factor):
    scores = causal_scores(query_head, key_head, factor)
    probs_wide = jnp.exp(scores - logsum[:, None])
    probs_half = probs_wide.astype(jnp.bfloat16)
    value_grad = jnp.dot(probs_half.T, result_grad, preferred_element_type=jnp.float32)
    row_dot = lax.optimization_barrier(jnp.sum(result_grad.astype(jnp.float32) * result_head.astype(jnp.float32), axis=1, keepdims=True))
    probs_grad = jnp.dot(result_grad, value_head.T, preferred_element_type=jnp.float32)
    score_grad = (probs_wide * (probs_grad - row_dot) * factor).astype(jnp.bfloat16)
    query_grad = jnp.dot(score_grad, key_head, preferred_element_type=jnp.float32)
    key_grad = jnp.dot(score_grad.T, query_head, preferred_element_type=jnp.float32)
    return (query_grad.astype(jnp.bfloat16), key_grad.astype(jnp.bfloat16), value_grad.astype(jnp.bfloat16))

def by_head(rows):
    width = rows.shape[-1]
    return rows.reshape(N_EXP, LENGTH, H, width).transpose(0, 2, 1, 3).reshape(N_EXP * H, LENGTH, width)

def from_head(rows):
    width = rows.shape[-1]
    return rows.reshape(N_EXP, H, LENGTH, width).transpose(0, 2, 1, 3).reshape(TOKENS, H, width)

def reference(tokens, routes, route_weights, norm_gain, w_query, w_kv_down, latent_gain, w_kv_up, w_output, ffn_gain, shared_gate, shared_up, shared_down, expert_gate, expert_up, expert_down, out_grad):
    factor = 1.0 / math.sqrt(DN + DR)
    token_wide = tokens.astype(jnp.float32)
    gain_first = norm_gain.astype(jnp.float32)
    normed_one = rms_scale(token_wide, gain_first).astype(jnp.bfloat16)
    positions = jnp.arange(TOKENS, dtype=jnp.int32) % LENGTH
    cosine_table, sine_table = rope_tables(positions, DR)
    query_raw = jnp.dot(normed_one, w_query, preferred_element_type=jnp.float32).reshape(TOKENS, H, DN + DR)
    query_rows = jnp.concatenate([query_raw[..., :DN], rotate(query_raw[..., DN:], cosine_table[:, None, :], sine_table[:, None, :])], axis=-1).astype(jnp.bfloat16)
    down_raw = jnp.dot(normed_one, w_kv_down, preferred_element_type=jnp.float32)
    latent_raw = down_raw[:, :R]
    rope_key = rotate(down_raw[:, R:], cosine_table, sine_table).astype(jnp.bfloat16)
    latent_wide = latent_gain.astype(jnp.float32)
    latent_rows = rms_scale(latent_raw, latent_wide).astype(jnp.bfloat16)
    up_raw = jnp.dot(latent_rows, w_kv_up, preferred_element_type=jnp.float32).reshape(TOKENS, H, DN + DV)
    key_rows = jnp.concatenate([up_raw[..., :DN].astype(jnp.bfloat16), jnp.broadcast_to(rope_key[:, None, :], (TOKENS, H, DR))], axis=-1)
    value_rows = up_raw[..., DN:].astype(jnp.bfloat16)
    query_heads = by_head(query_rows)
    key_heads = by_head(key_rows)
    value_heads = by_head(value_rows)
    result_heads, logsums = lax.map(lambda operands: attend_head(operands[0], operands[1], operands[2], factor), (query_heads, key_heads, value_heads))
    attention_rows = from_head(result_heads).reshape(TOKENS, H * DV)
    residual = token_wide + jnp.dot(attention_rows, w_output, preferred_element_type=jnp.float32)
    gain_second = ffn_gain.astype(jnp.float32)
    normed_two = rms_scale(residual, gain_second).astype(jnp.bfloat16)
    shared_gate_raw = jnp.dot(normed_two, shared_gate, preferred_element_type=jnp.float32)
    shared_up_raw = jnp.dot(normed_two, shared_up, preferred_element_type=jnp.float32)
    shared_hidden = (jax.nn.silu(shared_gate_raw) * shared_up_raw).astype(jnp.bfloat16)
    shared_out = jnp.dot(shared_hidden, shared_down, preferred_element_type=jnp.float32)
    blocks = TOKENS // TOK_DEV
    block_expert = routes.reshape(blocks, TOK_DEV * TOP)
    onehot = (block_expert[:, :, None] == jnp.arange(EXPERTS, dtype=jnp.int32)[None, None, :]).astype(jnp.int32)
    earlier = jnp.cumsum(onehot, axis=1) - onehot
    slot_within = lax.optimization_barrier(jnp.sum(earlier * onehot, axis=2))
    global_slot = (slot_within + jnp.arange(blocks, dtype=jnp.int32)[:, None] * CAP).reshape(-1)
    flat_expert = block_expert.reshape(-1)
    flat_token = jnp.arange(TOKENS * TOP, dtype=jnp.int32) // TOP
    flat_weight = route_weights.reshape(-1)
    slots_all = blocks * CAP
    grad_wide = out_grad.astype(jnp.float32)

    def per_expert(totals, expert):
        routed, routed_grad = totals
        place_slot = jnp.where(flat_expert == expert, global_slot, slots_all)
        token_at = jnp.zeros((slots_all,), jnp.int32).at[place_slot].set(flat_token, mode='drop')
        weight_at = jnp.zeros((slots_all,), jnp.float32).at[place_slot].set(flat_weight, mode='drop')
        live_at = jnp.zeros((slots_all,), jnp.float32).at[place_slot].set(1.0, mode='drop')
        rows_in = jnp.where(live_at[:, None] > 0, normed_two[token_at], jnp.zeros((), jnp.bfloat16))
        cot_rows = (weight_at[:, None] * grad_wide[token_at]).astype(jnp.bfloat16)
        out_sum = jnp.zeros((slots_all, D), jnp.float32)
        in_sum = jnp.zeros((slots_all, D), jnp.float32)
        gate_list = []
        up_list = []
        down_list = []
        for part_number in range(SPLITS):
            row_index = expert * SPLITS + part_number
            gate_part = expert_gate[row_index]
            up_part = expert_up[row_index]
            down_part = expert_down[row_index]
            gate_raw = jnp.dot(rows_in, gate_part, preferred_element_type=jnp.float32)
            up_raw_rows = jnp.dot(rows_in, up_part, preferred_element_type=jnp.float32)
            hidden = (jax.nn.silu(gate_raw) * up_raw_rows).astype(jnp.bfloat16)
            result = jnp.dot(hidden, down_part, preferred_element_type=jnp.float32).astype(jnp.bfloat16)
            out_sum = out_sum + result.astype(jnp.float32)
            down_list.append(jnp.dot(hidden.T, cot_rows, preferred_element_type=jnp.float32))
            hidden_grad = jnp.dot(cot_rows, down_part.T, preferred_element_type=jnp.float32)
            gate_rows_grad = (hidden_grad * up_raw_rows * silu_slope(gate_raw)).astype(jnp.bfloat16)
            up_rows_grad = (hidden_grad * jax.nn.silu(gate_raw)).astype(jnp.bfloat16)
            gate_list.append(jnp.dot(rows_in.T, gate_rows_grad, preferred_element_type=jnp.float32))
            up_list.append(jnp.dot(rows_in.T, up_rows_grad, preferred_element_type=jnp.float32))
            input_grad = (jnp.dot(gate_rows_grad, gate_part.T, preferred_element_type=jnp.float32) + jnp.dot(up_rows_grad, up_part.T, preferred_element_type=jnp.float32)).astype(jnp.bfloat16)
            in_sum = in_sum + input_grad.astype(jnp.float32)
        routed = routed.at[token_at].add(weight_at[:, None] * out_sum)
        routed_grad = routed_grad.at[token_at].add(live_at[:, None] * in_sum)
        return ((routed, routed_grad), (jnp.stack(gate_list), jnp.stack(up_list), jnp.stack(down_list)))
    start_totals = (jnp.zeros((TOKENS, D), jnp.float32), jnp.zeros((TOKENS, D), jnp.float32))
    (routed, routed_grad), (gate_grads, up_grads, down_grads) = lax.scan(per_expert, start_totals, jnp.arange(EXPERTS, dtype=jnp.int32))
    expert_gate_grad = gate_grads.reshape(EXPERTS * SPLITS, D, expert_gate.shape[2])
    expert_up_grad = up_grads.reshape(EXPERTS * SPLITS, D, expert_gate.shape[2])
    expert_down_grad = down_grads.reshape(EXPERTS * SPLITS, expert_gate.shape[2], D)
    output = (residual + shared_out + routed).astype(jnp.bfloat16)
    shared_hidden_grad = jnp.dot(out_grad, shared_down.T, preferred_element_type=jnp.float32)
    shared_down_grad = jnp.dot(shared_hidden.T, out_grad, preferred_element_type=jnp.float32)
    sgate_grad = (shared_hidden_grad * shared_up_raw * silu_slope(shared_gate_raw)).astype(jnp.bfloat16)
    sup_grad = (shared_hidden_grad * jax.nn.silu(shared_gate_raw)).astype(jnp.bfloat16)
    shared_gate_grad = jnp.dot(normed_two.T, sgate_grad, preferred_element_type=jnp.float32)
    shared_up_grad = jnp.dot(normed_two.T, sup_grad, preferred_element_type=jnp.float32)
    normed_two_grad = jnp.dot(sgate_grad, shared_gate.T, preferred_element_type=jnp.float32) + jnp.dot(sup_grad, shared_up.T, preferred_element_type=jnp.float32) + routed_grad
    _, pullback_two = jax.vjp(rms_scale, residual, gain_second)
    residual_norm_grad, ffn_gain_grad = pullback_two(normed_two_grad)
    residual_grad = grad_wide + residual_norm_grad
    residual_half = residual_grad.astype(jnp.bfloat16)
    w_output_grad = jnp.dot(attention_rows.T, residual_half, preferred_element_type=jnp.float32)
    attention_grad = jnp.dot(residual_half, w_output.T, preferred_element_type=jnp.float32).astype(jnp.bfloat16).reshape(TOKENS, H, DV)
    query_grad_heads, key_grad_heads, value_grad_heads = lax.map(lambda operands: attend_back(operands[0], operands[1], operands[2], operands[3], operands[4], operands[5], factor), (query_heads, key_heads, value_heads, result_heads, by_head(attention_grad), logsums))
    query_grad_rows = from_head(query_grad_heads)
    key_grad_rows = from_head(key_grad_heads)
    value_grad_rows = from_head(value_grad_heads)
    kv_grad = jnp.concatenate([key_grad_rows[..., :DN], value_grad_rows], axis=-1).reshape(TOKENS, H * (DN + DV))
    w_kv_up_grad = jnp.dot(latent_rows.T, kv_grad, preferred_element_type=jnp.float32)
    latent_grad = jnp.dot(kv_grad, w_kv_up.T, preferred_element_type=jnp.float32)
    rope_key_grad = lax.optimization_barrier(jnp.sum(key_grad_rows[..., DN:].astype(jnp.float32), axis=1))
    query_in_grad = jnp.concatenate([query_grad_rows[..., :DN].astype(jnp.float32), unrotate(query_grad_rows[..., DN:].astype(jnp.float32), cosine_table[:, None, :], sine_table[:, None, :])], axis=-1).reshape(TOKENS, H * (DN + DR)).astype(jnp.bfloat16)
    w_query_grad = jnp.dot(normed_one.T, query_in_grad, preferred_element_type=jnp.float32)
    _, pullback_latent = jax.vjp(rms_scale, latent_raw, latent_wide)
    latent_raw_grad, latent_gain_grad = pullback_latent(latent_grad)
    down_grad_rows = jnp.concatenate([latent_raw_grad, unrotate(rope_key_grad, cosine_table, sine_table)], axis=-1).astype(jnp.bfloat16)
    w_kv_down_grad = jnp.dot(normed_one.T, down_grad_rows, preferred_element_type=jnp.float32)
    normed_one_grad = jnp.dot(query_in_grad, w_query.T, preferred_element_type=jnp.float32) + jnp.dot(down_grad_rows, w_kv_down.T, preferred_element_type=jnp.float32)
    _, pullback_one = jax.vjp(rms_scale, token_wide, gain_first)
    token_norm_grad, norm_gain_grad = pullback_one(normed_one_grad)
    tokens_grad = (residual_grad + token_norm_grad).astype(jnp.bfloat16)
    return (output, tokens_grad, norm_gain_grad, w_query_grad, w_kv_down_grad, latent_gain_grad, w_kv_up_grad, w_output_grad, ffn_gain_grad, shared_gate_grad, shared_up_grad, shared_down_grad, expert_gate_grad, expert_up_grad, expert_down_grad)
```

```python
import math

import jax
import jax.numpy as jnp
from jax import lax
from jax.sharding import PartitionSpec as P

H = 16
DN = 128
DR = 64
DV = 128
R = 512
EXPERTS = 64
TOP = 6
CAP = 16


eps_norm = 1e-06
rope_base = 50000.0
BF = jnp.bfloat16
F32 = jnp.float32


def dot(a, b):
    return jnp.dot(a, b, preferred_element_type=F32)


def dot_t(a, b):
    return lax.dot_general(a, b, (((1,), (1,)), ((), ())), preferred_element_type=F32)


def t_dot(a, b):
    return lax.dot_general(a, b, (((0,), (0,)), ((), ())), preferred_element_type=F32)


def rope_tables(positions, width):
    middle = width // 2
    frequency = rope_base ** (-(jnp.arange(middle, dtype=F32) * 2.0 / width))
    angles = positions.astype(F32)[:, None] * frequency[None, :]
    return (jnp.cos(angles), jnp.sin(angles))


def rotate(values, cosine_table, sine_table):
    middle = values.shape[-1] // 2
    leading = values[..., :middle]
    trailing = values[..., middle:]
    return jnp.concatenate(
        [
            leading * cosine_table - trailing * sine_table,
            trailing * cosine_table + leading * sine_table,
        ],
        axis=-1,
    )


def silu_slope(gate_values):
    sigmoid = jax.nn.sigmoid(gate_values)
    return sigmoid * (1.0 + gate_values * (1.0 - sigmoid))


def norm_back(dy, v, inverse, gain):
    hat = v * inverse
    scaled = dy * gain
    dv = inverse * (scaled - hat * jnp.mean(scaled * hat, axis=-1, keepdims=True))
    return dv, dy * hat


def inverse_rms(v):
    return lax.rsqrt(jnp.mean(v * v, axis=-1, keepdims=True) + eps_norm)


def swap(x, axis, mask):
    n = lax.axis_size(axis)
    return lax.ppermute(x, axis, [(i, i ^ mask) for i in range(n)])


def after(x, *earlier):
    return lax.optimization_barrier((x, *earlier))[0]


class Lane:
    def __init__(self, axis, depth):
        self.axis = axis
        self.depth = depth
        self.sent = []

    def send(self, x, mask):
        if len(self.sent) >= self.depth:
            x = after(x, self.sent[-self.depth])
        got = swap(x, self.axis, mask)
        self.sent.append(got)
        return got

    def chips(self, x):
        chips = lax.axis_size("seq") // 2
        return [x] + [self.send(x, 2 * k) for k in range(1, chips)]

    def group(self, x):
        evens = self.chips(x)
        return evens + [swap(b, "seq", 1) for b in evens]

    def scatter(self, even, odd):
        chips = lax.axis_size("seq") // 2
        rows = even.shape[0] // chips
        got = swap(odd.astype(BF), "seq", 1)
        blocks = [
            even[k * rows : (k + 1) * rows] + got[k * rows : (k + 1) * rows].astype(F32)
            for k in range(chips)
        ]
        total = blocks[0]
        for k in range(1, chips):
            total = total + self.send(blocks[k].astype(BF), 2 * k).astype(F32)
        return total

    def stack(self, x):
        n = lax.axis_size("exp")
        me = lax.axis_index("exp")
        out = jnp.zeros((n, *x.shape), x.dtype)
        for j in range(n):
            block = x if j == 0 else self.send(x, j)
            out = lax.dynamic_update_slice_in_dim(out, block[None], me ^ j, 0)
        return out

    def sum_stack(self, x):
        n = lax.axis_size("exp")
        me = lax.axis_index("exp")
        total = lax.dynamic_index_in_dim(x, me, 0, keepdims=False)
        for j in range(1, n):
            piece = lax.dynamic_index_in_dim(x, me ^ j, 0, keepdims=False).astype(BF)
            total = total + self.send(piece, j).astype(F32)
        return total


def relative_order(count):
    chips = count // 2
    return [2 * k for k in range(chips)] + [2 * k + 1 for k in range(chips)]


def scatter_small(x):
    for axis in ("exp", "seq"):
        n = lax.axis_size(axis)
        me = lax.axis_index(axis)
        total = lax.dynamic_index_in_dim(x, me, 0, keepdims=False)
        for j in range(1, n):
            piece = lax.dynamic_index_in_dim(x, me ^ j, 0, keepdims=False)
            total = total + swap(piece, axis, j)
        x = total
    return x


def columns_first(x, blocks):
    rows, columns = x.shape
    return x.reshape(rows, blocks, columns // blocks).transpose(1, 0, 2)


def columns_last(x):
    blocks, rows, w = x.shape
    return x.transpose(1, 0, 2).reshape(rows, blocks * w)


def shards(
    tokens,
    routes,
    route_weights,
    norm_gain,
    w_query,
    w_kv_down,
    latent_gain,
    w_kv_up,
    w_output,
    ffn_gain,
    shared_gate,
    shared_up,
    shared_down,
    expert_gate,
    expert_up,
    expert_down,
    out_grad,
):
    count, width = tokens.shape
    n_seq = lax.axis_size("seq")
    n_exp = lax.axis_size("exp")
    seq = lax.axis_index("seq")
    order = relative_order(n_seq)
    place = {r: p for p, r in enumerate(order)}
    chips = n_seq // 2
    heads = H // n_seq
    length = count * n_seq
    half = length // 2
    pieces = expert_gate.shape[0]
    parts_per = pieces * n_seq * n_exp // EXPERTS
    factor = 1.0 / math.sqrt(DN + DR)
    gain_rows = norm_gain.shape[0]
    latent_rows_local = latent_gain.shape[0]
    along = Lane("seq", 3)
    across = Lane("exp", 2)

    packed = jnp.concatenate(
        [
            w_kv_down,
            norm_gain[:, None],
            ffn_gain[:, None],
            jnp.pad(latent_gain, (0, gain_rows - latent_rows_local))[:, None],
            jnp.zeros((gain_rows, 61), BF),
        ],
        axis=1,
    )
    packed_even = jnp.stack(along.chips(packed))
    query_stack = across.stack(w_query)
    token_blocks = along.group(tokens)
    packed_even = across.stack(packed_even)
    packed_odd = swap(packed_even, "seq", 1)
    up_stack = across.stack(w_kv_up)
    route_pack = jnp.concatenate([routes.astype(F32).T, route_weights.T], axis=0)
    route_blocks = along.group(route_pack)
    output_even = jnp.concatenate(along.chips(w_output), axis=0)
    output_even = across.stack(output_even)
    output_odd = swap(output_even, "seq", 1)
    shared_stack = across.stack(jnp.stack([shared_gate, shared_up]))
    grad_blocks = along.group(out_grad)
    drop_stack = across.stack(shared_down)

    packed_all = jnp.zeros((n_exp, n_seq, gain_rows, packed.shape[1]), BF)
    for p in range(n_seq):
        block = packed_even[:, p] if p < chips else packed_odd[:, p - chips]
        packed_all = lax.dynamic_update_slice_in_dim(
            packed_all, block[:, None], seq ^ order[p], 1
        )
    packed_all = packed_all.reshape(width, packed.shape[1])
    query_cols = query_stack.reshape(width, w_query.shape[1])
    up_cols = up_stack.reshape(R, w_kv_up.shape[1])
    output_full = jnp.concatenate([columns_last(output_even), columns_last(output_odd)], axis=0)
    gate_cols = shared_stack[:, 0].reshape(width, shared_gate.shape[1])
    lift_cols = shared_stack[:, 1].reshape(width, shared_up.shape[1])
    drop_rows = columns_last(drop_stack)
    down_full = packed_all[:, : R + DR]
    gain_first = packed_all[:, R + DR].astype(F32)
    gain_second = packed_all[:, R + DR + 1].astype(F32)
    latent_wide = (
        packed_all[:, R + DR + 2]
        .reshape(n_exp * n_seq, gain_rows)[:, :latent_rows_local]
        .reshape(R)
        .astype(F32)
    )

    token_all = lax.optimization_barrier(jnp.concatenate(token_blocks, axis=0))
    token_wide = token_all.astype(F32)
    inverse_one = inverse_rms(token_wide)
    normed_one = (token_wide * inverse_one * gain_first).astype(BF)
    positions = jnp.concatenate(
        [(seq ^ r) * count + jnp.arange(count, dtype=jnp.int32) for r in order]
    )
    cosine_table, sine_table = rope_tables(positions, DR)
    allowed = positions[:, None] >= positions[None, :]
    query_raw = dot(normed_one, query_cols)
    down_raw = dot(normed_one, down_full)
    latent_raw = down_raw[:, :R]
    rope_key = rotate(down_raw[:, R:], cosine_table, sine_table).astype(BF)
    inverse_latent = inverse_rms(latent_raw)
    latent_all = (latent_raw * inverse_latent * latent_wide).astype(BF)
    up_raw = dot(latent_all, up_cols).astype(BF)
    query_heads, key_heads, value_heads = [], [], []
    for n in range(heads):
        own = query_raw[:, n * (DN + DR) : (n + 1) * (DN + DR)]
        query_heads.append(
            jnp.concatenate(
                [own[:, :DN], rotate(own[:, DN:], cosine_table, sine_table)], axis=1
            ).astype(BF)
        )
        own = up_raw[:, n * (DN + DV) : (n + 1) * (DN + DV)]
        key_heads.append(jnp.concatenate([own[:, :DN], rope_key], axis=1))
        value_heads.append(own[:, DN:])
    results, logsums = [], []
    for n in range(heads):
        scores = jnp.where(allowed, dot_t(query_heads[n], key_heads[n]) * factor, -1e30)
        exponent = jnp.exp(scores)
        row_sum = jnp.sum(exponent, axis=1, keepdims=True)
        results.append(dot((exponent / row_sum).astype(BF), value_heads[n]).astype(BF))
        logsums.append(jnp.log(row_sum))
    result = jnp.concatenate(results, axis=1)

    result_blocks = along.group(result)
    aligned = []
    for q, block in enumerate(result_blocks):
        aligned.append(
            jnp.concatenate(
                [
                    block[place[order[q] ^ r] * count : (place[order[q] ^ r] + 1) * count]
                    for r in order
                ],
                axis=0,
            )
        )
    attention = jnp.concatenate(aligned, axis=1)
    residual = token_wide + dot(attention, output_full)
    inverse_two = inverse_rms(residual)
    normed_two = (residual * inverse_two * gain_second).astype(BF)

    column = jnp.stack(
        [
            ((other * n_seq + seq) * pieces + i) // parts_per
            for i in range(pieces)
            for other in range(n_exp)
        ]
    )
    kinds = n_exp * pieces
    route_all = jnp.stack(route_blocks)
    named = route_all[:, None, :TOP, :].astype(jnp.int32) == column[None, :, None, None]
    matched = jnp.any(named, axis=2)
    match_weight = jnp.sum(jnp.where(named, route_all[:, None, TOP:, :], 0.0), axis=2)
    earlier = (jnp.arange(count)[:, None] < jnp.arange(count)[None, :]).astype(BF)
    rank = jnp.dot(matched.astype(BF), earlier, preferred_element_type=F32).astype(jnp.int32)
    chosen = (rank[:, :, None, :] == jnp.arange(CAP, dtype=jnp.int32)[None, None, :, None]) & (
        matched[:, :, None, :]
    )
    select = chosen.astype(BF).reshape(n_seq, kinds * CAP, count)
    weighted = jnp.where(chosen, match_weight[:, :, None, :], 0.0).reshape(
        n_seq, kinds * CAP, count
    )
    slot_weight = jnp.sum(weighted, axis=2, keepdims=True)
    weighted_high = weighted.astype(BF)
    weighted_low = (weighted - weighted_high.astype(F32)).astype(BF)

    def spread(rows):
        shaped = rows.reshape(n_seq, pieces, n_exp, CAP, width).transpose(1, 2, 0, 3, 4)
        return [give(shaped[i].reshape(n_exp, n_seq * CAP, width)) for i in range(pieces)]

    def give(rows):
        return lax.all_to_all(rows, "exp", split_axis=0, concat_axis=0, tiled=True)

    def join(parts):
        shaped = jnp.stack(parts).reshape(pieces, n_exp, n_seq, CAP, width)
        return shaped.transpose(2, 0, 1, 3, 4).reshape(n_seq, kinds * CAP, width)

    grad_all = jnp.stack(grad_blocks)
    cot_rows = (
        jnp.einsum("bst,btd->bsd", select, grad_all, preferred_element_type=F32) * slot_weight
    ).astype(BF)
    received_grad = spread(cot_rows)
    send_rows = jnp.einsum(
        "bst,btd->bsd",
        select,
        normed_two.reshape(n_seq, count, width),
        preferred_element_type=F32,
    ).astype(BF)
    received = spread(send_rows)

    results_back, grads_back, gate_grads, up_grads, down_grads = [], [], [], [], []
    for i in range(pieces):
        rows = received[i].reshape(n_exp * n_seq * CAP, width)
        cots = received_grad[i].reshape(n_exp * n_seq * CAP, width)
        hidden_grad = dot_t(cots, expert_down[i])
        gate_raw = dot(rows, expert_gate[i])
        lift_raw = dot(rows, expert_up[i])
        expert_hidden = (jax.nn.silu(gate_raw) * lift_raw).astype(BF)
        gate_rows_grad = (hidden_grad * lift_raw * silu_slope(gate_raw)).astype(BF)
        up_rows_grad = (hidden_grad * jax.nn.silu(gate_raw)).astype(BF)
        input_grad = (
            dot_t(gate_rows_grad, expert_gate[i]) + dot_t(up_rows_grad, expert_up[i])
        ).astype(BF)
        grads_back.append(give(input_grad.reshape(n_exp, n_seq * CAP, width)))
        expert_result = dot(expert_hidden, expert_down[i]).astype(BF)
        results_back.append(give(expert_result.reshape(n_exp, n_seq * CAP, width)))
        down_grads.append(t_dot(expert_hidden, cots))
        gate_grads.append(t_dot(rows, gate_rows_grad))
        up_grads.append(t_dot(rows, up_rows_grad))
    expert_gate_grad = jnp.stack(gate_grads)
    expert_up_grad = jnp.stack(up_grads)
    expert_down_grad = jnp.stack(down_grads)
    returned_grad = join(grads_back)
    routed_grad = jnp.einsum(
        "bst,bsd->btd", select, returned_grad, preferred_element_type=F32
    ).reshape(length, width)

    grad_rows = grad_all.reshape(length, width)
    shared_gate_raw = dot(normed_two, gate_cols)
    shared_up_raw = dot(normed_two, lift_cols)
    shared_hidden = (jax.nn.silu(shared_gate_raw) * shared_up_raw).astype(BF)
    shared_hidden_grad = dot_t(grad_rows, drop_rows)
    sgate_grad = (shared_hidden_grad * shared_up_raw * silu_slope(shared_gate_raw)).astype(BF)
    sup_grad = (shared_hidden_grad * jax.nn.silu(shared_gate_raw)).astype(BF)
    two_part = dot_t(sgate_grad, gate_cols) + dot_t(sup_grad, lift_cols) + routed_grad
    two_grad = along.scatter(two_part[:half], two_part[half:])
    shared_grad_stack = jnp.stack(
        [
            t_dot(normed_two, sgate_grad).reshape(n_exp, width // n_exp, -1),
            t_dot(normed_two, sup_grad).reshape(n_exp, width // n_exp, -1),
        ],
        axis=1,
    )

    residual_norm_grad, second_terms = norm_back(
        two_grad, residual[:count], inverse_two[:count], gain_second
    )
    residual_grad = out_grad.astype(F32) + residual_norm_grad
    residual_half = residual_grad.astype(BF)
    all_heads = dot_t(residual_half, output_full).astype(BF)
    wide = heads * DV
    pairs = [
        jnp.stack(
            [
                all_heads[:, k * wide : (k + 1) * wide],
                all_heads[:, (chips + k) * wide : (chips + k + 1) * wide],
            ]
        )
        for k in range(chips)
    ]
    pairs = [pairs[0]] + [along.send(pairs[k], 2 * k) for k in range(1, chips)]
    other_half = swap(jnp.stack([pair[1] for pair in pairs]), "seq", 1)
    attention_grad = jnp.concatenate(
        [jnp.stack([pair[0] for pair in pairs]), other_half], axis=0
    ).reshape(length, wide)
    half_all = along.group(residual_half)

    returned = join(results_back)
    routed = (
        jnp.einsum("bst,bsd->btd", weighted_high, returned, preferred_element_type=F32)
        + jnp.einsum("bst,bsd->btd", weighted_low, returned, preferred_element_type=F32)
    ).reshape(length, width)
    out_part = dot(shared_hidden, drop_rows) + routed

    query_grads, kv_grads, rope_part = [], [], 0.0
    for n in range(heads):
        own = attention_grad[:, n * DV : (n + 1) * DV]
        scores = jnp.where(allowed, dot_t(query_heads[n], key_heads[n]) * factor, -1e30)
        probs_wide = jnp.exp(scores - logsums[n])
        value_grad = t_dot(probs_wide.astype(BF), own).astype(BF)
        row_dot = jnp.sum(own.astype(F32) * results[n].astype(F32), axis=1, keepdims=True)
        probs_grad = dot_t(own, value_heads[n])
        score_grad = (probs_wide * (probs_grad - row_dot) * factor).astype(BF)
        query_grad = dot(score_grad, key_heads[n]).astype(BF).astype(F32)
        key_grad = t_dot(score_grad, query_heads[n]).astype(BF)
        query_grads += [query_grad[:, :DN], rotate(query_grad[:, DN:], cosine_table, -sine_table)]
        kv_grads += [key_grad[:, :DN], value_grad]
        rope_part = rope_part + key_grad[:, DN:].astype(F32)
    query_in_grad = jnp.concatenate(query_grads, axis=1).astype(BF)
    kv_grad = jnp.concatenate(kv_grads, axis=1)
    latent_part = jnp.concatenate([dot_t(kv_grad, up_cols), rope_part], axis=1)
    latent_grad = along.scatter(latent_part[:half], latent_part[half:])
    one_part = dot_t(query_in_grad, query_cols)
    one_grad = along.scatter(one_part[:half], one_part[half:])
    latent_raw_grad, latent_terms = norm_back(
        latent_grad[:, :R], latent_raw[:count], inverse_latent[:count], latent_wide
    )
    down_rows = jnp.concatenate(
        [
            latent_raw_grad,
            rotate(latent_grad[:, R:], cosine_table[:count], -sine_table[:count]),
        ],
        axis=1,
    ).astype(BF)
    down_rows_all = jnp.concatenate(along.group(down_rows), axis=0)
    output = (residual[:count] + along.scatter(out_part[:half], out_part[half:])).astype(BF)

    shared_out = across.sum_stack(shared_grad_stack)
    drop_out = across.sum_stack(columns_first(t_dot(shared_hidden, grad_rows), n_exp))
    output_out = across.sum_stack(
        columns_first(t_dot(result, jnp.concatenate(half_all, axis=0)), n_exp)
    )
    up_out = across.sum_stack(t_dot(latent_all, kv_grad).reshape(n_exp, R // n_exp, -1))
    query_out = across.sum_stack(
        t_dot(normed_one, query_in_grad).reshape(n_exp, width // n_exp, -1)
    )
    mine = lax.dynamic_slice_in_dim(
        normed_one.reshape(length, n_exp, n_seq * gain_rows), seq * gain_rows, gain_rows, 2
    ).reshape(length, n_exp * gain_rows)
    down_out = across.sum_stack(t_dot(mine, down_rows_all).reshape(n_exp, gain_rows, -1))

    down_back = dot_t(down_rows, down_full)
    one_hat = token_wide * inverse_one
    first_sum = jnp.sum(one_part * one_hat, axis=0) + jnp.sum(down_back * one_hat[:count], axis=0)
    token_norm_grad, _ = norm_back(
        one_grad + down_back, token_wide[:count], inverse_one[:count], gain_first
    )
    tokens_grad = (residual_grad + token_norm_grad).astype(BF)
    small = scatter_small(
        jnp.concatenate(
            [
                first_sum.reshape(n_exp, n_seq, gain_rows),
                jnp.sum(second_terms, axis=0).reshape(n_exp, n_seq, gain_rows),
                jnp.sum(latent_terms, axis=0).reshape(n_exp, n_seq, latent_rows_local),
            ],
            axis=2,
        )
    )
    return (
        output,
        tokens_grad,
        small[:gain_rows],
        query_out,
        down_out,
        small[2 * gain_rows :],
        up_out,
        output_out,
        small[gain_rows : 2 * gain_rows],
        shared_out[0],
        shared_out[1],
        drop_out,
        expert_gate_grad,
        expert_up_grad,
        expert_down_grad,
    )


def solution(mesh):
    rows = P(("exp", "seq"), None)
    line = P(("exp", "seq"))
    grid = P("exp", "seq")
    turned = P("seq", "exp")
    part = P(("exp", "seq"), None, None)
    return jax.shard_map(
        shards,
        mesh=mesh,
        in_specs=(
            rows,
            rows,
            rows,
            line,
            grid,
            rows,
            line,
            grid,
            turned,
            line,
            grid,
            grid,
            turned,
            part,
            part,
            part,
            rows,
        ),
        out_specs=(
            rows,
            rows,
            line,
            grid,
            rows,
            line,
            grid,
            turned,
            line,
            grid,
            grid,
            turned,
            part,
            part,
            part,
        ),
        check_vma=False,
    )
```

```python
import math

import jax
import jax.numpy as jnp
from jax import lax
from jax.experimental import pallas as pl
from jax.experimental.pallas import tpu as pltpu
from jax.sharding import PartitionSpec as P

H = 16
DN = 128
DR = 64
DV = 128
R = 512
EXPERTS = 64
TOP = 6
CAP = 16


eps_norm = 1e-06
rope_base = 50000.0
BF = jnp.bfloat16
F32 = jnp.float32


def dot(a, b):
    return jnp.dot(a, b, preferred_element_type=F32)


def dot_t(a, b):
    return lax.dot_general(a, b, (((1,), (1,)), ((), ())), preferred_element_type=F32)


def t_dot(a, b):
    return lax.dot_general(a, b, (((0,), (0,)), ((), ())), preferred_element_type=F32)


def rope_tables(positions, width):
    middle = width // 2
    frequency = rope_base ** (-(jnp.arange(middle, dtype=F32) * 2.0 / width))
    angles = positions.astype(F32)[:, None] * frequency[None, :]
    return (jnp.cos(angles), jnp.sin(angles))


def rotate(values, cosine_table, sine_table):
    middle = values.shape[-1] // 2
    leading = values[..., :middle]
    trailing = values[..., middle:]
    return jnp.concatenate(
        [
            leading * cosine_table - trailing * sine_table,
            trailing * cosine_table + leading * sine_table,
        ],
        axis=-1,
    )


def silu_slope(gate_values):
    sigmoid = jax.nn.sigmoid(gate_values)
    return sigmoid * (1.0 + gate_values * (1.0 - sigmoid))


def norm_back(dy, v, inverse, gain):
    hat = v * inverse
    scaled = dy * gain
    dv = inverse * (scaled - hat * jnp.mean(scaled * hat, axis=-1, keepdims=True))
    return dv, dy * hat


def inverse_rms(v):
    return lax.rsqrt(jnp.mean(v * v, axis=-1, keepdims=True) + eps_norm)


LIMIT = 56 * 1024 * 1024
ANY = pl.BlockSpec(memory_space=pl.ANY)
SCALARS = pl.BlockSpec(memory_space=pltpu.SMEM)


def whole(shape):
    return pl.BlockSpec(shape, lambda *grid: (0,) * len(shape))


def arrange(index, blocks, outs, plan):
    def kernel(index_ref, *refs):
        sources = refs[: len(blocks)]
        targets = refs[len(blocks) :]
        for block, source, out, target in plan:
            targets[out][target(index_ref)] = sources[block][source]

    size = sum(math.prod(s) * 2 for s in outs)
    return pl.pallas_call(
        kernel,
        out_shape=[jax.ShapeDtypeStruct(s, BF) for s in outs],
        in_specs=[SCALARS] + [pl.BlockSpec(memory_space=pltpu.VMEM)] * len(blocks),
        out_specs=[pl.BlockSpec(memory_space=pltpu.VMEM)] * len(outs),
        compiler_params=pltpu.CompilerParams(vmem_limit_bytes=LIMIT),
        cost_estimate=pl.CostEstimate(flops=0, transcendentals=0, bytes_accessed=2 * size),
        name="arrange",
    )(index, *blocks)


def span(start, size):
    return pl.ds(pl.multiple_of(start * size, size), size)


def turned(v, cosine, sine):
    middle = v.shape[1] // 2
    return v * cosine + jnp.concatenate([v[:, middle:], v[:, :middle]], axis=1) * sine


def project(index, chip, pair, gain, w_query, w_down, latent_gain, w_up, cosine, sine, heads, length, earlier):
    count, width = pair[0].shape
    wide = DN + DR
    many = len(w_query)
    kept = list(earlier or ())
    query_rows = w_query[0].shape[0]

    def kernel(index_ref, a_ref, b_ref, g_ref, wd_ref, lg_ref, *refs):
        wq_refs = refs[:many]
        wu_ref, c_ref, s_ref = refs[many : many + 3]
        n_ref, l_ref, r_ref, q_ref, k_ref, v_ref = refs[many + 3 + len(kept) :]
        me = index_ref[0]
        x = jnp.where(pl.program_id(0) == 0, a_ref[...], b_ref[...]).astype(F32)
        inverse = lax.rsqrt(jnp.mean(x * x, axis=1, keepdims=True) + eps_norm)
        n_ref[...] = (x * inverse * g_ref[...]).astype(BF)
        down = dot(n_ref[...], wd_ref[...])
        raw = down[:, :R]
        r_ref[...] = raw
        inverse = lax.rsqrt(jnp.mean(raw * raw, axis=1, keepdims=True) + eps_norm)
        l_ref[...] = (raw * inverse * lg_ref[...]).astype(BF)
        query = 0.0
        for j in range(many):
            query = query + dot(n_ref[:, span(me ^ j, query_rows)], wq_refs[j][...])
        up = dot(l_ref[...], wu_ref[...]).astype(BF)
        cosine, sine = c_ref[...], s_ref[...]
        zeros = jnp.zeros((count, 256 - wide), BF)
        rope = jnp.concatenate([turned(down[:, R : R + DR], cosine, sine).astype(BF), zeros], axis=1)
        for n in range(heads):
            own = query[:, n * wide : (n + 1) * wide]
            q_ref[n, :, :DN] = own[:, :DN].astype(BF)
            q_ref[n, :, DN:] = jnp.concatenate(
                [turned(own[:, DN:], cosine, sine).astype(BF), zeros], axis=1
            )
            k_ref[n, :, :DN] = up[:, n * (DN + DV) : n * (DN + DV) + DN]
            k_ref[n, :, DN:] = rope
            v_ref[n] = up[:, n * (DN + DV) + DN : (n + 1) * (DN + DV)]

    chips = length // count // 2

    def rows(w):
        return pl.BlockSpec((count, w), lambda i: (chip + i * chips, 0))

    def head_rows(w):
        return pl.BlockSpec((heads, count, w), lambda i: (0, chip + i * chips, 0))

    columns = w_query[0].shape[1] + w_down.shape[1]
    first = 6 + many + 3
    return pl.pallas_call(
        kernel,
        grid=(2,),
        in_specs=[
            SCALARS,
            whole((count, width)),
            whole((count, width)),
            whole((1, width)),
            whole(w_down.shape),
            whole((1, R)),
        ]
        + [whole(w.shape) for w in w_query]
        + [whole(w_up.shape), rows(DR), rows(DR)]
        + [ANY] * len(kept),
        out_specs=[rows(width), rows(R), rows(R), head_rows(256), head_rows(256), head_rows(DV)],
        out_shape=[
            jax.ShapeDtypeStruct((length, width), BF),
            jax.ShapeDtypeStruct((length, R), BF),
            jax.ShapeDtypeStruct((length, R), F32),
            jax.ShapeDtypeStruct((heads, length, 256), BF),
            jax.ShapeDtypeStruct((heads, length, 256), BF),
            jax.ShapeDtypeStruct((heads, length, DV), BF),
        ],
        input_output_aliases={first + n: n for n in range(len(kept))},
        compiler_params=pltpu.CompilerParams(vmem_limit_bytes=LIMIT),
        cost_estimate=pl.CostEstimate(
            flops=4 * count * (width * columns + R * w_up.shape[1]),
            transcendentals=0,
            bytes_accessed=8 * count * width + 2 * width * columns,
        ),
        name="project",
    )(index, *pair, gain, w_down, latent_gain, *w_query, w_up, cosine, sine, *kept)


def attend(query, key, value, row_position, column_position, factor):
    heads, length, _ = query.shape
    tile = 256

    def kernel(q_ref, k_ref, v_ref, row_ref, column_ref, o_ref, s_ref):
        allowed = column_ref[...] <= row_ref[...]
        for n in range(heads):
            scores = dot_t(k_ref[n], q_ref[n]) * factor
            exponent = jnp.where(allowed, jnp.exp(jnp.where(allowed, scores, -1e30)), 0.0)
            total = jnp.sum(exponent, axis=0, keepdims=True)
            probs = (exponent / total).astype(BF)
            o_ref[:, n * DV : (n + 1) * DV] = t_dot(v_ref[n], probs).T.astype(BF)
            s_ref[n : n + 1, :] = jnp.log(total)

    return pl.pallas_call(
        kernel,
        grid=(length // tile,),
        in_specs=[
            pl.BlockSpec((heads, tile, 256), lambda i: (0, i, 0)),
            whole(key.shape),
            whole(value.shape),
            pl.BlockSpec((1, tile), lambda i: (0, i)),
            whole((length, 1)),
        ],
        out_specs=[
            pl.BlockSpec((tile, heads * DV), lambda i: (i, 0)),
            pl.BlockSpec((heads, tile), lambda i: (0, i)),
        ],
        out_shape=[
            jax.ShapeDtypeStruct((length, heads * DV), BF),
            jax.ShapeDtypeStruct((heads, length), F32),
        ],
        compiler_params=pltpu.CompilerParams(vmem_limit_bytes=LIMIT),
        cost_estimate=pl.CostEstimate(
            flops=2 * heads * length * length * (256 + DV),
            transcendentals=heads * length * length,
            bytes_accessed=4 * heads * length * 640,
        ),
        name="attend",
    )(query, key, value, row_position, column_position)


def attend_back(query, key, value, result, result_grad, logsum, row_position, column_position, cosine, sine, w_up, factor):
    heads, length, _ = query.shape
    tile = 256
    steps = length // tile
    wide = DN + DR

    def kernel(q_ref, k_ref, v_ref, o_ref, do_ref, ls_ref, row_ref, column_ref, c_ref, s_ref, wu_ref, dq_ref, kv_ref, lp_ref, rope_ref, dk_acc, dv_acc, kt):
        step = pl.program_id(0)

        @pl.when(step == 0)
        def _():
            dk_acc[...] = jnp.zeros_like(dk_acc)
            dv_acc[...] = jnp.zeros_like(dv_acc)
            for n in range(heads):
                kt[n] = k_ref[n].T

        allowed = column_ref[...] <= row_ref[...]
        cosine, sine = c_ref[...], s_ref[...]
        parts = []
        for n in range(heads):
            q = q_ref[n]
            grad = do_ref[:, n * DV : (n + 1) * DV]
            scores = jnp.where(allowed, dot_t(k_ref[n], q) * factor, -1e30)
            probs = jnp.exp(scores - ls_ref[n : n + 1, :])
            dv_acc[n] += dot(probs.astype(BF), grad)
            product = grad.astype(F32) * o_ref[:, n * DV : (n + 1) * DV].astype(F32)
            row_dot = jnp.sum(product.T, axis=0, keepdims=True)
            probs_grad = dot_t(v_ref[n], grad)
            score_grad = (probs * (probs_grad - row_dot) * factor).astype(BF)
            dk_acc[n] += dot(score_grad, q)
            query_grad = dot(kt[n], score_grad).T.astype(BF)
            parts.append(query_grad[:, :DN])
            parts.append(turned(query_grad[:, DN:wide].astype(F32), cosine, sine).astype(BF))
        dq_ref[...] = jnp.concatenate(parts, axis=1)

        @pl.when(step == steps - 1)
        def _():
            rope = jnp.zeros((length, DR), F32)
            for n in range(heads):
                key_grad = dk_acc[n].astype(BF)
                value_grad = dv_acc[n].astype(BF)
                base = n * (DN + DV)
                kv_ref[:, base : base + DN] = key_grad[:, :DN]
                kv_ref[:, base + DN : base + DN + DV] = value_grad
                rope = rope + key_grad[:, DN:wide].astype(F32)
            lp_ref[...] = dot_t(kv_ref[...], wu_ref[...])
            rope_ref[...] = rope

    return pl.pallas_call(
        kernel,
        grid=(steps,),
        in_specs=[
            pl.BlockSpec((heads, tile, 256), lambda i: (0, i, 0)),
            whole(key.shape),
            whole(value.shape),
            pl.BlockSpec((tile, heads * DV), lambda i: (i, 0)),
            pl.BlockSpec((tile, heads * DV), lambda i: (i, 0)),
            pl.BlockSpec((heads, tile), lambda i: (0, i)),
            pl.BlockSpec((1, tile), lambda i: (0, i)),
            whole((length, 1)),
            pl.BlockSpec((tile, DR), lambda i: (i, 0)),
            pl.BlockSpec((tile, DR), lambda i: (i, 0)),
            whole(w_up.shape),
        ],
        out_specs=[
            pl.BlockSpec((tile, heads * wide), lambda i: (i, 0)),
            whole((length, heads * (DN + DV))),
            whole((length, R)),
            whole((length, DR)),
        ],
        out_shape=[
            jax.ShapeDtypeStruct((length, heads * wide), BF),
            jax.ShapeDtypeStruct((length, heads * (DN + DV)), BF),
            jax.ShapeDtypeStruct((length, R), F32),
            jax.ShapeDtypeStruct((length, DR), F32),
        ],
        scratch_shapes=[
            pltpu.VMEM((heads, length, 256), F32),
            pltpu.VMEM((heads, length, DV), F32),
            pltpu.VMEM((heads, 256, length), BF),
        ],
        compiler_params=pltpu.CompilerParams(vmem_limit_bytes=LIMIT),
        cost_estimate=pl.CostEstimate(
            flops=2 * heads * length * length * (3 * 256 + 2 * DV),
            transcendentals=heads * length * length,
            bytes_accessed=8 * heads * length * 640,
        ),
        name="attend_back",
    )(query, key, value, result, result_grad, logsum, row_position, column_position, cosine, sine, w_up)


def add_norm(token_blocks, blocks, w_output, gain):
    count, width = token_blocks[0].shape
    many = len(blocks)
    length = count * many
    tile = 2 * count
    depth = blocks[0].shape[1]

    def kernel(w_ref, g_ref, *refs):
        parts, tokens = refs[:many], refs[many : 2 * many]
        n_ref, r_ref, x_ref = refs[2 * many :]
        rows = []
        for q in range(many):
            block = parts[q][...]
            if q % 2:
                block = jnp.concatenate([block[count:], block[:count]], axis=0)
            rows.append(block)
        total = dot(jnp.concatenate(rows, axis=1), w_ref[...])
        for i in range(many // 2):

            @pl.when(pl.program_id(0) == i)
            def _():
                x_ref[:count] = tokens[2 * i][...]
                x_ref[count:] = tokens[2 * i + 1][...]

        total = total + x_ref[...].astype(F32)
        inverse = lax.rsqrt(jnp.mean(total * total, axis=1, keepdims=True) + eps_norm)
        n_ref[...] = (total * inverse * g_ref[...]).astype(BF)

        @pl.when(pl.program_id(0) == 0)
        def _():
            r_ref[...] = total[:count]

    def source(q):
        return pl.BlockSpec((tile, depth), lambda i: (i ^ (q >> 1), 0))

    return pl.pallas_call(
        kernel,
        grid=(length // tile,),
        in_specs=[whole(w_output.shape), whole((1, width))]
        + [source(q) for q in range(many)]
        + [whole((count, width))] * many,
        out_specs=[pl.BlockSpec((tile, width), lambda i: (i, 0)), whole((count, width))],
        out_shape=[
            jax.ShapeDtypeStruct((length, width), BF),
            jax.ShapeDtypeStruct((count, width), F32),
        ],
        scratch_shapes=[pltpu.VMEM((tile, width), BF)],
        compiler_params=pltpu.CompilerParams(vmem_limit_bytes=LIMIT),
        cost_estimate=pl.CostEstimate(
            flops=2 * length * width * w_output.shape[0],
            transcendentals=0,
            bytes_accessed=6 * length * width + 2 * width * w_output.shape[0],
        ),
        name="add_norm",
    )(w_output, gain, *blocks, *token_blocks)


def expert(rows, cots, gate, up, down, piece):
    count, width = rows.shape
    units = gate.shape[2]
    tile = min(512, count)
    step = 256
    full = units // step
    rest = units % step
    spans = [(n * step, step) for n in range(full)] + ([(full * step, rest)] if rest else [])

    def kernel(x_ref, c_ref, gate_hbm, up_hbm, down_hbm, res_ref, in_ref, h_ref, gg_ref, ug_ref, wg, wu, wd, acc_r, acc_i, sems):
        first = pl.program_id(0) == 0

        def copies(n, start, size):
            span = pl.ds(start, size)
            return [
                pltpu.make_async_copy(gate_hbm.at[piece, :, span], wg.at[:, span], sems.at[0, n]),
                pltpu.make_async_copy(up_hbm.at[piece, :, span], wu.at[:, span], sems.at[1, n]),
                pltpu.make_async_copy(down_hbm.at[piece, span, :], wd.at[span, :], sems.at[2, n]),
            ]

        @pl.when(first)
        def _():
            for n, (start, size) in enumerate(spans):
                for copy in copies(n, start, size):
                    copy.start()

        acc_r[...] = jnp.zeros_like(acc_r)
        acc_i[...] = jnp.zeros_like(acc_i)

        def chunk(n, start, size):
            @pl.when(first)
            def _():
                for copy in copies(n, start, size):
                    copy.wait()

            span = pl.ds(start, size)
            x, c = x_ref[...], c_ref[...]
            w_gate, w_up, w_down = wg[:, span], wu[:, span], wd[span, :]
            g = dot(x, w_gate)
            u = dot(x, w_up)
            hidden_grad = dot_t(c, w_down)
            s = jax.nn.sigmoid(g)
            silu = g * s
            hidden = (silu * u).astype(BF)
            gate_grad = (hidden_grad * u * (s * (1.0 + g * (1.0 - s)))).astype(BF)
            up_grad = (hidden_grad * silu).astype(BF)
            h_ref[:, span] = hidden
            gg_ref[:, span] = gate_grad
            ug_ref[:, span] = up_grad
            acc_r[...] += dot(hidden, w_down)
            acc_i[...] += dot_t(gate_grad, w_gate) + dot_t(up_grad, w_up)

        if full:

            @pl.loop(0, full)
            def _(n):
                chunk(n, pl.multiple_of(n * step, step), step)

        if rest:
            chunk(full, full * step, rest)
        res_ref[...] = acc_r[...].astype(BF)
        in_ref[...] = acc_i[...].astype(BF)

    def block(w):
        return pl.BlockSpec((tile, w), lambda i: (i, 0))

    def array(w):
        return jax.ShapeDtypeStruct((count, w), BF)

    return pl.pallas_call(
        kernel,
        grid=(count // tile,),
        in_specs=[block(width), block(width), ANY, ANY, ANY],
        out_specs=[block(width), block(width), block(units), block(units), block(units)],
        out_shape=[array(width), array(width), array(units), array(units), array(units)],
        scratch_shapes=[
            pltpu.VMEM((width, units), BF),
            pltpu.VMEM((width, units), BF),
            pltpu.VMEM((units, width), BF),
            pltpu.VMEM((tile, width), F32),
            pltpu.VMEM((tile, width), F32),
            pltpu.SemaphoreType.DMA((3, len(spans))),
        ],
        compiler_params=pltpu.CompilerParams(vmem_limit_bytes=LIMIT),
        cost_estimate=pl.CostEstimate(
            flops=12 * count * width * units,
            transcendentals=count * units,
            bytes_accessed=6 * width * units + 8 * count * width + 6 * count * units,
        ),
        name="expert",
    )(rows, cots, gate, up, down)


def expert_weights(rows, cots, hidden, gate_grad, up_grad, piece, pieces, earlier):
    count, width = rows.shape
    units = hidden.shape[1]
    tile = 256

    def kernel(x_ref, c_ref, h_ref, gg_ref, ug_ref, *refs):
        g_ref, u_ref, d_ref = refs[-3:]
        g_ref[0] = t_dot(x_ref[...], gg_ref[...])
        u_ref[0] = t_dot(x_ref[...], ug_ref[...])
        d_ref[0] = t_dot(h_ref[...], c_ref[...])

    tall = pl.BlockSpec((1, tile, units), lambda i: (piece, i, 0))
    flat = pl.BlockSpec((1, units, tile), lambda i: (piece, 0, i))
    column = pl.BlockSpec((count, tile), lambda i: (0, i))
    kept = list(earlier or ())
    return pl.pallas_call(
        kernel,
        grid=(width // tile,),
        in_specs=[column, column] + [whole((count, units))] * 3 + [ANY] * len(kept),
        out_specs=[tall, tall, flat],
        out_shape=[
            jax.ShapeDtypeStruct((pieces, width, units), F32),
            jax.ShapeDtypeStruct((pieces, width, units), F32),
            jax.ShapeDtypeStruct((pieces, units, width), F32),
        ],
        input_output_aliases={5 + n: n for n in range(len(kept))},
        compiler_params=pltpu.CompilerParams(vmem_limit_bytes=LIMIT),
        cost_estimate=pl.CostEstimate(
            flops=6 * count * width * units,
            transcendentals=0,
            bytes_accessed=12 * width * units + 4 * count * width,
        ),
        name="expert_weights",
    )(rows, cots, hidden, gate_grad, up_grad, *kept)


def dispatch(select, rows, slot_weight, pieces):
    blocks, slots, count = select.shape
    width = rows.shape[1]
    others = slots // pieces // CAP

    def kernel(m_ref, x_ref, *refs):
        got = dot(m_ref[0], x_ref[...])
        if slot_weight is not None:
            got = got * refs[0][0]
        got = got.astype(BF)
        for i in range(pieces):
            for j in range(others):
                start = (i * others + j) * CAP
                refs[-pieces + i][j] = got[start : start + CAP]

    weights = [] if slot_weight is None else [slot_weight]
    out = pl.BlockSpec((others, CAP, width), lambda b: (0, b, 0))
    return pl.pallas_call(
        kernel,
        grid=(blocks,),
        in_specs=[
            pl.BlockSpec((1, slots, count), lambda b: (b, 0, 0)),
            pl.BlockSpec((count, width), lambda b: (b, 0)),
        ]
        + [pl.BlockSpec((1, slots, 1), lambda b: (b, 0, 0))] * len(weights),
        out_specs=[out] * pieces,
        out_shape=[jax.ShapeDtypeStruct((others, blocks * CAP, width), BF)] * pieces,
        compiler_params=pltpu.CompilerParams(vmem_limit_bytes=LIMIT),
        cost_estimate=pl.CostEstimate(
            flops=2 * blocks * slots * count * width,
            transcendentals=0,
            bytes_accessed=2 * blocks * (slots + count) * width,
        ),
        name="dispatch",
    )(select, rows, *weights)


def combine(base, masks, returned, products, dtype):
    half = masks[0].shape[0] // 2
    slots, count = masks[0].shape[1:]
    pieces = len(returned)
    others, _, width = returned[0].shape
    many = len(masks)

    def kernel(*refs):
        mask_refs, row_refs = refs[:many], refs[many : many + pieces]
        rest, out_ref = refs[many + pieces : -1], refs[-1]
        rows = jnp.concatenate([row_refs[i][j] for i in range(pieces) for j in range(others)], axis=0)
        total = 0.0
        for n, (_, _, flipped) in enumerate(products):
            total = total + (dot_t if flipped else dot)(rest[2 * n][...], rest[2 * n + 1][...])
        for mask_ref in mask_refs:
            total = total + t_dot(mask_ref[0], rows)
        out_ref[...] = total.astype(dtype)

    factors = []
    specs = []
    for left, right, _ in products:
        factors += [left, right]
        specs += [
            pl.BlockSpec((count, left.shape[1]), lambda b: (base + b, 0)),
            whole(right.shape),
        ]
    return pl.pallas_call(
        kernel,
        grid=(half,),
        in_specs=[pl.BlockSpec((1, slots, count), lambda b: (base + b, 0, 0))] * many
        + [pl.BlockSpec((others, CAP, width), lambda b: (0, base + b, 0))] * pieces
        + specs,
        out_specs=pl.BlockSpec((count, width), lambda b: (b, 0)),
        out_shape=jax.ShapeDtypeStruct((half * count, width), dtype),
        compiler_params=pltpu.CompilerParams(vmem_limit_bytes=LIMIT),
        cost_estimate=pl.CostEstimate(
            flops=2 * half * count * width * (many * slots + sum(p[0].shape[1] for p in products)),
            transcendentals=0,
            bytes_accessed=half * count * width * 6,
        ),
        name="combine",
    )(*masks, *returned, *factors)


def swap(x, axis, mask):
    n = lax.axis_size(axis)
    return lax.ppermute(x, axis, [(i, i ^ mask) for i in range(n)])


def after(x, *earlier):
    return lax.optimization_barrier((x, *earlier))[0]


class Lane:
    def __init__(self, axis, depth):
        self.axis = axis
        self.depth = depth
        self.sent = []

    def send(self, x, mask):
        if len(self.sent) >= self.depth:
            x = after(x, self.sent[-self.depth])
        got = swap(x, self.axis, mask)
        self.sent.append(got)
        return got

    def chips(self, x):
        chips = lax.axis_size("seq") // 2
        return [x] + [self.send(x, 2 * k) for k in range(1, chips)]

    def group(self, x):
        evens = self.chips(x)
        return evens + [swap(b, "seq", 1) for b in evens]

    def scatter(self, even, odd):
        chips = lax.axis_size("seq") // 2
        rows = even.shape[0] // chips
        got = swap(odd.astype(BF), "seq", 1)
        blocks = [
            even[k * rows : (k + 1) * rows] + got[k * rows : (k + 1) * rows].astype(F32)
            for k in range(chips)
        ]
        total = blocks[0]
        for k in range(1, chips):
            total = total + self.send(blocks[k].astype(BF), 2 * k).astype(F32)
        return total

    def others(self, x):
        return [x] + [self.send(x, j) for j in range(1, lax.axis_size("exp"))]

    def sum_stack(self, x):
        n = lax.axis_size("exp")
        me = lax.axis_index("exp")
        total = lax.dynamic_index_in_dim(x, me, 0, keepdims=False)
        for j in range(1, n):
            piece = lax.dynamic_index_in_dim(x, me ^ j, 0, keepdims=False).astype(BF)
            total = total + self.send(piece, j).astype(F32)
        return total


def relative_order(count):
    chips = count // 2
    return [2 * k for k in range(chips)] + [2 * k + 1 for k in range(chips)]


def scatter_small(x):
    for axis in ("exp", "seq"):
        n = lax.axis_size(axis)
        me = lax.axis_index(axis)
        total = lax.dynamic_index_in_dim(x, me, 0, keepdims=False)
        for j in range(1, n):
            piece = lax.dynamic_index_in_dim(x, me ^ j, 0, keepdims=False)
            total = total + swap(piece, axis, j)
        x = total
    return x


def columns_first(x, blocks):
    rows, columns = x.shape
    return x.reshape(rows, blocks, columns // blocks).transpose(1, 0, 2)


def columns_last(x):
    blocks, rows, w = x.shape
    return x.transpose(1, 0, 2).reshape(rows, blocks * w)


def shards(
    tokens,
    routes,
    route_weights,
    norm_gain,
    w_query,
    w_kv_down,
    latent_gain,
    w_kv_up,
    w_output,
    ffn_gain,
    shared_gate,
    shared_up,
    shared_down,
    expert_gate,
    expert_up,
    expert_down,
    out_grad,
):
    count, width = tokens.shape
    n_seq = lax.axis_size("seq")
    n_exp = lax.axis_size("exp")
    seq = lax.axis_index("seq")
    order = relative_order(n_seq)
    chips = n_seq // 2
    heads = H // n_seq
    length = count * n_seq
    half = length // 2
    pieces = expert_gate.shape[0]
    parts_per = pieces * n_seq * n_exp // EXPERTS
    factor = 1.0 / math.sqrt(DN + DR)
    gain_rows = norm_gain.shape[0]
    latent_rows_local = latent_gain.shape[0]
    along = Lane("seq", 3)
    across = Lane("exp", 2)

    index = jnp.stack([lax.axis_index("exp"), seq]).astype(jnp.int32)
    extra = jnp.stack(
        [norm_gain, ffn_gain, jnp.pad(latent_gain, (0, gain_rows - latent_rows_local))]
    )
    packed = jnp.concatenate(
        [w_kv_down, jnp.pad(extra, ((0, 13), (0, w_kv_down.shape[1] - gain_rows)))], axis=0
    )
    packed_even = jnp.stack(along.chips(packed))
    query_parts = across.others(w_query)
    token_blocks = along.group(tokens)
    packed_parts = across.others(packed_even)
    packed_parts = packed_parts + [swap(x, "seq", 1) for x in packed_parts]
    up_parts = across.others(w_kv_up)
    route_pack = jnp.concatenate([routes.astype(F32).T, route_weights.T], axis=0)
    route_blocks = along.group(route_pack)
    output_even = jnp.concatenate(along.chips(w_output), axis=0)
    shared_parts = across.others(jnp.stack([shared_gate, shared_up]))
    drop_parts = across.others(shared_down)
    output_parts = across.others(output_even)
    output_parts = output_parts + [swap(x, "seq", 1) for x in output_parts]
    grad_blocks = along.group(out_grad)

    plan = []
    for n in range(2 * n_exp):
        for k in range(chips):

            def where(ref, n=n, k=k):
                return (ref[0] ^ (n % n_exp)) * n_seq + (ref[1] ^ (2 * k + n // n_exp))

            plan.append(
                (
                    n,
                    (k, slice(0, gain_rows)),
                    0,
                    lambda ref, where=where: (span(where(ref), gain_rows), slice(None)),
                )
            )
            plan.append(
                (
                    n,
                    (k, slice(gain_rows, gain_rows + 16)),
                    1,
                    lambda ref, where=where: (where(ref),),
                )
            )
    down_full, extra_all = arrange(
        index,
        packed_parts,
        [(width, R + DR), (n_exp * n_seq, 16, R + DR)],
        plan,
    )
    gain_first = extra_all[:, 0, :gain_rows].reshape(1, width).astype(F32)
    gain_second = extra_all[:, 1, :gain_rows].reshape(1, width).astype(F32)
    latent_wide = extra_all[:, 2, :latent_rows_local].reshape(1, R).astype(F32)
    block_rows = width // n_exp
    everything = slice(None)
    (up_cols,) = arrange(
        index,
        up_parts,
        [(R, w_kv_up.shape[1])],
        [
            (j, (everything,), 0, lambda ref, j=j: (span(ref[0] ^ j, R // n_exp), everything))
            for j in range(n_exp)
        ],
    )
    gate_cols, lift_cols = arrange(
        index,
        shared_parts,
        [(width, shared_gate.shape[1])] * 2,
        [
            (j, (n,), n, lambda ref, j=j: (span(ref[0] ^ j, block_rows), everything))
            for j in range(n_exp)
            for n in range(2)
        ],
    )
    (drop_rows,) = arrange(
        index,
        drop_parts,
        [(shared_down.shape[0], width)],
        [
            (j, (everything,), 0, lambda ref, j=j: (everything, span(ref[0] ^ j, block_rows)))
            for j in range(n_exp)
        ],
    )
    output_half = H * DV // 2
    (output_full,) = arrange(
        index,
        output_parts,
        [(H * DV, width)],
        [
            (
                n,
                (everything,),
                0,
                lambda ref, n=n: (
                    slice(n // n_exp * output_half, (n // n_exp + 1) * output_half),
                    span(ref[0] ^ (n % n_exp), block_rows),
                ),
            )
            for n in range(2 * n_exp)
        ],
    )

    positions = jnp.concatenate(
        [(seq ^ r) * count + jnp.arange(count, dtype=jnp.int32) for r in order]
    )
    row_position, column_position = positions[None, :], positions[:, None]
    cosine_table, sine_table = rope_tables(positions, DR)
    cosine_wide = jnp.concatenate([cosine_table, cosine_table], axis=1)
    sine_wide = jnp.concatenate([-sine_table, sine_table], axis=1)
    projected = None
    for k in range(chips):
        projected = project(
            index,
            k,
            (token_blocks[k], token_blocks[chips + k]),
            gain_first,
            query_parts,
            down_full,
            latent_wide,
            up_cols,
            cosine_wide,
            sine_wide,
            heads,
            length,
            projected,
        )
    normed_one, latent_all, latent_raw, query_heads, key_heads, value_heads = projected
    result, logsum = attend(
        query_heads, key_heads, value_heads, row_position, column_position, factor
    )

    result_blocks = along.group(result)
    normed_two, residual = add_norm(token_blocks, result_blocks, output_full, gain_second)
    inverse_two = inverse_rms(residual)

    column = jnp.stack(
        [
            ((other * n_seq + seq) * pieces + i) // parts_per
            for i in range(pieces)
            for other in range(n_exp)
        ]
    )
    kinds = n_exp * pieces
    route_all = jnp.stack(route_blocks)
    named = route_all[:, None, :TOP, :].astype(jnp.int32) == column[None, :, None, None]
    matched = jnp.any(named, axis=2)
    match_weight = jnp.sum(jnp.where(named, route_all[:, None, TOP:, :], 0.0), axis=2)
    earlier = (jnp.arange(count)[:, None] < jnp.arange(count)[None, :]).astype(BF)
    rank = jnp.dot(matched.astype(BF), earlier, preferred_element_type=F32).astype(jnp.int32)
    chosen = (rank[:, :, None, :] == jnp.arange(CAP, dtype=jnp.int32)[None, None, :, None]) & (
        matched[:, :, None, :]
    )
    select = chosen.astype(BF).reshape(n_seq, kinds * CAP, count)
    weighted = jnp.where(chosen, match_weight[:, :, None, :], 0.0).reshape(
        n_seq, kinds * CAP, count
    )
    slot_weight = jnp.sum(weighted, axis=2, keepdims=True)
    weighted_high = weighted.astype(BF)
    weighted_low = (weighted - weighted_high.astype(F32)).astype(BF)

    def give(rows):
        return lax.all_to_all(rows, "exp", split_axis=0, concat_axis=0, tiled=True)

    grad_rows = jnp.concatenate(grad_blocks, axis=0)
    send_cots = dispatch(select, grad_rows, slot_weight, pieces)
    received_grad = [give(rows) for rows in send_cots]
    send_rows = dispatch(select, normed_two, None, pieces)
    received = [give(rows) for rows in send_rows]

    slot_rows = n_exp * n_seq * CAP
    pairs = []
    results_back, grads_back, kept = [], [], []
    for i in range(pieces):
        rows = received[i].reshape(slot_rows, width)
        cots = received_grad[i].reshape(slot_rows, width)
        expert_result, input_grad, *saved = expert(
            rows, cots, expert_gate, expert_up, expert_down, i
        )
        grads_back.append(give(input_grad.reshape(n_exp, n_seq * CAP, width)))
        results_back.append(expert_result.reshape(n_exp, n_seq * CAP, width))
        kept.append((rows, cots, *saved))
    last = input_grad
    results_back = [give(after(rows, grads_back[-1])) for rows in results_back]
    expert_grads = None
    for i in range(pieces):
        expert_grads = expert_weights(after(kept[i][0], last), *kept[i][1:], i, pieces, expert_grads)
    expert_gate_grad, expert_up_grad, expert_down_grad = expert_grads

    shared_rows = after(normed_two, *send_rows)
    shared_gate_raw = dot(shared_rows, gate_cols)
    shared_up_raw = dot(shared_rows, lift_cols)
    shared_hidden = (jax.nn.silu(shared_gate_raw) * shared_up_raw).astype(BF)
    shared_hidden_grad = dot_t(grad_rows, drop_rows)
    sgate_grad = (shared_hidden_grad * shared_up_raw * silu_slope(shared_gate_raw)).astype(BF)
    sup_grad = (shared_hidden_grad * jax.nn.silu(shared_gate_raw)).astype(BF)
    two_products = [(sgate_grad, gate_cols, True), (sup_grad, lift_cols, True)]
    two_odd = combine(chips, [select], grads_back, two_products, BF)
    two_even = combine(0, [select], grads_back, two_products, F32)
    two_grad = along.scatter(two_even, two_odd)
    shared_grad_stack = jnp.stack(
        [
            t_dot(shared_rows, sgate_grad).reshape(n_exp, width // n_exp, -1),
            t_dot(shared_rows, sup_grad).reshape(n_exp, width // n_exp, -1),
        ],
        axis=1,
    )

    residual_norm_grad, second_terms = norm_back(
        two_grad, residual, inverse_two, gain_second
    )
    residual_grad = out_grad.astype(F32) + residual_norm_grad
    residual_half = residual_grad.astype(BF)
    all_heads = dot_t(residual_half, output_full).astype(BF)
    wide = heads * DV
    pairs = [
        jnp.stack(
            [
                all_heads[:, k * wide : (k + 1) * wide],
                all_heads[:, (chips + k) * wide : (chips + k + 1) * wide],
            ]
        )
        for k in range(chips)
    ]
    pairs = [pairs[0]] + [along.send(pairs[k], 2 * k) for k in range(1, chips)]
    other_half = swap(jnp.stack([pair[1] for pair in pairs]), "seq", 1)
    attention_grad = jnp.concatenate(
        [jnp.stack([pair[0] for pair in pairs]), other_half], axis=0
    ).reshape(length, wide)
    half_all = along.group(residual_half)

    out_products = [(shared_hidden, drop_rows, False)]
    out_masks = [weighted_high, weighted_low]
    out_odd = combine(chips, out_masks, results_back, out_products, BF)
    out_even = combine(0, out_masks, results_back, out_products, F32)

    query_in_grad, kv_grad, latent_part, rope_part = attend_back(
        query_heads,
        key_heads,
        value_heads,
        result,
        attention_grad,
        logsum,
        row_position,
        column_position,
        cosine_wide,
        -sine_wide,
        up_cols,
        factor,
    )
    latent_part = jnp.concatenate([latent_part, rope_part], axis=1)
    latent_grad = along.scatter(latent_part[:half], latent_part[half:])
    (query_cols,) = arrange(
        index,
        query_parts,
        [(width, w_query.shape[1])],
        [
            (j, (everything,), 0, lambda ref, j=j: (span(ref[0] ^ j, block_rows), everything))
            for j in range(n_exp)
        ],
    )
    one_part = dot_t(query_in_grad, query_cols)
    one_grad = along.scatter(one_part[:half], one_part[half:])
    latent_raw_grad, latent_terms = norm_back(
        latent_grad[:, :R], latent_raw[:count], inverse_rms(latent_raw[:count]), latent_wide
    )
    down_rows = jnp.concatenate(
        [
            latent_raw_grad,
            rotate(latent_grad[:, R:], cosine_table[:count], -sine_table[:count]),
        ],
        axis=1,
    ).astype(BF)
    down_rows_all = jnp.concatenate(along.group(down_rows), axis=0)
    output = (residual + along.scatter(out_even, out_odd)).astype(BF)

    shared_out = across.sum_stack(shared_grad_stack)
    drop_out = across.sum_stack(columns_first(t_dot(shared_hidden, grad_rows), n_exp))
    output_out = across.sum_stack(
        columns_first(t_dot(result, jnp.concatenate(half_all, axis=0)), n_exp)
    )
    up_out = across.sum_stack(t_dot(latent_all, kv_grad).reshape(n_exp, R // n_exp, -1))
    query_out = across.sum_stack(
        t_dot(normed_one, query_in_grad).reshape(n_exp, width // n_exp, -1)
    )
    mine = lax.dynamic_slice_in_dim(
        normed_one.reshape(length, n_exp, n_seq * gain_rows), seq * gain_rows, gain_rows, 2
    ).reshape(length, n_exp * gain_rows)
    down_out = across.sum_stack(t_dot(mine, down_rows_all).reshape(n_exp, gain_rows, -1))

    down_back = dot_t(down_rows, down_full)
    token_wide = jnp.concatenate(token_blocks, axis=0).astype(F32)
    inverse_one = inverse_rms(token_wide)
    one_hat = token_wide * inverse_one
    first_sum = jnp.sum(one_part * one_hat, axis=0) + jnp.sum(down_back * one_hat[:count], axis=0)
    token_norm_grad, _ = norm_back(
        one_grad + down_back, token_wide[:count], inverse_one[:count], gain_first
    )
    tokens_grad = (residual_grad + token_norm_grad).astype(BF)
    small = scatter_small(
        jnp.concatenate(
            [
                first_sum.reshape(n_exp, n_seq, gain_rows),
                jnp.sum(second_terms, axis=0).reshape(n_exp, n_seq, gain_rows),
                jnp.sum(latent_terms, axis=0).reshape(n_exp, n_seq, latent_rows_local),
            ],
            axis=2,
        )
    )
    return (
        output,
        tokens_grad,
        small[:gain_rows],
        query_out,
        down_out,
        small[2 * gain_rows :],
        up_out,
        output_out,
        small[gain_rows : 2 * gain_rows],
        shared_out[0],
        shared_out[1],
        drop_out,
        expert_gate_grad,
        expert_up_grad,
        expert_down_grad,
    )


def solution(mesh):
    rows = P(("exp", "seq"), None)
    line = P(("exp", "seq"))
    grid = P("exp", "seq")
    turned = P("seq", "exp")
    part = P(("exp", "seq"), None, None)
    return jax.shard_map(
        shards,
        mesh=mesh,
        in_specs=(
            rows,
            rows,
            rows,
            line,
            grid,
            rows,
            line,
            grid,
            turned,
            line,
            grid,
            grid,
            turned,
            part,
            part,
            part,
            rows,
        ),
        out_specs=(
            rows,
            rows,
            line,
            grid,
            rows,
            line,
            grid,
            turned,
            line,
            grid,
            grid,
            turned,
            part,
            part,
            part,
        ),
        check_vma=False,
    )
```

```python
import math

import jax
import jax.numpy as jnp
from jax import lax
from jax.experimental import pallas as pl
from jax.experimental.pallas import tpu as pltpu
from jax.sharding import PartitionSpec as P

H = 16
DN = 128
DR = 64
DV = 128
R = 512
EXPERTS = 64
TOP = 6
CAP = 16


eps_norm = 1e-06
rope_base = 50000.0
BF = jnp.bfloat16
F32 = jnp.float32


def dot(a, b):
    return jnp.dot(a, b, preferred_element_type=F32)


def dot_t(a, b):
    return lax.dot_general(a, b, (((1,), (1,)), ((), ())), preferred_element_type=F32)


def t_dot(a, b):
    return lax.dot_general(a, b, (((0,), (0,)), ((), ())), preferred_element_type=F32)


def rope_tables(positions, width):
    middle = width // 2
    frequency = rope_base ** (-(jnp.arange(middle, dtype=F32) * 2.0 / width))
    angles = positions.astype(F32)[:, None] * frequency[None, :]
    return (jnp.cos(angles), jnp.sin(angles))


def rotate(values, cosine_table, sine_table):
    middle = values.shape[-1] // 2
    leading = values[..., :middle]
    trailing = values[..., middle:]
    return jnp.concatenate(
        [
            leading * cosine_table - trailing * sine_table,
            trailing * cosine_table + leading * sine_table,
        ],
        axis=-1,
    )


def silu_slope(gate_values):
    sigmoid = jax.nn.sigmoid(gate_values)
    return sigmoid * (1.0 + gate_values * (1.0 - sigmoid))


def norm_back(dy, v, inverse, gain):
    hat = v * inverse
    scaled = dy * gain
    dv = inverse * (scaled - hat * jnp.mean(scaled * hat, axis=-1, keepdims=True))
    return dv, dy * hat


def inverse_rms(v):
    return lax.rsqrt(jnp.mean(v * v, axis=-1, keepdims=True) + eps_norm)


LIMIT = 56 * 1024 * 1024
ANY = pl.BlockSpec(memory_space=pl.ANY)
SCALARS = pl.BlockSpec(memory_space=pltpu.SMEM)


def whole(shape):
    return pl.BlockSpec(shape, lambda *grid: (0,) * len(shape))


def arrange(index, blocks, outs, plan):
    def kernel(index_ref, *refs):
        sources = refs[: len(blocks)]
        targets = refs[len(blocks) :]
        for block, source, out, target in plan:
            targets[out][target(index_ref)] = sources[block][source]

    size = sum(math.prod(s) * 2 for s in outs)
    return pl.pallas_call(
        kernel,
        out_shape=[jax.ShapeDtypeStruct(s, BF) for s in outs],
        in_specs=[SCALARS] + [pl.BlockSpec(memory_space=pltpu.VMEM)] * len(blocks),
        out_specs=[pl.BlockSpec(memory_space=pltpu.VMEM)] * len(outs),
        compiler_params=pltpu.CompilerParams(vmem_limit_bytes=LIMIT),
        cost_estimate=pl.CostEstimate(flops=0, transcendentals=0, bytes_accessed=2 * size),
        name="arrange",
    )(index, *blocks)


def span(start, size):
    return pl.ds(pl.multiple_of(start * size, size), size)


def turned(v, cosine, sine):
    middle = v.shape[1] // 2
    return v * cosine + jnp.concatenate([v[:, middle:], v[:, :middle]], axis=1) * sine


def project(index, token_blocks, gain, w_first, w_down, latent_gain, w_up, cosine, sine, heads):
    count, width = token_blocks[0].shape
    chips = len(token_blocks) // 2
    half = chips * count
    wide = DN + DR
    many = len(w_first)
    query_rows = w_first[0].shape[0]
    columns = heads * wide

    def kernel(index_ref, g_ref, wd_ref, lg_ref, wu_ref, c_ref, s_ref, *refs):
        tokens, weights = refs[: 2 * chips], refs[2 * chips : 2 * chips + many]
        n_ref, l_ref, r_ref, q_ref, k_ref, v_ref, x_ref = refs[2 * chips + many :]
        me = index_ref[0]
        for h in range(2):

            @pl.when(pl.program_id(0) == h)
            def _():
                for k in range(chips):
                    x_ref[k * count : (k + 1) * count] = tokens[h * chips + k][...]

        x = x_ref[...].astype(F32)
        inverse = lax.rsqrt(jnp.mean(x * x, axis=1, keepdims=True) + eps_norm)
        n_ref[...] = (x * inverse * g_ref[...]).astype(BF)
        down = dot(n_ref[...], wd_ref[...])
        raw = down[:, :R]
        r_ref[...] = raw
        inverse = lax.rsqrt(jnp.mean(raw * raw, axis=1, keepdims=True) + eps_norm)
        l_ref[...] = (raw * inverse * lg_ref[...]).astype(BF)
        query = 0.0
        for j in range(many):
            query = query + dot(n_ref[:, span(me ^ j, query_rows)], weights[j][:, :columns])
        up = dot(l_ref[...], wu_ref[...]).astype(BF)
        cosine, sine = c_ref[...], s_ref[...]
        zeros = jnp.zeros((half, 256 - wide), BF)
        rope = jnp.concatenate([turned(down[:, R : R + DR], cosine, sine).astype(BF), zeros], axis=1)
        for n in range(heads):
            own = query[:, n * wide : (n + 1) * wide]
            q_ref[n, :, :DN] = own[:, :DN].astype(BF)
            q_ref[n, :, DN:] = jnp.concatenate(
                [turned(own[:, DN:], cosine, sine).astype(BF), zeros], axis=1
            )
            k_ref[n, :, :DN] = up[:, n * (DN + DV) : n * (DN + DV) + DN]
            k_ref[n, :, DN:] = rope
            v_ref[n] = up[:, n * (DN + DV) + DN : (n + 1) * (DN + DV)]

    def rows(w):
        return pl.BlockSpec((half, w), lambda i: (i, 0))

    def head_rows(w):
        return pl.BlockSpec((heads, half, w), lambda i: (0, i, 0))

    length = 2 * half
    return pl.pallas_call(
        kernel,
        grid=(2,),
        in_specs=[
            SCALARS,
            whole((1, width)),
            whole(w_down.shape),
            whole((1, R)),
            whole(w_up.shape),
            rows(DR),
            rows(DR),
        ]
        + [whole((count, width))] * (2 * chips)
        + [whole(w.shape) for w in w_first],
        out_specs=[rows(width), rows(R), rows(R), head_rows(256), head_rows(256), head_rows(DV)],
        out_shape=[
            jax.ShapeDtypeStruct((length, width), BF),
            jax.ShapeDtypeStruct((length, R), BF),
            jax.ShapeDtypeStruct((length, R), F32),
            jax.ShapeDtypeStruct((heads, length, 256), BF),
            jax.ShapeDtypeStruct((heads, length, 256), BF),
            jax.ShapeDtypeStruct((heads, length, DV), BF),
        ],
        scratch_shapes=[pltpu.VMEM((half, width), BF)],
        compiler_params=pltpu.CompilerParams(vmem_limit_bytes=LIMIT),
        cost_estimate=pl.CostEstimate(
            flops=2 * length * (width * (columns + w_down.shape[1]) + R * w_up.shape[1]),
            transcendentals=0,
            bytes_accessed=4 * length * width + 2 * width * (columns + w_down.shape[1]),
        ),
        name="project",
    )(index, gain, w_down, latent_gain, w_up, cosine, sine, *token_blocks, *w_first)


def query_back(index, base, query_grad, w_first, normed, gain, dtype):
    length, columns = query_grad.shape
    half = length // 2
    width = normed.shape[1]
    many = len(w_first)
    query_rows = w_first[0].shape[0]

    def kernel(index_ref, q_ref, n_ref, g_ref, *refs):
        weights, (o_ref, t_ref) = refs[:many], refs[many:]
        me = index_ref[0]
        for j in range(many):
            where = span(me ^ j, query_rows)
            part = dot_t(q_ref[...], weights[j][:, :columns])
            o_ref[:, where] = part.astype(dtype)
            t_ref[:, where] = jnp.sum(
                part * n_ref[:, where].astype(F32), axis=0, keepdims=True
            ) / g_ref[:, where]

    return pl.pallas_call(
        kernel,
        grid=(1,),
        in_specs=[
            SCALARS,
            pl.BlockSpec((half, columns), lambda i: (base, 0)),
            pl.BlockSpec((half, width), lambda i: (base, 0)),
            whole((1, width)),
        ]
        + [whole(w.shape) for w in w_first],
        out_specs=[whole((half, width)), whole((1, width))],
        out_shape=[
            jax.ShapeDtypeStruct((half, width), dtype),
            jax.ShapeDtypeStruct((1, width), F32),
        ],
        compiler_params=pltpu.CompilerParams(vmem_limit_bytes=LIMIT),
        cost_estimate=pl.CostEstimate(
            flops=2 * half * columns * width, transcendentals=0, bytes_accessed=8 * half * width
        ),
        name="query_back",
    )(index, query_grad, normed, gain, *w_first)


def attend(query, key, value, row_position, column_position, factor):
    heads, length, _ = query.shape
    tile = 256

    def kernel(q_ref, k_ref, v_ref, row_ref, column_ref, o_ref, s_ref):
        allowed = column_ref[...] <= row_ref[...]
        for n in range(heads):
            scores = dot_t(k_ref[n], q_ref[n]) * factor
            exponent = jnp.where(allowed, jnp.exp(jnp.where(allowed, scores, -1e30)), 0.0)
            total = jnp.sum(exponent, axis=0, keepdims=True)
            probs = (exponent / total).astype(BF)
            o_ref[:, n * DV : (n + 1) * DV] = t_dot(v_ref[n], probs).T.astype(BF)
            s_ref[n : n + 1, :] = jnp.log(total)

    return pl.pallas_call(
        kernel,
        grid=(length // tile,),
        in_specs=[
            pl.BlockSpec((heads, tile, 256), lambda i: (0, i, 0)),
            whole(key.shape),
            whole(value.shape),
            pl.BlockSpec((1, tile), lambda i: (0, i)),
            whole((length, 1)),
        ],
        out_specs=[
            pl.BlockSpec((tile, heads * DV), lambda i: (i, 0)),
            pl.BlockSpec((heads, tile), lambda i: (0, i)),
        ],
        out_shape=[
            jax.ShapeDtypeStruct((length, heads * DV), BF),
            jax.ShapeDtypeStruct((heads, length), F32),
        ],
        compiler_params=pltpu.CompilerParams(vmem_limit_bytes=LIMIT),
        cost_estimate=pl.CostEstimate(
            flops=2 * heads * length * length * (256 + DV),
            transcendentals=heads * length * length,
            bytes_accessed=4 * heads * length * 640,
        ),
        name="attend",
    )(query, key, value, row_position, column_position)


def attend_back(query, key, value, result, result_grad, logsum, row_position, column_position, cosine, sine, w_up, latent_all, latent_gain, factor):
    heads, length, _ = query.shape
    tile = 256
    steps = length // tile
    wide = DN + DR

    def kernel(q_ref, k_ref, v_ref, o_ref, do_ref, ls_ref, row_ref, column_ref, c_ref, s_ref, wu_ref, l_ref, lg_ref, dq_ref, kv_ref, lp_ref, t_ref, dk_acc, dv_acc, kt):
        step = pl.program_id(0)

        @pl.when(step == 0)
        def _():
            dk_acc[...] = jnp.zeros_like(dk_acc)
            dv_acc[...] = jnp.zeros_like(dv_acc)
            for n in range(heads):
                kt[n] = k_ref[n].T

        allowed = column_ref[...] <= row_ref[...]
        cosine, sine = c_ref[...], s_ref[...]
        parts = []
        for n in range(heads):
            q = q_ref[n]
            grad = do_ref[:, n * DV : (n + 1) * DV]
            scores = jnp.where(allowed, dot_t(k_ref[n], q) * factor, -1e30)
            probs = jnp.exp(scores - ls_ref[n : n + 1, :])
            dv_acc[n] += dot(probs.astype(BF), grad)
            product = grad.astype(F32) * o_ref[:, n * DV : (n + 1) * DV].astype(F32)
            row_dot = jnp.sum(product.T, axis=0, keepdims=True)
            probs_grad = dot_t(v_ref[n], grad)
            score_grad = (probs * (probs_grad - row_dot) * factor).astype(BF)
            dk_acc[n] += dot(score_grad, q)
            query_grad = dot(kt[n], score_grad).T.astype(BF)
            parts.append(query_grad[:, :DN])
            parts.append(turned(query_grad[:, DN:wide].astype(F32), cosine, sine).astype(BF))
        dq_ref[...] = jnp.concatenate(parts, axis=1)

        @pl.when(step == steps - 1)
        def _():
            rope = jnp.zeros((length, DR), F32)
            for n in range(heads):
                key_grad = dk_acc[n].astype(BF)
                value_grad = dv_acc[n].astype(BF)
                base = n * (DN + DV)
                kv_ref[:, base : base + DN] = key_grad[:, :DN]
                kv_ref[:, base + DN : base + DN + DV] = value_grad
                rope = rope + key_grad[:, DN:wide].astype(F32)
            latent = dot_t(kv_ref[...], wu_ref[...])
            lp_ref[:, :R] = latent
            lp_ref[:, R:] = rope
            t_ref[...] = jnp.sum(
                latent * l_ref[...].astype(F32), axis=0, keepdims=True
            ) / lg_ref[...]

    return pl.pallas_call(
        kernel,
        grid=(steps,),
        in_specs=[
            pl.BlockSpec((heads, tile, 256), lambda i: (0, i, 0)),
            whole(key.shape),
            whole(value.shape),
            pl.BlockSpec((tile, heads * DV), lambda i: (i, 0)),
            pl.BlockSpec((tile, heads * DV), lambda i: (i, 0)),
            pl.BlockSpec((heads, tile), lambda i: (0, i)),
            pl.BlockSpec((1, tile), lambda i: (0, i)),
            whole((length, 1)),
            pl.BlockSpec((tile, DR), lambda i: (i, 0)),
            pl.BlockSpec((tile, DR), lambda i: (i, 0)),
            whole(w_up.shape),
            whole((length, R)),
            whole((1, R)),
        ],
        out_specs=[
            pl.BlockSpec((tile, heads * wide), lambda i: (i, 0)),
            whole((length, heads * (DN + DV))),
            whole((length, R + DR)),
            whole((1, R)),
        ],
        out_shape=[
            jax.ShapeDtypeStruct((length, heads * wide), BF),
            jax.ShapeDtypeStruct((length, heads * (DN + DV)), BF),
            jax.ShapeDtypeStruct((length, R + DR), F32),
            jax.ShapeDtypeStruct((1, R), F32),
        ],
        scratch_shapes=[
            pltpu.VMEM((heads, length, 256), F32),
            pltpu.VMEM((heads, length, DV), F32),
            pltpu.VMEM((heads, 256, length), BF),
        ],
        compiler_params=pltpu.CompilerParams(vmem_limit_bytes=LIMIT),
        cost_estimate=pl.CostEstimate(
            flops=2 * heads * length * length * (3 * 256 + 2 * DV),
            transcendentals=heads * length * length,
            bytes_accessed=8 * heads * length * 640,
        ),
        name="attend_back",
    )(query, key, value, result, result_grad, logsum, row_position, column_position, cosine, sine, w_up, latent_all, latent_gain)


def add_norm(token_blocks, blocks, w_even, w_odd, gain):
    count, width = token_blocks[0].shape
    many = len(blocks)
    chips = many // 2
    half = chips * count
    length = count * many
    depth = blocks[0].shape[1]

    def kernel(we_ref, wo_ref, g_ref, *refs):
        parts, tokens = refs[:many], refs[many : 2 * many]
        n_ref, r_ref, x_ref, a_ref = refs[2 * many :]
        for q in range(many):
            for p in range(chips):
                other = p ^ (q % chips)
                a_ref[p * count : (p + 1) * count, q * depth : (q + 1) * depth] = parts[q][
                    other * count : (other + 1) * count
                ]
        for h in range(2):

            @pl.when(pl.program_id(0) == h)
            def _():
                for k in range(chips):
                    x_ref[k * count : (k + 1) * count] = tokens[h * chips + k][...]

        middle = chips * depth
        total = dot(a_ref[:, :middle], we_ref[...]) + dot(a_ref[:, middle:], wo_ref[...])
        total = total + x_ref[...].astype(F32)
        inverse = lax.rsqrt(jnp.mean(total * total, axis=1, keepdims=True) + eps_norm)
        n_ref[...] = (total * inverse * g_ref[...]).astype(BF)

        @pl.when(pl.program_id(0) == 0)
        def _():
            r_ref[...] = total[:count]

    def source(q):
        return pl.BlockSpec((half, depth), lambda i: (i ^ (q // chips), 0))

    return pl.pallas_call(
        kernel,
        grid=(2,),
        in_specs=[whole(w_even.shape), whole(w_odd.shape), whole((1, width))]
        + [source(q) for q in range(many)]
        + [whole((count, width))] * many,
        out_specs=[pl.BlockSpec((half, width), lambda i: (i, 0)), whole((count, width))],
        out_shape=[
            jax.ShapeDtypeStruct((length, width), BF),
            jax.ShapeDtypeStruct((count, width), F32),
        ],
        scratch_shapes=[pltpu.VMEM((half, width), BF), pltpu.VMEM((half, many * depth), BF)],
        compiler_params=pltpu.CompilerParams(vmem_limit_bytes=LIMIT),
        cost_estimate=pl.CostEstimate(
            flops=4 * length * width * w_even.shape[0],
            transcendentals=0,
            bytes_accessed=6 * length * width + 4 * width * w_even.shape[0],
        ),
        name="add_norm",
    )(w_even, w_odd, gain, *blocks, *token_blocks)


def expert(rows, cots, gate, up, down, piece):
    count, width = rows.shape
    units = gate.shape[2]
    tile = min(512, count)
    step = 256
    full = units // step
    rest = units % step
    spans = [(n * step, step) for n in range(full)] + ([(full * step, rest)] if rest else [])

    def kernel(x_ref, c_ref, gate_hbm, up_hbm, down_hbm, res_ref, in_ref, h_ref, gg_ref, ug_ref, wg, wu, wd, acc_r, acc_i, sems):
        first = pl.program_id(0) == 0

        def copies(n, start, size):
            span = pl.ds(start, size)
            return [
                pltpu.make_async_copy(gate_hbm.at[piece, :, span], wg.at[:, span], sems.at[0, n]),
                pltpu.make_async_copy(up_hbm.at[piece, :, span], wu.at[:, span], sems.at[1, n]),
                pltpu.make_async_copy(down_hbm.at[piece, span, :], wd.at[span, :], sems.at[2, n]),
            ]

        @pl.when(first)
        def _():
            for n, (start, size) in enumerate(spans):
                for copy in copies(n, start, size):
                    copy.start()

        acc_r[...] = jnp.zeros_like(acc_r)
        acc_i[...] = jnp.zeros_like(acc_i)

        def chunk(n, start, size):
            @pl.when(first)
            def _():
                for copy in copies(n, start, size):
                    copy.wait()

            span = pl.ds(start, size)
            x, c = x_ref[...], c_ref[...]
            w_gate, w_up, w_down = wg[:, span], wu[:, span], wd[span, :]
            g = dot(x, w_gate)
            u = dot(x, w_up)
            hidden_grad = dot_t(c, w_down)
            s = jax.nn.sigmoid(g)
            silu = g * s
            hidden = (silu * u).astype(BF)
            gate_grad = (hidden_grad * u * (s * (1.0 + g * (1.0 - s)))).astype(BF)
            up_grad = (hidden_grad * silu).astype(BF)
            h_ref[:, span] = hidden
            gg_ref[:, span] = gate_grad
            ug_ref[:, span] = up_grad
            acc_r[...] += dot(hidden, w_down)
            acc_i[...] += dot_t(gate_grad, w_gate) + dot_t(up_grad, w_up)

        if full:

            @pl.loop(0, full)
            def _(n):
                chunk(n, pl.multiple_of(n * step, step), step)

        if rest:
            chunk(full, full * step, rest)
        res_ref[...] = acc_r[...].astype(BF)
        in_ref[...] = acc_i[...].astype(BF)

    def block(w):
        return pl.BlockSpec((tile, w), lambda i: (i, 0))

    def array(w):
        return jax.ShapeDtypeStruct((count, w), BF)

    return pl.pallas_call(
        kernel,
        grid=(count // tile,),
        in_specs=[block(width), block(width), ANY, ANY, ANY],
        out_specs=[block(width), block(width), block(units), block(units), block(units)],
        out_shape=[array(width), array(width), array(units), array(units), array(units)],
        scratch_shapes=[
            pltpu.VMEM((width, units), BF),
            pltpu.VMEM((width, units), BF),
            pltpu.VMEM((units, width), BF),
            pltpu.VMEM((tile, width), F32),
            pltpu.VMEM((tile, width), F32),
            pltpu.SemaphoreType.DMA((3, len(spans))),
        ],
        compiler_params=pltpu.CompilerParams(vmem_limit_bytes=LIMIT),
        cost_estimate=pl.CostEstimate(
            flops=12 * count * width * units,
            transcendentals=count * units,
            bytes_accessed=6 * width * units + 8 * count * width + 6 * count * units,
        ),
        name="expert",
    )(rows, cots, gate, up, down)


def expert_weights(rows, cots, hidden, gate_grad, up_grad, piece, pieces, earlier):
    count, width = rows.shape
    units = hidden.shape[1]
    tile = 256

    def kernel(x_ref, c_ref, h_ref, gg_ref, ug_ref, *refs):
        g_ref, u_ref, d_ref = refs[-3:]
        g_ref[0] = t_dot(x_ref[...], gg_ref[...])
        u_ref[0] = t_dot(x_ref[...], ug_ref[...])
        d_ref[0] = t_dot(h_ref[...], c_ref[...])

    tall = pl.BlockSpec((1, tile, units), lambda i: (piece, i, 0))
    flat = pl.BlockSpec((1, units, tile), lambda i: (piece, 0, i))
    column = pl.BlockSpec((count, tile), lambda i: (0, i))
    kept = list(earlier or ())
    return pl.pallas_call(
        kernel,
        grid=(width // tile,),
        in_specs=[column, column] + [whole((count, units))] * 3 + [ANY] * len(kept),
        out_specs=[tall, tall, flat],
        out_shape=[
            jax.ShapeDtypeStruct((pieces, width, units), F32),
            jax.ShapeDtypeStruct((pieces, width, units), F32),
            jax.ShapeDtypeStruct((pieces, units, width), F32),
        ],
        input_output_aliases={5 + n: n for n in range(len(kept))},
        compiler_params=pltpu.CompilerParams(vmem_limit_bytes=LIMIT),
        cost_estimate=pl.CostEstimate(
            flops=6 * count * width * units,
            transcendentals=0,
            bytes_accessed=12 * width * units + 4 * count * width,
        ),
        name="expert_weights",
    )(rows, cots, hidden, gate_grad, up_grad, *kept)


def dispatch(select, rows, slot_weight, pieces):
    blocks, slots, count = select.shape
    width = rows.shape[1]
    others = slots // pieces // CAP

    def kernel(m_ref, x_ref, *refs):
        got = dot(m_ref[0], x_ref[...])
        if slot_weight is not None:
            got = got * refs[0][0]
        got = got.astype(BF)
        for i in range(pieces):
            for j in range(others):
                start = (i * others + j) * CAP
                refs[-pieces + i][j] = got[start : start + CAP]

    weights = [] if slot_weight is None else [slot_weight]
    out = pl.BlockSpec((others, CAP, width), lambda b: (0, b, 0))
    return pl.pallas_call(
        kernel,
        grid=(blocks,),
        in_specs=[
            pl.BlockSpec((1, slots, count), lambda b: (b, 0, 0)),
            pl.BlockSpec((count, width), lambda b: (b, 0)),
        ]
        + [pl.BlockSpec((1, slots, 1), lambda b: (b, 0, 0))] * len(weights),
        out_specs=[out] * pieces,
        out_shape=[jax.ShapeDtypeStruct((others, blocks * CAP, width), BF)] * pieces,
        compiler_params=pltpu.CompilerParams(vmem_limit_bytes=LIMIT),
        cost_estimate=pl.CostEstimate(
            flops=2 * blocks * slots * count * width,
            transcendentals=0,
            bytes_accessed=2 * blocks * (slots + count) * width,
        ),
        name="dispatch",
    )(select, rows, *weights)


def down_weights(normed, down_rows, sums, gain_rows):
    count, columns = down_rows.shape
    devices, extra, _ = sums.shape
    per = 128 // gain_rows

    def kernel(n_ref, d_ref, s_ref, o_ref):
        part = t_dot(n_ref[...], d_ref[...]).astype(BF)
        for i in range(per):
            o_ref[i, :gain_rows] = part[i * gain_rows : (i + 1) * gain_rows]
            o_ref[i, gain_rows:] = s_ref[i]

    return pl.pallas_call(
        kernel,
        grid=(devices // per,),
        in_specs=[
            pl.BlockSpec((count, 128), lambda i: (0, i)),
            whole((count, columns)),
            pl.BlockSpec((per, extra, columns), lambda i: (i, 0, 0)),
        ],
        out_specs=pl.BlockSpec((per, gain_rows + extra, columns), lambda i: (i, 0, 0)),
        out_shape=jax.ShapeDtypeStruct((devices, gain_rows + extra, columns), BF),
        cost_estimate=pl.CostEstimate(
            flops=2 * devices * gain_rows * count * columns,
            transcendentals=0,
            bytes_accessed=4 * devices * (gain_rows + extra) * columns,
        ),
        name="down_weights",
    )(normed, down_rows, sums)


def combine(base, masks, returned, products, dtype):
    half = masks[0].shape[0] // 2
    slots, count = masks[0].shape[1:]
    pieces = len(returned)
    others, _, width = returned[0].shape
    many = len(masks)

    tile = 512

    def kernel(*refs):
        mask_refs, row_refs = refs[:many], refs[many : many + pieces]
        rest, out_ref = refs[many + pieces : -1], refs[-1]
        total = 0.0
        for n, (_, _, flipped) in enumerate(products):
            total = total + (dot_t if flipped else dot)(rest[2 * n][...], rest[2 * n + 1][...])
        for b in range(half):
            rows = jnp.concatenate(
                [
                    row_refs[i][j, b * CAP : (b + 1) * CAP]
                    for i in range(pieces)
                    for j in range(others)
                ],
                axis=0,
            )
            block = total[b * count : (b + 1) * count]
            for mask_ref in mask_refs:
                block = block + t_dot(mask_ref[b], rows)
            out_ref[b * count : (b + 1) * count] = block.astype(dtype)

    factors = []
    specs = []
    for left, right, flipped in products:
        factors += [left, right]
        specs.append(pl.BlockSpec((half * count, left.shape[1]), lambda t: (base, 0)))
        if flipped:
            specs.append(pl.BlockSpec((tile, right.shape[1]), lambda t: (t, 0)))
        else:
            specs.append(pl.BlockSpec((right.shape[0], tile), lambda t: (0, t)))
    return pl.pallas_call(
        kernel,
        grid=(width // tile,),
        in_specs=[pl.BlockSpec((half, slots, count), lambda t: (base, 0, 0))] * many
        + [pl.BlockSpec((others, half * CAP, tile), lambda t: (0, base, t))] * pieces
        + specs,
        out_specs=pl.BlockSpec((half * count, tile), lambda t: (0, t)),
        out_shape=jax.ShapeDtypeStruct((half * count, width), dtype),
        compiler_params=pltpu.CompilerParams(vmem_limit_bytes=LIMIT),
        cost_estimate=pl.CostEstimate(
            flops=2 * half * count * width * (many * slots + sum(p[0].shape[1] for p in products)),
            transcendentals=0,
            bytes_accessed=half * count * width * 6,
        ),
        name="combine",
    )(*masks, *returned, *factors)


def swap(x, axis, mask):
    n = lax.axis_size(axis)
    return lax.ppermute(x, axis, [(i, i ^ mask) for i in range(n)])


def after(x, *earlier):
    return lax.optimization_barrier((x, *earlier))[0]


class Lane:
    def __init__(self, axis, depth):
        self.axis = axis
        self.depth = depth
        self.sent = []

    def send(self, x, mask):
        if len(self.sent) >= self.depth:
            x = after(x, self.sent[-self.depth])
        got = swap(x, self.axis, mask)
        self.sent.append(got)
        return got

    def chips(self, x):
        chips = lax.axis_size("seq") // 2
        return [x] + [self.send(x, 2 * k) for k in range(1, chips)]

    def group(self, x):
        evens = self.chips(x)
        rows = x.shape[0]
        everything = slice(None)
        (even,) = arrange(
            jnp.zeros((1,), jnp.int32),
            evens,
            [(rows * len(evens), x.shape[1])],
            [
                (k, everything, 0, lambda ref, k=k: (slice(k * rows, (k + 1) * rows), everything))
                for k in range(len(evens))
            ],
        )
        return even, swap(even, "seq", 1)

    def scatter(self, even, odd):
        chips = lax.axis_size("seq") // 2
        rows = even.shape[0] // chips
        got = swap(odd.astype(BF), "seq", 1)
        blocks = [
            even[k * rows : (k + 1) * rows] + got[k * rows : (k + 1) * rows].astype(F32)
            for k in range(chips)
        ]
        total = blocks[0]
        for k in range(1, chips):
            total = total + self.send(blocks[k].astype(BF), 2 * k).astype(F32)
        return total

    def others(self, x):
        return [x] + [self.send(x, j) for j in range(1, lax.axis_size("exp"))]

def relative_order(count):
    chips = count // 2
    return [2 * k for k in range(chips)] + [2 * k + 1 for k in range(chips)]


def sum_exp(x, axis):
    return lax.psum_scatter(x.astype(BF), "exp", scatter_dimension=axis, tiled=True).astype(F32)


def shards(
    tokens,
    routes,
    route_weights,
    norm_gain,
    w_query,
    w_kv_down,
    latent_gain,
    w_kv_up,
    w_output,
    ffn_gain,
    shared_gate,
    shared_up,
    shared_down,
    expert_gate,
    expert_up,
    expert_down,
    out_grad,
):
    count, width = tokens.shape
    n_seq = lax.axis_size("seq")
    n_exp = lax.axis_size("exp")
    seq = lax.axis_index("seq")
    order = relative_order(n_seq)
    chips = n_seq // 2
    heads = H // n_seq
    length = count * n_seq
    half = length // 2
    pieces = expert_gate.shape[0]
    parts_per = pieces * n_seq * n_exp // EXPERTS
    factor = 1.0 / math.sqrt(DN + DR)
    gain_rows = norm_gain.shape[0]
    latent_rows_local = latent_gain.shape[0]
    along = Lane("seq", 3)
    across = Lane("exp", 2)

    index = jnp.stack([lax.axis_index("exp"), seq]).astype(jnp.int32)
    packed = jnp.concatenate(
        [
            w_kv_down,
            norm_gain[:, None],
            ffn_gain[:, None],
            jnp.pad(latent_gain, (0, gain_rows - latent_rows_local))[:, None],
            jnp.zeros((gain_rows, 61), BF),
        ],
        axis=1,
    )
    down_full = lax.all_gather(packed, ("exp", "seq"), axis=0, tiled=True)
    gate_cols = lax.all_gather(shared_gate, "exp", axis=0, tiled=True)
    lift_cols = lax.all_gather(shared_up, "exp", axis=0, tiled=True)
    drop_rows = lax.all_gather(shared_down, "exp", axis=1, tiled=True)
    token_even = along.chips(tokens)
    token_odd = [swap(x, "seq", 1) for x in token_even]
    token_blocks = token_even + token_odd
    ratio = w_query.shape[0] // w_kv_up.shape[0]
    slim = w_kv_up.shape[1] // ratio
    first_parts = across.others(
        jnp.concatenate(
            [
                w_query,
                jnp.concatenate(
                    [w_kv_up[:, g * slim : (g + 1) * slim] for g in range(ratio)], axis=0
                ),
            ],
            axis=1,
        )
    )
    output_even = jnp.concatenate(along.chips(after(w_output, *token_odd)), axis=0)
    route_pack = jnp.concatenate([routes.astype(F32).T, route_weights.T], axis=0)
    route_even = jnp.stack(along.chips(after(route_pack, *token_odd)))
    route_all = jnp.concatenate([route_even, swap(route_even, "seq", 1)], axis=0)
    output_parts = across.others(output_even)

    everything = slice(None)
    block_rows = width // n_exp
    gain_first = down_full[:, R + DR].astype(F32).reshape(1, width)
    gain_second = down_full[:, R + DR + 1].astype(F32).reshape(1, width)
    latent_wide = (
        down_full[:, R + DR + 2]
        .reshape(n_exp * n_seq, gain_rows)[:, :latent_rows_local]
        .reshape(1, R)
        .astype(F32)
    )
    up_rows = w_kv_up.shape[0]
    query_width = w_query.shape[1]
    (up_cols,) = arrange(
        index,
        first_parts,
        [(R, w_kv_up.shape[1])],
        [
            (
                j,
                (slice(g * up_rows, (g + 1) * up_rows), slice(query_width, query_width + slim)),
                0,
                lambda ref, j=j, g=g: (
                    span(ref[0] ^ j, up_rows),
                    slice(g * slim, (g + 1) * slim),
                ),
            )
            for j in range(n_exp)
            for g in range(ratio)
        ],
    )
    (output_even,) = arrange(
        index,
        output_parts,
        [(H * DV // 2, width)],
        [
            (j, everything, 0, lambda ref, j=j: (everything, span(ref[0] ^ j, block_rows)))
            for j in range(n_exp)
        ],
    )
    output_odd = swap(output_even, "seq", 1)

    positions = jnp.concatenate(
        [(seq ^ r) * count + jnp.arange(count, dtype=jnp.int32) for r in order]
    )
    row_position, column_position = positions[None, :], positions[:, None]
    cosine_table, sine_table = rope_tables(positions, DR)
    cosine_wide = jnp.concatenate([cosine_table, cosine_table], axis=1)
    sine_wide = jnp.concatenate([-sine_table, sine_table], axis=1)
    normed_one, latent_all, latent_raw, query_heads, key_heads, value_heads = project(
        index,
        token_blocks,
        gain_first,
        first_parts,
        down_full,
        latent_wide,
        up_cols,
        cosine_wide,
        sine_wide,
        heads,
    )
    result, logsum = attend(
        query_heads, key_heads, value_heads, row_position, column_position, factor
    )

    result_even = along.chips(result)
    result_blocks = result_even + [swap(x, "seq", 1) for x in result_even]
    normed_two, residual = add_norm(
        token_blocks, result_blocks, output_even, output_odd, gain_second
    )
    inverse_two = inverse_rms(residual)
    grad_even, grad_odd = along.group(out_grad)
    (grad_rows,) = arrange(
        index,
        [grad_even, grad_odd],
        [(length, width)],
        [
            (h, everything, 0, lambda ref, h=h: (slice(h * half, (h + 1) * half), everything))
            for h in range(2)
        ],
    )

    column = jnp.stack(
        [
            ((other * n_seq + seq) * pieces + i) // parts_per
            for i in range(pieces)
            for other in range(n_exp)
        ]
    )
    kinds = n_exp * pieces
    named = route_all[:, None, :TOP, :].astype(jnp.int32) == column[None, :, None, None]
    matched = jnp.any(named, axis=2)
    match_weight = jnp.sum(jnp.where(named, route_all[:, None, TOP:, :], 0.0), axis=2)
    earlier = (jnp.arange(count)[:, None] < jnp.arange(count)[None, :]).astype(BF)
    rank = jnp.dot(matched.astype(BF), earlier, preferred_element_type=F32).astype(jnp.int32)
    chosen = (rank[:, :, None, :] == jnp.arange(CAP, dtype=jnp.int32)[None, None, :, None]) & (
        matched[:, :, None, :]
    )
    select = chosen.astype(BF).reshape(n_seq, kinds * CAP, count)
    weighted = jnp.where(chosen, match_weight[:, :, None, :], 0.0).reshape(
        n_seq, kinds * CAP, count
    )
    slot_weight = jnp.sum(weighted, axis=2, keepdims=True)
    weighted_high = weighted.astype(BF)
    weighted_low = (weighted - weighted_high.astype(F32)).astype(BF)

    def give(rows):
        return lax.all_to_all(rows, "exp", split_axis=0, concat_axis=0, tiled=True)

    send_cots = dispatch(select, grad_rows, slot_weight, pieces)
    received_grad = [give(rows) for rows in send_cots]
    send_rows = dispatch(select, normed_two, None, pieces)
    received = [give(rows) for rows in send_rows]

    own_heads = jnp.concatenate(
        [block[p * count : (p + 1) * count] for p, block in enumerate(result_blocks)], axis=1
    )
    attention_parts = across.others(after(own_heads, received_grad[-1]))

    slot_rows = n_exp * n_seq * CAP
    pairs = []
    results_back, grads_back, kept = [], [], []
    for i in range(pieces):
        rows = received[i].reshape(slot_rows, width)
        cots = received_grad[i].reshape(slot_rows, width)
        expert_result, input_grad, *saved = expert(
            rows, cots, expert_gate, expert_up, expert_down, i
        )
        grads_back.append(give(input_grad.reshape(n_exp, n_seq * CAP, width)))
        results_back.append(expert_result.reshape(n_exp, n_seq * CAP, width))
        kept.append((rows, cots, *saved))
    last = input_grad
    results_back = [give(after(rows, grads_back[-1])) for rows in results_back]
    expert_grads = None
    for i in range(pieces):
        expert_grads = expert_weights(after(kept[i][0], last), *kept[i][1:], i, pieces, expert_grads)
    expert_gate_grad, expert_up_grad, expert_down_grad = expert_grads

    shared_rows = after(normed_two, *send_rows)
    shared_gate_raw = dot(shared_rows, gate_cols)
    shared_up_raw = dot(shared_rows, lift_cols)
    shared_hidden = (jax.nn.silu(shared_gate_raw) * shared_up_raw).astype(BF)
    shared_hidden_grad = dot_t(grad_rows, drop_rows)
    sgate_grad = (shared_hidden_grad * shared_up_raw * silu_slope(shared_gate_raw)).astype(BF)
    sup_grad = (shared_hidden_grad * jax.nn.silu(shared_gate_raw)).astype(BF)
    two_products = [(sgate_grad, gate_cols, True), (sup_grad, lift_cols, True)]
    two_odd = combine(1, [select], grads_back, two_products, BF)
    two_even = combine(0, [select], grads_back, two_products, F32)
    two_grad = along.scatter(two_even, two_odd)
    gate_out = sum_exp(t_dot(shared_rows, sgate_grad), 0)
    lift_out = sum_exp(t_dot(shared_rows, sup_grad), 0)
    drop_out = sum_exp(t_dot(shared_hidden, grad_rows), 1)

    two_grad = after(two_grad, *expert_grads, results_back[0])
    residual_norm_grad, second_terms = norm_back(
        two_grad, residual, inverse_two, gain_second
    )
    residual_grad = out_grad.astype(F32) + residual_norm_grad
    residual_half = residual_grad.astype(BF)
    even_heads = dot_t(residual_half, output_even).astype(BF)
    odd_heads = dot_t(residual_half, output_odd).astype(BF)
    wide = heads * DV
    pairs = [
        jnp.stack([even_heads[:, k * wide : (k + 1) * wide], odd_heads[:, k * wide : (k + 1) * wide]])
        for k in range(chips)
    ]
    pairs = [pairs[0]] + [along.send(pairs[k], 2 * k) for k in range(1, chips)]
    other_half = swap(jnp.stack([pair[1] for pair in pairs]), "seq", 1)
    attention_grad = jnp.concatenate(
        [jnp.stack([pair[0] for pair in pairs]), other_half], axis=0
    ).reshape(length, wide)
    mine = lax.axis_index("exp")
    column_blocks = [
        lax.dynamic_slice_in_dim(residual_half, (mine ^ j) * block_rows, block_rows, 1)
        for j in range(n_exp)
    ]
    column_blocks = [column_blocks[0]] + [
        across.send(column_blocks[j], j) for j in range(1, n_exp)
    ]
    output_part = t_dot(
        jnp.concatenate(attention_parts, axis=0), jnp.concatenate(column_blocks, axis=0)
    )
    output_out = along.scatter(output_part[: H * DV // 2], output_part[H * DV // 2 :])

    out_products = [(shared_hidden, drop_rows, False)]
    out_masks = [weighted_high, weighted_low]
    out_odd = combine(1, out_masks, results_back, out_products, BF)
    out_even = combine(0, out_masks, results_back, out_products, F32)

    query_in_grad, kv_grad, latent_part, latent_sum = attend_back(
        query_heads,
        key_heads,
        value_heads,
        result,
        after(attention_grad, out_odd, out_even),
        logsum,
        row_position,
        column_position,
        cosine_wide,
        -sine_wide,
        up_cols,
        latent_all,
        latent_wide,
        factor,
    )
    latent_grad = along.scatter(latent_part[:half], latent_part[half:])
    one_odd, odd_sum = query_back(
        index, 1, query_in_grad, first_parts, normed_one, gain_first, BF
    )
    one_even, even_sum = query_back(
        index, 0, query_in_grad, first_parts, normed_one, gain_first, F32
    )
    one_grad = along.scatter(one_even, one_odd)
    up_out = sum_exp(t_dot(latent_all, kv_grad), 0)
    query_out = sum_exp(t_dot(normed_one, query_in_grad), 0)
    latent_raw_grad, _ = norm_back(
        latent_grad[:, :R], latent_raw[:count], inverse_rms(latent_raw[:count]), latent_wide
    )
    down_rows = jnp.concatenate(
        [
            latent_raw_grad,
            rotate(latent_grad[:, R:], cosine_table[:count], -sine_table[:count]),
        ],
        axis=1,
    ).astype(BF)
    devices = n_exp * n_seq
    sums = jnp.concatenate(
        [
            (odd_sum + even_sum).reshape(devices, gain_rows),
            jnp.sum(second_terms, axis=0).reshape(devices, gain_rows),
            latent_sum.reshape(devices, latent_rows_local),
        ],
        axis=1,
    )
    many = sums.shape[1]
    sums = jnp.pad(sums[:, None, :], ((0, 0), (0, 15), (0, R + DR - many))).astype(BF)
    down_part = down_weights(normed_one, down_rows, sums, gain_rows)
    down_sum = lax.psum_scatter(
        down_part.reshape(devices * (gain_rows + 16), R + DR),
        ("exp", "seq"),
        scatter_dimension=0,
        tiled=True,
    ).astype(F32)
    down_out = down_sum[:gain_rows]
    small = down_sum[gain_rows, :many]
    first_out = small[:gain_rows] + jnp.sum(
        w_kv_down.astype(F32) * down_out, axis=1
    ) / norm_gain.astype(F32)
    output = (residual + along.scatter(out_even, out_odd)).astype(BF)

    down_back = dot_t(down_rows, down_full[:, : R + DR])
    token_wide = tokens.astype(F32)
    token_norm_grad, _ = norm_back(
        one_grad + down_back, token_wide, inverse_rms(token_wide), gain_first
    )
    tokens_grad = (residual_grad + token_norm_grad).astype(BF)
    return (
        output,
        tokens_grad,
        first_out,
        query_out,
        down_out,
        small[2 * gain_rows : many],
        up_out,
        output_out,
        small[gain_rows : 2 * gain_rows],
        gate_out,
        lift_out,
        drop_out,
        expert_gate_grad,
        expert_up_grad,
        expert_down_grad,
    )


def solution(mesh):
    rows = P(("exp", "seq"), None)
    line = P(("exp", "seq"))
    grid = P("exp", "seq")
    turned = P("seq", "exp")
    part = P(("exp", "seq"), None, None)
    return jax.shard_map(
        shards,
        mesh=mesh,
        in_specs=(
            rows,
            rows,
            rows,
            line,
            grid,
            rows,
            line,
            grid,
            turned,
            line,
            grid,
            grid,
            turned,
            part,
            part,
            part,
            rows,
        ),
        out_specs=(
            rows,
            rows,
            line,
            grid,
            rows,
            line,
            grid,
            turned,
            line,
            grid,
            grid,
            turned,
            part,
            part,
            part,
        ),
        check_vma=False,
    )
```

```python
import math

import jax
import jax.numpy as jnp
from jax import lax
from jax.experimental import pallas as pl
from jax.experimental.pallas import tpu as pltpu
from jax.sharding import PartitionSpec as P

H = 16
DN = 128
DR = 64
DV = 128
R = 512
EXPERTS = 64
TOP = 6
CAP = 16


eps_norm = 1e-06
rope_base = 50000.0
BF = jnp.bfloat16
F32 = jnp.float32


def dot(a, b):
    return jnp.dot(a, b, preferred_element_type=F32)


def dot_t(a, b):
    return lax.dot_general(a, b, (((1,), (1,)), ((), ())), preferred_element_type=F32)


def t_dot(a, b):
    return lax.dot_general(a, b, (((0,), (0,)), ((), ())), preferred_element_type=F32)


def rope_tables(positions, width):
    middle = width // 2
    frequency = rope_base ** (-(jnp.arange(middle, dtype=F32) * 2.0 / width))
    angles = positions.astype(F32)[:, None] * frequency[None, :]
    return (jnp.cos(angles), jnp.sin(angles))


def rotate(values, cosine_table, sine_table):
    middle = values.shape[-1] // 2
    leading = values[..., :middle]
    trailing = values[..., middle:]
    return jnp.concatenate(
        [
            leading * cosine_table - trailing * sine_table,
            trailing * cosine_table + leading * sine_table,
        ],
        axis=-1,
    )


def silu_slope(gate_values):
    sigmoid = jax.nn.sigmoid(gate_values)
    return sigmoid * (1.0 + gate_values * (1.0 - sigmoid))


def norm_back(dy, v, inverse, gain):
    hat = v * inverse
    scaled = dy * gain
    dv = inverse * (scaled - hat * jnp.mean(scaled * hat, axis=-1, keepdims=True))
    return dv, dy * hat


def inverse_rms(v):
    return lax.rsqrt(jnp.mean(v * v, axis=-1, keepdims=True) + eps_norm)


LIMIT = 56 * 1024 * 1024
LIGHT = pl.CostEstimate(flops=0, transcendentals=0, bytes_accessed=0)
ANY = pl.BlockSpec(memory_space=pl.ANY)
SCALARS = pl.BlockSpec(memory_space=pltpu.SMEM)


def whole(shape):
    return pl.BlockSpec(shape, lambda *grid: (0,) * len(shape))


def arrange(index, blocks, outs, plan):
    def kernel(index_ref, *refs):
        sources = refs[: len(blocks)]
        targets = refs[len(blocks) :]
        for block, source, out, target in plan:
            targets[out][target(index_ref)] = sources[block][source]

    return pl.pallas_call(
        kernel,
        out_shape=[jax.ShapeDtypeStruct(s, BF) for s in outs],
        in_specs=[SCALARS] + [pl.BlockSpec(memory_space=pltpu.VMEM)] * len(blocks),
        out_specs=[pl.BlockSpec(memory_space=pltpu.VMEM)] * len(outs),
        compiler_params=pltpu.CompilerParams(vmem_limit_bytes=LIMIT),
        cost_estimate=LIGHT,
        name="arrange",
    )(index, *blocks)


def span(start, size):
    return pl.ds(pl.multiple_of(start * size, size), size)


def turned(v, cosine, sine):
    middle = v.shape[1] // 2
    return v * cosine + jnp.concatenate([v[:, middle:], v[:, :middle]], axis=1) * sine


def project(token_blocks, gain, w_first, w_down, latent_gain, w_up, cosine, sine, heads):
    count, width = token_blocks[0].shape
    chips = len(token_blocks) // 2
    half = chips * count
    wide = DN + DR
    columns = heads * wide

    def kernel(g_ref, wd_ref, lg_ref, wu_ref, c_ref, s_ref, *refs):
        tokens, w_ref = refs[: 2 * chips], refs[2 * chips]
        n_ref, l_ref, r_ref, q_ref, k_ref, v_ref, x_ref = refs[2 * chips + 1 :]
        for h in range(2):

            @pl.when(pl.program_id(0) == h)
            def _():
                for k in range(chips):
                    x_ref[k * count : (k + 1) * count] = tokens[h * chips + k][...]

        x = x_ref[...].astype(F32)
        inverse = lax.rsqrt(jnp.mean(x * x, axis=1, keepdims=True) + eps_norm)
        n_ref[...] = (x * inverse * g_ref[...]).astype(BF)
        down = dot(n_ref[...], wd_ref[...])
        raw = down[:, :R]
        r_ref[...] = raw
        inverse = lax.rsqrt(jnp.mean(raw * raw, axis=1, keepdims=True) + eps_norm)
        l_ref[...] = (raw * inverse * lg_ref[...]).astype(BF)
        query = dot(n_ref[...], w_ref[:, :columns])
        up = dot(l_ref[...], wu_ref[...]).astype(BF)
        cosine, sine = c_ref[...], s_ref[...]
        zeros = jnp.zeros((half, 256 - wide), BF)
        rope = jnp.concatenate([turned(down[:, R : R + DR], cosine, sine).astype(BF), zeros], axis=1)
        for n in range(heads):
            own = query[:, n * wide : (n + 1) * wide]
            q_ref[n, :, :DN] = own[:, :DN].astype(BF)
            q_ref[n, :, DN:] = jnp.concatenate(
                [turned(own[:, DN:], cosine, sine).astype(BF), zeros], axis=1
            )
            k_ref[n, :, :DN] = up[:, n * (DN + DV) : n * (DN + DV) + DN]
            k_ref[n, :, DN:] = rope
            v_ref[n] = up[:, n * (DN + DV) + DN : (n + 1) * (DN + DV)]

    def rows(w):
        return pl.BlockSpec((half, w), lambda i: (i, 0))

    def head_rows(w):
        return pl.BlockSpec((heads, half, w), lambda i: (0, i, 0))

    length = 2 * half
    return pl.pallas_call(
        kernel,
        grid=(2,),
        in_specs=[
            whole((1, width)),
            whole(w_down.shape),
            whole((1, R)),
            whole(w_up.shape),
            rows(DR),
            rows(DR),
        ]
        + [whole((count, width))] * (2 * chips)
        + [whole(w_first.shape)],
        out_specs=[rows(width), rows(R), rows(R), head_rows(256), head_rows(256), head_rows(DV)],
        out_shape=[
            jax.ShapeDtypeStruct((length, width), BF),
            jax.ShapeDtypeStruct((length, R), BF),
            jax.ShapeDtypeStruct((length, R), F32),
            jax.ShapeDtypeStruct((heads, length, 256), BF),
            jax.ShapeDtypeStruct((heads, length, 256), BF),
            jax.ShapeDtypeStruct((heads, length, DV), BF),
        ],
        scratch_shapes=[pltpu.VMEM((half, width), BF)],
        compiler_params=pltpu.CompilerParams(vmem_limit_bytes=LIMIT),
        cost_estimate=LIGHT,
        name="project",
    )(gain, w_down, latent_gain, w_up, cosine, sine, *token_blocks, w_first)


def query_back(base, query_grad, w_first, normed, gain, dtype):
    length, columns = query_grad.shape
    half = length // 2
    width = normed.shape[1]
    tile = 512

    def kernel(q_ref, n_ref, g_ref, w_ref, o_ref, t_ref):
        part = dot_t(q_ref[...], w_ref[:, :columns])
        o_ref[...] = part.astype(dtype)
        product = part * n_ref[...].astype(F32)
        t_ref[...] = jnp.sum(product, axis=0, keepdims=True) / g_ref[...]

    return pl.pallas_call(
        kernel,
        grid=(width // tile,),
        in_specs=[
            pl.BlockSpec((half, columns), lambda i: (base, 0)),
            pl.BlockSpec((half, tile), lambda i: (base, i)),
            pl.BlockSpec((1, tile), lambda i: (0, i)),
            pl.BlockSpec((tile, w_first.shape[1]), lambda i: (i, 0)),
        ],
        out_specs=[
            pl.BlockSpec((half, tile), lambda i: (0, i)),
            pl.BlockSpec((1, tile), lambda i: (0, i)),
        ],
        out_shape=[
            jax.ShapeDtypeStruct((half, width), dtype),
            jax.ShapeDtypeStruct((1, width), F32),
        ],
        compiler_params=pltpu.CompilerParams(vmem_limit_bytes=LIMIT),
        cost_estimate=LIGHT,
        name="query_back",
    )(query_grad, normed, gain, w_first)


def attend(query, key, value, row_position, column_position, factor):
    heads, length, _ = query.shape
    tile = 256

    def kernel(q_ref, k_ref, v_ref, row_ref, column_ref, o_ref, s_ref):
        allowed = column_ref[...] <= row_ref[...]
        for n in range(heads):
            scores = dot_t(k_ref[n], q_ref[n]) * factor
            exponent = jnp.where(allowed, jnp.exp(jnp.where(allowed, scores, -1e30)), 0.0)
            total = jnp.sum(exponent, axis=0, keepdims=True)
            probs = (exponent / total).astype(BF)
            o_ref[:, n * DV : (n + 1) * DV] = t_dot(v_ref[n], probs).T.astype(BF)
            s_ref[n : n + 1, :] = jnp.log(total)

    return pl.pallas_call(
        kernel,
        grid=(length // tile,),
        in_specs=[
            pl.BlockSpec((heads, tile, 256), lambda i: (0, i, 0)),
            whole(key.shape),
            whole(value.shape),
            pl.BlockSpec((1, tile), lambda i: (0, i)),
            whole((length, 1)),
        ],
        out_specs=[
            pl.BlockSpec((tile, heads * DV), lambda i: (i, 0)),
            pl.BlockSpec((heads, tile), lambda i: (0, i)),
        ],
        out_shape=[
            jax.ShapeDtypeStruct((length, heads * DV), BF),
            jax.ShapeDtypeStruct((heads, length), F32),
        ],
        compiler_params=pltpu.CompilerParams(vmem_limit_bytes=LIMIT),
        cost_estimate=LIGHT,
        name="attend",
    )(query, key, value, row_position, column_position)


def attend_back(query, key, value, result, result_grad, logsum, row_position, column_position, cosine, sine, w_up, latent_all, latent_gain, factor):
    heads, length, _ = query.shape
    tile = 256
    steps = length // tile
    wide = DN + DR

    def kernel(q_ref, k_ref, v_ref, o_ref, do_ref, ls_ref, row_ref, column_ref, c_ref, s_ref, wu_ref, l_ref, lg_ref, dq_ref, kv_ref, lp_ref, t_ref, dk_acc, dv_acc, kt):
        step = pl.program_id(0)

        @pl.when(step == 0)
        def _():
            dk_acc[...] = jnp.zeros_like(dk_acc)
            dv_acc[...] = jnp.zeros_like(dv_acc)
            for n in range(heads):
                kt[n] = k_ref[n].T

        allowed = column_ref[...] <= row_ref[...]
        cosine, sine = c_ref[...], s_ref[...]
        parts = []
        for n in range(heads):
            q = q_ref[n]
            grad = do_ref[:, n * DV : (n + 1) * DV]
            scores = jnp.where(allowed, dot_t(k_ref[n], q) * factor, -1e30)
            probs = jnp.exp(scores - ls_ref[n : n + 1, :])
            dv_acc[n] += dot(probs.astype(BF), grad)
            product = grad.astype(F32) * o_ref[:, n * DV : (n + 1) * DV].astype(F32)
            row_dot = jnp.sum(product.T, axis=0, keepdims=True)
            probs_grad = dot_t(v_ref[n], grad)
            score_grad = (probs * (probs_grad - row_dot) * factor).astype(BF)
            dk_acc[n] += dot(score_grad, q)
            query_grad = dot(kt[n], score_grad).T.astype(BF)
            parts.append(query_grad[:, :DN])
            parts.append(turned(query_grad[:, DN:wide].astype(F32), cosine, sine).astype(BF))
        dq_ref[...] = jnp.concatenate(parts, axis=1)

        @pl.when(step == steps - 1)
        def _():
            rope = jnp.zeros((length, DR), F32)
            for n in range(heads):
                key_grad = dk_acc[n].astype(BF)
                value_grad = dv_acc[n].astype(BF)
                base = n * (DN + DV)
                kv_ref[:, base : base + DN] = key_grad[:, :DN]
                kv_ref[:, base + DN : base + DN + DV] = value_grad
                rope = rope + key_grad[:, DN:wide].astype(F32)
            latent = dot_t(kv_ref[...], wu_ref[...])
            lp_ref[:, :R] = latent
            lp_ref[:, R:] = rope
            t_ref[...] = jnp.sum(
                latent * l_ref[...].astype(F32), axis=0, keepdims=True
            ) / lg_ref[...]

    return pl.pallas_call(
        kernel,
        grid=(steps,),
        in_specs=[
            pl.BlockSpec((heads, tile, 256), lambda i: (0, i, 0)),
            whole(key.shape),
            whole(value.shape),
            pl.BlockSpec((tile, heads * DV), lambda i: (i, 0)),
            pl.BlockSpec((tile, heads * DV), lambda i: (i, 0)),
            pl.BlockSpec((heads, tile), lambda i: (0, i)),
            pl.BlockSpec((1, tile), lambda i: (0, i)),
            whole((length, 1)),
            pl.BlockSpec((tile, DR), lambda i: (i, 0)),
            pl.BlockSpec((tile, DR), lambda i: (i, 0)),
            whole(w_up.shape),
            whole((length, R)),
            whole((1, R)),
        ],
        out_specs=[
            pl.BlockSpec((tile, heads * wide), lambda i: (i, 0)),
            whole((length, heads * (DN + DV))),
            whole((length, R + DR)),
            whole((1, R)),
        ],
        out_shape=[
            jax.ShapeDtypeStruct((length, heads * wide), BF),
            jax.ShapeDtypeStruct((length, heads * (DN + DV)), BF),
            jax.ShapeDtypeStruct((length, R + DR), F32),
            jax.ShapeDtypeStruct((1, R), F32),
        ],
        scratch_shapes=[
            pltpu.VMEM((heads, length, 256), F32),
            pltpu.VMEM((heads, length, DV), F32),
            pltpu.VMEM((heads, 256, length), BF),
        ],
        compiler_params=pltpu.CompilerParams(vmem_limit_bytes=LIMIT),
        cost_estimate=LIGHT,
        name="attend_back",
    )(query, key, value, result, result_grad, logsum, row_position, column_position, cosine, sine, w_up, latent_all, latent_gain)


def add_norm(token_blocks, blocks, w_even, w_odd, gain):
    count, width = token_blocks[0].shape
    many = len(blocks)
    chips = many // 2
    half = chips * count
    length = count * many
    depth = blocks[0].shape[1]

    def kernel(we_ref, wo_ref, g_ref, *refs):
        parts, tokens = refs[:many], refs[many : 2 * many]
        n_ref, r_ref, x_ref, a_ref = refs[2 * many :]
        for q in range(many):
            for p in range(chips):
                other = p ^ (q % chips)
                a_ref[p * count : (p + 1) * count, q * depth : (q + 1) * depth] = parts[q][
                    other * count : (other + 1) * count
                ]
        for h in range(2):

            @pl.when(pl.program_id(0) == h)
            def _():
                for k in range(chips):
                    x_ref[k * count : (k + 1) * count] = tokens[h * chips + k][...]

        middle = chips * depth
        total = dot(a_ref[:, :middle], we_ref[...]) + dot(a_ref[:, middle:], wo_ref[...])
        total = total + x_ref[...].astype(F32)
        inverse = lax.rsqrt(jnp.mean(total * total, axis=1, keepdims=True) + eps_norm)
        n_ref[...] = (total * inverse * g_ref[...]).astype(BF)

        @pl.when(pl.program_id(0) == 0)
        def _():
            r_ref[...] = total[:count]

    def source(q):
        return pl.BlockSpec((half, depth), lambda i: (i ^ (q // chips), 0))

    return pl.pallas_call(
        kernel,
        grid=(2,),
        in_specs=[whole(w_even.shape), whole(w_odd.shape), whole((1, width))]
        + [source(q) for q in range(many)]
        + [whole((count, width))] * many,
        out_specs=[pl.BlockSpec((half, width), lambda i: (i, 0)), whole((count, width))],
        out_shape=[
            jax.ShapeDtypeStruct((length, width), BF),
            jax.ShapeDtypeStruct((count, width), F32),
        ],
        scratch_shapes=[pltpu.VMEM((half, width), BF), pltpu.VMEM((half, many * depth), BF)],
        compiler_params=pltpu.CompilerParams(vmem_limit_bytes=LIMIT),
        cost_estimate=LIGHT,
        name="add_norm",
    )(w_even, w_odd, gain, *blocks, *token_blocks)


def expert(rows, cots, gate, up, down, piece):
    count, width = rows.shape
    units = gate.shape[2]
    tile = min(512, count)
    step = 256
    full = units // step
    rest = units % step
    spans = [(n * step, step) for n in range(full)] + ([(full * step, rest)] if rest else [])

    def kernel(x_ref, c_ref, gate_hbm, up_hbm, down_hbm, res_ref, in_ref, h_ref, gg_ref, ug_ref, wg, wu, wd, acc_r, acc_i, sems):
        first = pl.program_id(0) == 0

        def copies(n, start, size):
            span = pl.ds(start, size)
            return [
                pltpu.make_async_copy(gate_hbm.at[piece, :, span], wg.at[:, span], sems.at[0, n]),
                pltpu.make_async_copy(up_hbm.at[piece, :, span], wu.at[:, span], sems.at[1, n]),
                pltpu.make_async_copy(down_hbm.at[piece, span, :], wd.at[span, :], sems.at[2, n]),
            ]

        @pl.when(first)
        def _():
            for n, (start, size) in enumerate(spans):
                for copy in copies(n, start, size):
                    copy.start()

        acc_r[...] = jnp.zeros_like(acc_r)
        acc_i[...] = jnp.zeros_like(acc_i)

        def chunk(n, start, size):
            @pl.when(first)
            def _():
                for copy in copies(n, start, size):
                    copy.wait()

            span = pl.ds(start, size)
            x, c = x_ref[...], c_ref[...]
            w_gate, w_up, w_down = wg[:, span], wu[:, span], wd[span, :]
            g = dot(x, w_gate)
            u = dot(x, w_up)
            hidden_grad = dot_t(c, w_down)
            s = jax.nn.sigmoid(g)
            silu = g * s
            hidden = (silu * u).astype(BF)
            gate_grad = (hidden_grad * u * (s * (1.0 + g * (1.0 - s)))).astype(BF)
            up_grad = (hidden_grad * silu).astype(BF)
            h_ref[:, span] = hidden
            gg_ref[:, span] = gate_grad
            ug_ref[:, span] = up_grad
            acc_r[...] += dot(hidden, w_down)
            acc_i[...] += dot_t(gate_grad, w_gate) + dot_t(up_grad, w_up)

        if full:

            @pl.loop(0, full)
            def _(n):
                chunk(n, pl.multiple_of(n * step, step), step)

        if rest:
            chunk(full, full * step, rest)
        res_ref[...] = acc_r[...].astype(BF)
        in_ref[...] = acc_i[...].astype(BF)

    def block(w):
        return pl.BlockSpec((tile, w), lambda i: (i, 0))

    def array(w):
        return jax.ShapeDtypeStruct((count, w), BF)

    return pl.pallas_call(
        kernel,
        grid=(count // tile,),
        in_specs=[block(width), block(width), ANY, ANY, ANY],
        out_specs=[block(width), block(width), block(units), block(units), block(units)],
        out_shape=[array(width), array(width), array(units), array(units), array(units)],
        scratch_shapes=[
            pltpu.VMEM((width, units), BF),
            pltpu.VMEM((width, units), BF),
            pltpu.VMEM((units, width), BF),
            pltpu.VMEM((tile, width), F32),
            pltpu.VMEM((tile, width), F32),
            pltpu.SemaphoreType.DMA((3, len(spans))),
        ],
        compiler_params=pltpu.CompilerParams(vmem_limit_bytes=LIMIT),
        cost_estimate=LIGHT,
        name="expert",
    )(rows, cots, gate, up, down)


def expert_weights(rows, cots, hidden, gate_grad, up_grad, piece, pieces, earlier):
    count, width = rows.shape
    units = hidden.shape[1]
    tile = 256

    def kernel(x_ref, c_ref, h_ref, gg_ref, ug_ref, *refs):
        g_ref, u_ref, d_ref = refs[-3:]
        g_ref[0] = t_dot(x_ref[...], gg_ref[...])
        u_ref[0] = t_dot(x_ref[...], ug_ref[...])
        d_ref[0] = t_dot(h_ref[...], c_ref[...])

    tall = pl.BlockSpec((1, tile, units), lambda i: (piece, i, 0))
    flat = pl.BlockSpec((1, units, tile), lambda i: (piece, 0, i))
    column = pl.BlockSpec((count, tile), lambda i: (0, i))
    kept = list(earlier or ())
    return pl.pallas_call(
        kernel,
        grid=(width // tile,),
        in_specs=[column, column] + [whole((count, units))] * 3 + [ANY] * len(kept),
        out_specs=[tall, tall, flat],
        out_shape=[
            jax.ShapeDtypeStruct((pieces, width, units), F32),
            jax.ShapeDtypeStruct((pieces, width, units), F32),
            jax.ShapeDtypeStruct((pieces, units, width), F32),
        ],
        input_output_aliases={5 + n: n for n in range(len(kept))},
        compiler_params=pltpu.CompilerParams(vmem_limit_bytes=LIMIT),
        cost_estimate=LIGHT,
        name="expert_weights",
    )(rows, cots, hidden, gate_grad, up_grad, *kept)


def dispatch(select, rows, slot_weight, pieces):
    blocks, slots, count = select.shape
    width = rows.shape[1]
    others = slots // pieces // CAP

    def kernel(m_ref, x_ref, *refs):
        got = dot(m_ref[0], x_ref[...])
        if slot_weight is not None:
            got = got * refs[0][0]
        got = got.astype(BF)
        for i in range(pieces):
            for j in range(others):
                start = (i * others + j) * CAP
                refs[-pieces + i][j] = got[start : start + CAP]

    weights = [] if slot_weight is None else [slot_weight]
    out = pl.BlockSpec((others, CAP, width), lambda b: (0, b, 0))
    return pl.pallas_call(
        kernel,
        grid=(blocks,),
        in_specs=[
            pl.BlockSpec((1, slots, count), lambda b: (b, 0, 0)),
            pl.BlockSpec((count, width), lambda b: (b, 0)),
        ]
        + [pl.BlockSpec((1, slots, 1), lambda b: (b, 0, 0))] * len(weights),
        out_specs=[out] * pieces,
        out_shape=[jax.ShapeDtypeStruct((others, blocks * CAP, width), BF)] * pieces,
        compiler_params=pltpu.CompilerParams(vmem_limit_bytes=LIMIT),
        cost_estimate=LIGHT,
        name="dispatch",
    )(select, rows, *weights)


def down_weights(index, normed, down_even, down_odd, others, n_seq, gain_rows):
    length, _ = normed.shape
    half, columns = down_even.shape
    per = 128 // gain_rows

    def kernel(index_ref, n_ref, e_ref, d_ref, o_ref, part):
        part[...] = t_dot(n_ref[:half], e_ref[...]) + t_dot(n_ref[half:], d_ref[...])
        o_ref[0] = part[span(index_ref[1] % per, gain_rows)]

    return pl.pallas_call(
        kernel,
        grid_spec=pltpu.PrefetchScalarGridSpec(
            num_scalar_prefetch=1,
            grid=(others,),
            in_specs=[
                pl.BlockSpec(
                    (length, 128), lambda i, ref: (0, (i * n_seq + ref[1]) * gain_rows // 128)
                ),
                pl.BlockSpec((half, columns), lambda i, ref: (0, 0)),
                pl.BlockSpec((half, columns), lambda i, ref: (0, 0)),
            ],
            out_specs=pl.BlockSpec((1, gain_rows, columns), lambda i, ref: (i, 0, 0)),
            scratch_shapes=[pltpu.VMEM((128, columns), F32)],
        ),
        out_shape=jax.ShapeDtypeStruct((others, gain_rows, columns), F32),
        compiler_params=pltpu.CompilerParams(vmem_limit_bytes=LIMIT),
        cost_estimate=LIGHT,
        name="down_weights",
    )(index, normed, down_even, down_odd)


def combine(base, masks, returned, products, dtype):
    half = masks[0].shape[0] // 2
    slots, count = masks[0].shape[1:]
    pieces = len(returned)
    others, _, width = returned[0].shape
    many = len(masks)

    tile = 512

    def kernel(*refs):
        mask_refs, row_refs = refs[:many], refs[many : many + pieces]
        rest, out_ref = refs[many + pieces : -1], refs[-1]
        total = 0.0
        for n, (_, _, flipped) in enumerate(products):
            total = total + (dot_t if flipped else dot)(rest[2 * n][...], rest[2 * n + 1][...])
        for b in range(half):
            rows = jnp.concatenate(
                [
                    row_refs[i][j, b * CAP : (b + 1) * CAP]
                    for i in range(pieces)
                    for j in range(others)
                ],
                axis=0,
            )
            block = total[b * count : (b + 1) * count]
            for mask_ref in mask_refs:
                block = block + t_dot(mask_ref[b], rows)
            out_ref[b * count : (b + 1) * count] = block.astype(dtype)

    factors = []
    specs = []
    for left, right, flipped in products:
        factors += [left, right]
        specs.append(pl.BlockSpec((half * count, left.shape[1]), lambda t: (base, 0)))
        if flipped:
            specs.append(pl.BlockSpec((tile, right.shape[1]), lambda t: (t, 0)))
        else:
            specs.append(pl.BlockSpec((right.shape[0], tile), lambda t: (0, t)))
    return pl.pallas_call(
        kernel,
        grid=(width // tile,),
        in_specs=[pl.BlockSpec((half, slots, count), lambda t: (base, 0, 0))] * many
        + [pl.BlockSpec((others, half * CAP, tile), lambda t: (0, base, t))] * pieces
        + specs,
        out_specs=pl.BlockSpec((half * count, tile), lambda t: (0, t)),
        out_shape=jax.ShapeDtypeStruct((half * count, width), dtype),
        compiler_params=pltpu.CompilerParams(vmem_limit_bytes=LIMIT),
        cost_estimate=LIGHT,
        name="combine",
    )(*masks, *returned, *factors)


def swap(x, axis, mask):
    n = lax.axis_size(axis)
    return lax.ppermute(x, axis, [(i, i ^ mask) for i in range(n)])


def after(x, *earlier):
    return lax.optimization_barrier((x, *earlier))[0]


class Lane:
    def __init__(self, axis, depth):
        self.axis = axis
        self.depth = depth
        self.sent = []

    def send(self, x, mask):
        if len(self.sent) >= self.depth:
            x = after(x, self.sent[-self.depth])
        got = swap(x, self.axis, mask)
        self.sent.append(got)
        return got

    def chips(self, x):
        chips = lax.axis_size("seq") // 2
        return [x] + [self.send(x, 2 * k) for k in range(1, chips)]

    def group(self, x):
        return self.pair(self.chips(x))

    def pair(self, evens):
        rows, columns = evens[0].shape
        everything = slice(None)
        (even,) = arrange(
            jnp.zeros((1,), jnp.int32),
            evens,
            [(rows * len(evens), columns)],
            [
                (k, everything, 0, lambda ref, k=k: (slice(k * rows, (k + 1) * rows), everything))
                for k in range(len(evens))
            ],
        )
        return even, swap(even, "seq", 1)

    def scatter(self, even, odd):
        return self.finish(self.begin(even, odd))

    def begin(self, even, odd):
        chips = lax.axis_size("seq") // 2
        rows = even.shape[0] // chips
        got = swap(odd.astype(BF), "seq", 1)
        blocks = [
            even[k * rows : (k + 1) * rows] + got[k * rows : (k + 1) * rows].astype(F32)
            for k in range(chips)
        ]
        return blocks[:1] + [block.astype(BF) for block in blocks[1:]]

    def finish(self, blocks, *gates):
        got = [self.send(blocks[k], 2 * k) for k in range(1, len(blocks))]
        total = blocks[0]
        for block in got:
            total = total + after(block, *gates).astype(F32)
        return total

    def corners(self, x):
        if lax.axis_size("exp") != 4:
            return [(j, 0, y) for j, y in enumerate(self.others(x))]
        middle = x.shape[0] // 2
        one, two = self.send(x, 1), self.send(x, 2)
        return [
            (0, 0, x),
            (1, 0, one),
            (2, 0, two),
            (3, 0, self.send(two[:middle], 1)),
            (3, middle, self.send(one[middle:], 2)),
        ]

    def others(self, x):
        return [x] + [self.send(x, j) for j in range(1, lax.axis_size("exp"))]

def relative_order(count):
    chips = count // 2
    return [2 * k for k in range(chips)] + [2 * k + 1 for k in range(chips)]


def sum_exp(x, axis):
    return lax.psum_scatter(x.astype(BF), "exp", scatter_dimension=axis, tiled=True).astype(F32)


def shards(
    tokens,
    routes,
    route_weights,
    norm_gain,
    w_query,
    w_kv_down,
    latent_gain,
    w_kv_up,
    w_output,
    ffn_gain,
    shared_gate,
    shared_up,
    shared_down,
    expert_gate,
    expert_up,
    expert_down,
    out_grad,
):
    count, width = tokens.shape
    n_seq = lax.axis_size("seq")
    n_exp = lax.axis_size("exp")
    seq = lax.axis_index("seq")
    order = relative_order(n_seq)
    chips = n_seq // 2
    heads = H // n_seq
    length = count * n_seq
    half = length // 2
    pieces = expert_gate.shape[0]
    parts_per = pieces * n_seq * n_exp // EXPERTS
    factor = 1.0 / math.sqrt(DN + DR)
    gain_rows = norm_gain.shape[0]
    latent_rows_local = latent_gain.shape[0]
    along = Lane("seq", 3)
    across = Lane("exp", 3)
    free = Lane("seq", 3)

    index = jnp.stack([lax.axis_index("exp"), seq]).astype(jnp.int32)
    ratio = w_query.shape[0] // w_kv_up.shape[0]
    slim = w_kv_up.shape[1] // ratio
    columns = w_kv_down.shape[1]
    high = lax.reduce_precision(route_weights, 8, 7)
    middle = lax.reduce_precision(route_weights - high, 8, 7)
    low = route_weights - high - middle
    route_pack = jnp.concatenate([routes.astype(F32), high, middle, low], axis=1).astype(BF).T
    lines = route_pack.shape[0] // 4
    gains = jnp.concatenate([norm_gain, ffn_gain, latent_gain])
    packed = jnp.concatenate(
        [
            w_kv_down,
            jnp.pad(gains, (0, columns - gains.shape[0]))[None, :],
            jnp.pad(
                route_pack.reshape(4, lines, count).transpose(1, 0, 2).reshape(lines, 4 * count),
                ((0, 15 - lines), (0, columns - 4 * count)),
            ),
        ],
        axis=0,
    )
    packed_even = jnp.stack(free.chips(packed))
    token_even = along.chips(tokens)
    first_all = lax.all_gather(
        jnp.concatenate(
            [
                w_query,
                jnp.concatenate(
                    [w_kv_up[:, g * slim : (g + 1) * slim] for g in range(ratio)], axis=0
                ),
            ],
            axis=1,
        ),
        "exp",
        axis=0,
        tiled=True,
    )
    packed_parts = across.others(packed_even)
    packed_even = jnp.stack(packed_parts)
    packed_odd = swap(packed_even, "seq", 1)
    token_odd = [swap(x, "seq", 1) for x in token_even[:2]]
    token_odd += [swap(after(x, *token_odd), "seq", 1) for x in token_even[2:]]
    token_blocks = token_even + token_odd
    output_even = jnp.concatenate(along.chips(after(w_output, *token_odd)), axis=0)
    output_parts = across.corners(output_even)
    early = first_all
    gate_cols = lax.all_gather(after(shared_gate, early), "exp", axis=0, tiled=True)
    lift_cols = lax.all_gather(after(shared_up, early), "exp", axis=0, tiled=True)
    drop_rows = lax.all_gather(after(shared_down, early), "exp", axis=1, tiled=True)
    grad_even = along.chips(out_grad)

    everything = slice(None)
    block_rows = width // n_exp
    plan = []
    for h in range(2):
        for j in range(n_exp):
            for k in range(chips):

                def where(ref, h=h, j=j, k=k):
                    return (ref[0] ^ j) * n_seq + (ref[1] ^ (2 * k + h))

                plan.append(
                    (
                        h,
                        (j, k, slice(0, gain_rows)),
                        0,
                        lambda ref, where=where: (span(where(ref), gain_rows), everything),
                    )
                )
                plan.append(
                    (
                        h,
                        (j, k, slice(gain_rows, gain_rows + 16)),
                        1,
                        lambda ref, where=where: (where(ref),),
                    )
                )
    down_full, extra_all = arrange(
        index,
        [packed_even, packed_odd],
        [(width, columns), (n_exp * n_seq, 16, columns)],
        plan,
    )
    gain_first = extra_all[:, 0, :gain_rows].reshape(1, width).astype(F32)
    gain_second = extra_all[:, 0, gain_rows : 2 * gain_rows].reshape(1, width).astype(F32)
    latent_wide = (
        extra_all[:, 0, 2 * gain_rows : 2 * gain_rows + latent_rows_local]
        .reshape(1, R)
        .astype(F32)
    )
    route_all = jnp.concatenate(
        [packed_even[0, :, gain_rows + 1 :], packed_odd[0, :, gain_rows + 1 :]], axis=0
    )[:, :lines, : 4 * count]
    route_all = route_all.reshape(n_seq, lines, 4, count).transpose(0, 2, 1, 3)
    route_all = route_all.reshape(n_seq, 4 * lines, count).astype(F32)
    route_all = jnp.concatenate(
        [
            route_all[:, :TOP],
            route_all[:, TOP : 2 * TOP]
            + route_all[:, 2 * TOP : 3 * TOP]
            + route_all[:, 3 * TOP :],
        ],
        axis=1,
    )
    up_rows = w_kv_up.shape[0]
    query_width = w_query.shape[1]
    (up_cols,) = arrange(
        index,
        [first_all],
        [(R, w_kv_up.shape[1])],
        [
            (
                0,
                (
                    slice((j * ratio + g) * up_rows, (j * ratio + g + 1) * up_rows),
                    slice(query_width, query_width + slim),
                ),
                0,
                lambda ref, j=j, g=g: (
                    slice(j * up_rows, (j + 1) * up_rows),
                    slice(g * slim, (g + 1) * slim),
                ),
            )
            for j in range(n_exp)
            for g in range(ratio)
        ],
    )
    (output_even,) = arrange(
        index,
        [part[2] for part in output_parts],
        [(H * DV // 2, width)],
        [
            (
                n,
                everything,
                0,
                lambda ref, j=j, at=at, x=x: (
                    slice(at, at + x.shape[0]),
                    span(ref[0] ^ j, block_rows),
                ),
            )
            for n, (j, at, x) in enumerate(output_parts)
        ],
    )
    output_odd = swap(output_even, "seq", 1)

    positions = jnp.concatenate(
        [(seq ^ r) * count + jnp.arange(count, dtype=jnp.int32) for r in order]
    )
    row_position, column_position = positions[None, :], positions[:, None]
    cosine_table, sine_table = rope_tables(positions, DR)
    cosine_wide = jnp.concatenate([cosine_table, cosine_table], axis=1)
    sine_wide = jnp.concatenate([-sine_table, sine_table], axis=1)
    normed_one, latent_all, latent_raw, query_heads, key_heads, value_heads = project(
        token_blocks,
        gain_first,
        first_all,
        down_full,
        latent_wide,
        up_cols,
        cosine_wide,
        sine_wide,
        heads,
    )
    result, logsum = attend(
        query_heads, key_heads, value_heads, row_position, column_position, factor
    )

    grad_even, grad_odd = along.pair([after(x, result) for x in grad_even])

    column = jnp.stack(
        [
            ((other * n_seq + seq) * pieces + i) // parts_per
            for i in range(pieces)
            for other in range(n_exp)
        ]
    )
    kinds = n_exp * pieces
    named = route_all[:, None, :TOP, :].astype(jnp.int32) == column[None, :, None, None]
    matched = jnp.any(named, axis=2)
    match_weight = jnp.sum(jnp.where(named, route_all[:, None, TOP:, :], 0.0), axis=2)
    earlier = (jnp.arange(count)[:, None] < jnp.arange(count)[None, :]).astype(BF)
    rank = jnp.dot(matched.astype(BF), earlier, preferred_element_type=F32).astype(jnp.int32)
    chosen = (rank[:, :, None, :] == jnp.arange(CAP, dtype=jnp.int32)[None, None, :, None]) & (
        matched[:, :, None, :]
    )
    select = chosen.astype(BF).reshape(n_seq, kinds * CAP, count)
    weighted = jnp.where(chosen, match_weight[:, :, None, :], 0.0).reshape(
        n_seq, kinds * CAP, count
    )
    slot_weight = jnp.sum(weighted, axis=2, keepdims=True)
    weighted_high = weighted.astype(BF)
    weighted_low = (weighted - weighted_high.astype(F32)).astype(BF)

    def give(rows):
        return lax.all_to_all(rows, "exp", split_axis=0, concat_axis=0, tiled=True)

    (grad_rows,) = arrange(
        index,
        [grad_even, grad_odd],
        [(length, width)],
        [
            (h, everything, 0, lambda ref, h=h: (slice(h * half, (h + 1) * half), everything))
            for h in range(2)
        ],
    )
    send_cots = dispatch(select, grad_rows, slot_weight, pieces)
    received_grad = [give(rows) for rows in send_cots]

    result_even = along.chips(result)
    gathered = (gate_cols, lift_cols, drop_rows)
    result_even = [after(x, *send_cots, *gathered) for x in result_even]
    result_blocks = result_even + [swap(x, "seq", 1) for x in result_even]
    normed_two, residual = add_norm(
        token_blocks,
        [after(result_blocks[0], received_grad[0])] + result_blocks[1:],
        output_even,
        output_odd,
        gain_second,
    )
    inverse_two = inverse_rms(residual)
    send_rows = dispatch(select, normed_two, None, pieces)
    received = [give(after(send_rows[0], *received_grad))]

    (own_heads,) = arrange(
        index,
        result_blocks,
        [(count, H * DV)],
        [
            (
                p,
                (slice(p * count, (p + 1) * count), everything),
                0,
                lambda ref, p=p: (everything, slice(p * heads * DV, (p + 1) * heads * DV)),
            )
            for p in range(n_seq)
        ],
    )

    shared_rows = after(normed_two, *send_rows)
    shared_gate_raw = dot(shared_rows, gate_cols)
    shared_up_raw = dot(shared_rows, lift_cols)
    shared_hidden = (jax.nn.silu(shared_gate_raw) * shared_up_raw).astype(BF)
    shared_hidden_grad = dot_t(grad_rows, drop_rows)
    sgate_grad = (shared_hidden_grad * shared_up_raw * silu_slope(shared_gate_raw)).astype(BF)
    sup_grad = (shared_hidden_grad * jax.nn.silu(shared_gate_raw)).astype(BF)
    received += [give(after(rows, sgate_grad, sup_grad)) for rows in send_rows[1:]]

    slot_rows = n_exp * n_seq * CAP
    pairs = []
    results_back, grads_back, kept = [], [], []
    for i in range(pieces):
        rows = received[i].reshape(slot_rows, width)
        cots = received_grad[i].reshape(slot_rows, width)
        expert_result, input_grad, *saved = expert(
            rows, cots, expert_gate, expert_up, expert_down, i
        )
        grads_back.append(give(input_grad.reshape(n_exp, n_seq * CAP, width)))
        results_back.append(expert_result.reshape(n_exp, n_seq * CAP, width))
        kept.append((rows, cots, *saved))
    two_products = [(sgate_grad, gate_cols, True), (sup_grad, lift_cols, True)]
    two_odd = combine(1, [select], grads_back, two_products, BF)
    two_even = combine(0, [select], grads_back, two_products, F32)
    two_blocks = along.begin(two_even, two_odd)
    expert_grads = None
    back = []
    for i in range(pieces):
        back.append(give(after(results_back[i], *(two_blocks if i == 0 else expert_grads))))
        expert_grads = expert_weights(
            after(kept[i][0], *([input_grad] if i == 0 else back[:1])),
            *kept[i][1:],
            i,
            pieces,
            expert_grads,
        )
    results_back = back
    expert_gate_grad, expert_up_grad, expert_down_grad = expert_grads
    two_grad = along.finish(two_blocks, *expert_grads)
    gate_out = sum_exp(t_dot(after(shared_rows, *two_blocks), sgate_grad), 0)
    lift_out = sum_exp(t_dot(after(shared_rows, *two_blocks), sup_grad), 0)
    drop_out = sum_exp(t_dot(after(shared_hidden, *two_blocks), grad_rows), 1)

    residual_norm_grad, second_terms = norm_back(
        two_grad, residual, inverse_two, gain_second
    )
    residual_grad = out_grad.astype(F32) + residual_norm_grad
    residual_half = residual_grad.astype(BF)
    even_heads = dot_t(residual_half, output_even).astype(BF)
    odd_heads = dot_t(residual_half, output_odd).astype(BF)
    wide = heads * DV
    pairs = [
        jnp.stack([even_heads[:, k * wide : (k + 1) * wide], odd_heads[:, k * wide : (k + 1) * wide]])
        for k in range(chips)
    ]
    stacks = pairs
    pairs = [pairs[0]] + [along.send(pairs[k], 2 * k) for k in range(1, chips)]
    other_half = swap(jnp.stack([pair[1] for pair in pairs]), "seq", 1)
    attention_grad = jnp.concatenate(
        [jnp.stack([pair[0] for pair in pairs]), other_half], axis=0
    ).reshape(length, wide)
    out_products = [(shared_hidden, drop_rows, False)]
    out_masks = [weighted_high, weighted_low]
    out_masks = [after(mask, *stacks) for mask in out_masks]
    out_odd = combine(1, out_masks, results_back, out_products, BF)
    out_even = combine(0, out_masks, results_back, out_products, F32)
    out_blocks = along.begin(out_even, out_odd)
    output_got = [along.send(out_blocks[k], 2 * k) for k in range(chips - 1, 0, -1)]

    query_in_grad, kv_grad, latent_part, latent_sum = attend_back(
        query_heads,
        key_heads,
        value_heads,
        result,
        after(attention_grad, *out_blocks),
        logsum,
        row_position,
        column_position,
        cosine_wide,
        -sine_wide,
        up_cols,
        latent_all,
        latent_wide,
        factor,
    )
    query_in_grad = after(query_in_grad, *output_got[:2])
    one_odd, odd_sum = query_back(1, query_in_grad, first_all, normed_one, gain_first, BF)
    one_even, even_sum = query_back(0, query_in_grad, first_all, normed_one, gain_first, F32)
    sums = jnp.concatenate(
        [
            (odd_sum + even_sum).reshape(n_exp, n_seq, gain_rows),
            jnp.sum(second_terms, axis=0).reshape(n_exp, n_seq, gain_rows),
            latent_sum.reshape(n_exp, n_seq, latent_rows_local),
        ],
        axis=2,
    )
    many = sums.shape[2]
    turn = (seq ^ jnp.array(order))[:, None] == jnp.arange(n_seq)[None, :]
    sums = jnp.einsum("ps,esw->pew", turn.astype(F32), sums, precision=lax.Precision.HIGHEST)
    sums = jnp.pad(
        sums.reshape(n_seq, 1, n_exp * many), ((0, 0), (0, 15), (0, columns - n_exp * many))
    )
    latent_part = jnp.concatenate([latent_part.reshape(n_seq, count, columns), sums], axis=1)
    latent_part = latent_part.reshape(n_seq * (count + 16), columns)
    latent_grad = along.scatter(
        latent_part[: chips * (count + 16)], latent_part[chips * (count + 16) :]
    )
    one_blocks = along.begin(one_even, one_odd)
    one_got = [along.send(one_blocks[k], 2 * k) for k in range(chips - 1, 0, -1)]
    mine = lax.axis_index("exp")
    late = Lane("exp", 1)
    attention_parts = late.others(after(own_heads, *one_blocks))
    column_blocks = [
        lax.dynamic_slice_in_dim(
            after(residual_half, *one_blocks), (mine ^ j) * block_rows, block_rows, 1
        )
        for j in range(n_exp)
    ]
    column_blocks = [column_blocks[0]] + [
        late.send(column_blocks[j], j) for j in range(1, n_exp)
    ]
    output_part = t_dot(
        jnp.concatenate(attention_parts, axis=0), jnp.concatenate(column_blocks, axis=0)
    )
    output_blocks = along.begin(output_part[: H * DV // 2], output_part[H * DV // 2 :])
    up_part = t_dot(after(latent_all, *one_blocks), kv_grad).astype(BF)
    query_part = t_dot(after(normed_one, *one_blocks), query_in_grad).astype(BF)
    up_out = sum_exp(up_part, 0)
    query_out = sum_exp(query_part, 0)
    sums = latent_grad[count, : n_exp * many].reshape(n_exp, 1, many)
    latent_grad = latent_grad[:count]
    latent_raw_grad, _ = norm_back(
        latent_grad[:, :R], latent_raw[:count], inverse_rms(latent_raw[:count]), latent_wide
    )
    down_rows = jnp.concatenate(
        [
            latent_raw_grad,
            rotate(latent_grad[:, R:], cosine_table[:count], -sine_table[:count]),
        ],
        axis=1,
    ).astype(BF)
    down_even, down_odd = free.pair([after(x, *one_got) for x in free.chips(down_rows)])
    down_part = down_weights(index, normed_one, down_even, down_odd, n_exp, n_seq, gain_rows)
    down_part = jnp.concatenate(
        [
            down_part,
            jnp.pad(sums, ((0, 0), (0, 15), (0, columns - many))),
        ],
        axis=1,
    )
    down_sum = lax.dynamic_index_in_dim(down_part, mine, 0, keepdims=False)
    for j in range(1, n_exp):
        piece = lax.dynamic_index_in_dim(down_part, mine ^ j, 0, keepdims=False).astype(BF)
        down_sum = down_sum + swap(piece, "exp", j).astype(F32)
    down_out = down_sum[:gain_rows]
    small = down_sum[gain_rows, :many]
    first_out = small[:gain_rows] + jnp.sum(
        w_kv_down.astype(F32) * down_out, axis=1
    ) / norm_gain.astype(F32)

    output = residual + out_blocks[0]
    for block in output_got:
        output = output + after(block, *one_blocks).astype(F32)
    output = output.astype(BF)
    output_out = free.finish(output_blocks)
    one_grad = one_blocks[0]
    for block in one_got:
        block = after(block, up_part, query_part, down_sum, *output_blocks)
        one_grad = one_grad + block.astype(F32)
    down_back = dot_t(down_rows, down_full)
    token_wide = tokens.astype(F32)
    token_norm_grad, _ = norm_back(
        one_grad + down_back, token_wide, inverse_rms(token_wide), gain_first
    )
    tokens_grad = (residual_grad + token_norm_grad).astype(BF)
    return (
        output,
        tokens_grad,
        first_out,
        query_out,
        down_out,
        small[2 * gain_rows : many],
        up_out,
        output_out,
        small[gain_rows : 2 * gain_rows],
        gate_out,
        lift_out,
        drop_out,
        expert_gate_grad,
        expert_up_grad,
        expert_down_grad,
    )


def solution(mesh):
    rows = P(("exp", "seq"), None)
    line = P(("exp", "seq"))
    grid = P("exp", "seq")
    turned = P("seq", "exp")
    part = P(("exp", "seq"), None, None)
    return jax.shard_map(
        shards,
        mesh=mesh,
        in_specs=(
            rows,
            rows,
            rows,
            line,
            grid,
            rows,
            line,
            grid,
            turned,
            line,
            grid,
            grid,
            turned,
            part,
            part,
            part,
            rows,
        ),
        out_specs=(
            rows,
            rows,
            line,
            grid,
            rows,
            line,
            grid,
            turned,
            line,
            grid,
            grid,
            turned,
            part,
            part,
            part,
        ),
        check_vma=False,
    )
```

```python
import math

import jax
import jax.numpy as jnp
from jax import lax
from jax.experimental import pallas as pl
from jax.experimental.pallas import tpu as pltpu
from jax.sharding import PartitionSpec as P

H = 16
DN = 128
DR = 64
DV = 128
R = 512
EXPERTS = 64
TOP = 6
CAP = 16


eps_norm = 1e-06
rope_base = 50000.0
BF = jnp.bfloat16
F32 = jnp.float32


def dot(a, b):
    return jnp.dot(a, b, preferred_element_type=F32)


def dot_t(a, b):
    return lax.dot_general(a, b, (((1,), (1,)), ((), ())), preferred_element_type=F32)


def t_dot(a, b):
    return lax.dot_general(a, b, (((0,), (0,)), ((), ())), preferred_element_type=F32)


def rope_tables(positions, width):
    middle = width // 2
    frequency = rope_base ** (-(jnp.arange(middle, dtype=F32) * 2.0 / width))
    angles = positions.astype(F32)[:, None] * frequency[None, :]
    return (jnp.cos(angles), jnp.sin(angles))


def rotate(values, cosine_table, sine_table):
    middle = values.shape[-1] // 2
    leading = values[..., :middle]
    trailing = values[..., middle:]
    return jnp.concatenate(
        [
            leading * cosine_table - trailing * sine_table,
            trailing * cosine_table + leading * sine_table,
        ],
        axis=-1,
    )


def silu_slope(gate_values):
    sigmoid = jax.nn.sigmoid(gate_values)
    return sigmoid * (1.0 + gate_values * (1.0 - sigmoid))


def norm_back(dy, v, inverse, gain):
    hat = v * inverse
    scaled = dy * gain
    dv = inverse * (scaled - hat * jnp.mean(scaled * hat, axis=-1, keepdims=True))
    return dv, dy * hat


def inverse_rms(v):
    return lax.rsqrt(jnp.mean(v * v, axis=-1, keepdims=True) + eps_norm)


LIMIT = 56 * 1024 * 1024
LIGHT = pl.CostEstimate(flops=0, transcendentals=0, bytes_accessed=0)
ANY = pl.BlockSpec(memory_space=pl.ANY)
SCALARS = pl.BlockSpec(memory_space=pltpu.SMEM)


def whole(shape):
    return pl.BlockSpec(shape, lambda *grid: (0,) * len(shape))


def arrange(index, blocks, outs, plan):
    def kernel(index_ref, *refs):
        sources = refs[: len(blocks)]
        targets = refs[len(blocks) :]
        for block, source, out, target in plan:
            targets[out][target(index_ref)] = sources[block][source]

    return pl.pallas_call(
        kernel,
        out_shape=[jax.ShapeDtypeStruct(s, BF) for s in outs],
        in_specs=[SCALARS] + [pl.BlockSpec(memory_space=pltpu.VMEM)] * len(blocks),
        out_specs=[pl.BlockSpec(memory_space=pltpu.VMEM)] * len(outs),
        compiler_params=pltpu.CompilerParams(vmem_limit_bytes=LIMIT),
        cost_estimate=LIGHT,
        name="arrange",
    )(index, *blocks)


def span(start, size):
    return pl.ds(pl.multiple_of(start * size, size), size)


def turned(v, cosine, sine):
    middle = v.shape[1] // 2
    return v * cosine + jnp.concatenate([v[:, middle:], v[:, :middle]], axis=1) * sine


def project(token_blocks, gain, w_first, w_down, latent_gain, w_up, cosine, sine, heads):
    count, width = token_blocks[0].shape
    chips = len(token_blocks) // 2
    half = chips * count
    wide = DN + DR
    columns = heads * wide

    def kernel(g_ref, wd_ref, lg_ref, wu_ref, c_ref, s_ref, *refs):
        tokens, w_ref = refs[: 2 * chips], refs[2 * chips]
        n_ref, l_ref, r_ref, q_ref, k_ref, v_ref, x_ref = refs[2 * chips + 1 :]
        for h in range(2):

            @pl.when(pl.program_id(0) == h)
            def _():
                for k in range(chips):
                    x_ref[k * count : (k + 1) * count] = tokens[h * chips + k][...]

        x = x_ref[...].astype(F32)
        inverse = lax.rsqrt(jnp.mean(x * x, axis=1, keepdims=True) + eps_norm)
        n_ref[...] = (x * inverse * g_ref[...]).astype(BF)
        down = dot(n_ref[...], wd_ref[...])
        raw = down[:, :R]
        r_ref[...] = raw
        inverse = lax.rsqrt(jnp.mean(raw * raw, axis=1, keepdims=True) + eps_norm)
        l_ref[...] = (raw * inverse * lg_ref[...]).astype(BF)
        query = dot(n_ref[...], w_ref[:, :columns])
        up = dot(l_ref[...], wu_ref[...]).astype(BF)
        cosine, sine = c_ref[...], s_ref[...]
        zeros = jnp.zeros((half, 256 - wide), BF)
        rope = jnp.concatenate([turned(down[:, R : R + DR], cosine, sine).astype(BF), zeros], axis=1)
        for n in range(heads):
            own = query[:, n * wide : (n + 1) * wide]
            q_ref[n, :, :DN] = own[:, :DN].astype(BF)
            q_ref[n, :, DN:] = jnp.concatenate(
                [turned(own[:, DN:], cosine, sine).astype(BF), zeros], axis=1
            )
            k_ref[n, :, :DN] = up[:, n * (DN + DV) : n * (DN + DV) + DN]
            k_ref[n, :, DN:] = rope
            v_ref[n] = up[:, n * (DN + DV) + DN : (n + 1) * (DN + DV)]

    def rows(w):
        return pl.BlockSpec((half, w), lambda i: (i, 0))

    def head_rows(w):
        return pl.BlockSpec((heads, half, w), lambda i: (0, i, 0))

    length = 2 * half
    return pl.pallas_call(
        kernel,
        grid=(2,),
        in_specs=[
            whole((1, width)),
            whole(w_down.shape),
            whole((1, R)),
            whole(w_up.shape),
            rows(DR),
            rows(DR),
        ]
        + [whole((count, width))] * (2 * chips)
        + [whole(w_first.shape)],
        out_specs=[rows(width), rows(R), rows(R), head_rows(256), head_rows(256), head_rows(DV)],
        out_shape=[
            jax.ShapeDtypeStruct((length, width), BF),
            jax.ShapeDtypeStruct((length, R), BF),
            jax.ShapeDtypeStruct((length, R), F32),
            jax.ShapeDtypeStruct((heads, length, 256), BF),
            jax.ShapeDtypeStruct((heads, length, 256), BF),
            jax.ShapeDtypeStruct((heads, length, DV), BF),
        ],
        scratch_shapes=[pltpu.VMEM((half, width), BF)],
        compiler_params=pltpu.CompilerParams(vmem_limit_bytes=LIMIT),
        cost_estimate=LIGHT,
        name="project",
    )(gain, w_down, latent_gain, w_up, cosine, sine, *token_blocks, w_first)


def query_back(base, query_grad, w_first, normed, gain, dtype):
    length, columns = query_grad.shape
    half = length // 2
    width = normed.shape[1]
    tile = 512

    def kernel(q_ref, n_ref, g_ref, w_ref, o_ref, t_ref):
        part = dot_t(q_ref[...], w_ref[:, :columns])
        o_ref[...] = part.astype(dtype)
        product = part * n_ref[...].astype(F32)
        t_ref[...] = jnp.sum(product, axis=0, keepdims=True) / g_ref[...]

    return pl.pallas_call(
        kernel,
        grid=(width // tile,),
        in_specs=[
            pl.BlockSpec((half, columns), lambda i: (base, 0)),
            pl.BlockSpec((half, tile), lambda i: (base, i)),
            pl.BlockSpec((1, tile), lambda i: (0, i)),
            pl.BlockSpec((tile, w_first.shape[1]), lambda i: (i, 0)),
        ],
        out_specs=[
            pl.BlockSpec((half, tile), lambda i: (0, i)),
            pl.BlockSpec((1, tile), lambda i: (0, i)),
        ],
        out_shape=[
            jax.ShapeDtypeStruct((half, width), dtype),
            jax.ShapeDtypeStruct((1, width), F32),
        ],
        compiler_params=pltpu.CompilerParams(vmem_limit_bytes=LIMIT),
        cost_estimate=LIGHT,
        name="query_back",
    )(query_grad, normed, gain, w_first)


def attend(query, key, value, row_position, column_position, factor):
    heads, length, _ = query.shape
    tile = 256

    def kernel(q_ref, k_ref, v_ref, row_ref, column_ref, o_ref, s_ref):
        allowed = column_ref[...] <= row_ref[...]
        for n in range(heads):
            scores = dot_t(k_ref[n], q_ref[n]) * factor
            exponent = jnp.where(allowed, jnp.exp(jnp.where(allowed, scores, -1e30)), 0.0)
            total = jnp.sum(exponent, axis=0, keepdims=True)
            probs = (exponent / total).astype(BF)
            o_ref[:, n * DV : (n + 1) * DV] = t_dot(v_ref[n], probs).T.astype(BF)
            s_ref[n : n + 1, :] = jnp.log(total)

    return pl.pallas_call(
        kernel,
        grid=(length // tile,),
        in_specs=[
            pl.BlockSpec((heads, tile, 256), lambda i: (0, i, 0)),
            whole(key.shape),
            whole(value.shape),
            pl.BlockSpec((1, tile), lambda i: (0, i)),
            whole((length, 1)),
        ],
        out_specs=[
            pl.BlockSpec((tile, heads * DV), lambda i: (i, 0)),
            pl.BlockSpec((heads, tile), lambda i: (0, i)),
        ],
        out_shape=[
            jax.ShapeDtypeStruct((length, heads * DV), BF),
            jax.ShapeDtypeStruct((heads, length), F32),
        ],
        compiler_params=pltpu.CompilerParams(vmem_limit_bytes=LIMIT),
        cost_estimate=LIGHT,
        name="attend",
    )(query, key, value, row_position, column_position)


def attend_back(query, key, value, result, result_grad, logsum, row_position, column_position, cosine, sine, w_up, latent_all, latent_gain, factor):
    heads, length, _ = query.shape
    tile = 256
    steps = length // tile
    wide = DN + DR

    def kernel(q_ref, k_ref, v_ref, o_ref, do_ref, ls_ref, row_ref, column_ref, c_ref, s_ref, wu_ref, l_ref, lg_ref, dq_ref, kv_ref, lp_ref, t_ref, dk_acc, dv_acc, kt):
        step = pl.program_id(0)

        @pl.when(step == 0)
        def _():
            dk_acc[...] = jnp.zeros_like(dk_acc)
            dv_acc[...] = jnp.zeros_like(dv_acc)
            for n in range(heads):
                kt[n] = k_ref[n].T

        allowed = column_ref[...] <= row_ref[...]
        cosine, sine = c_ref[...], s_ref[...]
        parts = []
        for n in range(heads):
            q = q_ref[n]
            grad = do_ref[:, n * DV : (n + 1) * DV]
            scores = jnp.where(allowed, dot_t(k_ref[n], q) * factor, -1e30)
            probs = jnp.exp(scores - ls_ref[n : n + 1, :])
            dv_acc[n] += dot(probs.astype(BF), grad)
            product = grad.astype(F32) * o_ref[:, n * DV : (n + 1) * DV].astype(F32)
            row_dot = jnp.sum(product.T, axis=0, keepdims=True)
            probs_grad = dot_t(v_ref[n], grad)
            score_grad = (probs * (probs_grad - row_dot) * factor).astype(BF)
            dk_acc[n] += dot(score_grad, q)
            query_grad = dot(kt[n], score_grad).T.astype(BF)
            parts.append(query_grad[:, :DN])
            parts.append(turned(query_grad[:, DN:wide].astype(F32), cosine, sine).astype(BF))
        dq_ref[...] = jnp.concatenate(parts, axis=1)

        @pl.when(step == steps - 1)
        def _():
            rope = jnp.zeros((length, DR), F32)
            for n in range(heads):
                key_grad = dk_acc[n].astype(BF)
                value_grad = dv_acc[n].astype(BF)
                base = n * (DN + DV)
                kv_ref[:, base : base + DN] = key_grad[:, :DN]
                kv_ref[:, base + DN : base + DN + DV] = value_grad
                rope = rope + key_grad[:, DN:wide].astype(F32)
            latent = dot_t(kv_ref[...], wu_ref[...])
            lp_ref[:, :R] = latent
            lp_ref[:, R:] = rope
            t_ref[...] = jnp.sum(
                latent * l_ref[...].astype(F32), axis=0, keepdims=True
            ) / lg_ref[...]

    return pl.pallas_call(
        kernel,
        grid=(steps,),
        in_specs=[
            pl.BlockSpec((heads, tile, 256), lambda i: (0, i, 0)),
            whole(key.shape),
            whole(value.shape),
            pl.BlockSpec((tile, heads * DV), lambda i: (i, 0)),
            pl.BlockSpec((tile, heads * DV), lambda i: (i, 0)),
            pl.BlockSpec((heads, tile), lambda i: (0, i)),
            pl.BlockSpec((1, tile), lambda i: (0, i)),
            whole((length, 1)),
            pl.BlockSpec((tile, DR), lambda i: (i, 0)),
            pl.BlockSpec((tile, DR), lambda i: (i, 0)),
            whole(w_up.shape),
            whole((length, R)),
            whole((1, R)),
        ],
        out_specs=[
            pl.BlockSpec((tile, heads * wide), lambda i: (i, 0)),
            whole((length, heads * (DN + DV))),
            whole((length, R + DR)),
            whole((1, R)),
        ],
        out_shape=[
            jax.ShapeDtypeStruct((length, heads * wide), BF),
            jax.ShapeDtypeStruct((length, heads * (DN + DV)), BF),
            jax.ShapeDtypeStruct((length, R + DR), F32),
            jax.ShapeDtypeStruct((1, R), F32),
        ],
        scratch_shapes=[
            pltpu.VMEM((heads, length, 256), F32),
            pltpu.VMEM((heads, length, DV), F32),
            pltpu.VMEM((heads, 256, length), BF),
        ],
        compiler_params=pltpu.CompilerParams(vmem_limit_bytes=LIMIT),
        cost_estimate=LIGHT,
        name="attend_back",
    )(query, key, value, result, result_grad, logsum, row_position, column_position, cosine, sine, w_up, latent_all, latent_gain)


def add_norm(token_blocks, blocks, w_even, w_odd, gain):
    count, width = token_blocks[0].shape
    many = len(blocks)
    chips = many // 2
    half = chips * count
    length = count * many
    depth = blocks[0].shape[1]

    def kernel(we_ref, wo_ref, g_ref, *refs):
        parts, tokens = refs[:many], refs[many : 2 * many]
        n_ref, r_ref, x_ref, a_ref = refs[2 * many :]
        for q in range(many):
            for p in range(chips):
                other = p ^ (q % chips)
                a_ref[p * count : (p + 1) * count, q * depth : (q + 1) * depth] = parts[q][
                    other * count : (other + 1) * count
                ]
        for h in range(2):

            @pl.when(pl.program_id(0) == h)
            def _():
                for k in range(chips):
                    x_ref[k * count : (k + 1) * count] = tokens[h * chips + k][...]

        middle = chips * depth
        total = dot(a_ref[:, :middle], we_ref[...]) + dot(a_ref[:, middle:], wo_ref[...])
        total = total + x_ref[...].astype(F32)
        inverse = lax.rsqrt(jnp.mean(total * total, axis=1, keepdims=True) + eps_norm)
        n_ref[...] = (total * inverse * g_ref[...]).astype(BF)

        @pl.when(pl.program_id(0) == 0)
        def _():
            r_ref[...] = total[:count]

    def source(q):
        return pl.BlockSpec((half, depth), lambda i: (i ^ (q // chips), 0))

    return pl.pallas_call(
        kernel,
        grid=(2,),
        in_specs=[whole(w_even.shape), whole(w_odd.shape), whole((1, width))]
        + [source(q) for q in range(many)]
        + [whole((count, width))] * many,
        out_specs=[pl.BlockSpec((half, width), lambda i: (i, 0)), whole((count, width))],
        out_shape=[
            jax.ShapeDtypeStruct((length, width), BF),
            jax.ShapeDtypeStruct((count, width), F32),
        ],
        scratch_shapes=[pltpu.VMEM((half, width), BF), pltpu.VMEM((half, many * depth), BF)],
        compiler_params=pltpu.CompilerParams(vmem_limit_bytes=LIMIT),
        cost_estimate=LIGHT,
        name="add_norm",
    )(w_even, w_odd, gain, *blocks, *token_blocks)


def expert(rows, cots, gate, up, down, piece):
    count, width = rows.shape
    units = gate.shape[2]
    tile = min(512, count)
    step = 256
    full = units // step
    rest = units % step
    spans = [(n * step, step) for n in range(full)] + ([(full * step, rest)] if rest else [])

    def kernel(x_ref, c_ref, gate_hbm, up_hbm, down_hbm, res_ref, in_ref, h_ref, gg_ref, ug_ref, wg, wu, wd, acc_r, acc_i, sems):
        first = pl.program_id(0) == 0

        def copies(n, start, size):
            span = pl.ds(start, size)
            return [
                pltpu.make_async_copy(gate_hbm.at[piece, :, span], wg.at[:, span], sems.at[0, n]),
                pltpu.make_async_copy(up_hbm.at[piece, :, span], wu.at[:, span], sems.at[1, n]),
                pltpu.make_async_copy(down_hbm.at[piece, span, :], wd.at[span, :], sems.at[2, n]),
            ]

        @pl.when(first)
        def _():
            for n, (start, size) in enumerate(spans):
                for copy in copies(n, start, size):
                    copy.start()

        acc_r[...] = jnp.zeros_like(acc_r)
        acc_i[...] = jnp.zeros_like(acc_i)

        def chunk(n, start, size):
            @pl.when(first)
            def _():
                for copy in copies(n, start, size):
                    copy.wait()

            span = pl.ds(start, size)
            x, c = x_ref[...], c_ref[...]
            w_gate, w_up, w_down = wg[:, span], wu[:, span], wd[span, :]
            g = dot(x, w_gate)
            u = dot(x, w_up)
            hidden_grad = dot_t(c, w_down)
            s = jax.nn.sigmoid(g)
            silu = g * s
            hidden = (silu * u).astype(BF)
            gate_grad = (hidden_grad * u * (s * (1.0 + g * (1.0 - s)))).astype(BF)
            up_grad = (hidden_grad * silu).astype(BF)
            h_ref[:, span] = hidden
            gg_ref[:, span] = gate_grad
            ug_ref[:, span] = up_grad
            acc_r[...] += dot(hidden, w_down)
            acc_i[...] += dot_t(gate_grad, w_gate) + dot_t(up_grad, w_up)

        if full:

            @pl.loop(0, full)
            def _(n):
                chunk(n, pl.multiple_of(n * step, step), step)

        if rest:
            chunk(full, full * step, rest)
        res_ref[...] = acc_r[...].astype(BF)
        in_ref[...] = acc_i[...].astype(BF)

    def block(w):
        return pl.BlockSpec((tile, w), lambda i: (i, 0))

    def array(w):
        return jax.ShapeDtypeStruct((count, w), BF)

    return pl.pallas_call(
        kernel,
        grid=(count // tile,),
        in_specs=[block(width), block(width), ANY, ANY, ANY],
        out_specs=[block(width), block(width), block(units), block(units), block(units)],
        out_shape=[array(width), array(width), array(units), array(units), array(units)],
        scratch_shapes=[
            pltpu.VMEM((width, units), BF),
            pltpu.VMEM((width, units), BF),
            pltpu.VMEM((units, width), BF),
            pltpu.VMEM((tile, width), F32),
            pltpu.VMEM((tile, width), F32),
            pltpu.SemaphoreType.DMA((3, len(spans))),
        ],
        compiler_params=pltpu.CompilerParams(vmem_limit_bytes=LIMIT),
        cost_estimate=LIGHT,
        name="expert",
    )(rows, cots, gate, up, down)


def expert_weights(rows, cots, hidden, gate_grad, up_grad, piece, pieces, earlier):
    count, width = rows.shape
    units = hidden.shape[1]
    tile = 256

    def kernel(x_ref, c_ref, h_ref, gg_ref, ug_ref, *refs):
        g_ref, u_ref, d_ref = refs[-3:]
        g_ref[0] = t_dot(x_ref[...], gg_ref[...])
        u_ref[0] = t_dot(x_ref[...], ug_ref[...])
        d_ref[0] = t_dot(h_ref[...], c_ref[...])

    tall = pl.BlockSpec((1, tile, units), lambda i: (piece, i, 0))
    flat = pl.BlockSpec((1, units, tile), lambda i: (piece, 0, i))
    column = pl.BlockSpec((count, tile), lambda i: (0, i))
    kept = list(earlier or ())
    return pl.pallas_call(
        kernel,
        grid=(width // tile,),
        in_specs=[column, column] + [whole((count, units))] * 3 + [ANY] * len(kept),
        out_specs=[tall, tall, flat],
        out_shape=[
            jax.ShapeDtypeStruct((pieces, width, units), F32),
            jax.ShapeDtypeStruct((pieces, width, units), F32),
            jax.ShapeDtypeStruct((pieces, units, width), F32),
        ],
        input_output_aliases={5 + n: n for n in range(len(kept))},
        compiler_params=pltpu.CompilerParams(vmem_limit_bytes=LIMIT),
        cost_estimate=LIGHT,
        name="expert_weights",
    )(rows, cots, hidden, gate_grad, up_grad, *kept)


def dispatch(select, rows, slot_weight, pieces):
    blocks, slots, count = select.shape
    width = rows.shape[1]
    others = slots // pieces // CAP

    def kernel(m_ref, x_ref, *refs):
        got = dot(m_ref[0], x_ref[...])
        if slot_weight is not None:
            got = got * refs[0][0]
        got = got.astype(BF)
        for i in range(pieces):
            for j in range(others):
                start = (i * others + j) * CAP
                refs[-pieces + i][j] = got[start : start + CAP]

    weights = [] if slot_weight is None else [slot_weight]
    out = pl.BlockSpec((others, CAP, width), lambda b: (0, b, 0))
    return pl.pallas_call(
        kernel,
        grid=(blocks,),
        in_specs=[
            pl.BlockSpec((1, slots, count), lambda b: (b, 0, 0)),
            pl.BlockSpec((count, width), lambda b: (b, 0)),
        ]
        + [pl.BlockSpec((1, slots, 1), lambda b: (b, 0, 0))] * len(weights),
        out_specs=[out] * pieces,
        out_shape=[jax.ShapeDtypeStruct((others, blocks * CAP, width), BF)] * pieces,
        compiler_params=pltpu.CompilerParams(vmem_limit_bytes=LIMIT),
        cost_estimate=LIGHT,
        name="dispatch",
    )(select, rows, *weights)


def down_weights(index, normed, down_even, down_odd, others, n_seq, gain_rows):
    length, _ = normed.shape
    half, columns = down_even.shape
    per = 128 // gain_rows

    def kernel(index_ref, n_ref, e_ref, d_ref, o_ref, part):
        part[...] = t_dot(n_ref[:half], e_ref[...]) + t_dot(n_ref[half:], d_ref[...])
        o_ref[0] = part[span(index_ref[1] % per, gain_rows)]

    return pl.pallas_call(
        kernel,
        grid_spec=pltpu.PrefetchScalarGridSpec(
            num_scalar_prefetch=1,
            grid=(others,),
            in_specs=[
                pl.BlockSpec(
                    (length, 128), lambda i, ref: (0, (i * n_seq + ref[1]) * gain_rows // 128)
                ),
                pl.BlockSpec((half, columns), lambda i, ref: (0, 0)),
                pl.BlockSpec((half, columns), lambda i, ref: (0, 0)),
            ],
            out_specs=pl.BlockSpec((1, gain_rows, columns), lambda i, ref: (i, 0, 0)),
            scratch_shapes=[pltpu.VMEM((128, columns), F32)],
        ),
        out_shape=jax.ShapeDtypeStruct((others, gain_rows, columns), F32),
        compiler_params=pltpu.CompilerParams(vmem_limit_bytes=LIMIT),
        cost_estimate=LIGHT,
        name="down_weights",
    )(index, normed, down_even, down_odd)


def combine(base, masks, returned, products, dtype):
    half = masks[0].shape[0] // 2
    slots, count = masks[0].shape[1:]
    pieces = len(returned)
    others, _, width = returned[0].shape
    many = len(masks)

    tile = 512

    def kernel(*refs):
        mask_refs, row_refs = refs[:many], refs[many : many + pieces]
        rest, out_ref = refs[many + pieces : -1], refs[-1]
        total = 0.0
        for n, (_, _, flipped) in enumerate(products):
            total = total + (dot_t if flipped else dot)(rest[2 * n][...], rest[2 * n + 1][...])
        for b in range(half):
            rows = jnp.concatenate(
                [
                    row_refs[i][j, b * CAP : (b + 1) * CAP]
                    for i in range(pieces)
                    for j in range(others)
                ],
                axis=0,
            )
            block = total[b * count : (b + 1) * count]
            for mask_ref in mask_refs:
                block = block + t_dot(mask_ref[b], rows)
            out_ref[b * count : (b + 1) * count] = block.astype(dtype)

    factors = []
    specs = []
    for left, right, flipped in products:
        factors += [left, right]
        specs.append(pl.BlockSpec((half * count, left.shape[1]), lambda t: (base, 0)))
        if flipped:
            specs.append(pl.BlockSpec((tile, right.shape[1]), lambda t: (t, 0)))
        else:
            specs.append(pl.BlockSpec((right.shape[0], tile), lambda t: (0, t)))
    return pl.pallas_call(
        kernel,
        grid=(width // tile,),
        in_specs=[pl.BlockSpec((half, slots, count), lambda t: (base, 0, 0))] * many
        + [pl.BlockSpec((others, half * CAP, tile), lambda t: (0, base, t))] * pieces
        + specs,
        out_specs=pl.BlockSpec((half * count, tile), lambda t: (0, t)),
        out_shape=jax.ShapeDtypeStruct((half * count, width), dtype),
        compiler_params=pltpu.CompilerParams(vmem_limit_bytes=LIMIT),
        cost_estimate=LIGHT,
        name="combine",
    )(*masks, *returned, *factors)


def swap(x, axis, mask):
    n = lax.axis_size(axis)
    return lax.ppermute(x, axis, [(i, i ^ mask) for i in range(n)])


def after(x, *earlier):
    return lax.optimization_barrier((x, *earlier))[0]


class Lane:
    def __init__(self, axis, depth):
        self.axis = axis
        self.depth = depth
        self.sent = []

    def send(self, x, mask):
        if len(self.sent) >= self.depth:
            x = after(x, self.sent[-self.depth])
        got = swap(x, self.axis, mask)
        self.sent.append(got)
        return got

    def chips(self, x):
        chips = lax.axis_size("seq") // 2
        return [x] + [self.send(x, 2 * k) for k in range(1, chips)]

    def group(self, x):
        return self.pair(self.chips(x))

    def pair(self, evens):
        rows, columns = evens[0].shape
        everything = slice(None)
        (even,) = arrange(
            jnp.zeros((1,), jnp.int32),
            evens,
            [(rows * len(evens), columns)],
            [
                (k, everything, 0, lambda ref, k=k: (slice(k * rows, (k + 1) * rows), everything))
                for k in range(len(evens))
            ],
        )
        return even, swap(even, "seq", 1)

    def scatter(self, even, odd):
        return self.finish(self.begin(even, odd))

    def begin(self, even, odd):
        chips = lax.axis_size("seq") // 2
        rows = even.shape[0] // chips
        got = swap(odd.astype(BF), "seq", 1)
        blocks = [
            even[k * rows : (k + 1) * rows] + got[k * rows : (k + 1) * rows].astype(F32)
            for k in range(chips)
        ]
        return blocks[:1] + [block.astype(BF) for block in blocks[1:]]

    def finish(self, blocks, *gates):
        got = [self.send(blocks[k], 2 * k) for k in range(1, len(blocks))]
        total = blocks[0]
        for block in got:
            total = total + after(block, *gates).astype(F32)
        return total

    def corners(self, x, *gates):
        if lax.axis_size("exp") != 4:
            return [(j, 0, y) for j, y in enumerate(self.others(x))]
        middle = x.shape[0] // 2
        one, two = self.send(x, 1), self.send(x, 2)
        return [
            (0, 0, x),
            (1, 0, one),
            (2, 0, two),
            (3, 0, self.send(after(two[:middle], *gates), 1)),
            (3, middle, self.send(after(one[middle:], *gates), 2)),
        ]

    def others(self, x):
        return [x] + [self.send(x, j) for j in range(1, lax.axis_size("exp"))]

def relative_order(count):
    chips = count // 2
    return [2 * k for k in range(chips)] + [2 * k + 1 for k in range(chips)]


def sum_exp(x, axis):
    return lax.psum_scatter(x.astype(BF), "exp", scatter_dimension=axis, tiled=True).astype(F32)


def shards(
    tokens,
    routes,
    route_weights,
    norm_gain,
    w_query,
    w_kv_down,
    latent_gain,
    w_kv_up,
    w_output,
    ffn_gain,
    shared_gate,
    shared_up,
    shared_down,
    expert_gate,
    expert_up,
    expert_down,
    out_grad,
):
    count, width = tokens.shape
    n_seq = lax.axis_size("seq")
    n_exp = lax.axis_size("exp")
    seq = lax.axis_index("seq")
    order = relative_order(n_seq)
    chips = n_seq // 2
    heads = H // n_seq
    length = count * n_seq
    half = length // 2
    pieces = expert_gate.shape[0]
    parts_per = pieces * n_seq * n_exp // EXPERTS
    factor = 1.0 / math.sqrt(DN + DR)
    gain_rows = norm_gain.shape[0]
    latent_rows_local = latent_gain.shape[0]
    along = Lane("seq", 3)
    across = Lane("exp", 3)
    free = Lane("seq", 3)

    index = jnp.stack([lax.axis_index("exp"), seq]).astype(jnp.int32)
    ratio = w_query.shape[0] // w_kv_up.shape[0]
    slim = w_kv_up.shape[1] // ratio
    columns = w_kv_down.shape[1]
    high = lax.reduce_precision(route_weights, 8, 7)
    middle = lax.reduce_precision(route_weights - high, 8, 7)
    low = route_weights - high - middle
    route_pack = jnp.concatenate([routes.astype(F32), high, middle, low], axis=1).astype(BF).T
    lines = route_pack.shape[0] // 4
    gains = jnp.concatenate([norm_gain, ffn_gain, latent_gain])
    packed = jnp.concatenate(
        [
            w_kv_down,
            jnp.pad(gains, (0, columns - gains.shape[0]))[None, :],
            jnp.pad(
                route_pack.reshape(4, lines, count).transpose(1, 0, 2).reshape(lines, 4 * count),
                ((0, 15 - lines), (0, columns - 4 * count)),
            ),
        ],
        axis=0,
    )
    packed_even = jnp.stack(free.chips(packed))
    token_even = along.chips(tokens)
    first_all = lax.all_gather(
        jnp.concatenate(
            [
                w_query,
                jnp.concatenate(
                    [w_kv_up[:, g * slim : (g + 1) * slim] for g in range(ratio)], axis=0
                ),
            ],
            axis=1,
        ),
        "exp",
        axis=0,
        tiled=True,
    )
    packed_parts = across.others(packed_even)
    packed_even = jnp.stack(packed_parts)
    packed_odd = swap(packed_even, "seq", 1)
    token_odd = []
    for x in token_even:
        token_odd.append(swap(after(x, *token_odd), "seq", 1))
    token_blocks = token_even + token_odd
    output_even = along.chips(after(w_output, *token_odd, packed_odd))
    early = packed_parts[-1]
    gate_cols = lax.all_gather(after(shared_gate, early), "exp", axis=0, tiled=True)
    lift_cols = lax.all_gather(after(shared_up, early), "exp", axis=0, tiled=True)
    drop_rows = lax.all_gather(after(shared_down, early), "exp", axis=1, tiled=True)
    grad_even = along.chips(out_grad)

    everything = slice(None)
    block_rows = width // n_exp
    plan = []
    for h in range(2):
        for j in range(n_exp):
            for k in range(chips):

                def where(ref, h=h, j=j, k=k):
                    return (ref[0] ^ j) * n_seq + (ref[1] ^ (2 * k + h))

                plan.append(
                    (
                        h,
                        (j, k, slice(0, gain_rows)),
                        0,
                        lambda ref, where=where: (span(where(ref), gain_rows), everything),
                    )
                )
                plan.append(
                    (
                        h,
                        (j, k, slice(gain_rows, gain_rows + 16)),
                        1,
                        lambda ref, where=where: (where(ref),),
                    )
                )
    down_full, extra_all = arrange(
        index,
        [packed_even, packed_odd],
        [(width, columns), (n_exp * n_seq, 16, columns)],
        plan,
    )
    gain_first = extra_all[:, 0, :gain_rows].reshape(1, width).astype(F32)
    gain_second = extra_all[:, 0, gain_rows : 2 * gain_rows].reshape(1, width).astype(F32)
    latent_wide = (
        extra_all[:, 0, 2 * gain_rows : 2 * gain_rows + latent_rows_local]
        .reshape(1, R)
        .astype(F32)
    )
    route_all = jnp.concatenate(
        [packed_even[0, :, gain_rows + 1 :], packed_odd[0, :, gain_rows + 1 :]], axis=0
    )[:, :lines, : 4 * count]
    route_all = route_all.reshape(n_seq, lines, 4, count).transpose(0, 2, 1, 3)
    route_all = route_all.reshape(n_seq, 4 * lines, count).astype(F32)
    route_all = jnp.concatenate(
        [
            route_all[:, :TOP],
            route_all[:, TOP : 2 * TOP]
            + route_all[:, 2 * TOP : 3 * TOP]
            + route_all[:, 3 * TOP :],
        ],
        axis=1,
    )
    up_rows = w_kv_up.shape[0]
    query_width = w_query.shape[1]
    (up_cols,) = arrange(
        index,
        [first_all],
        [(R, w_kv_up.shape[1])],
        [
            (
                0,
                (
                    slice((j * ratio + g) * up_rows, (j * ratio + g + 1) * up_rows),
                    slice(query_width, query_width + slim),
                ),
                0,
                lambda ref, j=j, g=g: (
                    slice(j * up_rows, (j + 1) * up_rows),
                    slice(g * slim, (g + 1) * slim),
                ),
            )
            for j in range(n_exp)
            for g in range(ratio)
        ],
    )
    positions = jnp.concatenate(
        [(seq ^ r) * count + jnp.arange(count, dtype=jnp.int32) for r in order]
    )
    row_position, column_position = positions[None, :], positions[:, None]
    cosine_table, sine_table = rope_tables(positions, DR)
    cosine_wide = jnp.concatenate([cosine_table, cosine_table], axis=1)
    sine_wide = jnp.concatenate([-sine_table, sine_table], axis=1)
    normed_one, latent_all, latent_raw, query_heads, key_heads, value_heads = project(
        token_blocks,
        gain_first,
        first_all,
        down_full,
        latent_wide,
        up_cols,
        cosine_wide,
        sine_wide,
        heads,
    )
    output_even = jnp.concatenate([after(x, normed_one) for x in output_even], axis=0)
    result, logsum = attend(
        query_heads, key_heads, value_heads, row_position, column_position, factor
    )

    output_parts = across.corners(output_even, result, *grad_even[1:])
    (output_even,) = arrange(
        index,
        [part[2] for part in output_parts],
        [(H * DV // 2, width)],
        [
            (
                n,
                everything,
                0,
                lambda ref, j=j, at=at, x=x: (
                    slice(at, at + x.shape[0]),
                    span(ref[0] ^ j, block_rows),
                ),
            )
            for n, (j, at, x) in enumerate(output_parts)
        ],
    )
    output_odd = swap(output_even, "seq", 1)

    grad_even, grad_odd = along.pair([after(x, result) for x in grad_even])

    column = jnp.stack(
        [
            ((other * n_seq + seq) * pieces + i) // parts_per
            for i in range(pieces)
            for other in range(n_exp)
        ]
    )
    kinds = n_exp * pieces
    named = route_all[:, None, :TOP, :].astype(jnp.int32) == column[None, :, None, None]
    matched = jnp.any(named, axis=2)
    match_weight = jnp.sum(jnp.where(named, route_all[:, None, TOP:, :], 0.0), axis=2)
    earlier = (jnp.arange(count)[:, None] < jnp.arange(count)[None, :]).astype(BF)
    rank = jnp.dot(matched.astype(BF), earlier, preferred_element_type=F32).astype(jnp.int32)
    chosen = (rank[:, :, None, :] == jnp.arange(CAP, dtype=jnp.int32)[None, None, :, None]) & (
        matched[:, :, None, :]
    )
    select = chosen.astype(BF).reshape(n_seq, kinds * CAP, count)
    weighted = jnp.where(chosen, match_weight[:, :, None, :], 0.0).reshape(
        n_seq, kinds * CAP, count
    )
    slot_weight = jnp.sum(weighted, axis=2, keepdims=True)
    weighted_high = weighted.astype(BF)
    weighted_low = (weighted - weighted_high.astype(F32)).astype(BF)

    def give(rows):
        return lax.all_to_all(rows, "exp", split_axis=0, concat_axis=0, tiled=True)

    (grad_rows,) = arrange(
        index,
        [grad_even, grad_odd],
        [(length, width)],
        [
            (h, everything, 0, lambda ref, h=h: (slice(h * half, (h + 1) * half), everything))
            for h in range(2)
        ],
    )
    send_cots = dispatch(select, grad_rows, slot_weight, pieces)
    received_grad = [give(rows) for rows in send_cots]

    result_even = along.chips(result)
    gathered = (gate_cols, lift_cols, drop_rows)
    result_even = [after(x, *send_cots, *gathered) for x in result_even]
    result_blocks = result_even + [swap(x, "seq", 1) for x in result_even]
    normed_two, residual = add_norm(
        token_blocks,
        [after(result_blocks[0], received_grad[0])] + result_blocks[1:],
        output_even,
        output_odd,
        gain_second,
    )
    inverse_two = inverse_rms(residual)
    send_rows = dispatch(select, normed_two, None, pieces)
    received = [give(after(send_rows[0], *received_grad))]


    shared_rows = after(normed_two, *send_rows)
    shared_gate_raw = dot(shared_rows, gate_cols)
    shared_up_raw = dot(shared_rows, lift_cols)
    shared_hidden = (jax.nn.silu(shared_gate_raw) * shared_up_raw).astype(BF)
    shared_hidden_grad = dot_t(grad_rows, drop_rows)
    sgate_grad = (shared_hidden_grad * shared_up_raw * silu_slope(shared_gate_raw)).astype(BF)
    sup_grad = (shared_hidden_grad * jax.nn.silu(shared_gate_raw)).astype(BF)
    received += [give(after(rows, sgate_grad, sup_grad)) for rows in send_rows[1:]]

    slot_rows = n_exp * n_seq * CAP
    pairs = []
    results_back, grads_back, kept = [], [], []
    for i in range(pieces):
        rows = received[i].reshape(slot_rows, width)
        cots = received_grad[i].reshape(slot_rows, width)
        expert_result, input_grad, *saved = expert(
            rows, cots, expert_gate, expert_up, expert_down, i
        )
        grads_back.append(give(input_grad.reshape(n_exp, n_seq * CAP, width)))
        results_back.append(expert_result.reshape(n_exp, n_seq * CAP, width))
        kept.append((rows, cots, *saved))
    two_products = [(sgate_grad, gate_cols, True), (sup_grad, lift_cols, True)]
    expert_grads = expert_weights(
        after(kept[0][0], input_grad), *kept[0][1:], 0, pieces, None
    )
    select = after(select, *expert_grads)
    two_odd = combine(1, [select], grads_back, two_products, BF)
    two_even = combine(0, [select], grads_back, two_products, F32)
    two_blocks = along.begin(two_even, two_odd)
    back = []
    for i in range(pieces):
        back.append(give(after(results_back[i], *(two_blocks if i == 0 else expert_grads))))
        if i:
            expert_grads = expert_weights(
                after(kept[i][0], back[0]), *kept[i][1:], i, pieces, expert_grads
            )
    results_back = back
    expert_gate_grad, expert_up_grad, expert_down_grad = expert_grads
    two_grad = along.finish(two_blocks, *expert_grads)
    gate_out = sum_exp(t_dot(after(shared_rows, *two_blocks), sgate_grad), 0)
    lift_out = sum_exp(t_dot(after(shared_rows, *two_blocks), sup_grad), 0)
    drop_out = sum_exp(t_dot(after(shared_hidden, *two_blocks), grad_rows), 1)

    residual_norm_grad, second_terms = norm_back(
        two_grad, residual, inverse_two, gain_second
    )
    residual_grad = out_grad.astype(F32) + residual_norm_grad
    residual_half = residual_grad.astype(BF)
    even_heads = dot_t(residual_half, output_even).astype(BF)
    odd_heads = dot_t(residual_half, output_odd).astype(BF)
    wide = heads * DV
    pairs = [
        jnp.stack([even_heads[:, k * wide : (k + 1) * wide], odd_heads[:, k * wide : (k + 1) * wide]])
        for k in range(chips)
    ]
    stacks = pairs
    pairs = [pairs[0]] + [along.send(pairs[k], 2 * k) for k in range(1, chips)]
    other_half = swap(jnp.stack([pair[1] for pair in pairs]), "seq", 1)
    attention_grad = jnp.concatenate(
        [jnp.stack([pair[0] for pair in pairs]), other_half], axis=0
    ).reshape(length, wide)
    (own_heads,) = arrange(
        index,
        [after(result_blocks[0], *two_blocks)] + result_blocks[1:],
        [(count, H * DV)],
        [
            (
                p,
                (slice(p * count, (p + 1) * count), everything),
                0,
                lambda ref, p=p: (everything, slice(p * heads * DV, (p + 1) * heads * DV)),
            )
            for p in range(n_seq)
        ],
    )
    mine = lax.axis_index("exp")
    late = Lane("exp", 3)
    attention_parts = late.others(after(own_heads, attention_grad))
    column_blocks = [
        lax.dynamic_slice_in_dim(residual_half, (mine ^ j) * block_rows, block_rows, 1)
        for j in range(n_exp)
    ]
    column_blocks = [column_blocks[0]] + [
        late.send(column_blocks[j], j) for j in range(1, n_exp)
    ]

    out_products = [(shared_hidden, drop_rows, False)]
    out_masks = [weighted_high, weighted_low]
    out_masks = [after(mask, *stacks) for mask in out_masks]
    out_odd = combine(1, out_masks, results_back, out_products, BF)
    out_even = combine(0, out_masks, results_back, out_products, F32)
    out_blocks = along.begin(out_even, out_odd)
    output_got = [along.send(out_blocks[k], 2 * k) for k in range(chips - 1, 0, -1)]

    query_in_grad, kv_grad, latent_part, latent_sum = attend_back(
        query_heads,
        key_heads,
        value_heads,
        result,
        after(attention_grad, *out_blocks),
        logsum,
        row_position,
        column_position,
        cosine_wide,
        -sine_wide,
        up_cols,
        latent_all,
        latent_wide,
        factor,
    )
    query_in_grad = after(query_in_grad, *output_got[:2])
    one_odd, odd_sum = query_back(1, query_in_grad, first_all, normed_one, gain_first, BF)
    one_even, even_sum = query_back(0, query_in_grad, first_all, normed_one, gain_first, F32)
    sums = jnp.concatenate(
        [
            (odd_sum + even_sum).reshape(n_exp, n_seq, gain_rows),
            jnp.sum(second_terms, axis=0).reshape(n_exp, n_seq, gain_rows),
            latent_sum.reshape(n_exp, n_seq, latent_rows_local),
        ],
        axis=2,
    )
    many = sums.shape[2]
    turn = (seq ^ jnp.array(order))[:, None] == jnp.arange(n_seq)[None, :]
    sums = jnp.einsum("ps,esw->pew", turn.astype(F32), sums, precision=lax.Precision.HIGHEST)
    sums = jnp.pad(
        sums.reshape(n_seq, 1, n_exp * many), ((0, 0), (0, 15), (0, columns - n_exp * many))
    )
    latent_part = jnp.concatenate([latent_part.reshape(n_seq, count, columns), sums], axis=1)
    latent_part = latent_part.reshape(n_seq * (count + 16), columns)
    output_part = t_dot(
        jnp.concatenate([after(x, query_in_grad) for x in attention_parts], axis=0),
        jnp.concatenate([after(x, query_in_grad) for x in column_blocks], axis=0),
    )
    output_blocks = along.begin(output_part[: H * DV // 2], output_part[H * DV // 2 :])
    latent_grad = along.scatter(
        latent_part[: chips * (count + 16)], latent_part[chips * (count + 16) :]
    )
    one_blocks = along.begin(one_even, one_odd)
    one_got = [along.send(one_blocks[k], 2 * k) for k in range(chips - 1, 0, -1)]
    up_part = t_dot(after(latent_all, *one_blocks), kv_grad).astype(BF)
    query_part = t_dot(after(normed_one, *one_blocks), query_in_grad).astype(BF)
    up_out = sum_exp(up_part, 0)
    query_out = sum_exp(query_part, 0)
    sums = latent_grad[count, : n_exp * many].reshape(n_exp, 1, many)
    latent_grad = latent_grad[:count]
    latent_raw_grad, _ = norm_back(
        latent_grad[:, :R], latent_raw[:count], inverse_rms(latent_raw[:count]), latent_wide
    )
    down_rows = jnp.concatenate(
        [
            latent_raw_grad,
            rotate(latent_grad[:, R:], cosine_table[:count], -sine_table[:count]),
        ],
        axis=1,
    ).astype(BF)
    wide_got = [free.send(output_blocks[k], 2 * k) for k in range(chips - 1, 0, -1)]
    down_even, down_odd = free.pair(
        [after(x, *one_got, *wide_got) for x in free.chips(down_rows)]
    )
    down_part = down_weights(index, normed_one, down_even, down_odd, n_exp, n_seq, gain_rows)
    down_part = jnp.concatenate(
        [
            down_part,
            jnp.pad(sums, ((0, 0), (0, 15), (0, columns - many))),
        ],
        axis=1,
    )
    down_sum = lax.dynamic_index_in_dim(down_part, mine, 0, keepdims=False)
    for j in range(1, n_exp):
        piece = lax.dynamic_index_in_dim(down_part, mine ^ j, 0, keepdims=False).astype(BF)
        down_sum = down_sum + swap(piece, "exp", j).astype(F32)
    down_out = down_sum[:gain_rows]
    small = down_sum[gain_rows, :many]
    first_out = small[:gain_rows] + jnp.sum(
        w_kv_down.astype(F32) * down_out, axis=1
    ) / norm_gain.astype(F32)

    output = residual + out_blocks[0]
    for block in output_got:
        output = output + after(block, *one_blocks).astype(F32)
    output = output.astype(BF)
    output_out = output_blocks[0]
    for block in wide_got:
        output_out = output_out + block.astype(F32)
    one_grad = one_blocks[0]
    for block in one_got:
        block = after(block, up_part, query_part, gate_out, lift_out, drop_out)
        one_grad = one_grad + block.astype(F32)
    down_back = dot_t(down_rows, down_full)
    token_wide = tokens.astype(F32)
    token_norm_grad, _ = norm_back(
        one_grad + down_back, token_wide, inverse_rms(token_wide), gain_first
    )
    tokens_grad = (residual_grad + token_norm_grad).astype(BF)
    return (
        output,
        tokens_grad,
        first_out,
        query_out,
        down_out,
        small[2 * gain_rows : many],
        up_out,
        output_out,
        small[gain_rows : 2 * gain_rows],
        gate_out,
        lift_out,
        drop_out,
        expert_gate_grad,
        expert_up_grad,
        expert_down_grad,
    )


def solution(mesh):
    rows = P(("exp", "seq"), None)
    line = P(("exp", "seq"))
    grid = P("exp", "seq")
    turned = P("seq", "exp")
    part = P(("exp", "seq"), None, None)
    return jax.shard_map(
        shards,
        mesh=mesh,
        in_specs=(
            rows,
            rows,
            rows,
            line,
            grid,
            rows,
            line,
            grid,
            turned,
            line,
            grid,
            grid,
            turned,
            part,
            part,
            part,
            rows,
        ),
        out_specs=(
            rows,
            rows,
            line,
            grid,
            rows,
            line,
            grid,
            turned,
            line,
            grid,
            grid,
            turned,
            part,
            part,
            part,
        ),
        check_vma=False,
    )
```

```python
import math

import jax
import jax.numpy as jnp
from jax import lax
from jax.experimental import pallas as pl
from jax.experimental.pallas import tpu as pltpu
from jax.sharding import PartitionSpec as P

H = 16
DN = 128
DR = 64
DV = 128
R = 512
EXPERTS = 64
TOP = 6
CAP = 16


eps_norm = 1e-06
rope_base = 50000.0
BF = jnp.bfloat16
F32 = jnp.float32


def dot(a, b):
    return jnp.dot(a, b, preferred_element_type=F32)


def dot_t(a, b):
    return lax.dot_general(a, b, (((1,), (1,)), ((), ())), preferred_element_type=F32)


def t_dot(a, b):
    return lax.dot_general(a, b, (((0,), (0,)), ((), ())), preferred_element_type=F32)


def rope_tables(positions, width):
    middle = width // 2
    frequency = rope_base ** (-(jnp.arange(middle, dtype=F32) * 2.0 / width))
    angles = positions.astype(F32)[:, None] * frequency[None, :]
    return (jnp.cos(angles), jnp.sin(angles))


def rotate(values, cosine_table, sine_table):
    middle = values.shape[-1] // 2
    leading = values[..., :middle]
    trailing = values[..., middle:]
    return jnp.concatenate(
        [
            leading * cosine_table - trailing * sine_table,
            trailing * cosine_table + leading * sine_table,
        ],
        axis=-1,
    )


def silu_slope(gate_values):
    sigmoid = jax.nn.sigmoid(gate_values)
    return sigmoid * (1.0 + gate_values * (1.0 - sigmoid))


def norm_back(dy, v, inverse, gain):
    hat = v * inverse
    scaled = dy * gain
    dv = inverse * (scaled - hat * jnp.mean(scaled * hat, axis=-1, keepdims=True))
    return dv, dy * hat


def inverse_rms(v):
    return lax.rsqrt(jnp.mean(v * v, axis=-1, keepdims=True) + eps_norm)


LIMIT = 56 * 1024 * 1024
LIGHT = pl.CostEstimate(flops=0, transcendentals=0, bytes_accessed=0)
ANY = pl.BlockSpec(memory_space=pl.ANY)
SCALARS = pl.BlockSpec(memory_space=pltpu.SMEM)


def whole(shape):
    return pl.BlockSpec(shape, lambda *grid: (0,) * len(shape))


def arrange(index, blocks, outs, plan):
    def kernel(index_ref, *refs):
        sources = refs[: len(blocks)]
        targets = refs[len(blocks) :]
        for block, source, out, target in plan:
            targets[out][target(index_ref)] = sources[block][source]

    return pl.pallas_call(
        kernel,
        out_shape=[jax.ShapeDtypeStruct(s, BF) for s in outs],
        in_specs=[SCALARS] + [pl.BlockSpec(memory_space=pltpu.VMEM)] * len(blocks),
        out_specs=[pl.BlockSpec(memory_space=pltpu.VMEM)] * len(outs),
        compiler_params=pltpu.CompilerParams(vmem_limit_bytes=LIMIT),
        cost_estimate=LIGHT,
        name="arrange",
    )(index, *blocks)


def span(start, size):
    return pl.ds(pl.multiple_of(start * size, size), size)


def turned(v, cosine, sine):
    middle = v.shape[1] // 2
    return v * cosine + jnp.concatenate([v[:, middle:], v[:, :middle]], axis=1) * sine


def project(token_blocks, gain, w_first, w_down, latent_gain, w_up, cosine, sine, heads):
    count, width = token_blocks[0].shape
    chips = len(token_blocks) // 2
    half = chips * count
    wide = DN + DR
    columns = heads * wide

    def kernel(g_ref, wd_ref, lg_ref, wu_ref, c_ref, s_ref, *refs):
        tokens, w_ref = refs[: 2 * chips], refs[2 * chips]
        n_ref, l_ref, r_ref, q_ref, k_ref, v_ref, x_ref = refs[2 * chips + 1 :]
        for h in range(2):

            @pl.when(pl.program_id(0) == h)
            def _():
                for k in range(chips):
                    x_ref[k * count : (k + 1) * count] = tokens[h * chips + k][...]

        x = x_ref[...].astype(F32)
        inverse = lax.rsqrt(jnp.mean(x * x, axis=1, keepdims=True) + eps_norm)
        n_ref[...] = (x * inverse * g_ref[...]).astype(BF)
        down = dot(n_ref[...], wd_ref[...])
        raw = down[:, :R]
        r_ref[...] = raw
        inverse = lax.rsqrt(jnp.mean(raw * raw, axis=1, keepdims=True) + eps_norm)
        l_ref[...] = (raw * inverse * lg_ref[...]).astype(BF)
        query = dot(n_ref[...], w_ref[:, :columns])
        up = dot(l_ref[...], wu_ref[...]).astype(BF)
        cosine, sine = c_ref[...], s_ref[...]
        zeros = jnp.zeros((half, 256 - wide), BF)
        rope = jnp.concatenate([turned(down[:, R : R + DR], cosine, sine).astype(BF), zeros], axis=1)
        for n in range(heads):
            own = query[:, n * wide : (n + 1) * wide]
            q_ref[n, :, :DN] = own[:, :DN].astype(BF)
            q_ref[n, :, DN:] = jnp.concatenate(
                [turned(own[:, DN:], cosine, sine).astype(BF), zeros], axis=1
            )
            k_ref[n, :, :DN] = up[:, n * (DN + DV) : n * (DN + DV) + DN]
            k_ref[n, :, DN:] = rope
            v_ref[n] = up[:, n * (DN + DV) + DN : (n + 1) * (DN + DV)]

    def rows(w):
        return pl.BlockSpec((half, w), lambda i: (i, 0))

    def head_rows(w):
        return pl.BlockSpec((heads, half, w), lambda i: (0, i, 0))

    length = 2 * half
    return pl.pallas_call(
        kernel,
        grid=(2,),
        in_specs=[
            whole((1, width)),
            whole(w_down.shape),
            whole((1, R)),
            whole(w_up.shape),
            rows(DR),
            rows(DR),
        ]
        + [whole((count, width))] * (2 * chips)
        + [whole(w_first.shape)],
        out_specs=[rows(width), rows(R), rows(R), head_rows(256), head_rows(256), head_rows(DV)],
        out_shape=[
            jax.ShapeDtypeStruct((length, width), BF),
            jax.ShapeDtypeStruct((length, R), BF),
            jax.ShapeDtypeStruct((length, R), F32),
            jax.ShapeDtypeStruct((heads, length, 256), BF),
            jax.ShapeDtypeStruct((heads, length, 256), BF),
            jax.ShapeDtypeStruct((heads, length, DV), BF),
        ],
        scratch_shapes=[pltpu.VMEM((half, width), BF)],
        compiler_params=pltpu.CompilerParams(vmem_limit_bytes=LIMIT),
        cost_estimate=LIGHT,
        name="project",
    )(gain, w_down, latent_gain, w_up, cosine, sine, *token_blocks, w_first)


def query_back(base, query_grad, w_first, normed, gain, dtype):
    length, columns = query_grad.shape
    half = length // 2
    width = normed.shape[1]
    tile = 512

    def kernel(q_ref, n_ref, g_ref, w_ref, o_ref, t_ref):
        part = dot_t(q_ref[...], w_ref[:, :columns])
        o_ref[...] = part.astype(dtype)
        product = part * n_ref[...].astype(F32)
        t_ref[...] = jnp.sum(product, axis=0, keepdims=True) / g_ref[...]

    return pl.pallas_call(
        kernel,
        grid=(width // tile,),
        in_specs=[
            pl.BlockSpec((half, columns), lambda i: (base, 0)),
            pl.BlockSpec((half, tile), lambda i: (base, i)),
            pl.BlockSpec((1, tile), lambda i: (0, i)),
            pl.BlockSpec((tile, w_first.shape[1]), lambda i: (i, 0)),
        ],
        out_specs=[
            pl.BlockSpec((half, tile), lambda i: (0, i)),
            pl.BlockSpec((1, tile), lambda i: (0, i)),
        ],
        out_shape=[
            jax.ShapeDtypeStruct((half, width), dtype),
            jax.ShapeDtypeStruct((1, width), F32),
        ],
        compiler_params=pltpu.CompilerParams(vmem_limit_bytes=LIMIT),
        cost_estimate=LIGHT,
        name="query_back",
    )(query_grad, normed, gain, w_first)


def attend(query, key, value, row_position, column_position, factor):
    heads, length, _ = query.shape
    tile = 256

    def kernel(q_ref, k_ref, v_ref, row_ref, column_ref, o_ref, s_ref):
        allowed = column_ref[...] <= row_ref[...]
        for n in range(heads):
            scores = dot_t(k_ref[n], q_ref[n]) * factor
            exponent = jnp.where(allowed, jnp.exp(jnp.where(allowed, scores, -1e30)), 0.0)
            total = jnp.sum(exponent, axis=0, keepdims=True)
            probs = (exponent / total).astype(BF)
            o_ref[:, n * DV : (n + 1) * DV] = t_dot(v_ref[n], probs).T.astype(BF)
            s_ref[n : n + 1, :] = jnp.log(total)

    return pl.pallas_call(
        kernel,
        grid=(length // tile,),
        in_specs=[
            pl.BlockSpec((heads, tile, 256), lambda i: (0, i, 0)),
            whole(key.shape),
            whole(value.shape),
            pl.BlockSpec((1, tile), lambda i: (0, i)),
            whole((length, 1)),
        ],
        out_specs=[
            pl.BlockSpec((tile, heads * DV), lambda i: (i, 0)),
            pl.BlockSpec((heads, tile), lambda i: (0, i)),
        ],
        out_shape=[
            jax.ShapeDtypeStruct((length, heads * DV), BF),
            jax.ShapeDtypeStruct((heads, length), F32),
        ],
        compiler_params=pltpu.CompilerParams(vmem_limit_bytes=LIMIT),
        cost_estimate=LIGHT,
        name="attend",
    )(query, key, value, row_position, column_position)


def attend_back(query, key, value, result, result_grad, logsum, row_position, column_position, cosine, sine, w_up, latent_all, latent_gain, factor, columns):
    heads, length, _ = query.shape
    tile = 256
    steps = length // tile
    wide = DN + DR

    def kernel(q_ref, k_ref, v_ref, o_ref, do_ref, ls_ref, row_ref, column_ref, c_ref, s_ref, wu_ref, l_ref, lg_ref, dq_ref, kv_ref, lp_ref, t_ref, dk_acc, dv_acc, kt):
        step = pl.program_id(0)

        @pl.when(step == 0)
        def _():
            dk_acc[...] = jnp.zeros_like(dk_acc)
            dv_acc[...] = jnp.zeros_like(dv_acc)
            for n in range(heads):
                kt[n] = k_ref[n].T

        allowed = column_ref[...] <= row_ref[...]
        cosine, sine = c_ref[...], s_ref[...]
        parts = []
        for n in range(heads):
            q = q_ref[n]
            grad = do_ref[:, n * DV : (n + 1) * DV]
            scores = jnp.where(allowed, dot_t(k_ref[n], q) * factor, -1e30)
            probs = jnp.exp(scores - ls_ref[n : n + 1, :])
            dv_acc[n] += dot(probs.astype(BF), grad)
            product = grad.astype(F32) * o_ref[:, n * DV : (n + 1) * DV].astype(F32)
            row_dot = jnp.sum(product.T, axis=0, keepdims=True)
            probs_grad = dot_t(v_ref[n], grad)
            score_grad = (probs * (probs_grad - row_dot) * factor).astype(BF)
            dk_acc[n] += dot(score_grad, q)
            query_grad = dot(kt[n], score_grad).T.astype(BF)
            parts.append(query_grad[:, :DN])
            parts.append(turned(query_grad[:, DN:wide].astype(F32), cosine, sine).astype(BF))
        dq_ref[...] = jnp.concatenate(parts, axis=1)

        @pl.when(step == steps - 1)
        def _():
            rope = jnp.zeros((length, DR), F32)
            for n in range(heads):
                key_grad = dk_acc[n].astype(BF)
                value_grad = dv_acc[n].astype(BF)
                base = n * (DN + DV)
                kv_ref[:, base : base + DN] = key_grad[:, :DN]
                kv_ref[:, base + DN : base + DN + DV] = value_grad
                rope = rope + key_grad[:, DN:wide].astype(F32)
            latent = dot_t(kv_ref[...], wu_ref[...])
            lp_ref[:, :R] = latent
            lp_ref[:, R : R + DR] = rope
            lp_ref[:, R + DR :] = jnp.zeros((length, columns - R - DR), F32)
            t_ref[...] = jnp.sum(
                latent * l_ref[...].astype(F32), axis=0, keepdims=True
            ) / lg_ref[...]

    return pl.pallas_call(
        kernel,
        grid=(steps,),
        in_specs=[
            pl.BlockSpec((heads, tile, 256), lambda i: (0, i, 0)),
            whole(key.shape),
            whole(value.shape),
            pl.BlockSpec((tile, heads * DV), lambda i: (i, 0)),
            pl.BlockSpec((tile, heads * DV), lambda i: (i, 0)),
            pl.BlockSpec((heads, tile), lambda i: (0, i)),
            pl.BlockSpec((1, tile), lambda i: (0, i)),
            whole((length, 1)),
            pl.BlockSpec((tile, DR), lambda i: (i, 0)),
            pl.BlockSpec((tile, DR), lambda i: (i, 0)),
            whole(w_up.shape),
            whole((length, R)),
            whole((1, R)),
        ],
        out_specs=[
            pl.BlockSpec((tile, heads * wide), lambda i: (i, 0)),
            whole((length, heads * (DN + DV))),
            whole((length, columns)),
            whole((1, R)),
        ],
        out_shape=[
            jax.ShapeDtypeStruct((length, heads * wide), BF),
            jax.ShapeDtypeStruct((length, heads * (DN + DV)), BF),
            jax.ShapeDtypeStruct((length, columns), F32),
            jax.ShapeDtypeStruct((1, R), F32),
        ],
        scratch_shapes=[
            pltpu.VMEM((heads, length, 256), F32),
            pltpu.VMEM((heads, length, DV), F32),
            pltpu.VMEM((heads, 256, length), BF),
        ],
        compiler_params=pltpu.CompilerParams(vmem_limit_bytes=LIMIT),
        cost_estimate=LIGHT,
        name="attend_back",
    )(query, key, value, result, result_grad, logsum, row_position, column_position, cosine, sine, w_up, latent_all, latent_gain)


def add_norm(token_blocks, blocks, w_even, w_odd, gain):
    count, width = token_blocks[0].shape
    many = len(blocks)
    chips = many // 2
    half = chips * count
    length = count * many
    depth = blocks[0].shape[1]

    def kernel(we_ref, wo_ref, g_ref, *refs):
        parts, tokens = refs[:many], refs[many : 2 * many]
        n_ref, r_ref, x_ref, a_ref = refs[2 * many :]
        for q in range(many):
            for p in range(chips):
                other = p ^ (q % chips)
                a_ref[p * count : (p + 1) * count, q * depth : (q + 1) * depth] = parts[q][
                    other * count : (other + 1) * count
                ]
        for h in range(2):

            @pl.when(pl.program_id(0) == h)
            def _():
                for k in range(chips):
                    x_ref[k * count : (k + 1) * count] = tokens[h * chips + k][...]

        middle = chips * depth
        total = dot(a_ref[:, :middle], we_ref[...]) + dot(a_ref[:, middle:], wo_ref[...])
        total = total + x_ref[...].astype(F32)
        inverse = lax.rsqrt(jnp.mean(total * total, axis=1, keepdims=True) + eps_norm)
        n_ref[...] = (total * inverse * g_ref[...]).astype(BF)

        @pl.when(pl.program_id(0) == 0)
        def _():
            r_ref[...] = total[:count]

    def source(q):
        return pl.BlockSpec((half, depth), lambda i: (i ^ (q // chips), 0))

    return pl.pallas_call(
        kernel,
        grid=(2,),
        in_specs=[whole(w_even.shape), whole(w_odd.shape), whole((1, width))]
        + [source(q) for q in range(many)]
        + [whole((count, width))] * many,
        out_specs=[pl.BlockSpec((half, width), lambda i: (i, 0)), whole((count, width))],
        out_shape=[
            jax.ShapeDtypeStruct((length, width), BF),
            jax.ShapeDtypeStruct((count, width), F32),
        ],
        scratch_shapes=[pltpu.VMEM((half, width), BF), pltpu.VMEM((half, many * depth), BF)],
        compiler_params=pltpu.CompilerParams(vmem_limit_bytes=LIMIT),
        cost_estimate=LIGHT,
        name="add_norm",
    )(w_even, w_odd, gain, *blocks, *token_blocks)


def expert(rows, cots, gate, up, down, piece):
    count, width = rows.shape
    units = gate.shape[2]
    tile = min(512, count)
    step = 256
    full = units // step
    rest = units % step
    spans = [(n * step, step) for n in range(full)] + ([(full * step, rest)] if rest else [])

    def kernel(x_ref, c_ref, gate_hbm, up_hbm, down_hbm, res_ref, in_ref, h_ref, gg_ref, ug_ref, wg, wu, wd, acc_r, acc_i, sems):
        first = pl.program_id(0) == 0

        def copies(n, start, size):
            span = pl.ds(start, size)
            return [
                pltpu.make_async_copy(gate_hbm.at[piece, :, span], wg.at[:, span], sems.at[0, n]),
                pltpu.make_async_copy(up_hbm.at[piece, :, span], wu.at[:, span], sems.at[1, n]),
                pltpu.make_async_copy(down_hbm.at[piece, span, :], wd.at[span, :], sems.at[2, n]),
            ]

        @pl.when(first)
        def _():
            for n, (start, size) in enumerate(spans):
                for copy in copies(n, start, size):
                    copy.start()

        acc_r[...] = jnp.zeros_like(acc_r)
        acc_i[...] = jnp.zeros_like(acc_i)

        def chunk(n, start, size):
            @pl.when(first)
            def _():
                for copy in copies(n, start, size):
                    copy.wait()

            span = pl.ds(start, size)
            x, c = x_ref[...], c_ref[...]
            w_gate, w_up, w_down = wg[:, span], wu[:, span], wd[span, :]
            g = dot(x, w_gate)
            u = dot(x, w_up)
            hidden_grad = dot_t(c, w_down)
            s = jax.nn.sigmoid(g)
            silu = g * s
            hidden = (silu * u).astype(BF)
            gate_grad = (hidden_grad * u * (s * (1.0 + g * (1.0 - s)))).astype(BF)
            up_grad = (hidden_grad * silu).astype(BF)
            h_ref[:, span] = hidden
            gg_ref[:, span] = gate_grad
            ug_ref[:, span] = up_grad
            acc_r[...] += dot(hidden, w_down)
            acc_i[...] += dot_t(gate_grad, w_gate) + dot_t(up_grad, w_up)

        if full:

            @pl.loop(0, full)
            def _(n):
                chunk(n, pl.multiple_of(n * step, step), step)

        if rest:
            chunk(full, full * step, rest)
        res_ref[...] = acc_r[...].astype(BF)
        in_ref[...] = acc_i[...].astype(BF)

    def block(w):
        return pl.BlockSpec((tile, w), lambda i: (i, 0))

    def array(w):
        return jax.ShapeDtypeStruct((count, w), BF)

    return pl.pallas_call(
        kernel,
        grid=(count // tile,),
        in_specs=[block(width), block(width), ANY, ANY, ANY],
        out_specs=[block(width), block(width), block(units), block(units), block(units)],
        out_shape=[array(width), array(width), array(units), array(units), array(units)],
        scratch_shapes=[
            pltpu.VMEM((width, units), BF),
            pltpu.VMEM((width, units), BF),
            pltpu.VMEM((units, width), BF),
            pltpu.VMEM((tile, width), F32),
            pltpu.VMEM((tile, width), F32),
            pltpu.SemaphoreType.DMA((3, len(spans))),
        ],
        compiler_params=pltpu.CompilerParams(vmem_limit_bytes=LIMIT),
        cost_estimate=LIGHT,
        name="expert",
    )(rows, cots, gate, up, down)


def shared(rows, cots, gate, up, down):
    count, width = rows.shape
    units = gate.shape[1]
    tile = 256

    def kernel(x_ref, c_ref, wg_ref, wu_ref, wd_ref, h_ref, gg_ref, ug_ref):
        g = dot(x_ref[...], wg_ref[...])
        u = dot(x_ref[...], wu_ref[...])
        hidden_grad = dot_t(c_ref[...], wd_ref[...])
        s = jax.nn.sigmoid(g)
        silu = g * s
        h_ref[...] = (silu * u).astype(BF)
        gg_ref[...] = (hidden_grad * u * (s * (1.0 + g * (1.0 - s)))).astype(BF)
        ug_ref[...] = (hidden_grad * silu).astype(BF)

    row = pl.BlockSpec((tile, width), lambda i: (i, 0))
    unit = pl.BlockSpec((tile, units), lambda i: (i, 0))
    return pl.pallas_call(
        kernel,
        grid=(count // tile,),
        in_specs=[row, row, whole(gate.shape), whole(up.shape), whole(down.shape)],
        out_specs=[unit] * 3,
        out_shape=[jax.ShapeDtypeStruct((count, units), BF)] * 3,
        compiler_params=pltpu.CompilerParams(vmem_limit_bytes=LIMIT),
        cost_estimate=LIGHT,
        name="shared",
    )(rows, cots, gate, up, down)


def expert_weights(rows, cots, hidden, gate_grad, up_grad, piece, pieces, earlier, dtype=F32):
    count, width = rows.shape
    units = hidden.shape[1]
    tile = 256

    def kernel(x_ref, c_ref, h_ref, gg_ref, ug_ref, *refs):
        g_ref, u_ref, d_ref = refs[-3:]
        g_ref[0] = t_dot(x_ref[...], gg_ref[...]).astype(dtype)
        u_ref[0] = t_dot(x_ref[...], ug_ref[...]).astype(dtype)
        d_ref[0] = t_dot(h_ref[...], c_ref[...]).astype(dtype)

    tall = pl.BlockSpec((1, tile, units), lambda i: (piece, i, 0))
    flat = pl.BlockSpec((1, units, tile), lambda i: (piece, 0, i))
    column = pl.BlockSpec((count, tile), lambda i: (0, i))
    kept = list(earlier or ())
    return pl.pallas_call(
        kernel,
        grid=(width // tile,),
        in_specs=[column, column] + [whole((count, units))] * 3 + [ANY] * len(kept),
        out_specs=[tall, tall, flat],
        out_shape=[
            jax.ShapeDtypeStruct((pieces, width, units), dtype),
            jax.ShapeDtypeStruct((pieces, width, units), dtype),
            jax.ShapeDtypeStruct((pieces, units, width), dtype),
        ],
        input_output_aliases={5 + n: n for n in range(len(kept))},
        compiler_params=pltpu.CompilerParams(vmem_limit_bytes=LIMIT),
        cost_estimate=LIGHT,
        name="expert_weights",
    )(rows, cots, hidden, gate_grad, up_grad, *kept)


def dispatch(select, rows, slot_weight, pieces):
    blocks, slots, count = select.shape
    width = rows.shape[1]
    others = slots // pieces // CAP

    def kernel(m_ref, x_ref, *refs):
        got = dot(m_ref[0], x_ref[...])
        if slot_weight is not None:
            got = got * refs[0][0]
        got = got.astype(BF)
        for i in range(pieces):
            for j in range(others):
                start = (i * others + j) * CAP
                refs[-pieces + i][j] = got[start : start + CAP]

    weights = [] if slot_weight is None else [slot_weight]
    out = pl.BlockSpec((others, CAP, width), lambda b: (0, b, 0))
    return pl.pallas_call(
        kernel,
        grid=(blocks,),
        in_specs=[
            pl.BlockSpec((1, slots, count), lambda b: (b, 0, 0)),
            pl.BlockSpec((count, width), lambda b: (b, 0)),
        ]
        + [pl.BlockSpec((1, slots, 1), lambda b: (b, 0, 0))] * len(weights),
        out_specs=[out] * pieces,
        out_shape=[jax.ShapeDtypeStruct((others, blocks * CAP, width), BF)] * pieces,
        compiler_params=pltpu.CompilerParams(vmem_limit_bytes=LIMIT),
        cost_estimate=LIGHT,
        name="dispatch",
    )(select, rows, *weights)


def down_weights(index, normed, down_even, down_odd, others, n_seq, gain_rows):
    length, _ = normed.shape
    half, columns = down_even.shape
    per = 128 // gain_rows

    def kernel(index_ref, n_ref, e_ref, d_ref, o_ref, part):
        part[...] = t_dot(n_ref[:half], e_ref[...]) + t_dot(n_ref[half:], d_ref[...])
        o_ref[0] = part[span(index_ref[1] % per, gain_rows)]

    return pl.pallas_call(
        kernel,
        grid_spec=pltpu.PrefetchScalarGridSpec(
            num_scalar_prefetch=1,
            grid=(others,),
            in_specs=[
                pl.BlockSpec(
                    (length, 128), lambda i, ref: (0, (i * n_seq + ref[1]) * gain_rows // 128)
                ),
                pl.BlockSpec((half, columns), lambda i, ref: (0, 0)),
                pl.BlockSpec((half, columns), lambda i, ref: (0, 0)),
            ],
            out_specs=pl.BlockSpec((1, gain_rows, columns), lambda i, ref: (i, 0, 0)),
            scratch_shapes=[pltpu.VMEM((128, columns), F32)],
        ),
        out_shape=jax.ShapeDtypeStruct((others, gain_rows, columns), F32),
        compiler_params=pltpu.CompilerParams(vmem_limit_bytes=LIMIT),
        cost_estimate=LIGHT,
        name="down_weights",
    )(index, normed, down_even, down_odd)


def combine(base, masks, returned, products, dtype):
    half = masks[0].shape[0] // 2
    slots, count = masks[0].shape[1:]
    pieces = len(returned)
    others, _, width = returned[0].shape
    many = len(masks)

    tile = 512

    def kernel(*refs):
        mask_refs, row_refs = refs[:many], refs[many : many + pieces]
        rest, out_ref = refs[many + pieces : -1], refs[-1]
        total = 0.0
        for n, (_, _, flipped) in enumerate(products):
            total = total + (dot_t if flipped else dot)(rest[2 * n][...], rest[2 * n + 1][...])
        for b in range(half):
            rows = jnp.concatenate(
                [
                    row_refs[i][j, b * CAP : (b + 1) * CAP]
                    for i in range(pieces)
                    for j in range(others)
                ],
                axis=0,
            )
            block = total[b * count : (b + 1) * count]
            for mask_ref in mask_refs:
                block = block + t_dot(mask_ref[b], rows)
            out_ref[b * count : (b + 1) * count] = block.astype(dtype)

    factors = []
    specs = []
    for left, right, flipped in products:
        factors += [left, right]
        specs.append(pl.BlockSpec((half * count, left.shape[1]), lambda t: (base, 0)))
        if flipped:
            specs.append(pl.BlockSpec((tile, right.shape[1]), lambda t: (t, 0)))
        else:
            specs.append(pl.BlockSpec((right.shape[0], tile), lambda t: (0, t)))
    return pl.pallas_call(
        kernel,
        grid=(width // tile,),
        in_specs=[pl.BlockSpec((half, slots, count), lambda t: (base, 0, 0))] * many
        + [pl.BlockSpec((others, half * CAP, tile), lambda t: (0, base, t))] * pieces
        + specs,
        out_specs=pl.BlockSpec((half * count, tile), lambda t: (0, t)),
        out_shape=jax.ShapeDtypeStruct((half * count, width), dtype),
        compiler_params=pltpu.CompilerParams(vmem_limit_bytes=LIMIT),
        cost_estimate=LIGHT,
        name="combine",
    )(*masks, *returned, *factors)


def swap(x, axis, mask):
    n = lax.axis_size(axis)
    return lax.ppermute(x, axis, [(i, i ^ mask) for i in range(n)])


def after(x, *earlier):
    return lax.optimization_barrier((x, *earlier))[0]


class Lane:
    def __init__(self, axis, depth):
        self.axis = axis
        self.depth = depth
        self.sent = []

    def send(self, x, mask):
        if len(self.sent) >= self.depth:
            x = after(x, self.sent[-self.depth])
        got = swap(x, self.axis, mask)
        self.sent.append(got)
        return got

    def chips(self, x):
        chips = lax.axis_size("seq") // 2
        return [x] + [self.send(x, 2 * k) for k in range(1, chips)]

    def group(self, x):
        return self.pair(self.chips(x))

    def pair(self, evens):
        even = stacked(evens)
        return even, swap(even, "seq", 1)

    def scatter(self, even, odd):
        return self.finish(self.begin(even, odd))

    def begin(self, even, odd):
        chips = lax.axis_size("seq") // 2
        rows = even.shape[0] // chips
        got = swap(odd.astype(BF), "seq", 1)
        blocks = [
            even[k * rows : (k + 1) * rows] + got[k * rows : (k + 1) * rows].astype(F32)
            for k in range(chips)
        ]
        return blocks[:1] + [block.astype(BF) for block in blocks[1:]]

    def finish(self, blocks, *gates):
        got = [self.send(blocks[k], 2 * k) for k in range(1, len(blocks))]
        total = blocks[0]
        for block in got:
            total = total + after(block, *gates).astype(F32)
        return total

    def corners(self, x, *gates):
        if lax.axis_size("exp") != 4:
            return [(j, 0, y) for j, y in enumerate(self.others(x))]
        middle = x.shape[0] // 2
        one, two = self.send(x, 1), self.send(x, 2)
        return [
            (0, 0, x),
            (1, 0, one),
            (2, 0, two),
            (3, 0, self.send(part(after(two, *gates), 0, middle), 1)),
            (3, middle, self.send(part(after(one, *gates), middle, middle), 2)),
        ]

    def others(self, x):
        return [x] + [self.send(x, j) for j in range(1, lax.axis_size("exp"))]

def siblings(blocks, *gates):
    got = {}
    for k in range(len(blocks) - 1, 1, -1):
        got[k] = swap(after(blocks[k], *got.values()), "seq", 1)
    gates += tuple(got.values())
    for k in range(min(2, len(blocks))):
        got[k] = swap(after(blocks[k], *gates), "seq", 1)
    return [got[k] for k in range(len(blocks))]


def stacked(blocks):
    rows, columns = blocks[0].shape
    everything = slice(None)
    (whole_array,) = arrange(
        jnp.zeros((1,), jnp.int32),
        blocks,
        [(rows * len(blocks), columns)],
        [
            (k, everything, 0, lambda ref, k=k: (slice(k * rows, (k + 1) * rows), everything))
            for k in range(len(blocks))
        ],
    )
    return whole_array


def part(x, start, rows):
    (piece,) = arrange(
        jnp.zeros((1,), jnp.int32),
        [x],
        [(rows, x.shape[1])],
        [(0, (slice(start, start + rows),), 0, lambda ref: (slice(0, rows),))],
    )
    return piece


def relative_order(count):
    chips = count // 2
    return [2 * k for k in range(chips)] + [2 * k + 1 for k in range(chips)]


def sum_exp(x, axis):
    return lax.psum_scatter(x.astype(BF), "exp", scatter_dimension=axis, tiled=True).astype(F32)


def shards(
    tokens,
    routes,
    route_weights,
    norm_gain,
    w_query,
    w_kv_down,
    latent_gain,
    w_kv_up,
    w_output,
    ffn_gain,
    shared_gate,
    shared_up,
    shared_down,
    expert_gate,
    expert_up,
    expert_down,
    out_grad,
):
    count, width = tokens.shape
    n_seq = lax.axis_size("seq")
    n_exp = lax.axis_size("exp")
    seq = lax.axis_index("seq")
    order = relative_order(n_seq)
    chips = n_seq // 2
    heads = H // n_seq
    length = count * n_seq
    half = length // 2
    pieces = expert_gate.shape[0]
    parts_per = pieces * n_seq * n_exp // EXPERTS
    factor = 1.0 / math.sqrt(DN + DR)
    gain_rows = norm_gain.shape[0]
    latent_rows_local = latent_gain.shape[0]
    along = Lane("seq", 3)
    across = Lane("exp", 3)
    free = Lane("seq", 3)

    index = jnp.stack([lax.axis_index("exp"), seq]).astype(jnp.int32)
    ratio = w_query.shape[0] // w_kv_up.shape[0]
    slim = w_kv_up.shape[1] // ratio
    columns = -(-w_kv_down.shape[1] // 128) * 128
    high = lax.reduce_precision(route_weights, 8, 7)
    middle = lax.reduce_precision(route_weights - high, 8, 7)
    low = route_weights - high - middle
    route_pack = jnp.concatenate([routes.astype(F32), high, middle, low], axis=1).astype(BF).T
    lines = route_pack.shape[0] // 4
    gains = jnp.concatenate([norm_gain, ffn_gain, latent_gain])
    packed = jnp.concatenate(
        [
            jnp.pad(w_kv_down, ((0, 0), (0, columns - R - DR))),
            jnp.pad(gains, (0, columns - gains.shape[0]))[None, :],
            jnp.pad(
                route_pack.reshape(4, lines, count).transpose(1, 0, 2).reshape(lines, 4 * count),
                ((0, 15 - lines), (0, columns - 4 * count)),
            ),
        ],
        axis=0,
    )
    packed_even = stacked(free.chips(packed))
    token_even = along.chips(tokens)
    first_all = lax.all_gather(
        jnp.concatenate(
            [
                w_query,
                jnp.concatenate(
                    [w_kv_up[:, g * slim : (g + 1) * slim] for g in range(ratio)], axis=0
                ),
            ],
            axis=1,
        ),
        "exp",
        axis=0,
        tiled=True,
    )
    packed_parts = across.others(packed_even)
    packed_even = stacked(packed_parts)
    packed_odd = swap(packed_even, "seq", 1)
    early = packed_parts[-1]
    gate_cols = lax.all_gather(after(shared_gate, early), "exp", axis=0, tiled=True)
    lift_cols = lax.all_gather(after(shared_up, early), "exp", axis=0, tiled=True)
    drop_rows = lax.all_gather(after(shared_down, early), "exp", axis=1, tiled=True)

    everything = slice(None)
    block_rows = width // n_exp
    plan = []
    deep = gain_rows + 16
    for h in range(2):
        for j in range(n_exp):
            for k in range(chips):

                def where(ref, h=h, j=j, k=k):
                    return (ref[0] ^ j) * n_seq + (ref[1] ^ (2 * k + h))

                plan.append(
                    (
                        h,
                        (
                            slice((j * chips + k) * deep, (j * chips + k) * deep + gain_rows),
                            slice(0, R + DR),
                        ),
                        0,
                        lambda ref, where=where: (span(where(ref), gain_rows), everything),
                    )
                )
                plan.append(
                    (
                        h,
                        (slice((j * chips + k) * deep + gain_rows, (j * chips + k + 1) * deep),),
                        1,
                        lambda ref, where=where: (where(ref),),
                    )
                )
    down_full, extra_all = arrange(
        index,
        [packed_even, packed_odd],
        [(width, R + DR), (n_exp * n_seq, 16, columns)],
        plan,
    )
    gain_first = extra_all[:, 0, :gain_rows].reshape(1, width).astype(F32)
    gain_second = extra_all[:, 0, gain_rows : 2 * gain_rows].reshape(1, width).astype(F32)
    latent_wide = (
        extra_all[:, 0, 2 * gain_rows : 2 * gain_rows + latent_rows_local]
        .reshape(1, R)
        .astype(F32)
    )
    route_all = jnp.concatenate(
        [
            x[: chips * deep].reshape(chips, deep, columns)[:, gain_rows + 1 :]
            for x in (packed_even, packed_odd)
        ],
        axis=0,
    )[:, :lines, : 4 * count]
    route_all = route_all.reshape(n_seq, lines, 4, count).transpose(0, 2, 1, 3)
    route_all = route_all.reshape(n_seq, 4 * lines, count).astype(F32)
    route_all = jnp.concatenate(
        [
            route_all[:, :TOP],
            route_all[:, TOP : 2 * TOP]
            + route_all[:, 2 * TOP : 3 * TOP]
            + route_all[:, 3 * TOP :],
        ],
        axis=1,
    )
    up_rows = w_kv_up.shape[0]
    query_width = w_query.shape[1]
    (up_cols,) = arrange(
        index,
        [first_all],
        [(R, w_kv_up.shape[1])],
        [
            (
                0,
                (
                    slice((j * ratio + g) * up_rows, (j * ratio + g + 1) * up_rows),
                    slice(query_width, query_width + slim),
                ),
                0,
                lambda ref, j=j, g=g: (
                    slice(j * up_rows, (j + 1) * up_rows),
                    slice(g * slim, (g + 1) * slim),
                ),
            )
            for j in range(n_exp)
            for g in range(ratio)
        ],
    )
    token_odd = {}
    for k in range(chips - 1, -1, -1):
        token_odd[k] = swap(after(token_even[k], *token_odd.values()), "seq", 1)
    token_odd = [token_odd[k] for k in range(chips)]
    token_blocks = token_even + token_odd
    output_even = free.chips(after(w_output, *token_odd, packed_odd))
    grad_even = along.chips(after(out_grad, *token_odd))

    column = jnp.stack(
        [
            ((other * n_seq + seq) * pieces + i) // parts_per
            for i in range(pieces)
            for other in range(n_exp)
        ]
    )
    kinds = n_exp * pieces
    named = route_all[:, None, :TOP, :].astype(jnp.int32) == column[None, :, None, None]
    matched = jnp.any(named, axis=2)
    match_weight = jnp.sum(jnp.where(named, route_all[:, None, TOP:, :], 0.0), axis=2)
    earlier = (jnp.arange(count)[:, None] < jnp.arange(count)[None, :]).astype(BF)
    rank = jnp.dot(matched.astype(BF), earlier, preferred_element_type=F32).astype(jnp.int32)
    chosen = (rank[:, :, None, :] == jnp.arange(CAP, dtype=jnp.int32)[None, None, :, None]) & (
        matched[:, :, None, :]
    )
    select = chosen.astype(BF).reshape(n_seq, kinds * CAP, count)
    weighted = jnp.where(chosen, match_weight[:, :, None, :], 0.0).reshape(
        n_seq, kinds * CAP, count
    )
    slot_weight = jnp.sum(weighted, axis=2, keepdims=True)
    weighted_high = weighted.astype(BF)
    weighted_low = (weighted - weighted_high.astype(F32)).astype(BF)

    positions = jnp.concatenate(
        [(seq ^ r) * count + jnp.arange(count, dtype=jnp.int32) for r in order]
    )
    row_position, column_position = positions[None, :], positions[:, None]
    cosine_table, sine_table = rope_tables(positions, DR)
    cosine_wide = jnp.concatenate([cosine_table, cosine_table], axis=1)
    sine_wide = jnp.concatenate([-sine_table, sine_table], axis=1)
    gain_first = after(gain_first, select, slot_weight, column_position)
    normed_one, latent_all, latent_raw, query_heads, key_heads, value_heads = project(
        token_blocks,
        gain_first,
        first_all,
        down_full,
        latent_wide,
        up_cols,
        cosine_wide,
        sine_wide,
        heads,
    )
    output_even = stacked([after(x, normed_one) for x in output_even])
    result, logsum = attend(
        query_heads, key_heads, value_heads, row_position, column_position, factor
    )

    output_parts = across.corners(output_even, result, *grad_even[1:])
    (output_even,) = arrange(
        index,
        [part[2] for part in output_parts],
        [(H * DV // 2, width)],
        [
            (
                n,
                everything,
                0,
                lambda ref, j=j, at=at, x=x: (
                    slice(at, at + x.shape[0]),
                    span(ref[0] ^ j, block_rows),
                ),
            )
            for n, (j, at, x) in enumerate(output_parts)
        ],
    )
    output_odd = swap(output_even, "seq", 1)

    grad_even, grad_odd = along.pair([after(x, result) for x in grad_even])

    def give(rows):
        return lax.all_to_all(rows, "exp", split_axis=0, concat_axis=0, tiled=True)

    grad_rows = stacked([grad_even, grad_odd])
    send_cots = dispatch(select, grad_rows, slot_weight, pieces)
    received_grad = [give(rows) for rows in send_cots]

    result_even = along.chips(result)
    gathered = (gate_cols, lift_cols, drop_rows)
    result_even = [after(x, received_grad[0], *gathered) for x in result_even]
    result_blocks = result_even + siblings(result_even)
    normed_two, residual = add_norm(
        token_blocks,
        result_blocks,
        output_even,
        output_odd,
        gain_second,
    )
    inverse_two = inverse_rms(residual)
    send_rows = dispatch(select, after(normed_two, *received_grad), None, pieces)
    received = [give(after(send_rows[0], *received_grad))]


    received += [give(after(x, received[0])) for x in send_rows[1:]]

    slot_rows = n_exp * n_seq * CAP
    pairs = []
    results_back, grads_back, kept = [], [], []
    for i in range(pieces):
        rows = received[i].reshape(slot_rows, width)
        cots = received_grad[i].reshape(slot_rows, width)
        expert_result, input_grad, *saved = expert(
            rows, cots, expert_gate, expert_up, expert_down, i
        )
        grads_back.append(give(input_grad.reshape(n_exp, n_seq * CAP, width)))
        results_back.append(expert_result.reshape(n_exp, n_seq * CAP, width))
        kept.append((rows, cots, *saved))
    shared_rows = after(normed_two, input_grad)
    shared_hidden, sgate_grad, sup_grad = shared(
        shared_rows, grad_rows, gate_cols, lift_cols, drop_rows
    )
    two_products = [(sgate_grad, gate_cols, True), (sup_grad, lift_cols, True)]
    expert_grads = expert_weights(
        after(kept[0][0], input_grad), *kept[0][1:], 0, pieces, None
    )
    gate_part, lift_part, drop_part = expert_weights(
        shared_rows, grad_rows, shared_hidden, sgate_grad, sup_grad, 0, 1, None, BF
    )
    token_wide = tokens.astype(F32)
    token_inverse = inverse_rms(token_wide)
    select = after(select, *expert_grads, gate_part, lift_part, drop_part, token_inverse)
    two_odd = combine(1, [select], grads_back, two_products, BF)
    two_even = combine(0, [select], grads_back, two_products, F32)
    two_blocks = along.begin(two_even, two_odd)
    back = []
    for i in range(pieces):
        back.append(give(after(results_back[i], *(two_blocks if i == 0 else expert_grads))))
        if i:
            expert_grads = expert_weights(
                after(kept[i][0], back[0]), *kept[i][1:], i, pieces, expert_grads
            )
    results_back = back
    expert_gate_grad, expert_up_grad, expert_down_grad = expert_grads
    (own_heads,) = arrange(
        index,
        [after(result_blocks[0], *two_blocks)] + result_blocks[1:],
        [(count, H * DV)],
        [
            (
                p,
                (slice(p * count, (p + 1) * count), everything),
                0,
                lambda ref, p=p: (everything, slice(p * heads * DV, (p + 1) * heads * DV)),
            )
            for p in range(n_seq)
        ],
    )
    gate_part, lift_part, drop_part = [
        after(x[0], *two_blocks) for x in (gate_part, lift_part, drop_part)
    ]
    gate_out, lift_out, drop_out = sum_exp(gate_part, 0), sum_exp(lift_part, 0), sum_exp(drop_part, 1)
    two_grad = along.finish(
        two_blocks, *expert_grads, own_heads
    )
    residual_norm_grad, second_terms = norm_back(
        two_grad, residual, inverse_two, gain_second
    )
    residual_grad = out_grad.astype(F32) + residual_norm_grad
    residual_half = residual_grad.astype(BF)
    even_heads = dot_t(residual_half, output_even).astype(BF)
    odd_heads = dot_t(residual_half, output_odd).astype(BF)
    wide = heads * DV
    pairs = [
        jnp.stack([even_heads[:, k * wide : (k + 1) * wide], odd_heads[:, k * wide : (k + 1) * wide]])
        for k in range(chips)
    ]
    stacks = pairs
    pairs = [pairs[0]] + [along.send(pairs[k], 2 * k) for k in range(1, chips)]
    other_half = swap(jnp.stack([pair[1] for pair in pairs]), "seq", 1)
    attention_grad = jnp.concatenate(
        [jnp.stack([pair[0] for pair in pairs]), other_half], axis=0
    ).reshape(length, wide)
    mine = lax.axis_index("exp")
    out_products = [(shared_hidden, drop_rows, False)]
    out_masks = [weighted_high, weighted_low]
    out_masks = [after(mask, *stacks, *pairs[1:]) for mask in out_masks]
    out_odd = combine(1, out_masks, results_back, out_products, BF)
    out_even = combine(0, out_masks, results_back, out_products, F32)
    out_blocks = along.begin(out_even, out_odd)
    output_got = [along.send(out_blocks[k], 2 * k) for k in range(chips - 1, 0, -1)]

    query_in_grad, kv_grad, latent_part, latent_sum = attend_back(
        query_heads,
        key_heads,
        value_heads,
        result,
        after(attention_grad, *out_blocks),
        logsum,
        row_position,
        column_position,
        cosine_wide,
        -sine_wide,
        up_cols,
        latent_all,
        latent_wide,
        factor,
        columns,
    )
    late = Lane("exp", 2)
    attention_parts = late.others(after(own_heads, query_in_grad))
    one_odd, odd_sum = query_back(1, query_in_grad, first_all, normed_one, gain_first, BF)
    one_even, even_sum = query_back(0, query_in_grad, first_all, normed_one, gain_first, F32)
    sums = jnp.concatenate(
        [
            (odd_sum + even_sum).reshape(n_exp, n_seq, gain_rows),
            jnp.sum(second_terms, axis=0).reshape(n_exp, n_seq, gain_rows),
            after(latent_sum, *output_got[:2], *attention_parts[1:]).reshape(n_exp, n_seq, latent_rows_local),
        ],
        axis=2,
    )
    many = sums.shape[2]
    turn = (seq ^ jnp.array(order))[:, None] == jnp.arange(n_seq)[None, :]
    sums = jnp.einsum("ps,esw->pew", turn.astype(F32), sums, precision=lax.Precision.HIGHEST)
    sums = jnp.pad(
        sums.reshape(n_seq, 1, n_exp * many), ((0, 0), (0, 15), (0, columns - n_exp * many))
    )
    latent_part = jnp.concatenate([latent_part.reshape(n_seq, count, columns), sums], axis=1)
    latent_part = latent_part.reshape(n_seq * (count + 16), columns)
    latent_grad = along.scatter(
        latent_part[: chips * (count + 16)], latent_part[chips * (count + 16) :]
    )
    one_blocks = along.begin(one_even, one_odd)
    one_got = [along.send(one_blocks[k], 2 * k) for k in range(chips - 1, 0, -1)]
    column_blocks = [
        lax.dynamic_slice_in_dim(residual_half, (mine ^ j) * block_rows, block_rows, 1)
        for j in range(n_exp)
    ]
    column_blocks = [column_blocks[0]] + [
        swap(after(column_blocks[j], one_got[-1]), "exp", j) for j in range(1, n_exp)
    ]
    output_part = t_dot(
        jnp.concatenate([after(x, *one_blocks) for x in attention_parts], axis=0),
        jnp.concatenate([after(x, *one_blocks) for x in column_blocks], axis=0),
    )
    output_blocks = along.begin(output_part[: H * DV // 2], output_part[H * DV // 2 :])
    up_part = t_dot(after(latent_all, one_odd), kv_grad).astype(BF)
    query_part = t_dot(after(normed_one, one_odd), query_in_grad).astype(BF)
    up_out = sum_exp(up_part, 0)
    query_out = sum_exp(query_part, 0)
    sums = latent_grad[count, : n_exp * many].reshape(n_exp, 1, many)
    latent_grad = latent_grad[:count]
    latent_raw_grad, _ = norm_back(
        latent_grad[:, :R], latent_raw[:count], inverse_rms(latent_raw[:count]), latent_wide
    )
    down_rows = jnp.concatenate(
        [
            latent_raw_grad,
            rotate(latent_grad[:, R : R + DR], cosine_table[:count], -sine_table[:count]),
            jnp.zeros((count, columns - R - DR), F32),
        ],
        axis=1,
    ).astype(BF)
    down_even, down_odd = free.pair(
        [after(x, *one_got, *output_blocks) for x in free.chips(down_rows)]
    )
    wide_got = [
        swap(after(output_blocks[k], down_even), "seq", 2 * k) for k in range(chips - 1, 0, -1)
    ]
    down_part = down_weights(index, normed_one, down_even, down_odd, n_exp, n_seq, gain_rows)
    down_part = jnp.concatenate(
        [
            down_part,
            jnp.pad(sums, ((0, 0), (0, 15), (0, columns - many))),
        ],
        axis=1,
    )
    down_sum = lax.dynamic_index_in_dim(down_part, mine, 0, keepdims=False)
    for j in range(1, n_exp):
        piece = lax.dynamic_index_in_dim(down_part, mine ^ j, 0, keepdims=False).astype(BF)
        down_sum = down_sum + swap(piece, "exp", j).astype(F32)
    down_out = down_sum[:gain_rows, : R + DR]
    small = down_sum[gain_rows, :many]
    first_out = small[:gain_rows] + jnp.sum(
        w_kv_down.astype(F32) * down_out, axis=1
    ) / norm_gain.astype(F32)

    output = residual + out_blocks[0]
    for block in output_got:
        output = output + after(block, *one_blocks).astype(F32)
    output = output.astype(BF)
    output_out = output_blocks[0]
    for block in wide_got:
        output_out = output_out + block.astype(F32)
    one_grad = one_blocks[0]
    for block in one_got:
        block = after(block, up_part, query_part, gate_out, lift_out, drop_out)
        one_grad = one_grad + block.astype(F32)
    down_back = dot_t(down_rows[:, : R + DR], down_full)
    token_norm_grad, _ = norm_back(
        one_grad + down_back, token_wide, token_inverse, gain_first
    )
    tokens_grad = (residual_grad + token_norm_grad).astype(BF)
    return (
        output,
        tokens_grad,
        first_out,
        query_out,
        down_out,
        small[2 * gain_rows : many],
        up_out,
        output_out,
        small[gain_rows : 2 * gain_rows],
        gate_out,
        lift_out,
        drop_out,
        expert_gate_grad,
        expert_up_grad,
        expert_down_grad,
    )


def solution(mesh):
    rows = P(("exp", "seq"), None)
    line = P(("exp", "seq"))
    grid = P("exp", "seq")
    turned = P("seq", "exp")
    part = P(("exp", "seq"), None, None)
    return jax.shard_map(
        shards,
        mesh=mesh,
        in_specs=(
            rows,
            rows,
            rows,
            line,
            grid,
            rows,
            line,
            grid,
            turned,
            line,
            grid,
            grid,
            turned,
            part,
            part,
            part,
            rows,
        ),
        out_specs=(
            rows,
            rows,
            line,
            grid,
            rows,
            line,
            grid,
            turned,
            line,
            grid,
            grid,
            turned,
            part,
            part,
            part,
        ),
        check_vma=False,
    )
```

```python
import math

import jax
import jax.numpy as jnp
from jax import lax
from jax.experimental import pallas as pl
from jax.experimental.pallas import tpu as pltpu
from jax.sharding import PartitionSpec as P

H = 16
DN = 128
DR = 64
DV = 128
R = 512
EXPERTS = 64
TOP = 6
CAP = 16


eps_norm = 1e-06
rope_base = 50000.0
BF = jnp.bfloat16
F32 = jnp.float32


def dot(a, b):
    return jnp.dot(a, b, preferred_element_type=F32)


def dot_t(a, b):
    return lax.dot_general(a, b, (((1,), (1,)), ((), ())), preferred_element_type=F32)


def t_dot(a, b):
    return lax.dot_general(a, b, (((0,), (0,)), ((), ())), preferred_element_type=F32)


def rope_tables(positions, width):
    middle = width // 2
    frequency = rope_base ** (-(jnp.arange(middle, dtype=F32) * 2.0 / width))
    angles = positions.astype(F32)[:, None] * frequency[None, :]
    return (jnp.cos(angles), jnp.sin(angles))


def rotate(values, cosine_table, sine_table):
    middle = values.shape[-1] // 2
    leading = values[..., :middle]
    trailing = values[..., middle:]
    return jnp.concatenate(
        [
            leading * cosine_table - trailing * sine_table,
            trailing * cosine_table + leading * sine_table,
        ],
        axis=-1,
    )


def silu_slope(gate_values):
    sigmoid = jax.nn.sigmoid(gate_values)
    return sigmoid * (1.0 + gate_values * (1.0 - sigmoid))


def norm_back(dy, v, inverse, gain):
    hat = v * inverse
    scaled = dy * gain
    dv = inverse * (scaled - hat * jnp.mean(scaled * hat, axis=-1, keepdims=True))
    return dv, dy * hat


def inverse_rms(v):
    return lax.rsqrt(jnp.mean(v * v, axis=-1, keepdims=True) + eps_norm)


LIMIT = 56 * 1024 * 1024
LIGHT = pl.CostEstimate(flops=0, transcendentals=0, bytes_accessed=0)
ANY = pl.BlockSpec(memory_space=pl.ANY)
SCALARS = pl.BlockSpec(memory_space=pltpu.SMEM)


def whole(shape):
    return pl.BlockSpec(shape, lambda *grid: (0,) * len(shape))


def arrange(index, blocks, outs, plan):
    def kernel(index_ref, *refs):
        sources = refs[: len(blocks)]
        targets = refs[len(blocks) :]
        for block, source, out, target in plan:
            targets[out][target(index_ref)] = sources[block][source]

    return pl.pallas_call(
        kernel,
        out_shape=[jax.ShapeDtypeStruct(s, BF) for s in outs],
        in_specs=[SCALARS] + [pl.BlockSpec(memory_space=pltpu.VMEM)] * len(blocks),
        out_specs=[pl.BlockSpec(memory_space=pltpu.VMEM)] * len(outs),
        compiler_params=pltpu.CompilerParams(vmem_limit_bytes=LIMIT),
        cost_estimate=LIGHT,
        name="arrange",
    )(index, *blocks)


def span(start, size):
    return pl.ds(pl.multiple_of(start * size, size), size)


def turned(v, cosine, sine):
    middle = v.shape[1] // 2
    return v * cosine + jnp.concatenate([v[:, middle:], v[:, :middle]], axis=1) * sine


def project(token_blocks, gain, w_first, w_down, latent_gain, w_up, cosine, sine, heads):
    count, width = token_blocks[0].shape
    chips = len(token_blocks) // 2
    half = chips * count
    wide = DN + DR
    columns = heads * wide

    def kernel(g_ref, wd_ref, lg_ref, wu_ref, c_ref, s_ref, *refs):
        tokens, w_ref = refs[: 2 * chips], refs[2 * chips]
        n_ref, l_ref, r_ref, q_ref, k_ref, v_ref, x_ref = refs[2 * chips + 1 :]
        for h in range(2):

            @pl.when(pl.program_id(0) == h)
            def _():
                for k in range(chips):
                    x_ref[k * count : (k + 1) * count] = tokens[h * chips + k][...]

        x = x_ref[...].astype(F32)
        inverse = lax.rsqrt(jnp.mean(x * x, axis=1, keepdims=True) + eps_norm)
        n_ref[...] = (x * inverse * g_ref[...]).astype(BF)
        down = dot(n_ref[...], wd_ref[...])
        raw = down[:, :R]
        r_ref[...] = raw
        inverse = lax.rsqrt(jnp.mean(raw * raw, axis=1, keepdims=True) + eps_norm)
        l_ref[...] = (raw * inverse * lg_ref[...]).astype(BF)
        query = dot(n_ref[...], w_ref[:, :columns])
        up = dot(l_ref[...], wu_ref[...]).astype(BF)
        cosine, sine = c_ref[...], s_ref[...]
        zeros = jnp.zeros((half, 256 - wide), BF)
        rope = jnp.concatenate([turned(down[:, R : R + DR], cosine, sine).astype(BF), zeros], axis=1)
        for n in range(heads):
            own = query[:, n * wide : (n + 1) * wide]
            q_ref[n, :, :DN] = own[:, :DN].astype(BF)
            q_ref[n, :, DN:] = jnp.concatenate(
                [turned(own[:, DN:], cosine, sine).astype(BF), zeros], axis=1
            )
            k_ref[n, :, :DN] = up[:, n * (DN + DV) : n * (DN + DV) + DN]
            k_ref[n, :, DN:] = rope
            v_ref[n] = up[:, n * (DN + DV) + DN : (n + 1) * (DN + DV)]

    def rows(w):
        return pl.BlockSpec((half, w), lambda i: (i, 0))

    def head_rows(w):
        return pl.BlockSpec((heads, half, w), lambda i: (0, i, 0))

    length = 2 * half
    return pl.pallas_call(
        kernel,
        grid=(2,),
        in_specs=[
            whole((1, width)),
            whole(w_down.shape),
            whole((1, R)),
            whole(w_up.shape),
            rows(DR),
            rows(DR),
        ]
        + [whole((count, width))] * (2 * chips)
        + [whole(w_first.shape)],
        out_specs=[rows(width), rows(R), rows(R), head_rows(256), head_rows(256), head_rows(DV)],
        out_shape=[
            jax.ShapeDtypeStruct((length, width), BF),
            jax.ShapeDtypeStruct((length, R), BF),
            jax.ShapeDtypeStruct((length, R), F32),
            jax.ShapeDtypeStruct((heads, length, 256), BF),
            jax.ShapeDtypeStruct((heads, length, 256), BF),
            jax.ShapeDtypeStruct((heads, length, DV), BF),
        ],
        scratch_shapes=[pltpu.VMEM((half, width), BF)],
        compiler_params=pltpu.CompilerParams(vmem_limit_bytes=LIMIT),
        cost_estimate=LIGHT,
        name="project",
    )(gain, w_down, latent_gain, w_up, cosine, sine, *token_blocks, w_first)


def query_back(base, query_grad, w_first, normed, gain, dtype):
    length, columns = query_grad.shape
    half = length // 2
    width = normed.shape[1]
    tile = 512

    def kernel(q_ref, n_ref, g_ref, w_ref, o_ref, t_ref):
        part = dot_t(q_ref[...], w_ref[:, :columns])
        o_ref[...] = part.astype(dtype)
        product = part * n_ref[...].astype(F32)
        t_ref[...] = jnp.sum(product, axis=0, keepdims=True) / g_ref[...]

    return pl.pallas_call(
        kernel,
        grid=(width // tile,),
        in_specs=[
            pl.BlockSpec((half, columns), lambda i: (base, 0)),
            pl.BlockSpec((half, tile), lambda i: (base, i)),
            pl.BlockSpec((1, tile), lambda i: (0, i)),
            pl.BlockSpec((tile, w_first.shape[1]), lambda i: (i, 0)),
        ],
        out_specs=[
            pl.BlockSpec((half, tile), lambda i: (0, i)),
            pl.BlockSpec((1, tile), lambda i: (0, i)),
        ],
        out_shape=[
            jax.ShapeDtypeStruct((half, width), dtype),
            jax.ShapeDtypeStruct((1, width), F32),
        ],
        compiler_params=pltpu.CompilerParams(vmem_limit_bytes=LIMIT),
        cost_estimate=LIGHT,
        name="query_back",
    )(query_grad, normed, gain, w_first)


def attend(query, key, value, row_position, column_position, factor):
    heads, length, _ = query.shape
    tile = 256

    def kernel(q_ref, k_ref, v_ref, row_ref, column_ref, o_ref, s_ref):
        allowed = column_ref[...] <= row_ref[...]
        for n in range(heads):
            scores = dot_t(k_ref[n], q_ref[n]) * factor
            exponent = jnp.where(allowed, jnp.exp(jnp.where(allowed, scores, -1e30)), 0.0)
            total = jnp.sum(exponent, axis=0, keepdims=True)
            probs = (exponent / total).astype(BF)
            o_ref[:, n * DV : (n + 1) * DV] = t_dot(v_ref[n], probs).T.astype(BF)
            s_ref[n : n + 1, :] = jnp.log(total)

    return pl.pallas_call(
        kernel,
        grid=(length // tile,),
        in_specs=[
            pl.BlockSpec((heads, tile, 256), lambda i: (0, i, 0)),
            whole(key.shape),
            whole(value.shape),
            pl.BlockSpec((1, tile), lambda i: (0, i)),
            whole((length, 1)),
        ],
        out_specs=[
            pl.BlockSpec((tile, heads * DV), lambda i: (i, 0)),
            pl.BlockSpec((heads, tile), lambda i: (0, i)),
        ],
        out_shape=[
            jax.ShapeDtypeStruct((length, heads * DV), BF),
            jax.ShapeDtypeStruct((heads, length), F32),
        ],
        compiler_params=pltpu.CompilerParams(vmem_limit_bytes=LIMIT),
        cost_estimate=LIGHT,
        name="attend",
    )(query, key, value, row_position, column_position)


def attend_back(query, key, value, result, result_grad, logsum, row_position, column_position, cosine, sine, w_up, latent_all, latent_gain, factor, columns):
    heads, length, _ = query.shape
    tile = 256
    steps = length // tile
    wide = DN + DR

    def kernel(q_ref, k_ref, v_ref, o_ref, do_ref, ls_ref, row_ref, column_ref, c_ref, s_ref, wu_ref, l_ref, lg_ref, dq_ref, kv_ref, lp_ref, t_ref, dk_acc, dv_acc, kt):
        step = pl.program_id(0)

        @pl.when(step == 0)
        def _():
            dk_acc[...] = jnp.zeros_like(dk_acc)
            dv_acc[...] = jnp.zeros_like(dv_acc)
            for n in range(heads):
                kt[n] = k_ref[n].T

        allowed = column_ref[...] <= row_ref[...]
        cosine, sine = c_ref[...], s_ref[...]
        parts = []
        for n in range(heads):
            q = q_ref[n]
            grad = do_ref[:, n * DV : (n + 1) * DV]
            scores = jnp.where(allowed, dot_t(k_ref[n], q) * factor, -1e30)
            probs = jnp.exp(scores - ls_ref[n : n + 1, :])
            dv_acc[n] += dot(probs.astype(BF), grad)
            product = grad.astype(F32) * o_ref[:, n * DV : (n + 1) * DV].astype(F32)
            row_dot = jnp.sum(product.T, axis=0, keepdims=True)
            probs_grad = dot_t(v_ref[n], grad)
            score_grad = (probs * (probs_grad - row_dot) * factor).astype(BF)
            dk_acc[n] += dot(score_grad, q)
            query_grad = dot(kt[n], score_grad).T.astype(BF)
            parts.append(query_grad[:, :DN])
            parts.append(turned(query_grad[:, DN:wide].astype(F32), cosine, sine).astype(BF))
        dq_ref[...] = jnp.concatenate(parts, axis=1)

        @pl.when(step == steps - 1)
        def _():
            rope = jnp.zeros((length, DR), F32)
            for n in range(heads):
                key_grad = dk_acc[n].astype(BF)
                value_grad = dv_acc[n].astype(BF)
                base = n * (DN + DV)
                kv_ref[:, base : base + DN] = key_grad[:, :DN]
                kv_ref[:, base + DN : base + DN + DV] = value_grad
                rope = rope + key_grad[:, DN:wide].astype(F32)
            latent = dot_t(kv_ref[...], wu_ref[...])
            lp_ref[:, :R] = latent
            lp_ref[:, R : R + DR] = rope
            lp_ref[:, R + DR :] = jnp.zeros((length, columns - R - DR), F32)
            t_ref[...] = jnp.sum(
                latent * l_ref[...].astype(F32), axis=0, keepdims=True
            ) / lg_ref[...]

    return pl.pallas_call(
        kernel,
        grid=(steps,),
        in_specs=[
            pl.BlockSpec((heads, tile, 256), lambda i: (0, i, 0)),
            whole(key.shape),
            whole(value.shape),
            pl.BlockSpec((tile, heads * DV), lambda i: (i, 0)),
            pl.BlockSpec((tile, heads * DV), lambda i: (i, 0)),
            pl.BlockSpec((heads, tile), lambda i: (0, i)),
            pl.BlockSpec((1, tile), lambda i: (0, i)),
            whole((length, 1)),
            pl.BlockSpec((tile, DR), lambda i: (i, 0)),
            pl.BlockSpec((tile, DR), lambda i: (i, 0)),
            whole(w_up.shape),
            whole((length, R)),
            whole((1, R)),
        ],
        out_specs=[
            pl.BlockSpec((tile, heads * wide), lambda i: (i, 0)),
            whole((length, heads * (DN + DV))),
            whole((length, columns)),
            whole((1, R)),
        ],
        out_shape=[
            jax.ShapeDtypeStruct((length, heads * wide), BF),
            jax.ShapeDtypeStruct((length, heads * (DN + DV)), BF),
            jax.ShapeDtypeStruct((length, columns), F32),
            jax.ShapeDtypeStruct((1, R), F32),
        ],
        scratch_shapes=[
            pltpu.VMEM((heads, length, 256), F32),
            pltpu.VMEM((heads, length, DV), F32),
            pltpu.VMEM((heads, 256, length), BF),
        ],
        compiler_params=pltpu.CompilerParams(vmem_limit_bytes=LIMIT),
        cost_estimate=LIGHT,
        name="attend_back",
    )(query, key, value, result, result_grad, logsum, row_position, column_position, cosine, sine, w_up, latent_all, latent_gain)


def add_norm(token_blocks, blocks, w_even, w_odd, gain):
    count, width = token_blocks[0].shape
    many = len(blocks)
    chips = many // 2
    half = chips * count
    length = count * many
    depth = blocks[0].shape[1]

    def kernel(we_ref, wo_ref, g_ref, *refs):
        parts, tokens = refs[:many], refs[many : 2 * many]
        n_ref, r_ref, x_ref, a_ref = refs[2 * many :]
        for q in range(many):
            for p in range(chips):
                other = p ^ (q % chips)
                a_ref[p * count : (p + 1) * count, q * depth : (q + 1) * depth] = parts[q][
                    other * count : (other + 1) * count
                ]
        for h in range(2):

            @pl.when(pl.program_id(0) == h)
            def _():
                for k in range(chips):
                    x_ref[k * count : (k + 1) * count] = tokens[h * chips + k][...]

        middle = chips * depth
        total = dot(a_ref[:, :middle], we_ref[...]) + dot(a_ref[:, middle:], wo_ref[...])
        total = total + x_ref[...].astype(F32)
        inverse = lax.rsqrt(jnp.mean(total * total, axis=1, keepdims=True) + eps_norm)
        n_ref[...] = (total * inverse * g_ref[...]).astype(BF)

        @pl.when(pl.program_id(0) == 0)
        def _():
            r_ref[...] = total[:count]

    def source(q):
        return pl.BlockSpec((half, depth), lambda i: (i ^ (q // chips), 0))

    return pl.pallas_call(
        kernel,
        grid=(2,),
        in_specs=[whole(w_even.shape), whole(w_odd.shape), whole((1, width))]
        + [source(q) for q in range(many)]
        + [whole((count, width))] * many,
        out_specs=[pl.BlockSpec((half, width), lambda i: (i, 0)), whole((count, width))],
        out_shape=[
            jax.ShapeDtypeStruct((length, width), BF),
            jax.ShapeDtypeStruct((count, width), F32),
        ],
        scratch_shapes=[pltpu.VMEM((half, width), BF), pltpu.VMEM((half, many * depth), BF)],
        compiler_params=pltpu.CompilerParams(vmem_limit_bytes=LIMIT),
        cost_estimate=LIGHT,
        name="add_norm",
    )(w_even, w_odd, gain, *blocks, *token_blocks)


def expert(rows, cots, gate, up, down, piece):
    count, width = rows.shape
    units = gate.shape[2]
    tile = min(512, count)
    step = 256
    full = units // step
    rest = units % step
    spans = [(n * step, step) for n in range(full)] + ([(full * step, rest)] if rest else [])

    def kernel(x_ref, c_ref, gate_hbm, up_hbm, down_hbm, res_ref, in_ref, h_ref, gg_ref, ug_ref, wg, wu, wd, acc_r, acc_i, sems):
        first = pl.program_id(0) == 0

        def copies(n, start, size):
            span = pl.ds(start, size)
            return [
                pltpu.make_async_copy(gate_hbm.at[piece, :, span], wg.at[:, span], sems.at[0, n]),
                pltpu.make_async_copy(up_hbm.at[piece, :, span], wu.at[:, span], sems.at[1, n]),
                pltpu.make_async_copy(down_hbm.at[piece, span, :], wd.at[span, :], sems.at[2, n]),
            ]

        @pl.when(first)
        def _():
            for n, (start, size) in enumerate(spans):
                for copy in copies(n, start, size):
                    copy.start()

        acc_r[...] = jnp.zeros_like(acc_r)
        acc_i[...] = jnp.zeros_like(acc_i)

        def chunk(n, start, size):
            @pl.when(first)
            def _():
                for copy in copies(n, start, size):
                    copy.wait()

            span = pl.ds(start, size)
            x, c = x_ref[...], c_ref[...]
            w_gate, w_up, w_down = wg[:, span], wu[:, span], wd[span, :]
            g = dot(x, w_gate)
            u = dot(x, w_up)
            hidden_grad = dot_t(c, w_down)
            s = jax.nn.sigmoid(g)
            silu = g * s
            hidden = (silu * u).astype(BF)
            gate_grad = (hidden_grad * u * (s * (1.0 + g * (1.0 - s)))).astype(BF)
            up_grad = (hidden_grad * silu).astype(BF)
            h_ref[:, span] = hidden
            gg_ref[:, span] = gate_grad
            ug_ref[:, span] = up_grad
            acc_r[...] += dot(hidden, w_down)
            acc_i[...] += dot_t(gate_grad, w_gate) + dot_t(up_grad, w_up)

        if full:

            @pl.loop(0, full)
            def _(n):
                chunk(n, pl.multiple_of(n * step, step), step)

        if rest:
            chunk(full, full * step, rest)
        res_ref[...] = acc_r[...].astype(BF)
        in_ref[...] = acc_i[...].astype(BF)

    def block(w):
        return pl.BlockSpec((tile, w), lambda i: (i, 0))

    def array(w):
        return jax.ShapeDtypeStruct((count, w), BF)

    return pl.pallas_call(
        kernel,
        grid=(count // tile,),
        in_specs=[block(width), block(width), ANY, ANY, ANY],
        out_specs=[block(width), block(width), block(units), block(units), block(units)],
        out_shape=[array(width), array(width), array(units), array(units), array(units)],
        scratch_shapes=[
            pltpu.VMEM((width, units), BF),
            pltpu.VMEM((width, units), BF),
            pltpu.VMEM((units, width), BF),
            pltpu.VMEM((tile, width), F32),
            pltpu.VMEM((tile, width), F32),
            pltpu.SemaphoreType.DMA((3, len(spans))),
        ],
        compiler_params=pltpu.CompilerParams(vmem_limit_bytes=LIMIT),
        cost_estimate=LIGHT,
        name="expert",
    )(rows, cots, gate, up, down)


def shared(rows, cots, gate, up, down):
    count, width = rows.shape
    units = gate.shape[1]
    tile = 256

    def kernel(x_ref, c_ref, wg_ref, wu_ref, wd_ref, h_ref, gg_ref, ug_ref):
        g = dot(x_ref[...], wg_ref[...])
        u = dot(x_ref[...], wu_ref[...])
        hidden_grad = dot_t(c_ref[...], wd_ref[...])
        s = jax.nn.sigmoid(g)
        silu = g * s
        h_ref[...] = (silu * u).astype(BF)
        gg_ref[...] = (hidden_grad * u * (s * (1.0 + g * (1.0 - s)))).astype(BF)
        ug_ref[...] = (hidden_grad * silu).astype(BF)

    row = pl.BlockSpec((tile, width), lambda i: (i, 0))
    unit = pl.BlockSpec((tile, units), lambda i: (i, 0))
    return pl.pallas_call(
        kernel,
        grid=(count // tile,),
        in_specs=[row, row, whole(gate.shape), whole(up.shape), whole(down.shape)],
        out_specs=[unit] * 3,
        out_shape=[jax.ShapeDtypeStruct((count, units), BF)] * 3,
        compiler_params=pltpu.CompilerParams(vmem_limit_bytes=LIMIT),
        cost_estimate=LIGHT,
        name="shared",
    )(rows, cots, gate, up, down)


def expert_weights(rows, cots, hidden, gate_grad, up_grad, piece, pieces, earlier, dtype=F32):
    count, width = rows.shape
    units = hidden.shape[1]
    tile = 256

    def kernel(x_ref, c_ref, h_ref, gg_ref, ug_ref, *refs):
        g_ref, u_ref, d_ref = refs[-3:]
        g_ref[0] = t_dot(x_ref[...], gg_ref[...]).astype(dtype)
        u_ref[0] = t_dot(x_ref[...], ug_ref[...]).astype(dtype)
        d_ref[0] = t_dot(h_ref[...], c_ref[...]).astype(dtype)

    tall = pl.BlockSpec((1, tile, units), lambda i: (piece, i, 0))
    flat = pl.BlockSpec((1, units, tile), lambda i: (piece, 0, i))
    column = pl.BlockSpec((count, tile), lambda i: (0, i))
    kept = list(earlier or ())
    return pl.pallas_call(
        kernel,
        grid=(width // tile,),
        in_specs=[column, column] + [whole((count, units))] * 3 + [ANY] * len(kept),
        out_specs=[tall, tall, flat],
        out_shape=[
            jax.ShapeDtypeStruct((pieces, width, units), dtype),
            jax.ShapeDtypeStruct((pieces, width, units), dtype),
            jax.ShapeDtypeStruct((pieces, units, width), dtype),
        ],
        input_output_aliases={5 + n: n for n in range(len(kept))},
        compiler_params=pltpu.CompilerParams(vmem_limit_bytes=LIMIT),
        cost_estimate=LIGHT,
        name="expert_weights",
    )(rows, cots, hidden, gate_grad, up_grad, *kept)


def dispatch(select, rows, slot_weight, pieces):
    blocks, slots, count = select.shape
    width = rows.shape[1]
    others = slots // pieces // CAP

    def kernel(m_ref, x_ref, *refs):
        got = dot(m_ref[0], x_ref[...])
        if slot_weight is not None:
            got = got * refs[0][0]
        got = got.astype(BF)
        for i in range(pieces):
            for j in range(others):
                start = (i * others + j) * CAP
                refs[-pieces + i][j] = got[start : start + CAP]

    weights = [] if slot_weight is None else [slot_weight]
    out = pl.BlockSpec((others, CAP, width), lambda b: (0, b, 0))
    return pl.pallas_call(
        kernel,
        grid=(blocks,),
        in_specs=[
            pl.BlockSpec((1, slots, count), lambda b: (b, 0, 0)),
            pl.BlockSpec((count, width), lambda b: (b, 0)),
        ]
        + [pl.BlockSpec((1, slots, 1), lambda b: (b, 0, 0))] * len(weights),
        out_specs=[out] * pieces,
        out_shape=[jax.ShapeDtypeStruct((others, blocks * CAP, width), BF)] * pieces,
        compiler_params=pltpu.CompilerParams(vmem_limit_bytes=LIMIT),
        cost_estimate=LIGHT,
        name="dispatch",
    )(select, rows, *weights)


def down_weights(index, normed, down_even, down_odd, others, n_seq, gain_rows):
    length, _ = normed.shape
    half, columns = down_even.shape
    per = 128 // gain_rows

    def kernel(index_ref, n_ref, e_ref, d_ref, o_ref, part):
        part[...] = t_dot(n_ref[:half], e_ref[...]) + t_dot(n_ref[half:], d_ref[...])
        o_ref[0] = part[span(index_ref[1] % per, gain_rows)]

    return pl.pallas_call(
        kernel,
        grid_spec=pltpu.PrefetchScalarGridSpec(
            num_scalar_prefetch=1,
            grid=(others,),
            in_specs=[
                pl.BlockSpec(
                    (length, 128), lambda i, ref: (0, (i * n_seq + ref[1]) * gain_rows // 128)
                ),
                pl.BlockSpec((half, columns), lambda i, ref: (0, 0)),
                pl.BlockSpec((half, columns), lambda i, ref: (0, 0)),
            ],
            out_specs=pl.BlockSpec((1, gain_rows, columns), lambda i, ref: (i, 0, 0)),
            scratch_shapes=[pltpu.VMEM((128, columns), F32)],
        ),
        out_shape=jax.ShapeDtypeStruct((others, gain_rows, columns), F32),
        compiler_params=pltpu.CompilerParams(vmem_limit_bytes=LIMIT),
        cost_estimate=LIGHT,
        name="down_weights",
    )(index, normed, down_even, down_odd)


def output_weights(base, heads, columns, dtype):
    count, width = heads[0].shape
    wide = columns[0].shape[1]
    half = width // 2
    tile = 256
    many = len(heads)

    def kernel(*refs):
        total = 0.0
        for j in range(many):
            total = total + t_dot(refs[j][...], refs[many + j][...])
        refs[-1][...] = total.astype(dtype)

    return pl.pallas_call(
        kernel,
        grid=(half // tile,),
        in_specs=[pl.BlockSpec((count, tile), lambda i: (0, base * (half // tile) + i))] * many
        + [whole((count, wide))] * many,
        out_specs=pl.BlockSpec((tile, wide), lambda i: (i, 0)),
        out_shape=jax.ShapeDtypeStruct((half, wide), dtype),
        compiler_params=pltpu.CompilerParams(vmem_limit_bytes=LIMIT),
        cost_estimate=LIGHT,
        name="output_weights",
    )(*heads, *columns)


def combine(base, masks, returned, products, dtype):
    half = masks[0].shape[0] // 2
    slots, count = masks[0].shape[1:]
    pieces = len(returned)
    others, _, width = returned[0].shape
    many = len(masks)

    tile = 512

    def kernel(*refs):
        mask_refs, row_refs = refs[:many], refs[many : many + pieces]
        rest, out_ref = refs[many + pieces : -1], refs[-1]
        total = 0.0
        for n, (_, _, flipped) in enumerate(products):
            total = total + (dot_t if flipped else dot)(rest[2 * n][...], rest[2 * n + 1][...])
        for b in range(half):
            rows = jnp.concatenate(
                [
                    row_refs[i][j, b * CAP : (b + 1) * CAP]
                    for i in range(pieces)
                    for j in range(others)
                ],
                axis=0,
            )
            block = total[b * count : (b + 1) * count]
            for mask_ref in mask_refs:
                block = block + t_dot(mask_ref[b], rows)
            out_ref[b * count : (b + 1) * count] = block.astype(dtype)

    factors = []
    specs = []
    for left, right, flipped in products:
        factors += [left, right]
        specs.append(pl.BlockSpec((half * count, left.shape[1]), lambda t: (base, 0)))
        if flipped:
            specs.append(pl.BlockSpec((tile, right.shape[1]), lambda t: (t, 0)))
        else:
            specs.append(pl.BlockSpec((right.shape[0], tile), lambda t: (0, t)))
    return pl.pallas_call(
        kernel,
        grid=(width // tile,),
        in_specs=[pl.BlockSpec((half, slots, count), lambda t: (base, 0, 0))] * many
        + [pl.BlockSpec((others, half * CAP, tile), lambda t: (0, base, t))] * pieces
        + specs,
        out_specs=pl.BlockSpec((half * count, tile), lambda t: (0, t)),
        out_shape=jax.ShapeDtypeStruct((half * count, width), dtype),
        compiler_params=pltpu.CompilerParams(vmem_limit_bytes=LIMIT),
        cost_estimate=LIGHT,
        name="combine",
    )(*masks, *returned, *factors)


def swap(x, axis, mask):
    n = lax.axis_size(axis)
    return lax.ppermute(x, axis, [(i, i ^ mask) for i in range(n)])


def after(x, *earlier):
    return lax.optimization_barrier((x, *earlier))[0]


class Lane:
    def __init__(self, axis, depth):
        self.axis = axis
        self.depth = depth
        self.sent = []

    def send(self, x, mask):
        if len(self.sent) >= self.depth:
            x = after(x, self.sent[-self.depth])
        got = swap(x, self.axis, mask)
        self.sent.append(got)
        return got

    def chips(self, x):
        chips = lax.axis_size("seq") // 2
        return [x] + [self.send(x, 2 * k) for k in range(1, chips)]

    def group(self, x):
        return self.pair(self.chips(x))

    def pair(self, evens):
        even = stacked(evens)
        return even, swap(even, "seq", 1)

    def scatter(self, even, odd):
        return self.finish(self.begin(even, odd))

    def begin(self, even, odd):
        chips = lax.axis_size("seq") // 2
        rows = even.shape[0] // chips
        got = swap(odd.astype(BF), "seq", 1)
        blocks = [
            even[k * rows : (k + 1) * rows] + got[k * rows : (k + 1) * rows].astype(F32)
            for k in range(chips)
        ]
        return blocks[:1] + [block.astype(BF) for block in blocks[1:]]

    def finish(self, blocks, *gates):
        got = [self.send(blocks[k], 2 * k) for k in range(1, len(blocks))]
        total = blocks[0]
        for block in got:
            total = total + after(block, *gates).astype(F32)
        return total

    def corners(self, x, *gates):
        if lax.axis_size("exp") != 4:
            return [(j, 0, y) for j, y in enumerate(self.others(x))]
        middle = x.shape[0] // 2
        one, two = self.send(x, 1), self.send(x, 2)
        return [
            (0, 0, x),
            (1, 0, one),
            (2, 0, two),
            (3, 0, self.send(part(after(two, *gates), 0, middle), 1)),
            (3, middle, self.send(part(after(one, *gates), middle, middle), 2)),
        ]

    def others(self, x):
        return [x] + [self.send(x, j) for j in range(1, lax.axis_size("exp"))]

def siblings(blocks):
    got = {}
    for k in range(len(blocks) - 1, -1, -1):
        got[k] = swap(after(blocks[k], *got.values()), "seq", 1)
    return [got[k] for k in range(len(blocks))]


def stacked(blocks):
    rows, columns = blocks[0].shape
    everything = slice(None)
    (whole_array,) = arrange(
        jnp.zeros((1,), jnp.int32),
        blocks,
        [(rows * len(blocks), columns)],
        [
            (k, everything, 0, lambda ref, k=k: (slice(k * rows, (k + 1) * rows), everything))
            for k in range(len(blocks))
        ],
    )
    return whole_array


def part(x, start, rows):
    (piece,) = arrange(
        jnp.zeros((1,), jnp.int32),
        [x],
        [(rows, x.shape[1])],
        [(0, (slice(start, start + rows),), 0, lambda ref: (slice(0, rows),))],
    )
    return piece


def relative_order(count):
    chips = count // 2
    return [2 * k for k in range(chips)] + [2 * k + 1 for k in range(chips)]


def sum_exp(x, axis):
    return lax.psum_scatter(x.astype(BF), "exp", scatter_dimension=axis, tiled=True).astype(F32)


def shards(
    tokens,
    routes,
    route_weights,
    norm_gain,
    w_query,
    w_kv_down,
    latent_gain,
    w_kv_up,
    w_output,
    ffn_gain,
    shared_gate,
    shared_up,
    shared_down,
    expert_gate,
    expert_up,
    expert_down,
    out_grad,
):
    count, width = tokens.shape
    n_seq = lax.axis_size("seq")
    n_exp = lax.axis_size("exp")
    seq = lax.axis_index("seq")
    order = relative_order(n_seq)
    chips = n_seq // 2
    heads = H // n_seq
    length = count * n_seq
    half = length // 2
    pieces = expert_gate.shape[0]
    parts_per = pieces * n_seq * n_exp // EXPERTS
    factor = 1.0 / math.sqrt(DN + DR)
    gain_rows = norm_gain.shape[0]
    latent_rows_local = latent_gain.shape[0]
    along = Lane("seq", 3)
    across = Lane("exp", 3)
    free = Lane("seq", 3)

    index = jnp.stack([lax.axis_index("exp"), seq]).astype(jnp.int32)
    ratio = w_query.shape[0] // w_kv_up.shape[0]
    slim = w_kv_up.shape[1] // ratio
    columns = -(-w_kv_down.shape[1] // 128) * 128
    high = lax.reduce_precision(route_weights, 8, 7)
    middle = lax.reduce_precision(route_weights - high, 8, 7)
    low = route_weights - high - middle
    route_pack = jnp.concatenate([routes.astype(F32), high, middle, low], axis=1).astype(BF).T
    lines = route_pack.shape[0] // 4
    gains = jnp.concatenate([norm_gain, ffn_gain, latent_gain])
    packed = jnp.concatenate(
        [
            jnp.pad(w_kv_down, ((0, 0), (0, columns - R - DR))),
            jnp.pad(gains, (0, columns - gains.shape[0]))[None, :],
            jnp.pad(
                route_pack.reshape(4, lines, count).transpose(1, 0, 2).reshape(lines, 4 * count),
                ((0, 15 - lines), (0, columns - 4 * count)),
            ),
        ],
        axis=0,
    )
    packed_even = stacked(free.chips(packed))
    token_even = along.chips(tokens)
    first_all = lax.all_gather(
        jnp.concatenate(
            [
                w_query,
                jnp.concatenate(
                    [w_kv_up[:, g * slim : (g + 1) * slim] for g in range(ratio)], axis=0
                ),
            ],
            axis=1,
        ),
        "exp",
        axis=0,
        tiled=True,
    )
    packed_parts = across.others(packed_even)
    packed_even = stacked(packed_parts)
    packed_odd = swap(packed_even, "seq", 1)
    early = packed_parts[-1]
    gate_cols = lax.all_gather(after(shared_gate, early), "exp", axis=0, tiled=True)
    lift_cols = lax.all_gather(after(shared_up, early), "exp", axis=0, tiled=True)
    drop_rows = lax.all_gather(after(shared_down, early), "exp", axis=1, tiled=True)

    everything = slice(None)
    block_rows = width // n_exp
    plan = []
    deep = gain_rows + 16
    for h in range(2):
        for j in range(n_exp):
            for k in range(chips):

                def where(ref, h=h, j=j, k=k):
                    return (ref[0] ^ j) * n_seq + (ref[1] ^ (2 * k + h))

                plan.append(
                    (
                        h,
                        (
                            slice((j * chips + k) * deep, (j * chips + k) * deep + gain_rows),
                            slice(0, R + DR),
                        ),
                        0,
                        lambda ref, where=where: (span(where(ref), gain_rows), everything),
                    )
                )
                plan.append(
                    (
                        h,
                        (slice((j * chips + k) * deep + gain_rows, (j * chips + k + 1) * deep),),
                        1,
                        lambda ref, where=where: (where(ref),),
                    )
                )
    down_full, extra_all = arrange(
        index,
        [packed_even, packed_odd],
        [(width, R + DR), (n_exp * n_seq, 16, columns)],
        plan,
    )
    gain_first = extra_all[:, 0, :gain_rows].reshape(1, width).astype(F32)
    gain_second = extra_all[:, 0, gain_rows : 2 * gain_rows].reshape(1, width).astype(F32)
    latent_wide = (
        extra_all[:, 0, 2 * gain_rows : 2 * gain_rows + latent_rows_local]
        .reshape(1, R)
        .astype(F32)
    )
    route_all = jnp.concatenate(
        [
            x[: chips * deep].reshape(chips, deep, columns)[:, gain_rows + 1 :]
            for x in (packed_even, packed_odd)
        ],
        axis=0,
    )[:, :lines, : 4 * count]
    route_all = route_all.reshape(n_seq, lines, 4, count).transpose(0, 2, 1, 3)
    route_all = route_all.reshape(n_seq, 4 * lines, count).astype(F32)
    route_all = jnp.concatenate(
        [
            route_all[:, :TOP],
            route_all[:, TOP : 2 * TOP]
            + route_all[:, 2 * TOP : 3 * TOP]
            + route_all[:, 3 * TOP :],
        ],
        axis=1,
    )
    up_rows = w_kv_up.shape[0]
    query_width = w_query.shape[1]
    (up_cols,) = arrange(
        index,
        [first_all],
        [(R, w_kv_up.shape[1])],
        [
            (
                0,
                (
                    slice((j * ratio + g) * up_rows, (j * ratio + g + 1) * up_rows),
                    slice(query_width, query_width + slim),
                ),
                0,
                lambda ref, j=j, g=g: (
                    slice(j * up_rows, (j + 1) * up_rows),
                    slice(g * slim, (g + 1) * slim),
                ),
            )
            for j in range(n_exp)
            for g in range(ratio)
        ],
    )
    token_odd = siblings(token_even)
    token_blocks = token_even + token_odd
    output_even = free.chips(after(w_output, *token_odd, packed_odd))

    column = jnp.stack(
        [
            ((other * n_seq + seq) * pieces + i) // parts_per
            for i in range(pieces)
            for other in range(n_exp)
        ]
    )
    kinds = n_exp * pieces
    named = route_all[:, None, :TOP, :].astype(jnp.int32) == column[None, :, None, None]
    matched = jnp.any(named, axis=2)
    match_weight = jnp.sum(jnp.where(named, route_all[:, None, TOP:, :], 0.0), axis=2)
    earlier = (jnp.arange(count)[:, None] < jnp.arange(count)[None, :]).astype(BF)
    rank = jnp.dot(matched.astype(BF), earlier, preferred_element_type=F32).astype(jnp.int32)
    chosen = (rank[:, :, None, :] == jnp.arange(CAP, dtype=jnp.int32)[None, None, :, None]) & (
        matched[:, :, None, :]
    )
    select = chosen.astype(BF).reshape(n_seq, kinds * CAP, count)
    weighted = jnp.where(chosen, match_weight[:, :, None, :], 0.0).reshape(
        n_seq, kinds * CAP, count
    )
    slot_weight = jnp.sum(weighted, axis=2, keepdims=True)
    weighted_high = weighted.astype(BF)
    weighted_low = (weighted - weighted_high.astype(F32)).astype(BF)

    positions = jnp.concatenate(
        [(seq ^ r) * count + jnp.arange(count, dtype=jnp.int32) for r in order]
    )
    row_position, column_position = positions[None, :], positions[:, None]
    cosine_table, sine_table = rope_tables(positions, DR)
    cosine_wide = jnp.concatenate([cosine_table, cosine_table], axis=1)
    sine_wide = jnp.concatenate([-sine_table, sine_table], axis=1)
    gain_first = after(gain_first, column_position)
    normed_one, latent_all, latent_raw, query_heads, key_heads, value_heads = project(
        token_blocks,
        gain_first,
        first_all,
        down_full,
        latent_wide,
        up_cols,
        cosine_wide,
        sine_wide,
        heads,
    )
    output_even = stacked([after(x, normed_one) for x in output_even])
    result, logsum = attend(
        query_heads, key_heads, value_heads, row_position, column_position, factor
    )

    result_even = along.chips(result)
    output_parts = across.corners(output_even, result, *result_even[1:])
    output_sides = []
    for parts in (output_parts, [(j, at, swap(x, "seq", 1)) for j, at, x in output_parts]):
        output_sides += arrange(
            index,
            [x for _, _, x in parts],
            [(H * DV // 2, width)],
            [
                (
                    n,
                    everything,
                    0,
                    lambda ref, j=j, at=at, x=x: (
                        slice(at, at + x.shape[0]),
                        span(ref[0] ^ j, block_rows),
                    ),
                )
                for n, (j, at, x) in enumerate(parts)
            ],
        )
    output_even, output_odd = output_sides


    def give(rows):
        return lax.all_to_all(rows, "exp", split_axis=0, concat_axis=0, tiled=True)

    result_blocks = result_even + siblings(result_even)
    normed_two, residual = add_norm(
        token_blocks,
        result_blocks,
        output_even,
        output_odd,
        gain_second,
    )
    inverse_two = inverse_rms(residual)
    grad_even = along.chips(after(out_grad, *token_odd))
    send_rows = dispatch(select, normed_two, None, pieces)
    received = []
    for rows in send_rows:
        received.append(give(after(rows, *received)))
    grad_even, grad_odd = along.pair([after(x, *send_rows) for x in grad_even])
    grad_rows = stacked([grad_even, grad_odd])
    received_grad = []
    for rows in dispatch(select, grad_rows, slot_weight, pieces):
        received_grad.append(give(after(rows, *received, *received_grad)))

    shared_hidden, sgate_grad, sup_grad = shared(
        normed_two, grad_rows, gate_cols, lift_cols, drop_rows
    )
    gate_part, lift_part, drop_part = expert_weights(
        normed_two, grad_rows, shared_hidden, sgate_grad, sup_grad, 0, 1, None, BF
    )
    received[0] = after(received[0], gate_part, lift_part, drop_part)

    slot_rows = n_exp * n_seq * CAP
    pairs = []
    results_back, grads_back, kept = [], [], []
    for i in range(pieces):
        rows = received[i].reshape(slot_rows, width)
        cots = received_grad[i].reshape(slot_rows, width)
        expert_result, input_grad, *saved = expert(
            rows, cots, expert_gate, expert_up, expert_down, i
        )
        grads_back.append(give(input_grad.reshape(n_exp, n_seq * CAP, width)))
        results_back.append(expert_result.reshape(n_exp, n_seq * CAP, width))
        kept.append((rows, cots, *saved))
    two_products = [(sgate_grad, gate_cols, True), (sup_grad, lift_cols, True)]
    expert_grads = expert_weights(
        after(kept[0][0], input_grad), *kept[0][1:], 0, pieces, None
    )
    token_wide = tokens.astype(F32)
    token_inverse = inverse_rms(token_wide)
    select = after(select, *expert_grads, token_inverse)
    two_odd = combine(1, [select], grads_back, two_products, BF)
    two_even = combine(0, [select], grads_back, two_products, F32)
    two_blocks = along.begin(two_even, two_odd)
    back = []
    for i in range(pieces):
        back.append(give(after(results_back[i], *(two_blocks if i == 0 else expert_grads))))
        if i:
            expert_grads = expert_weights(
                after(kept[i][0], back[0]), *kept[i][1:], i, pieces, expert_grads
            )
    results_back = back
    expert_gate_grad, expert_up_grad, expert_down_grad = expert_grads
    (own_heads,) = arrange(
        index,
        [after(result_blocks[0], *two_blocks)] + result_blocks[1:],
        [(count, H * DV)],
        [
            (
                p,
                (slice(p * count, (p + 1) * count), everything),
                0,
                lambda ref, p=p: (everything, slice(p * heads * DV, (p + 1) * heads * DV)),
            )
            for p in range(n_seq)
        ],
    )
    gate_part, lift_part, drop_part = [
        after(x[0], *two_blocks) for x in (gate_part, lift_part, drop_part)
    ]
    gate_out, lift_out, drop_out = sum_exp(gate_part, 0), sum_exp(lift_part, 0), sum_exp(drop_part, 1)
    two_grad = along.finish(
        two_blocks, *expert_grads, own_heads
    )
    residual_norm_grad, second_terms = norm_back(
        two_grad, residual, inverse_two, gain_second
    )
    residual_grad = out_grad.astype(F32) + residual_norm_grad
    residual_half = residual_grad.astype(BF)
    even_heads = dot_t(residual_half, output_even).astype(BF)
    odd_heads = dot_t(residual_half, output_odd).astype(BF)
    wide = heads * DV
    pairs = [
        jnp.stack([even_heads[:, k * wide : (k + 1) * wide], odd_heads[:, k * wide : (k + 1) * wide]])
        for k in range(chips)
    ]
    stacks = pairs
    pairs = [pairs[0]] + [along.send(pairs[k], 2 * k) for k in range(1, chips)]
    other_half = swap(jnp.stack([pair[1] for pair in pairs]), "seq", 1)
    attention_grad = jnp.concatenate(
        [jnp.stack([pair[0] for pair in pairs]), other_half], axis=0
    ).reshape(length, wide)
    mine = lax.axis_index("exp")
    out_products = [(shared_hidden, drop_rows, False)]
    out_masks = [weighted_high, weighted_low]
    out_masks = [after(mask, *stacks, *pairs[1:]) for mask in out_masks]
    out_odd = combine(1, out_masks, results_back, out_products, BF)
    out_even = combine(0, out_masks, results_back, out_products, F32)
    out_blocks = along.begin(out_even, out_odd)
    output_got = [along.send(out_blocks[k], 2 * k) for k in range(chips - 1, 0, -1)]

    query_in_grad, kv_grad, latent_part, latent_sum = attend_back(
        query_heads,
        key_heads,
        value_heads,
        result,
        after(attention_grad, *out_blocks),
        logsum,
        row_position,
        column_position,
        cosine_wide,
        -sine_wide,
        up_cols,
        latent_all,
        latent_wide,
        factor,
        columns,
    )
    one_odd, odd_sum = query_back(1, query_in_grad, first_all, normed_one, gain_first, BF)
    one_even, even_sum = query_back(0, after(query_in_grad, *output_got[:2]), first_all, normed_one, gain_first, F32)
    late = Lane("exp", 3)
    attention_parts = late.others(after(own_heads, one_even))
    column_blocks = [
        lax.dynamic_slice_in_dim(residual_half, (mine ^ j) * block_rows, block_rows, 1)
        for j in range(n_exp)
    ]
    column_blocks = [column_blocks[0]] + [
        late.send(column_blocks[j], j) for j in range(1, n_exp)
    ]
    sums = jnp.concatenate(
        [
            (odd_sum + even_sum).reshape(n_exp, n_seq, gain_rows),
            jnp.sum(second_terms, axis=0).reshape(n_exp, n_seq, gain_rows),
            latent_sum.reshape(n_exp, n_seq, latent_rows_local),
        ],
        axis=2,
    )
    many = sums.shape[2]
    turn = (seq ^ jnp.array(order))[:, None] == jnp.arange(n_seq)[None, :]
    sums = jnp.einsum("ps,esw->pew", turn.astype(F32), sums, precision=lax.Precision.HIGHEST)
    sums = jnp.pad(
        sums.reshape(n_seq, 1, n_exp * many), ((0, 0), (0, 15), (0, columns - n_exp * many))
    )
    latent_part = jnp.concatenate([latent_part.reshape(n_seq, count, columns), sums], axis=1)
    latent_part = latent_part.reshape(n_seq * (count + 16), columns)
    latent_grad = along.scatter(
        latent_part[: chips * (count + 16)], latent_part[chips * (count + 16) :]
    )
    one_blocks = along.begin(one_even, one_odd)
    one_got = [along.send(one_blocks[k], 2 * k) for k in range(chips - 1, 0, -1)]
    output_odd_part = output_weights(1, attention_parts, column_blocks, BF)
    output_even_part = output_weights(0, attention_parts, column_blocks, F32)
    output_blocks = along.begin(output_even_part, output_odd_part)
    up_part = t_dot(after(latent_all, one_odd), kv_grad).astype(BF)
    query_part = t_dot(after(normed_one, one_odd), query_in_grad).astype(BF)
    up_out = sum_exp(up_part, 0)
    query_out = sum_exp(query_part, 0)
    sums = latent_grad[count, : n_exp * many].reshape(n_exp, 1, many)
    latent_grad = latent_grad[:count]
    latent_raw_grad, _ = norm_back(
        latent_grad[:, :R], latent_raw[:count], inverse_rms(latent_raw[:count]), latent_wide
    )
    down_rows = jnp.concatenate(
        [
            latent_raw_grad,
            rotate(latent_grad[:, R : R + DR], cosine_table[:count], -sine_table[:count]),
            jnp.zeros((count, columns - R - DR), F32),
        ],
        axis=1,
    ).astype(BF)
    down_even, down_odd = free.pair(
        [after(x, *one_got, *output_blocks) for x in free.chips(down_rows)]
    )
    wide_got = [
        swap(after(output_blocks[k], down_even), "seq", 2 * k) for k in range(chips - 1, 0, -1)
    ]
    down_part = down_weights(index, normed_one, down_even, down_odd, n_exp, n_seq, gain_rows)
    down_part = jnp.concatenate(
        [
            down_part,
            jnp.pad(sums, ((0, 0), (0, 15), (0, columns - many))),
        ],
        axis=1,
    )
    down_sum = lax.dynamic_index_in_dim(down_part, mine, 0, keepdims=False)
    for j in range(1, n_exp):
        piece = lax.dynamic_index_in_dim(down_part, mine ^ j, 0, keepdims=False).astype(BF)
        down_sum = down_sum + swap(piece, "exp", j).astype(F32)
    down_out = down_sum[:gain_rows, : R + DR]
    small = down_sum[gain_rows, :many]
    first_out = small[:gain_rows] + jnp.sum(
        w_kv_down.astype(F32) * down_out, axis=1
    ) / norm_gain.astype(F32)

    output = residual + out_blocks[0]
    for block in output_got:
        output = output + after(block, *one_blocks).astype(F32)
    output = output.astype(BF)
    output_out = output_blocks[0]
    for block in wide_got:
        output_out = output_out + block.astype(F32)
    one_grad = one_blocks[0]
    for block in one_got:
        block = after(block, up_part, query_part, gate_out, lift_out, drop_out)
        one_grad = one_grad + block.astype(F32)
    down_back = dot_t(down_rows[:, : R + DR], down_full)
    token_norm_grad, _ = norm_back(
        one_grad + down_back, token_wide, token_inverse, gain_first
    )
    tokens_grad = (residual_grad + token_norm_grad).astype(BF)
    return (
        output,
        tokens_grad,
        first_out,
        query_out,
        down_out,
        small[2 * gain_rows : many],
        up_out,
        output_out,
        small[gain_rows : 2 * gain_rows],
        gate_out,
        lift_out,
        drop_out,
        expert_gate_grad,
        expert_up_grad,
        expert_down_grad,
    )


def solution(mesh):
    rows = P(("exp", "seq"), None)
    line = P(("exp", "seq"))
    grid = P("exp", "seq")
    turned = P("seq", "exp")
    part = P(("exp", "seq"), None, None)
    return jax.shard_map(
        shards,
        mesh=mesh,
        in_specs=(
            rows,
            rows,
            rows,
            line,
            grid,
            rows,
            line,
            grid,
            turned,
            line,
            grid,
            grid,
            turned,
            part,
            part,
            part,
            rows,
        ),
        out_specs=(
            rows,
            rows,
            line,
            grid,
            rows,
            line,
            grid,
            turned,
            line,
            grid,
            grid,
            turned,
            part,
            part,
            part,
        ),
        check_vma=False,
    )
```

```python
import math

import jax
import jax.numpy as jnp
from jax import lax
from jax.experimental import pallas as pl
from jax.experimental.pallas import tpu as pltpu
from jax.sharding import PartitionSpec as P

H = 16
DN = 128
DR = 64
DV = 128
R = 512
EXPERTS = 64
TOP = 6
CAP = 16


eps_norm = 1e-06
rope_base = 50000.0
BF = jnp.bfloat16
F32 = jnp.float32


def dot(a, b):
    return jnp.dot(a, b, preferred_element_type=F32)


def dot_t(a, b):
    return lax.dot_general(a, b, (((1,), (1,)), ((), ())), preferred_element_type=F32)


def t_dot(a, b):
    return lax.dot_general(a, b, (((0,), (0,)), ((), ())), preferred_element_type=F32)


def rope_tables(positions, width):
    middle = width // 2
    frequency = rope_base ** (-(jnp.arange(middle, dtype=F32) * 2.0 / width))
    angles = positions.astype(F32)[:, None] * frequency[None, :]
    return (jnp.cos(angles), jnp.sin(angles))


def rotate(values, cosine_table, sine_table):
    middle = values.shape[-1] // 2
    leading = values[..., :middle]
    trailing = values[..., middle:]
    return jnp.concatenate(
        [
            leading * cosine_table - trailing * sine_table,
            trailing * cosine_table + leading * sine_table,
        ],
        axis=-1,
    )


def silu_slope(gate_values):
    sigmoid = jax.nn.sigmoid(gate_values)
    return sigmoid * (1.0 + gate_values * (1.0 - sigmoid))


def norm_back(dy, v, inverse, gain):
    hat = v * inverse
    scaled = dy * gain
    dv = inverse * (scaled - hat * jnp.mean(scaled * hat, axis=-1, keepdims=True))
    return dv, dy * hat


def inverse_rms(v):
    return lax.rsqrt(jnp.mean(v * v, axis=-1, keepdims=True) + eps_norm)


LIMIT = 56 * 1024 * 1024
LIGHT = pl.CostEstimate(flops=0, transcendentals=0, bytes_accessed=0)
ANY = pl.BlockSpec(memory_space=pl.ANY)
SCALARS = pl.BlockSpec(memory_space=pltpu.SMEM)


def whole(shape):
    return pl.BlockSpec(shape, lambda *grid: (0,) * len(shape))


def arrange(index, blocks, outs, plan):
    def kernel(index_ref, *refs):
        sources = refs[: len(blocks)]
        targets = refs[len(blocks) :]
        for block, source, out, target in plan:
            targets[out][target(index_ref)] = sources[block][source]

    return pl.pallas_call(
        kernel,
        out_shape=[jax.ShapeDtypeStruct(s, BF) for s in outs],
        in_specs=[SCALARS] + [pl.BlockSpec(memory_space=pltpu.VMEM)] * len(blocks),
        out_specs=[pl.BlockSpec(memory_space=pltpu.VMEM)] * len(outs),
        compiler_params=pltpu.CompilerParams(vmem_limit_bytes=LIMIT),
        cost_estimate=LIGHT,
        name="arrange",
    )(index, *blocks)


def span(start, size):
    return pl.ds(pl.multiple_of(start * size, size), size)


def turned(v, cosine, sine):
    middle = v.shape[1] // 2
    return v * cosine + jnp.concatenate([v[:, middle:], v[:, :middle]], axis=1) * sine


def project(token_blocks, gain, w_first, w_down, latent_gain, w_up, cosine, sine, heads):
    count, width = token_blocks[0].shape
    chips = len(token_blocks) // 2
    half = chips * count
    wide = DN + DR
    columns = heads * wide

    def kernel(g_ref, wd_ref, lg_ref, wu_ref, c_ref, s_ref, *refs):
        tokens, w_ref = refs[: 2 * chips], refs[2 * chips]
        n_ref, l_ref, r_ref, q_ref, k_ref, v_ref, x_ref = refs[2 * chips + 1 :]
        for h in range(2):

            @pl.when(pl.program_id(0) == h)
            def _():
                for k in range(chips):
                    x_ref[k * count : (k + 1) * count] = tokens[h * chips + k][...]

        x = x_ref[...].astype(F32)
        inverse = lax.rsqrt(jnp.mean(x * x, axis=1, keepdims=True) + eps_norm)
        n_ref[...] = (x * inverse * g_ref[...]).astype(BF)
        down = dot(n_ref[...], wd_ref[...])
        raw = down[:, :R]
        r_ref[...] = raw
        inverse = lax.rsqrt(jnp.mean(raw * raw, axis=1, keepdims=True) + eps_norm)
        l_ref[...] = (raw * inverse * lg_ref[...]).astype(BF)
        query = dot(n_ref[...], w_ref[:, :columns])
        up = dot(l_ref[...], wu_ref[...]).astype(BF)
        cosine, sine = c_ref[...], s_ref[...]
        zeros = jnp.zeros((half, 256 - wide), BF)
        rope = jnp.concatenate([turned(down[:, R : R + DR], cosine, sine).astype(BF), zeros], axis=1)
        for n in range(heads):
            own = query[:, n * wide : (n + 1) * wide]
            q_ref[n, :, :DN] = own[:, :DN].astype(BF)
            q_ref[n, :, DN:] = jnp.concatenate(
                [turned(own[:, DN:], cosine, sine).astype(BF), zeros], axis=1
            )
            k_ref[n, :, :DN] = up[:, n * (DN + DV) : n * (DN + DV) + DN]
            k_ref[n, :, DN:] = rope
            v_ref[n] = up[:, n * (DN + DV) + DN : (n + 1) * (DN + DV)]

    def rows(w):
        return pl.BlockSpec((half, w), lambda i: (i, 0))

    def head_rows(w):
        return pl.BlockSpec((heads, half, w), lambda i: (0, i, 0))

    length = 2 * half
    return pl.pallas_call(
        kernel,
        grid=(2,),
        in_specs=[
            whole((1, width)),
            whole(w_down.shape),
            whole((1, R)),
            whole(w_up.shape),
            rows(DR),
            rows(DR),
        ]
        + [whole((count, width))] * (2 * chips)
        + [whole(w_first.shape)],
        out_specs=[rows(width), rows(R), rows(R), head_rows(256), head_rows(256), head_rows(DV)],
        out_shape=[
            jax.ShapeDtypeStruct((length, width), BF),
            jax.ShapeDtypeStruct((length, R), BF),
            jax.ShapeDtypeStruct((length, R), F32),
            jax.ShapeDtypeStruct((heads, length, 256), BF),
            jax.ShapeDtypeStruct((heads, length, 256), BF),
            jax.ShapeDtypeStruct((heads, length, DV), BF),
        ],
        scratch_shapes=[pltpu.VMEM((half, width), BF)],
        compiler_params=pltpu.CompilerParams(vmem_limit_bytes=LIMIT),
        cost_estimate=LIGHT,
        name="project",
    )(gain, w_down, latent_gain, w_up, cosine, sine, *token_blocks, w_first)


def query_back(base, query_grad, w_first, normed, gain, dtype):
    length, columns = query_grad.shape
    half = length // 2
    width = normed.shape[1]
    tile = 512

    def kernel(q_ref, n_ref, g_ref, w_ref, o_ref, t_ref):
        part = dot_t(q_ref[...], w_ref[:, :columns])
        o_ref[...] = part.astype(dtype)
        product = part * n_ref[...].astype(F32)
        t_ref[...] = jnp.sum(product, axis=0, keepdims=True) / g_ref[...]

    return pl.pallas_call(
        kernel,
        grid=(width // tile,),
        in_specs=[
            pl.BlockSpec((half, columns), lambda i: (base, 0)),
            pl.BlockSpec((half, tile), lambda i: (base, i)),
            pl.BlockSpec((1, tile), lambda i: (0, i)),
            pl.BlockSpec((tile, w_first.shape[1]), lambda i: (i, 0)),
        ],
        out_specs=[
            pl.BlockSpec((half, tile), lambda i: (0, i)),
            pl.BlockSpec((1, tile), lambda i: (0, i)),
        ],
        out_shape=[
            jax.ShapeDtypeStruct((half, width), dtype),
            jax.ShapeDtypeStruct((1, width), F32),
        ],
        compiler_params=pltpu.CompilerParams(vmem_limit_bytes=LIMIT),
        cost_estimate=LIGHT,
        name="query_back",
    )(query_grad, normed, gain, w_first)


def attend(query, key, value, row_position, column_position, factor):
    heads, length, _ = query.shape
    tile = 256

    def kernel(q_ref, k_ref, v_ref, row_ref, column_ref, o_ref, s_ref):
        allowed = column_ref[...] <= row_ref[...]
        for n in range(heads):
            scores = dot_t(k_ref[n], q_ref[n]) * factor
            exponent = jnp.where(allowed, jnp.exp(jnp.where(allowed, scores, -1e30)), 0.0)
            total = jnp.sum(exponent, axis=0, keepdims=True)
            probs = (exponent / total).astype(BF)
            o_ref[:, n * DV : (n + 1) * DV] = t_dot(v_ref[n], probs).T.astype(BF)
            s_ref[n : n + 1, :] = jnp.log(total)

    return pl.pallas_call(
        kernel,
        grid=(length // tile,),
        in_specs=[
            pl.BlockSpec((heads, tile, 256), lambda i: (0, i, 0)),
            whole(key.shape),
            whole(value.shape),
            pl.BlockSpec((1, tile), lambda i: (0, i)),
            whole((length, 1)),
        ],
        out_specs=[
            pl.BlockSpec((tile, heads * DV), lambda i: (i, 0)),
            pl.BlockSpec((heads, tile), lambda i: (0, i)),
        ],
        out_shape=[
            jax.ShapeDtypeStruct((length, heads * DV), BF),
            jax.ShapeDtypeStruct((heads, length), F32),
        ],
        compiler_params=pltpu.CompilerParams(vmem_limit_bytes=LIMIT),
        cost_estimate=LIGHT,
        name="attend",
    )(query, key, value, row_position, column_position)


def attend_back(query, key, value, result, result_grad, logsum, row_position, column_position, cosine, sine, w_up, latent_all, latent_gain, factor):
    heads, length, _ = query.shape
    tile = 256
    steps = length // tile
    wide = DN + DR

    def kernel(q_ref, k_ref, v_ref, o_ref, do_ref, ls_ref, row_ref, column_ref, c_ref, s_ref, wu_ref, l_ref, lg_ref, dq_ref, kv_ref, lp_ref, t_ref, dk_acc, dv_acc, kt):
        step = pl.program_id(0)

        @pl.when(step == 0)
        def _():
            dk_acc[...] = jnp.zeros_like(dk_acc)
            dv_acc[...] = jnp.zeros_like(dv_acc)
            for n in range(heads):
                kt[n] = k_ref[n].T

        allowed = column_ref[...] <= row_ref[...]
        cosine, sine = c_ref[...], s_ref[...]
        parts = []
        for n in range(heads):
            q = q_ref[n]
            grad = do_ref[:, n * DV : (n + 1) * DV]
            scores = jnp.where(allowed, dot_t(k_ref[n], q) * factor, -1e30)
            probs = jnp.exp(scores - ls_ref[n : n + 1, :])
            dv_acc[n] += dot(probs.astype(BF), grad)
            product = grad.astype(F32) * o_ref[:, n * DV : (n + 1) * DV].astype(F32)
            row_dot = jnp.sum(product.T, axis=0, keepdims=True)
            probs_grad = dot_t(v_ref[n], grad)
            score_grad = (probs * (probs_grad - row_dot) * factor).astype(BF)
            dk_acc[n] += dot(score_grad, q)
            query_grad = dot(kt[n], score_grad).T.astype(BF)
            parts.append(query_grad[:, :DN])
            parts.append(turned(query_grad[:, DN:wide].astype(F32), cosine, sine).astype(BF))
        dq_ref[...] = jnp.concatenate(parts, axis=1)

        @pl.when(step == steps - 1)
        def _():
            rope = jnp.zeros((length, DR), F32)
            for n in range(heads):
                key_grad = dk_acc[n].astype(BF)
                value_grad = dv_acc[n].astype(BF)
                base = n * (DN + DV)
                kv_ref[:, base : base + DN] = key_grad[:, :DN]
                kv_ref[:, base + DN : base + DN + DV] = value_grad
                rope = rope + key_grad[:, DN:wide].astype(F32)
            latent = dot_t(kv_ref[...], wu_ref[...])
            lp_ref[:, :R] = latent
            lp_ref[:, R:] = rope
            t_ref[...] = jnp.sum(
                latent * l_ref[...].astype(F32), axis=0, keepdims=True
            ) / lg_ref[...]

    return pl.pallas_call(
        kernel,
        grid=(steps,),
        in_specs=[
            pl.BlockSpec((heads, tile, 256), lambda i: (0, i, 0)),
            whole(key.shape),
            whole(value.shape),
            pl.BlockSpec((tile, heads * DV), lambda i: (i, 0)),
            pl.BlockSpec((tile, heads * DV), lambda i: (i, 0)),
            pl.BlockSpec((heads, tile), lambda i: (0, i)),
            pl.BlockSpec((1, tile), lambda i: (0, i)),
            whole((length, 1)),
            pl.BlockSpec((tile, DR), lambda i: (i, 0)),
            pl.BlockSpec((tile, DR), lambda i: (i, 0)),
            whole(w_up.shape),
            whole((length, R)),
            whole((1, R)),
        ],
        out_specs=[
            pl.BlockSpec((tile, heads * wide), lambda i: (i, 0)),
            whole((length, heads * (DN + DV))),
            whole((length, R + DR)),
            whole((1, R)),
        ],
        out_shape=[
            jax.ShapeDtypeStruct((length, heads * wide), BF),
            jax.ShapeDtypeStruct((length, heads * (DN + DV)), BF),
            jax.ShapeDtypeStruct((length, R + DR), F32),
            jax.ShapeDtypeStruct((1, R), F32),
        ],
        scratch_shapes=[
            pltpu.VMEM((heads, length, 256), F32),
            pltpu.VMEM((heads, length, DV), F32),
            pltpu.VMEM((heads, 256, length), BF),
        ],
        compiler_params=pltpu.CompilerParams(vmem_limit_bytes=LIMIT),
        cost_estimate=LIGHT,
        name="attend_back",
    )(query, key, value, result, result_grad, logsum, row_position, column_position, cosine, sine, w_up, latent_all, latent_gain)


def add_norm(token_blocks, blocks, w_even, w_odd, gain):
    count, width = token_blocks[0].shape
    many = len(blocks)
    chips = many // 2
    half = chips * count
    length = count * many
    depth = blocks[0].shape[1]

    def kernel(we_ref, wo_ref, g_ref, *refs):
        parts, tokens = refs[:many], refs[many : 2 * many]
        n_ref, r_ref, x_ref, a_ref = refs[2 * many :]
        for q in range(many):
            for p in range(chips):
                other = p ^ (q % chips)
                a_ref[p * count : (p + 1) * count, q * depth : (q + 1) * depth] = parts[q][
                    other * count : (other + 1) * count
                ]
        for h in range(2):

            @pl.when(pl.program_id(0) == h)
            def _():
                for k in range(chips):
                    x_ref[k * count : (k + 1) * count] = tokens[h * chips + k][...]

        middle = chips * depth
        total = dot(a_ref[:, :middle], we_ref[...]) + dot(a_ref[:, middle:], wo_ref[...])
        total = total + x_ref[...].astype(F32)
        inverse = lax.rsqrt(jnp.mean(total * total, axis=1, keepdims=True) + eps_norm)
        n_ref[...] = (total * inverse * g_ref[...]).astype(BF)

        @pl.when(pl.program_id(0) == 0)
        def _():
            r_ref[...] = total[:count]

    def source(q):
        return pl.BlockSpec((half, depth), lambda i: (i ^ (q // chips), 0))

    return pl.pallas_call(
        kernel,
        grid=(2,),
        in_specs=[whole(w_even.shape), whole(w_odd.shape), whole((1, width))]
        + [source(q) for q in range(many)]
        + [whole((count, width))] * many,
        out_specs=[pl.BlockSpec((half, width), lambda i: (i, 0)), whole((count, width))],
        out_shape=[
            jax.ShapeDtypeStruct((length, width), BF),
            jax.ShapeDtypeStruct((count, width), F32),
        ],
        scratch_shapes=[pltpu.VMEM((half, width), BF), pltpu.VMEM((half, many * depth), BF)],
        compiler_params=pltpu.CompilerParams(vmem_limit_bytes=LIMIT),
        cost_estimate=LIGHT,
        name="add_norm",
    )(w_even, w_odd, gain, *blocks, *token_blocks)


def expert(rows, cots, gate, up, down, piece):
    count, width = rows.shape
    units = gate.shape[2]
    tile = min(512, count)
    step = 256
    full = units // step
    rest = units % step
    spans = [(n * step, step) for n in range(full)] + ([(full * step, rest)] if rest else [])

    def kernel(x_ref, c_ref, gate_hbm, up_hbm, down_hbm, res_ref, in_ref, h_ref, gg_ref, ug_ref, wg, wu, wd, acc_r, acc_i, sems):
        first = pl.program_id(0) == 0

        def copies(n, start, size):
            span = pl.ds(start, size)
            return [
                pltpu.make_async_copy(gate_hbm.at[piece, :, span], wg.at[:, span], sems.at[0, n]),
                pltpu.make_async_copy(up_hbm.at[piece, :, span], wu.at[:, span], sems.at[1, n]),
                pltpu.make_async_copy(down_hbm.at[piece, span, :], wd.at[span, :], sems.at[2, n]),
            ]

        @pl.when(first)
        def _():
            for n, (start, size) in enumerate(spans):
                for copy in copies(n, start, size):
                    copy.start()

        acc_r[...] = jnp.zeros_like(acc_r)
        acc_i[...] = jnp.zeros_like(acc_i)

        def chunk(n, start, size):
            @pl.when(first)
            def _():
                for copy in copies(n, start, size):
                    copy.wait()

            span = pl.ds(start, size)
            x, c = x_ref[...], c_ref[...]
            w_gate, w_up, w_down = wg[:, span], wu[:, span], wd[span, :]
            g = dot(x, w_gate)
            u = dot(x, w_up)
            hidden_grad = dot_t(c, w_down)
            s = jax.nn.sigmoid(g)
            silu = g * s
            hidden = (silu * u).astype(BF)
            gate_grad = (hidden_grad * u * (s * (1.0 + g * (1.0 - s)))).astype(BF)
            up_grad = (hidden_grad * silu).astype(BF)
            h_ref[:, span] = hidden
            gg_ref[:, span] = gate_grad
            ug_ref[:, span] = up_grad
            acc_r[...] += dot(hidden, w_down)
            acc_i[...] += dot_t(gate_grad, w_gate) + dot_t(up_grad, w_up)

        if full:

            @pl.loop(0, full)
            def _(n):
                chunk(n, pl.multiple_of(n * step, step), step)

        if rest:
            chunk(full, full * step, rest)
        res_ref[...] = acc_r[...].astype(BF)
        in_ref[...] = acc_i[...].astype(BF)

    def block(w):
        return pl.BlockSpec((tile, w), lambda i: (i, 0))

    def array(w):
        return jax.ShapeDtypeStruct((count, w), BF)

    return pl.pallas_call(
        kernel,
        grid=(count // tile,),
        in_specs=[block(width), block(width), ANY, ANY, ANY],
        out_specs=[block(width), block(width), block(units), block(units), block(units)],
        out_shape=[array(width), array(width), array(units), array(units), array(units)],
        scratch_shapes=[
            pltpu.VMEM((width, units), BF),
            pltpu.VMEM((width, units), BF),
            pltpu.VMEM((units, width), BF),
            pltpu.VMEM((tile, width), F32),
            pltpu.VMEM((tile, width), F32),
            pltpu.SemaphoreType.DMA((3, len(spans))),
        ],
        compiler_params=pltpu.CompilerParams(vmem_limit_bytes=LIMIT),
        cost_estimate=LIGHT,
        name="expert",
    )(rows, cots, gate, up, down)


def shared(rows, cots, gate, up, down):
    count, width = rows.shape
    units = gate.shape[1]
    tile = 256

    def kernel(x_ref, c_ref, wg_ref, wu_ref, wd_ref, h_ref, gg_ref, ug_ref):
        g = dot(x_ref[...], wg_ref[...])
        u = dot(x_ref[...], wu_ref[...])
        hidden_grad = dot_t(c_ref[...], wd_ref[...])
        s = jax.nn.sigmoid(g)
        silu = g * s
        h_ref[...] = (silu * u).astype(BF)
        gg_ref[...] = (hidden_grad * u * (s * (1.0 + g * (1.0 - s)))).astype(BF)
        ug_ref[...] = (hidden_grad * silu).astype(BF)

    row = pl.BlockSpec((tile, width), lambda i: (i, 0))
    unit = pl.BlockSpec((tile, units), lambda i: (i, 0))
    return pl.pallas_call(
        kernel,
        grid=(count // tile,),
        in_specs=[row, row, whole(gate.shape), whole(up.shape), whole(down.shape)],
        out_specs=[unit] * 3,
        out_shape=[jax.ShapeDtypeStruct((count, units), BF)] * 3,
        compiler_params=pltpu.CompilerParams(vmem_limit_bytes=LIMIT),
        cost_estimate=LIGHT,
        name="shared",
    )(rows, cots, gate, up, down)


def expert_weights(rows, cots, hidden, gate_grad, up_grad, piece, pieces, earlier, dtype=F32):
    count, width = rows.shape
    units = hidden.shape[1]
    tile = 256

    def kernel(x_ref, c_ref, h_ref, gg_ref, ug_ref, *refs):
        g_ref, u_ref, d_ref = refs[-3:]
        g_ref[0] = t_dot(x_ref[...], gg_ref[...]).astype(dtype)
        u_ref[0] = t_dot(x_ref[...], ug_ref[...]).astype(dtype)
        d_ref[0] = t_dot(h_ref[...], c_ref[...]).astype(dtype)

    tall = pl.BlockSpec((1, tile, units), lambda i: (piece, i, 0))
    flat = pl.BlockSpec((1, units, tile), lambda i: (piece, 0, i))
    column = pl.BlockSpec((count, tile), lambda i: (0, i))
    kept = list(earlier or ())
    return pl.pallas_call(
        kernel,
        grid=(width // tile,),
        in_specs=[column, column] + [whole((count, units))] * 3 + [ANY] * len(kept),
        out_specs=[tall, tall, flat],
        out_shape=[
            jax.ShapeDtypeStruct((pieces, width, units), dtype),
            jax.ShapeDtypeStruct((pieces, width, units), dtype),
            jax.ShapeDtypeStruct((pieces, units, width), dtype),
        ],
        input_output_aliases={5 + n: n for n in range(len(kept))},
        compiler_params=pltpu.CompilerParams(vmem_limit_bytes=LIMIT),
        cost_estimate=LIGHT,
        name="expert_weights",
    )(rows, cots, hidden, gate_grad, up_grad, *kept)


def dispatch(select, rows, slot_weight, pieces):
    blocks, slots, count = select.shape
    width = rows.shape[1]
    others = slots // pieces // CAP

    def kernel(m_ref, x_ref, *refs):
        got = dot(m_ref[0], x_ref[...])
        if slot_weight is not None:
            got = got * refs[0][0]
        got = got.astype(BF)
        for i in range(pieces):
            for j in range(others):
                start = (i * others + j) * CAP
                refs[-pieces + i][j] = got[start : start + CAP]

    weights = [] if slot_weight is None else [slot_weight]
    out = pl.BlockSpec((others, CAP, width), lambda b: (0, b, 0))
    return pl.pallas_call(
        kernel,
        grid=(blocks,),
        in_specs=[
            pl.BlockSpec((1, slots, count), lambda b: (b, 0, 0)),
            pl.BlockSpec((count, width), lambda b: (b, 0)),
        ]
        + [pl.BlockSpec((1, slots, 1), lambda b: (b, 0, 0))] * len(weights),
        out_specs=[out] * pieces,
        out_shape=[jax.ShapeDtypeStruct((others, blocks * CAP, width), BF)] * pieces,
        compiler_params=pltpu.CompilerParams(vmem_limit_bytes=LIMIT),
        cost_estimate=LIGHT,
        name="dispatch",
    )(select, rows, *weights)


def down_weights(index, normed, down_even, down_odd, others, n_seq, gain_rows):
    length, _ = normed.shape
    half, columns = down_even.shape
    per = 128 // gain_rows

    def kernel(index_ref, n_ref, e_ref, d_ref, o_ref, part):
        part[...] = t_dot(n_ref[:half], e_ref[...]) + t_dot(n_ref[half:], d_ref[...])
        o_ref[0] = part[span(index_ref[1] % per, gain_rows)]

    return pl.pallas_call(
        kernel,
        grid_spec=pltpu.PrefetchScalarGridSpec(
            num_scalar_prefetch=1,
            grid=(others,),
            in_specs=[
                pl.BlockSpec(
                    (length, 128), lambda i, ref: (0, (i * n_seq + ref[1]) * gain_rows // 128)
                ),
                pl.BlockSpec((half, columns), lambda i, ref: (0, 0)),
                pl.BlockSpec((half, columns), lambda i, ref: (0, 0)),
            ],
            out_specs=pl.BlockSpec((1, gain_rows, columns), lambda i, ref: (i, 0, 0)),
            scratch_shapes=[pltpu.VMEM((128, columns), F32)],
        ),
        out_shape=jax.ShapeDtypeStruct((others, gain_rows, columns), F32),
        compiler_params=pltpu.CompilerParams(vmem_limit_bytes=LIMIT),
        cost_estimate=LIGHT,
        name="down_weights",
    )(index, normed, down_even, down_odd)


def combine(base, masks, returned, products, dtype):
    half = masks[0].shape[0] // 2
    slots, count = masks[0].shape[1:]
    pieces = len(returned)
    others, _, width = returned[0].shape
    many = len(masks)

    tile = 512

    def kernel(*refs):
        mask_refs, row_refs = refs[:many], refs[many : many + pieces]
        rest, out_ref = refs[many + pieces : -1], refs[-1]
        total = 0.0
        for n, (_, _, flipped) in enumerate(products):
            total = total + (dot_t if flipped else dot)(rest[2 * n][...], rest[2 * n + 1][...])
        for b in range(half):
            rows = jnp.concatenate(
                [
                    row_refs[i][j, b * CAP : (b + 1) * CAP]
                    for i in range(pieces)
                    for j in range(others)
                ],
                axis=0,
            )
            block = total[b * count : (b + 1) * count]
            for mask_ref in mask_refs:
                block = block + t_dot(mask_ref[b], rows)
            out_ref[b * count : (b + 1) * count] = block.astype(dtype)

    factors = []
    specs = []
    for left, right, flipped in products:
        factors += [left, right]
        specs.append(pl.BlockSpec((half * count, left.shape[1]), lambda t: (base, 0)))
        if flipped:
            specs.append(pl.BlockSpec((tile, right.shape[1]), lambda t: (t, 0)))
        else:
            specs.append(pl.BlockSpec((right.shape[0], tile), lambda t: (0, t)))
    return pl.pallas_call(
        kernel,
        grid=(width // tile,),
        in_specs=[pl.BlockSpec((half, slots, count), lambda t: (base, 0, 0))] * many
        + [pl.BlockSpec((others, half * CAP, tile), lambda t: (0, base, t))] * pieces
        + specs,
        out_specs=pl.BlockSpec((half * count, tile), lambda t: (0, t)),
        out_shape=jax.ShapeDtypeStruct((half * count, width), dtype),
        compiler_params=pltpu.CompilerParams(vmem_limit_bytes=LIMIT),
        cost_estimate=LIGHT,
        name="combine",
    )(*masks, *returned, *factors)


def swap(x, axis, mask):
    n = lax.axis_size(axis)
    return lax.ppermute(x, axis, [(i, i ^ mask) for i in range(n)])


def after(x, *earlier):
    return lax.optimization_barrier((x, *earlier))[0]


class Lane:
    def __init__(self, axis, depth):
        self.axis = axis
        self.depth = depth
        self.sent = []

    def send(self, x, mask):
        if len(self.sent) >= self.depth:
            x = after(x, self.sent[-self.depth])
        got = swap(x, self.axis, mask)
        self.sent.append(got)
        return got

    def chips(self, x):
        chips = lax.axis_size("seq") // 2
        return [x] + [self.send(x, 2 * k) for k in range(1, chips)]

    def group(self, x):
        return self.pair(self.chips(x))

    def pair(self, evens):
        rows, columns = evens[0].shape
        everything = slice(None)
        (even,) = arrange(
            jnp.zeros((1,), jnp.int32),
            evens,
            [(rows * len(evens), columns)],
            [
                (k, everything, 0, lambda ref, k=k: (slice(k * rows, (k + 1) * rows), everything))
                for k in range(len(evens))
            ],
        )
        return even, swap(even, "seq", 1)

    def scatter(self, even, odd):
        return self.finish(self.begin(even, odd))

    def begin(self, even, odd):
        chips = lax.axis_size("seq") // 2
        rows = even.shape[0] // chips
        got = swap(odd.astype(BF), "seq", 1)
        blocks = [
            even[k * rows : (k + 1) * rows] + got[k * rows : (k + 1) * rows].astype(F32)
            for k in range(chips)
        ]
        return blocks[:1] + [block.astype(BF) for block in blocks[1:]]

    def finish(self, blocks, *gates):
        got = [self.send(blocks[k], 2 * k) for k in range(1, len(blocks))]
        total = blocks[0]
        for block in got:
            total = total + after(block, *gates).astype(F32)
        return total

    def corners(self, x, *gates):
        if lax.axis_size("exp") != 4:
            return [(j, 0, y) for j, y in enumerate(self.others(x))]
        middle = x.shape[0] // 2
        one, two = self.send(x, 1), self.send(x, 2)
        return [
            (0, 0, x),
            (1, 0, one),
            (2, 0, two),
            (3, 0, self.send(after(two[:middle], *gates), 1)),
            (3, middle, self.send(after(one[middle:], *gates), 2)),
        ]

    def others(self, x):
        return [x] + [self.send(x, j) for j in range(1, lax.axis_size("exp"))]

def relative_order(count):
    chips = count // 2
    return [2 * k for k in range(chips)] + [2 * k + 1 for k in range(chips)]


def sum_exp(x, axis):
    return lax.psum_scatter(x.astype(BF), "exp", scatter_dimension=axis, tiled=True).astype(F32)


def shards(
    tokens,
    routes,
    route_weights,
    norm_gain,
    w_query,
    w_kv_down,
    latent_gain,
    w_kv_up,
    w_output,
    ffn_gain,
    shared_gate,
    shared_up,
    shared_down,
    expert_gate,
    expert_up,
    expert_down,
    out_grad,
):
    count, width = tokens.shape
    n_seq = lax.axis_size("seq")
    n_exp = lax.axis_size("exp")
    seq = lax.axis_index("seq")
    order = relative_order(n_seq)
    chips = n_seq // 2
    heads = H // n_seq
    length = count * n_seq
    half = length // 2
    pieces = expert_gate.shape[0]
    parts_per = pieces * n_seq * n_exp // EXPERTS
    factor = 1.0 / math.sqrt(DN + DR)
    gain_rows = norm_gain.shape[0]
    latent_rows_local = latent_gain.shape[0]
    along = Lane("seq", 3)
    across = Lane("exp", 3)
    free = Lane("seq", 3)

    index = jnp.stack([lax.axis_index("exp"), seq]).astype(jnp.int32)
    ratio = w_query.shape[0] // w_kv_up.shape[0]
    slim = w_kv_up.shape[1] // ratio
    columns = w_kv_down.shape[1]
    high = lax.reduce_precision(route_weights, 8, 7)
    middle = lax.reduce_precision(route_weights - high, 8, 7)
    low = route_weights - high - middle
    route_pack = jnp.concatenate([routes.astype(F32), high, middle, low], axis=1).astype(BF).T
    lines = route_pack.shape[0] // 4
    gains = jnp.concatenate([norm_gain, ffn_gain, latent_gain])
    packed = jnp.concatenate(
        [
            w_kv_down,
            jnp.pad(gains, (0, columns - gains.shape[0]))[None, :],
            jnp.pad(
                route_pack.reshape(4, lines, count).transpose(1, 0, 2).reshape(lines, 4 * count),
                ((0, 15 - lines), (0, columns - 4 * count)),
            ),
        ],
        axis=0,
    )
    packed_even = jnp.stack(free.chips(packed))
    token_even = along.chips(tokens)
    first_all = lax.all_gather(
        jnp.concatenate(
            [
                w_query,
                jnp.concatenate(
                    [w_kv_up[:, g * slim : (g + 1) * slim] for g in range(ratio)], axis=0
                ),
            ],
            axis=1,
        ),
        "exp",
        axis=0,
        tiled=True,
    )
    packed_parts = across.others(packed_even)
    packed_even = jnp.stack(packed_parts)
    packed_odd = swap(packed_even, "seq", 1)
    token_odd = []
    for x in token_even:
        token_odd.append(swap(after(x, *token_odd), "seq", 1))
    token_blocks = token_even + token_odd
    output_even = along.chips(after(w_output, *token_odd, packed_odd))
    early = packed_parts[-1]
    gate_cols = lax.all_gather(after(shared_gate, early), "exp", axis=0, tiled=True)
    lift_cols = lax.all_gather(after(shared_up, early), "exp", axis=0, tiled=True)
    drop_rows = lax.all_gather(after(shared_down, early), "exp", axis=1, tiled=True)
    grad_even = along.chips(out_grad)

    everything = slice(None)
    block_rows = width // n_exp
    plan = []
    for h in range(2):
        for j in range(n_exp):
            for k in range(chips):

                def where(ref, h=h, j=j, k=k):
                    return (ref[0] ^ j) * n_seq + (ref[1] ^ (2 * k + h))

                plan.append(
                    (
                        h,
                        (j, k, slice(0, gain_rows)),
                        0,
                        lambda ref, where=where: (span(where(ref), gain_rows), everything),
                    )
                )
                plan.append(
                    (
                        h,
                        (j, k, slice(gain_rows, gain_rows + 16)),
                        1,
                        lambda ref, where=where: (where(ref),),
                    )
                )
    down_full, extra_all = arrange(
        index,
        [packed_even, packed_odd],
        [(width, columns), (n_exp * n_seq, 16, columns)],
        plan,
    )
    gain_first = extra_all[:, 0, :gain_rows].reshape(1, width).astype(F32)
    gain_second = extra_all[:, 0, gain_rows : 2 * gain_rows].reshape(1, width).astype(F32)
    latent_wide = (
        extra_all[:, 0, 2 * gain_rows : 2 * gain_rows + latent_rows_local]
        .reshape(1, R)
        .astype(F32)
    )
    route_all = jnp.concatenate(
        [packed_even[0, :, gain_rows + 1 :], packed_odd[0, :, gain_rows + 1 :]], axis=0
    )[:, :lines, : 4 * count]
    route_all = route_all.reshape(n_seq, lines, 4, count).transpose(0, 2, 1, 3)
    route_all = route_all.reshape(n_seq, 4 * lines, count).astype(F32)
    route_all = jnp.concatenate(
        [
            route_all[:, :TOP],
            route_all[:, TOP : 2 * TOP]
            + route_all[:, 2 * TOP : 3 * TOP]
            + route_all[:, 3 * TOP :],
        ],
        axis=1,
    )
    up_rows = w_kv_up.shape[0]
    query_width = w_query.shape[1]
    (up_cols,) = arrange(
        index,
        [first_all],
        [(R, w_kv_up.shape[1])],
        [
            (
                0,
                (
                    slice((j * ratio + g) * up_rows, (j * ratio + g + 1) * up_rows),
                    slice(query_width, query_width + slim),
                ),
                0,
                lambda ref, j=j, g=g: (
                    slice(j * up_rows, (j + 1) * up_rows),
                    slice(g * slim, (g + 1) * slim),
                ),
            )
            for j in range(n_exp)
            for g in range(ratio)
        ],
    )
    positions = jnp.concatenate(
        [(seq ^ r) * count + jnp.arange(count, dtype=jnp.int32) for r in order]
    )
    row_position, column_position = positions[None, :], positions[:, None]
    cosine_table, sine_table = rope_tables(positions, DR)
    cosine_wide = jnp.concatenate([cosine_table, cosine_table], axis=1)
    sine_wide = jnp.concatenate([-sine_table, sine_table], axis=1)
    normed_one, latent_all, latent_raw, query_heads, key_heads, value_heads = project(
        token_blocks,
        gain_first,
        first_all,
        down_full,
        latent_wide,
        up_cols,
        cosine_wide,
        sine_wide,
        heads,
    )
    output_even = jnp.concatenate([after(x, normed_one) for x in output_even], axis=0)
    result, logsum = attend(
        query_heads, key_heads, value_heads, row_position, column_position, factor
    )

    output_parts = across.corners(output_even, result, *grad_even[1:])
    result_even = along.chips(result)
    (output_even,) = arrange(
        index,
        [part[2] for part in output_parts],
        [(H * DV // 2, width)],
        [
            (
                n,
                everything,
                0,
                lambda ref, j=j, at=at, x=x: (
                    slice(at, at + x.shape[0]),
                    span(ref[0] ^ j, block_rows),
                ),
            )
            for n, (j, at, x) in enumerate(output_parts)
        ],
    )
    output_odd = swap(output_even, "seq", 1)

    grad_even, grad_odd = along.pair([after(x, result) for x in grad_even])

    column = jnp.stack(
        [
            ((other * n_seq + seq) * pieces + i) // parts_per
            for i in range(pieces)
            for other in range(n_exp)
        ]
    )
    kinds = n_exp * pieces
    named = route_all[:, None, :TOP, :].astype(jnp.int32) == column[None, :, None, None]
    matched = jnp.any(named, axis=2)
    match_weight = jnp.sum(jnp.where(named, route_all[:, None, TOP:, :], 0.0), axis=2)
    earlier = (jnp.arange(count)[:, None] < jnp.arange(count)[None, :]).astype(BF)
    rank = jnp.dot(matched.astype(BF), earlier, preferred_element_type=F32).astype(jnp.int32)
    chosen = (rank[:, :, None, :] == jnp.arange(CAP, dtype=jnp.int32)[None, None, :, None]) & (
        matched[:, :, None, :]
    )
    select = chosen.astype(BF).reshape(n_seq, kinds * CAP, count)
    weighted = jnp.where(chosen, match_weight[:, :, None, :], 0.0).reshape(
        n_seq, kinds * CAP, count
    )
    slot_weight = jnp.sum(weighted, axis=2, keepdims=True)
    weighted_high = weighted.astype(BF)
    weighted_low = (weighted - weighted_high.astype(F32)).astype(BF)

    def give(rows):
        return lax.all_to_all(rows, "exp", split_axis=0, concat_axis=0, tiled=True)

    (grad_rows,) = arrange(
        index,
        [grad_even, grad_odd],
        [(length, width)],
        [
            (h, everything, 0, lambda ref, h=h: (slice(h * half, (h + 1) * half), everything))
            for h in range(2)
        ],
    )
    send_cots = dispatch(select, grad_rows, slot_weight, pieces)
    received_grad = [give(send_cots[0])]
    received_grad += [give(after(rows, *result_even[1:])) for rows in send_cots[1:]]

    gathered = (gate_cols, lift_cols, drop_rows)
    result_even = [after(x, *send_cots, *gathered) for x in result_even]
    result_blocks = result_even + [swap(x, "seq", 1) for x in result_even]
    normed_two, residual = add_norm(
        token_blocks,
        [after(result_blocks[0], received_grad[0])] + result_blocks[1:],
        output_even,
        output_odd,
        gain_second,
    )
    inverse_two = inverse_rms(residual)
    send_rows = dispatch(select, normed_two, None, pieces)
    received = [give(after(send_rows[0], *received_grad))]


    shared_rows = after(normed_two, *send_rows)
    shared_hidden, sgate_grad, sup_grad = shared(
        shared_rows, grad_rows, gate_cols, lift_cols, drop_rows
    )
    received[0] = after(received[0], shared_hidden)
    received += [give(after(rows, received[0])) for rows in send_rows[1:]]

    slot_rows = n_exp * n_seq * CAP
    pairs = []
    results_back, grads_back, kept = [], [], []
    for i in range(pieces):
        rows = received[i].reshape(slot_rows, width)
        cots = received_grad[i].reshape(slot_rows, width)
        expert_result, input_grad, *saved = expert(
            rows, cots, expert_gate, expert_up, expert_down, i
        )
        grads_back.append(give(input_grad.reshape(n_exp, n_seq * CAP, width)))
        results_back.append(expert_result.reshape(n_exp, n_seq * CAP, width))
        kept.append((rows, cots, *saved))
    two_products = [(sgate_grad, gate_cols, True), (sup_grad, lift_cols, True)]
    expert_grads = expert_weights(
        after(kept[0][0], input_grad), *kept[0][1:], 0, pieces, None
    )
    gate_part, lift_part, drop_part = expert_weights(
        after(shared_rows, input_grad), grad_rows, shared_hidden, sgate_grad, sup_grad, 0, 1, None, BF
    )
    select = after(select, *expert_grads, gate_part, lift_part, drop_part)
    two_odd = combine(1, [select], grads_back, two_products, BF)
    two_even = combine(0, [select], grads_back, two_products, F32)
    two_blocks = along.begin(two_even, two_odd)
    back = []
    for i in range(pieces):
        back.append(give(after(results_back[i], *(two_blocks if i == 0 else expert_grads))))
        if i:
            expert_grads = expert_weights(
                after(kept[i][0], back[0]), *kept[i][1:], i, pieces, expert_grads
            )
    results_back = back
    expert_gate_grad, expert_up_grad, expert_down_grad = expert_grads
    (own_heads,) = arrange(
        index,
        [after(result_blocks[0], *two_blocks)] + result_blocks[1:],
        [(count, H * DV)],
        [
            (
                p,
                (slice(p * count, (p + 1) * count), everything),
                0,
                lambda ref, p=p: (everything, slice(p * heads * DV, (p + 1) * heads * DV)),
            )
            for p in range(n_seq)
        ],
    )
    two_grad = along.finish(two_blocks, *expert_grads, own_heads)
    gate_part, lift_part, drop_part = [
        after(x[0], *two_blocks) for x in (gate_part, lift_part, drop_part)
    ]
    gate_out, lift_out, drop_out = sum_exp(gate_part, 0), sum_exp(lift_part, 0), sum_exp(drop_part, 1)

    residual_norm_grad, second_terms = norm_back(
        two_grad, residual, inverse_two, gain_second
    )
    residual_grad = out_grad.astype(F32) + residual_norm_grad
    residual_half = residual_grad.astype(BF)
    even_heads = dot_t(residual_half, output_even).astype(BF)
    odd_heads = dot_t(residual_half, output_odd).astype(BF)
    wide = heads * DV
    pairs = [
        jnp.stack([even_heads[:, k * wide : (k + 1) * wide], odd_heads[:, k * wide : (k + 1) * wide]])
        for k in range(chips)
    ]
    stacks = pairs
    pairs = [pairs[0]] + [along.send(pairs[k], 2 * k) for k in range(1, chips)]
    other_half = swap(jnp.stack([pair[1] for pair in pairs]), "seq", 1)
    attention_grad = jnp.concatenate(
        [jnp.stack([pair[0] for pair in pairs]), other_half], axis=0
    ).reshape(length, wide)
    mine = lax.axis_index("exp")
    late = Lane("exp", 3)
    attention_parts = late.others(after(own_heads, attention_grad))
    column_blocks = [
        lax.dynamic_slice_in_dim(residual_half, (mine ^ j) * block_rows, block_rows, 1)
        for j in range(n_exp)
    ]
    column_blocks = [column_blocks[0]] + [
        late.send(column_blocks[j], j) for j in range(1, n_exp)
    ]

    out_products = [(shared_hidden, drop_rows, False)]
    out_masks = [weighted_high, weighted_low]
    out_masks = [after(mask, *stacks, *pairs[1:]) for mask in out_masks]
    out_odd = combine(1, out_masks, results_back, out_products, BF)
    out_even = combine(0, out_masks, results_back, out_products, F32)
    out_blocks = along.begin(out_even, out_odd)
    output_got = [along.send(out_blocks[k], 2 * k) for k in range(chips - 1, 0, -1)]

    query_in_grad, kv_grad, latent_part, latent_sum = attend_back(
        query_heads,
        key_heads,
        value_heads,
        result,
        after(attention_grad, *out_blocks),
        logsum,
        row_position,
        column_position,
        cosine_wide,
        -sine_wide,
        up_cols,
        latent_all,
        latent_wide,
        factor,
    )
    query_in_grad = after(query_in_grad, *output_got)
    one_odd, odd_sum = query_back(1, query_in_grad, first_all, normed_one, gain_first, BF)
    one_even, even_sum = query_back(0, query_in_grad, first_all, normed_one, gain_first, F32)
    sums = jnp.concatenate(
        [
            (odd_sum + even_sum).reshape(n_exp, n_seq, gain_rows),
            jnp.sum(second_terms, axis=0).reshape(n_exp, n_seq, gain_rows),
            latent_sum.reshape(n_exp, n_seq, latent_rows_local),
        ],
        axis=2,
    )
    many = sums.shape[2]
    turn = (seq ^ jnp.array(order))[:, None] == jnp.arange(n_seq)[None, :]
    sums = jnp.einsum("ps,esw->pew", turn.astype(F32), sums, precision=lax.Precision.HIGHEST)
    sums = jnp.pad(
        sums.reshape(n_seq, 1, n_exp * many), ((0, 0), (0, 15), (0, columns - n_exp * many))
    )
    latent_part = jnp.concatenate([latent_part.reshape(n_seq, count, columns), sums], axis=1)
    latent_part = latent_part.reshape(n_seq * (count + 16), columns)
    output_part = t_dot(
        jnp.concatenate([after(x, query_in_grad) for x in attention_parts], axis=0),
        jnp.concatenate([after(x, query_in_grad) for x in column_blocks], axis=0),
    )
    output_blocks = along.begin(output_part[: H * DV // 2], output_part[H * DV // 2 :])
    latent_grad = along.scatter(
        latent_part[: chips * (count + 16)], latent_part[chips * (count + 16) :]
    )
    one_blocks = along.begin(one_even, one_odd)
    one_got = [along.send(one_blocks[k], 2 * k) for k in range(chips - 1, 0, -1)]
    up_part = t_dot(after(latent_all, *one_blocks), kv_grad).astype(BF)
    query_part = t_dot(after(normed_one, *one_blocks), query_in_grad).astype(BF)
    up_out = sum_exp(up_part, 0)
    query_out = sum_exp(query_part, 0)
    sums = latent_grad[count, : n_exp * many].reshape(n_exp, 1, many)
    latent_grad = latent_grad[:count]
    latent_raw_grad, _ = norm_back(
        latent_grad[:, :R], latent_raw[:count], inverse_rms(latent_raw[:count]), latent_wide
    )
    down_rows = jnp.concatenate(
        [
            latent_raw_grad,
            rotate(latent_grad[:, R:], cosine_table[:count], -sine_table[:count]),
        ],
        axis=1,
    ).astype(BF)
    wide_got = [free.send(output_blocks[k], 2 * k) for k in range(chips - 1, 0, -1)]
    down_even, down_odd = free.pair(
        [after(x, *one_got, *wide_got) for x in free.chips(down_rows)]
    )
    down_part = down_weights(index, normed_one, down_even, down_odd, n_exp, n_seq, gain_rows)
    down_part = jnp.concatenate(
        [
            down_part,
            jnp.pad(sums, ((0, 0), (0, 15), (0, columns - many))),
        ],
        axis=1,
    )
    down_sum = lax.dynamic_index_in_dim(down_part, mine, 0, keepdims=False)
    for j in range(1, n_exp):
        piece = lax.dynamic_index_in_dim(down_part, mine ^ j, 0, keepdims=False).astype(BF)
        down_sum = down_sum + swap(piece, "exp", j).astype(F32)
    down_out = down_sum[:gain_rows]
    small = down_sum[gain_rows, :many]
    first_out = small[:gain_rows] + jnp.sum(
        w_kv_down.astype(F32) * down_out, axis=1
    ) / norm_gain.astype(F32)

    output = residual + out_blocks[0]
    for block in output_got:
        output = output + after(block, *one_blocks).astype(F32)
    output = output.astype(BF)
    output_out = output_blocks[0]
    for block in wide_got:
        output_out = output_out + block.astype(F32)
    one_grad = one_blocks[0]
    for block in one_got:
        block = after(block, up_part, query_part, gate_out, lift_out, drop_out)
        one_grad = one_grad + block.astype(F32)
    down_back = dot_t(down_rows, down_full)
    token_wide = tokens.astype(F32)
    token_norm_grad, _ = norm_back(
        one_grad + down_back, token_wide, inverse_rms(token_wide), gain_first
    )
    tokens_grad = (residual_grad + token_norm_grad).astype(BF)
    return (
        output,
        tokens_grad,
        first_out,
        query_out,
        down_out,
        small[2 * gain_rows : many],
        up_out,
        output_out,
        small[gain_rows : 2 * gain_rows],
        gate_out,
        lift_out,
        drop_out,
        expert_gate_grad,
        expert_up_grad,
        expert_down_grad,
    )


def solution(mesh):
    rows = P(("exp", "seq"), None)
    line = P(("exp", "seq"))
    grid = P("exp", "seq")
    turned = P("seq", "exp")
    part = P(("exp", "seq"), None, None)
    return jax.shard_map(
        shards,
        mesh=mesh,
        in_specs=(
            rows,
            rows,
            rows,
            line,
            grid,
            rows,
            line,
            grid,
            turned,
            line,
            grid,
            grid,
            turned,
            part,
            part,
            part,
            rows,
        ),
        out_specs=(
            rows,
            rows,
            line,
            grid,
            rows,
            line,
            grid,
            turned,
            line,
            grid,
            grid,
            turned,
            part,
            part,
            part,
        ),
        check_vma=False,
    )
```

```python
import math

import jax
import jax.numpy as jnp
from jax import lax
from jax.experimental import pallas as pl
from jax.experimental.pallas import tpu as pltpu
from jax.sharding import PartitionSpec as P

H = 16
DN = 128
DR = 64
DV = 128
R = 512
EXPERTS = 64
TOP = 6
CAP = 16


eps_norm = 1e-06
rope_base = 50000.0
BF = jnp.bfloat16
F32 = jnp.float32


def dot(a, b):
    return jnp.dot(a, b, preferred_element_type=F32)


def dot_t(a, b):
    return lax.dot_general(a, b, (((1,), (1,)), ((), ())), preferred_element_type=F32)


def t_dot(a, b):
    return lax.dot_general(a, b, (((0,), (0,)), ((), ())), preferred_element_type=F32)


def rope_tables(positions, width):
    middle = width // 2
    frequency = rope_base ** (-(jnp.arange(middle, dtype=F32) * 2.0 / width))
    angles = positions.astype(F32)[:, None] * frequency[None, :]
    return (jnp.cos(angles), jnp.sin(angles))


def rotate(values, cosine_table, sine_table):
    middle = values.shape[-1] // 2
    leading = values[..., :middle]
    trailing = values[..., middle:]
    return jnp.concatenate(
        [
            leading * cosine_table - trailing * sine_table,
            trailing * cosine_table + leading * sine_table,
        ],
        axis=-1,
    )


def silu_slope(gate_values):
    sigmoid = jax.nn.sigmoid(gate_values)
    return sigmoid * (1.0 + gate_values * (1.0 - sigmoid))


def norm_back(dy, v, inverse, gain):
    hat = v * inverse
    scaled = dy * gain
    dv = inverse * (scaled - hat * jnp.mean(scaled * hat, axis=-1, keepdims=True))
    return dv, dy * hat


def inverse_rms(v):
    return lax.rsqrt(jnp.mean(v * v, axis=-1, keepdims=True) + eps_norm)


LIMIT = 56 * 1024 * 1024
LIGHT = pl.CostEstimate(flops=0, transcendentals=0, bytes_accessed=0)
ANY = pl.BlockSpec(memory_space=pl.ANY)
SCALARS = pl.BlockSpec(memory_space=pltpu.SMEM)


def whole(shape):
    return pl.BlockSpec(shape, lambda *grid: (0,) * len(shape))


def arrange(index, blocks, outs, plan):
    def kernel(index_ref, *refs):
        sources = refs[: len(blocks)]
        targets = refs[len(blocks) :]
        for block, source, out, target in plan:
            targets[out][target(index_ref)] = sources[block][source]

    return pl.pallas_call(
        kernel,
        out_shape=[jax.ShapeDtypeStruct(s, BF) for s in outs],
        in_specs=[SCALARS] + [pl.BlockSpec(memory_space=pltpu.VMEM)] * len(blocks),
        out_specs=[pl.BlockSpec(memory_space=pltpu.VMEM)] * len(outs),
        compiler_params=pltpu.CompilerParams(vmem_limit_bytes=LIMIT),
        cost_estimate=LIGHT,
        name="arrange",
    )(index, *blocks)


def span(start, size):
    return pl.ds(pl.multiple_of(start * size, size), size)


def turned(v, cosine, sine):
    middle = v.shape[1] // 2
    return v * cosine + jnp.concatenate([v[:, middle:], v[:, :middle]], axis=1) * sine


def project(token_blocks, gain, w_first, w_down, latent_gain, w_up, cosine, sine, heads):
    count, width = token_blocks[0].shape
    chips = len(token_blocks) // 2
    half = chips * count
    wide = DN + DR
    columns = heads * wide

    def kernel(g_ref, wd_ref, lg_ref, wu_ref, c_ref, s_ref, *refs):
        tokens, w_ref = refs[: 2 * chips], refs[2 * chips]
        n_ref, l_ref, r_ref, q_ref, k_ref, v_ref, x_ref = refs[2 * chips + 1 :]
        for h in range(2):

            @pl.when(pl.program_id(0) == h)
            def _():
                for k in range(chips):
                    x_ref[k * count : (k + 1) * count] = tokens[h * chips + k][...]

        x = x_ref[...].astype(F32)
        inverse = lax.rsqrt(jnp.mean(x * x, axis=1, keepdims=True) + eps_norm)
        n_ref[...] = (x * inverse * g_ref[...]).astype(BF)
        down = dot(n_ref[...], wd_ref[...])
        raw = down[:, :R]
        r_ref[...] = raw
        inverse = lax.rsqrt(jnp.mean(raw * raw, axis=1, keepdims=True) + eps_norm)
        l_ref[...] = (raw * inverse * lg_ref[...]).astype(BF)
        query = dot(n_ref[...], w_ref[:, :columns])
        up = dot(l_ref[...], wu_ref[...]).astype(BF)
        cosine, sine = c_ref[...], s_ref[...]
        zeros = jnp.zeros((half, 256 - wide), BF)
        rope = jnp.concatenate([turned(down[:, R : R + DR], cosine, sine).astype(BF), zeros], axis=1)
        for n in range(heads):
            own = query[:, n * wide : (n + 1) * wide]
            q_ref[n, :, :DN] = own[:, :DN].astype(BF)
            q_ref[n, :, DN:] = jnp.concatenate(
                [turned(own[:, DN:], cosine, sine).astype(BF), zeros], axis=1
            )
            k_ref[n, :, :DN] = up[:, n * (DN + DV) : n * (DN + DV) + DN]
            k_ref[n, :, DN:] = rope
            v_ref[n] = up[:, n * (DN + DV) + DN : (n + 1) * (DN + DV)]

    def rows(w):
        return pl.BlockSpec((half, w), lambda i: (i, 0))

    def head_rows(w):
        return pl.BlockSpec((heads, half, w), lambda i: (0, i, 0))

    length = 2 * half
    return pl.pallas_call(
        kernel,
        grid=(2,),
        in_specs=[
            whole((1, width)),
            whole(w_down.shape),
            whole((1, R)),
            whole(w_up.shape),
            rows(DR),
            rows(DR),
        ]
        + [whole((count, width))] * (2 * chips)
        + [whole(w_first.shape)],
        out_specs=[rows(width), rows(R), rows(R), head_rows(256), head_rows(256), head_rows(DV)],
        out_shape=[
            jax.ShapeDtypeStruct((length, width), BF),
            jax.ShapeDtypeStruct((length, R), BF),
            jax.ShapeDtypeStruct((length, R), F32),
            jax.ShapeDtypeStruct((heads, length, 256), BF),
            jax.ShapeDtypeStruct((heads, length, 256), BF),
            jax.ShapeDtypeStruct((heads, length, DV), BF),
        ],
        scratch_shapes=[pltpu.VMEM((half, width), BF)],
        compiler_params=pltpu.CompilerParams(vmem_limit_bytes=LIMIT),
        cost_estimate=LIGHT,
        name="project",
    )(gain, w_down, latent_gain, w_up, cosine, sine, *token_blocks, w_first)


def query_back(base, query_grad, w_first, normed, gain, dtype):
    length, columns = query_grad.shape
    half = length // 2
    width = normed.shape[1]
    tile = 512

    def kernel(q_ref, n_ref, g_ref, w_ref, o_ref, t_ref):
        part = dot_t(q_ref[...], w_ref[:, :columns])
        o_ref[...] = part.astype(dtype)
        product = part * n_ref[...].astype(F32)
        t_ref[...] = jnp.sum(product, axis=0, keepdims=True) / g_ref[...]

    return pl.pallas_call(
        kernel,
        grid=(width // tile,),
        in_specs=[
            pl.BlockSpec((half, columns), lambda i: (base, 0)),
            pl.BlockSpec((half, tile), lambda i: (base, i)),
            pl.BlockSpec((1, tile), lambda i: (0, i)),
            pl.BlockSpec((tile, w_first.shape[1]), lambda i: (i, 0)),
        ],
        out_specs=[
            pl.BlockSpec((half, tile), lambda i: (0, i)),
            pl.BlockSpec((1, tile), lambda i: (0, i)),
        ],
        out_shape=[
            jax.ShapeDtypeStruct((half, width), dtype),
            jax.ShapeDtypeStruct((1, width), F32),
        ],
        compiler_params=pltpu.CompilerParams(vmem_limit_bytes=LIMIT),
        cost_estimate=LIGHT,
        name="query_back",
    )(query_grad, normed, gain, w_first)


def attend(query, key, value, row_position, column_position, factor):
    heads, length, _ = query.shape
    tile = 256

    def kernel(q_ref, k_ref, v_ref, row_ref, column_ref, o_ref, s_ref):
        allowed = column_ref[...] <= row_ref[...]
        for n in range(heads):
            scores = dot_t(k_ref[n], q_ref[n]) * factor
            exponent = jnp.where(allowed, jnp.exp(jnp.where(allowed, scores, -1e30)), 0.0)
            total = jnp.sum(exponent, axis=0, keepdims=True)
            probs = (exponent / total).astype(BF)
            o_ref[:, n * DV : (n + 1) * DV] = t_dot(v_ref[n], probs).T.astype(BF)
            s_ref[n : n + 1, :] = jnp.log(total)

    return pl.pallas_call(
        kernel,
        grid=(length // tile,),
        in_specs=[
            pl.BlockSpec((heads, tile, 256), lambda i: (0, i, 0)),
            whole(key.shape),
            whole(value.shape),
            pl.BlockSpec((1, tile), lambda i: (0, i)),
            whole((length, 1)),
        ],
        out_specs=[
            pl.BlockSpec((tile, heads * DV), lambda i: (i, 0)),
            pl.BlockSpec((heads, tile), lambda i: (0, i)),
        ],
        out_shape=[
            jax.ShapeDtypeStruct((length, heads * DV), BF),
            jax.ShapeDtypeStruct((heads, length), F32),
        ],
        compiler_params=pltpu.CompilerParams(vmem_limit_bytes=LIMIT),
        cost_estimate=LIGHT,
        name="attend",
    )(query, key, value, row_position, column_position)


def attend_back(query, key, value, result, result_grad, logsum, row_position, column_position, cosine, sine, w_up, latent_all, latent_gain, factor, columns):
    heads, length, _ = query.shape
    tile = 256
    steps = length // tile
    wide = DN + DR

    def kernel(q_ref, k_ref, v_ref, o_ref, do_ref, ls_ref, row_ref, column_ref, c_ref, s_ref, wu_ref, l_ref, lg_ref, dq_ref, kv_ref, lp_ref, t_ref, dk_acc, dv_acc, kt):
        step = pl.program_id(0)

        @pl.when(step == 0)
        def _():
            dk_acc[...] = jnp.zeros_like(dk_acc)
            dv_acc[...] = jnp.zeros_like(dv_acc)
            for n in range(heads):
                kt[n] = k_ref[n].T

        allowed = column_ref[...] <= row_ref[...]
        cosine, sine = c_ref[...], s_ref[...]
        parts = []
        for n in range(heads):
            q = q_ref[n]
            grad = do_ref[:, n * DV : (n + 1) * DV]
            scores = jnp.where(allowed, dot_t(k_ref[n], q) * factor, -1e30)
            probs = jnp.exp(scores - ls_ref[n : n + 1, :])
            dv_acc[n] += dot(probs.astype(BF), grad)
            product = grad.astype(F32) * o_ref[:, n * DV : (n + 1) * DV].astype(F32)
            row_dot = jnp.sum(product.T, axis=0, keepdims=True)
            probs_grad = dot_t(v_ref[n], grad)
            score_grad = (probs * (probs_grad - row_dot) * factor).astype(BF)
            dk_acc[n] += dot(score_grad, q)
            query_grad = dot(kt[n], score_grad).T.astype(BF)
            parts.append(query_grad[:, :DN])
            parts.append(turned(query_grad[:, DN:wide].astype(F32), cosine, sine).astype(BF))
        dq_ref[...] = jnp.concatenate(parts, axis=1)

        @pl.when(step == steps - 1)
        def _():
            rope = jnp.zeros((length, DR), F32)
            for n in range(heads):
                key_grad = dk_acc[n].astype(BF)
                value_grad = dv_acc[n].astype(BF)
                base = n * (DN + DV)
                kv_ref[:, base : base + DN] = key_grad[:, :DN]
                kv_ref[:, base + DN : base + DN + DV] = value_grad
                rope = rope + key_grad[:, DN:wide].astype(F32)
            latent = dot_t(kv_ref[...], wu_ref[...])
            lp_ref[:, :R] = latent
            lp_ref[:, R : R + DR] = rope
            lp_ref[:, R + DR :] = jnp.zeros((length, columns - R - DR), F32)
            t_ref[...] = jnp.sum(
                latent * l_ref[...].astype(F32), axis=0, keepdims=True
            ) / lg_ref[...]

    return pl.pallas_call(
        kernel,
        grid=(steps,),
        in_specs=[
            pl.BlockSpec((heads, tile, 256), lambda i: (0, i, 0)),
            whole(key.shape),
            whole(value.shape),
            pl.BlockSpec((tile, heads * DV), lambda i: (i, 0)),
            pl.BlockSpec((tile, heads * DV), lambda i: (i, 0)),
            pl.BlockSpec((heads, tile), lambda i: (0, i)),
            pl.BlockSpec((1, tile), lambda i: (0, i)),
            whole((length, 1)),
            pl.BlockSpec((tile, DR), lambda i: (i, 0)),
            pl.BlockSpec((tile, DR), lambda i: (i, 0)),
            whole(w_up.shape),
            whole((length, R)),
            whole((1, R)),
        ],
        out_specs=[
            pl.BlockSpec((tile, heads * wide), lambda i: (i, 0)),
            whole((length, heads * (DN + DV))),
            whole((length, columns)),
            whole((1, R)),
        ],
        out_shape=[
            jax.ShapeDtypeStruct((length, heads * wide), BF),
            jax.ShapeDtypeStruct((length, heads * (DN + DV)), BF),
            jax.ShapeDtypeStruct((length, columns), F32),
            jax.ShapeDtypeStruct((1, R), F32),
        ],
        scratch_shapes=[
            pltpu.VMEM((heads, length, 256), F32),
            pltpu.VMEM((heads, length, DV), F32),
            pltpu.VMEM((heads, 256, length), BF),
        ],
        compiler_params=pltpu.CompilerParams(vmem_limit_bytes=LIMIT),
        cost_estimate=LIGHT,
        name="attend_back",
    )(query, key, value, result, result_grad, logsum, row_position, column_position, cosine, sine, w_up, latent_all, latent_gain)


def add_norm(token_blocks, blocks, w_even, w_odd, gain):
    count, width = token_blocks[0].shape
    many = len(blocks)
    chips = many // 2
    half = chips * count
    length = count * many
    depth = blocks[0].shape[1]

    def kernel(we_ref, wo_ref, g_ref, *refs):
        parts, tokens = refs[:many], refs[many : 2 * many]
        n_ref, r_ref, x_ref, a_ref = refs[2 * many :]
        for q in range(many):
            for p in range(chips):
                other = p ^ (q % chips)
                a_ref[p * count : (p + 1) * count, q * depth : (q + 1) * depth] = parts[q][
                    other * count : (other + 1) * count
                ]
        for h in range(2):

            @pl.when(pl.program_id(0) == h)
            def _():
                for k in range(chips):
                    x_ref[k * count : (k + 1) * count] = tokens[h * chips + k][...]

        middle = chips * depth
        total = dot(a_ref[:, :middle], we_ref[...]) + dot(a_ref[:, middle:], wo_ref[...])
        total = total + x_ref[...].astype(F32)
        inverse = lax.rsqrt(jnp.mean(total * total, axis=1, keepdims=True) + eps_norm)
        n_ref[...] = (total * inverse * g_ref[...]).astype(BF)

        @pl.when(pl.program_id(0) == 0)
        def _():
            r_ref[...] = total[:count]

    def source(q):
        return pl.BlockSpec((half, depth), lambda i: (i ^ (q // chips), 0))

    return pl.pallas_call(
        kernel,
        grid=(2,),
        in_specs=[whole(w_even.shape), whole(w_odd.shape), whole((1, width))]
        + [source(q) for q in range(many)]
        + [whole((count, width))] * many,
        out_specs=[pl.BlockSpec((half, width), lambda i: (i, 0)), whole((count, width))],
        out_shape=[
            jax.ShapeDtypeStruct((length, width), BF),
            jax.ShapeDtypeStruct((count, width), F32),
        ],
        scratch_shapes=[pltpu.VMEM((half, width), BF), pltpu.VMEM((half, many * depth), BF)],
        compiler_params=pltpu.CompilerParams(vmem_limit_bytes=LIMIT),
        cost_estimate=LIGHT,
        name="add_norm",
    )(w_even, w_odd, gain, *blocks, *token_blocks)


def expert(rows, cots, gate, up, down, piece):
    count, width = rows.shape
    units = gate.shape[2]
    tile = min(512, count)
    step = 256
    full = units // step
    rest = units % step
    spans = [(n * step, step) for n in range(full)] + ([(full * step, rest)] if rest else [])

    def kernel(x_ref, c_ref, gate_hbm, up_hbm, down_hbm, res_ref, in_ref, h_ref, gg_ref, ug_ref, wg, wu, wd, acc_r, acc_i, sems):
        first = pl.program_id(0) == 0

        def copies(n, start, size):
            span = pl.ds(start, size)
            return [
                pltpu.make_async_copy(gate_hbm.at[piece, :, span], wg.at[:, span], sems.at[0, n]),
                pltpu.make_async_copy(up_hbm.at[piece, :, span], wu.at[:, span], sems.at[1, n]),
                pltpu.make_async_copy(down_hbm.at[piece, span, :], wd.at[span, :], sems.at[2, n]),
            ]

        @pl.when(first)
        def _():
            for n, (start, size) in enumerate(spans):
                for copy in copies(n, start, size):
                    copy.start()

        acc_r[...] = jnp.zeros_like(acc_r)
        acc_i[...] = jnp.zeros_like(acc_i)

        def chunk(n, start, size):
            @pl.when(first)
            def _():
                for copy in copies(n, start, size):
                    copy.wait()

            span = pl.ds(start, size)
            x, c = x_ref[...], c_ref[...]
            w_gate, w_up, w_down = wg[:, span], wu[:, span], wd[span, :]
            g = dot(x, w_gate)
            u = dot(x, w_up)
            hidden_grad = dot_t(c, w_down)
            s = jax.nn.sigmoid(g)
            silu = g * s
            hidden = (silu * u).astype(BF)
            gate_grad = (hidden_grad * u * (s * (1.0 + g * (1.0 - s)))).astype(BF)
            up_grad = (hidden_grad * silu).astype(BF)
            h_ref[:, span] = hidden
            gg_ref[:, span] = gate_grad
            ug_ref[:, span] = up_grad
            acc_r[...] += dot(hidden, w_down)
            acc_i[...] += dot_t(gate_grad, w_gate) + dot_t(up_grad, w_up)

        if full:

            @pl.loop(0, full)
            def _(n):
                chunk(n, pl.multiple_of(n * step, step), step)

        if rest:
            chunk(full, full * step, rest)
        res_ref[...] = acc_r[...].astype(BF)
        in_ref[...] = acc_i[...].astype(BF)

    def block(w):
        return pl.BlockSpec((tile, w), lambda i: (i, 0))

    def array(w):
        return jax.ShapeDtypeStruct((count, w), BF)

    return pl.pallas_call(
        kernel,
        grid=(count // tile,),
        in_specs=[block(width), block(width), ANY, ANY, ANY],
        out_specs=[block(width), block(width), block(units), block(units), block(units)],
        out_shape=[array(width), array(width), array(units), array(units), array(units)],
        scratch_shapes=[
            pltpu.VMEM((width, units), BF),
            pltpu.VMEM((width, units), BF),
            pltpu.VMEM((units, width), BF),
            pltpu.VMEM((tile, width), F32),
            pltpu.VMEM((tile, width), F32),
            pltpu.SemaphoreType.DMA((3, len(spans))),
        ],
        compiler_params=pltpu.CompilerParams(vmem_limit_bytes=LIMIT),
        cost_estimate=LIGHT,
        name="expert",
    )(rows, cots, gate, up, down)


def shared(rows, cots, gate, up, down):
    count, width = rows.shape
    units = gate.shape[1]
    tile = 256

    def kernel(x_ref, c_ref, wg_ref, wu_ref, wd_ref, h_ref, gg_ref, ug_ref):
        g = dot(x_ref[...], wg_ref[...])
        u = dot(x_ref[...], wu_ref[...])
        hidden_grad = dot_t(c_ref[...], wd_ref[...])
        s = jax.nn.sigmoid(g)
        silu = g * s
        h_ref[...] = (silu * u).astype(BF)
        gg_ref[...] = (hidden_grad * u * (s * (1.0 + g * (1.0 - s)))).astype(BF)
        ug_ref[...] = (hidden_grad * silu).astype(BF)

    row = pl.BlockSpec((tile, width), lambda i: (i, 0))
    unit = pl.BlockSpec((tile, units), lambda i: (i, 0))
    return pl.pallas_call(
        kernel,
        grid=(count // tile,),
        in_specs=[row, row, whole(gate.shape), whole(up.shape), whole(down.shape)],
        out_specs=[unit] * 3,
        out_shape=[jax.ShapeDtypeStruct((count, units), BF)] * 3,
        compiler_params=pltpu.CompilerParams(vmem_limit_bytes=LIMIT),
        cost_estimate=LIGHT,
        name="shared",
    )(rows, cots, gate, up, down)


def expert_weights(rows, cots, hidden, gate_grad, up_grad, piece, pieces, earlier, dtype=F32):
    count, width = rows.shape
    units = hidden.shape[1]
    tile = 256

    def kernel(x_ref, c_ref, h_ref, gg_ref, ug_ref, *refs):
        g_ref, u_ref, d_ref = refs[-3:]
        g_ref[0] = t_dot(x_ref[...], gg_ref[...]).astype(dtype)
        u_ref[0] = t_dot(x_ref[...], ug_ref[...]).astype(dtype)
        d_ref[0] = t_dot(h_ref[...], c_ref[...]).astype(dtype)

    tall = pl.BlockSpec((1, tile, units), lambda i: (piece, i, 0))
    flat = pl.BlockSpec((1, units, tile), lambda i: (piece, 0, i))
    column = pl.BlockSpec((count, tile), lambda i: (0, i))
    kept = list(earlier or ())
    return pl.pallas_call(
        kernel,
        grid=(width // tile,),
        in_specs=[column, column] + [whole((count, units))] * 3 + [ANY] * len(kept),
        out_specs=[tall, tall, flat],
        out_shape=[
            jax.ShapeDtypeStruct((pieces, width, units), dtype),
            jax.ShapeDtypeStruct((pieces, width, units), dtype),
            jax.ShapeDtypeStruct((pieces, units, width), dtype),
        ],
        input_output_aliases={5 + n: n for n in range(len(kept))},
        compiler_params=pltpu.CompilerParams(vmem_limit_bytes=LIMIT),
        cost_estimate=LIGHT,
        name="expert_weights",
    )(rows, cots, hidden, gate_grad, up_grad, *kept)


def dispatch(select, rows, slot_weight, pieces):
    blocks, slots, count = select.shape
    width = rows.shape[1]
    others = slots // pieces // CAP

    def kernel(m_ref, x_ref, *refs):
        got = dot(m_ref[0], x_ref[...])
        if slot_weight is not None:
            got = got * refs[0][0]
        got = got.astype(BF)
        for i in range(pieces):
            for j in range(others):
                start = (i * others + j) * CAP
                refs[-pieces + i][j] = got[start : start + CAP]

    weights = [] if slot_weight is None else [slot_weight]
    out = pl.BlockSpec((others, CAP, width), lambda b: (0, b, 0))
    return pl.pallas_call(
        kernel,
        grid=(blocks,),
        in_specs=[
            pl.BlockSpec((1, slots, count), lambda b: (b, 0, 0)),
            pl.BlockSpec((count, width), lambda b: (b, 0)),
        ]
        + [pl.BlockSpec((1, slots, 1), lambda b: (b, 0, 0))] * len(weights),
        out_specs=[out] * pieces,
        out_shape=[jax.ShapeDtypeStruct((others, blocks * CAP, width), BF)] * pieces,
        compiler_params=pltpu.CompilerParams(vmem_limit_bytes=LIMIT),
        cost_estimate=LIGHT,
        name="dispatch",
    )(select, rows, *weights)


def down_weights(index, normed, down_even, down_odd, others, n_seq, gain_rows):
    length, _ = normed.shape
    half, columns = down_even.shape
    per = 128 // gain_rows

    def kernel(index_ref, n_ref, e_ref, d_ref, o_ref, part):
        part[...] = t_dot(n_ref[:half], e_ref[...]) + t_dot(n_ref[half:], d_ref[...])
        o_ref[0] = part[span(index_ref[1] % per, gain_rows)]

    return pl.pallas_call(
        kernel,
        grid_spec=pltpu.PrefetchScalarGridSpec(
            num_scalar_prefetch=1,
            grid=(others,),
            in_specs=[
                pl.BlockSpec(
                    (length, 128), lambda i, ref: (0, (i * n_seq + ref[1]) * gain_rows // 128)
                ),
                pl.BlockSpec((half, columns), lambda i, ref: (0, 0)),
                pl.BlockSpec((half, columns), lambda i, ref: (0, 0)),
            ],
            out_specs=pl.BlockSpec((1, gain_rows, columns), lambda i, ref: (i, 0, 0)),
            scratch_shapes=[pltpu.VMEM((128, columns), F32)],
        ),
        out_shape=jax.ShapeDtypeStruct((others, gain_rows, columns), F32),
        compiler_params=pltpu.CompilerParams(vmem_limit_bytes=LIMIT),
        cost_estimate=LIGHT,
        name="down_weights",
    )(index, normed, down_even, down_odd)


def output_weights(base, heads, columns, dtype):
    count, width = heads[0].shape
    wide = columns[0].shape[1]
    half = width // 2
    tile = 256
    many = len(heads)

    def kernel(*refs):
        total = 0.0
        for j in range(many):
            total = total + t_dot(refs[j][...], refs[many + j][...])
        refs[-1][...] = total.astype(dtype)

    return pl.pallas_call(
        kernel,
        grid=(half // tile,),
        in_specs=[pl.BlockSpec((count, tile), lambda i: (0, base * (half // tile) + i))] * many
        + [whole((count, wide))] * many,
        out_specs=pl.BlockSpec((tile, wide), lambda i: (i, 0)),
        out_shape=jax.ShapeDtypeStruct((half, wide), dtype),
        compiler_params=pltpu.CompilerParams(vmem_limit_bytes=LIMIT),
        cost_estimate=LIGHT,
        name="output_weights",
    )(*heads, *columns)


def combine(base, masks, returned, products, dtype):
    half = masks[0].shape[0] // 2
    slots, count = masks[0].shape[1:]
    pieces = len(returned)
    others, _, width = returned[0].shape
    many = len(masks)

    tile = 512

    def kernel(*refs):
        mask_refs, row_refs = refs[:many], refs[many : many + pieces]
        rest, out_ref = refs[many + pieces : -1], refs[-1]
        total = 0.0
        for n, (_, _, flipped) in enumerate(products):
            total = total + (dot_t if flipped else dot)(rest[2 * n][...], rest[2 * n + 1][...])
        for b in range(half):
            rows = jnp.concatenate(
                [
                    row_refs[i][j, b * CAP : (b + 1) * CAP]
                    for i in range(pieces)
                    for j in range(others)
                ],
                axis=0,
            )
            block = total[b * count : (b + 1) * count]
            for mask_ref in mask_refs:
                block = block + t_dot(mask_ref[b], rows)
            out_ref[b * count : (b + 1) * count] = block.astype(dtype)

    factors = []
    specs = []
    for left, right, flipped in products:
        factors += [left, right]
        specs.append(pl.BlockSpec((half * count, left.shape[1]), lambda t: (base, 0)))
        if flipped:
            specs.append(pl.BlockSpec((tile, right.shape[1]), lambda t: (t, 0)))
        else:
            specs.append(pl.BlockSpec((right.shape[0], tile), lambda t: (0, t)))
    return pl.pallas_call(
        kernel,
        grid=(width // tile,),
        in_specs=[pl.BlockSpec((half, slots, count), lambda t: (base, 0, 0))] * many
        + [pl.BlockSpec((others, half * CAP, tile), lambda t: (0, base, t))] * pieces
        + specs,
        out_specs=pl.BlockSpec((half * count, tile), lambda t: (0, t)),
        out_shape=jax.ShapeDtypeStruct((half * count, width), dtype),
        compiler_params=pltpu.CompilerParams(vmem_limit_bytes=LIMIT),
        cost_estimate=LIGHT,
        name="combine",
    )(*masks, *returned, *factors)


def swap(x, axis, mask):
    n = lax.axis_size(axis)
    return lax.ppermute(x, axis, [(i, i ^ mask) for i in range(n)])


def after(x, *earlier):
    return lax.optimization_barrier((x, *earlier))[0]


class Lane:
    def __init__(self, axis, depth):
        self.axis = axis
        self.depth = depth
        self.sent = []

    def send(self, x, mask):
        if len(self.sent) >= self.depth:
            x = after(x, self.sent[-self.depth])
        got = swap(x, self.axis, mask)
        self.sent.append(got)
        return got

    def chips(self, x):
        chips = lax.axis_size("seq") // 2
        return [x] + [self.send(x, 2 * k) for k in range(1, chips)]

    def group(self, x):
        return self.pair(self.chips(x))

    def pair(self, evens):
        even = stacked(evens)
        return even, swap(even, "seq", 1)

    def scatter(self, even, odd):
        return self.finish(self.begin(even, odd))

    def begin(self, even, odd):
        chips = lax.axis_size("seq") // 2
        rows = even.shape[0] // chips
        got = swap(odd.astype(BF), "seq", 1)
        blocks = [
            even[k * rows : (k + 1) * rows] + got[k * rows : (k + 1) * rows].astype(F32)
            for k in range(chips)
        ]
        return blocks[:1] + [block.astype(BF) for block in blocks[1:]]

    def finish(self, blocks, *gates):
        got = [self.send(blocks[k], 2 * k) for k in range(1, len(blocks))]
        total = blocks[0]
        for block in got:
            total = total + after(block, *gates).astype(F32)
        return total

    def corners(self, x, *gates):
        if lax.axis_size("exp") != 4:
            return [(j, 0, y) for j, y in enumerate(self.others(x))]
        middle = x.shape[0] // 2
        one, two = self.send(x, 1), self.send(x, 2)
        return [
            (0, 0, x),
            (1, 0, one),
            (2, 0, two),
            (3, 0, self.send(part(after(two, *gates), 0, middle), 1)),
            (3, middle, self.send(part(after(one, *gates), middle, middle), 2)),
        ]

    def others(self, x):
        return [x] + [self.send(x, j) for j in range(1, lax.axis_size("exp"))]

def siblings(blocks, *gates):
    got = {}
    for k in range(len(blocks) - 1, 1, -1):
        got[k] = swap(after(blocks[k], *got.values()), "seq", 1)
    gates += tuple(got.values())
    for k in range(min(2, len(blocks))):
        got[k] = swap(after(blocks[k], *gates), "seq", 1)
    return [got[k] for k in range(len(blocks))]


def stacked(blocks):
    rows, columns = blocks[0].shape
    everything = slice(None)
    (whole_array,) = arrange(
        jnp.zeros((1,), jnp.int32),
        blocks,
        [(rows * len(blocks), columns)],
        [
            (k, everything, 0, lambda ref, k=k: (slice(k * rows, (k + 1) * rows), everything))
            for k in range(len(blocks))
        ],
    )
    return whole_array


def part(x, start, rows):
    (piece,) = arrange(
        jnp.zeros((1,), jnp.int32),
        [x],
        [(rows, x.shape[1])],
        [(0, (slice(start, start + rows),), 0, lambda ref: (slice(0, rows),))],
    )
    return piece


def relative_order(count):
    chips = count // 2
    return [2 * k for k in range(chips)] + [2 * k + 1 for k in range(chips)]


def sum_exp(x, axis):
    return lax.psum_scatter(x.astype(BF), "exp", scatter_dimension=axis, tiled=True).astype(F32)


def shards(
    tokens,
    routes,
    route_weights,
    norm_gain,
    w_query,
    w_kv_down,
    latent_gain,
    w_kv_up,
    w_output,
    ffn_gain,
    shared_gate,
    shared_up,
    shared_down,
    expert_gate,
    expert_up,
    expert_down,
    out_grad,
):
    count, width = tokens.shape
    n_seq = lax.axis_size("seq")
    n_exp = lax.axis_size("exp")
    seq = lax.axis_index("seq")
    order = relative_order(n_seq)
    chips = n_seq // 2
    heads = H // n_seq
    length = count * n_seq
    half = length // 2
    pieces = expert_gate.shape[0]
    parts_per = pieces * n_seq * n_exp // EXPERTS
    factor = 1.0 / math.sqrt(DN + DR)
    gain_rows = norm_gain.shape[0]
    latent_rows_local = latent_gain.shape[0]
    along = Lane("seq", 3)
    across = Lane("exp", 3)
    free = Lane("seq", 3)

    index = jnp.stack([lax.axis_index("exp"), seq]).astype(jnp.int32)
    ratio = w_query.shape[0] // w_kv_up.shape[0]
    slim = w_kv_up.shape[1] // ratio
    columns = -(-w_kv_down.shape[1] // 128) * 128
    high = lax.reduce_precision(route_weights, 8, 7)
    middle = lax.reduce_precision(route_weights - high, 8, 7)
    low = route_weights - high - middle
    route_pack = jnp.concatenate([routes.astype(F32), high, middle, low], axis=1).astype(BF).T
    lines = route_pack.shape[0] // 4
    gains = jnp.concatenate([norm_gain, ffn_gain, latent_gain])
    packed = jnp.concatenate(
        [
            jnp.pad(w_kv_down, ((0, 0), (0, columns - R - DR))),
            jnp.pad(gains, (0, columns - gains.shape[0]))[None, :],
            jnp.pad(
                route_pack.reshape(4, lines, count).transpose(1, 0, 2).reshape(lines, 4 * count),
                ((0, 15 - lines), (0, columns - 4 * count)),
            ),
        ],
        axis=0,
    )
    packed_even = stacked(free.chips(packed))
    token_even = along.chips(tokens)
    first_all = lax.all_gather(
        jnp.concatenate(
            [
                w_query,
                jnp.concatenate(
                    [w_kv_up[:, g * slim : (g + 1) * slim] for g in range(ratio)], axis=0
                ),
            ],
            axis=1,
        ),
        "exp",
        axis=0,
        tiled=True,
    )
    packed_parts = across.others(packed_even)
    packed_even = stacked(packed_parts)
    packed_odd = swap(packed_even, "seq", 1)
    early = packed_parts[-1]
    gate_cols = lax.all_gather(after(shared_gate, early), "exp", axis=0, tiled=True)
    lift_cols = lax.all_gather(after(shared_up, early), "exp", axis=0, tiled=True)
    drop_rows = lax.all_gather(after(shared_down, early), "exp", axis=1, tiled=True)

    everything = slice(None)
    block_rows = width // n_exp
    plan = []
    deep = gain_rows + 16
    for h in range(2):
        for j in range(n_exp):
            for k in range(chips):

                def where(ref, h=h, j=j, k=k):
                    return (ref[0] ^ j) * n_seq + (ref[1] ^ (2 * k + h))

                plan.append(
                    (
                        h,
                        (
                            slice((j * chips + k) * deep, (j * chips + k) * deep + gain_rows),
                            slice(0, R + DR),
                        ),
                        0,
                        lambda ref, where=where: (span(where(ref), gain_rows), everything),
                    )
                )
                plan.append(
                    (
                        h,
                        (slice((j * chips + k) * deep + gain_rows, (j * chips + k + 1) * deep),),
                        1,
                        lambda ref, where=where: (where(ref),),
                    )
                )
    down_full, extra_all = arrange(
        index,
        [packed_even, packed_odd],
        [(width, R + DR), (n_exp * n_seq, 16, columns)],
        plan,
    )
    gain_first = extra_all[:, 0, :gain_rows].reshape(1, width).astype(F32)
    gain_second = extra_all[:, 0, gain_rows : 2 * gain_rows].reshape(1, width).astype(F32)
    latent_wide = (
        extra_all[:, 0, 2 * gain_rows : 2 * gain_rows + latent_rows_local]
        .reshape(1, R)
        .astype(F32)
    )
    route_all = jnp.concatenate(
        [
            x[: chips * deep].reshape(chips, deep, columns)[:, gain_rows + 1 :]
            for x in (packed_even, packed_odd)
        ],
        axis=0,
    )[:, :lines, : 4 * count]
    route_all = route_all.reshape(n_seq, lines, 4, count).transpose(0, 2, 1, 3)
    route_all = route_all.reshape(n_seq, 4 * lines, count).astype(F32)
    route_all = jnp.concatenate(
        [
            route_all[:, :TOP],
            route_all[:, TOP : 2 * TOP]
            + route_all[:, 2 * TOP : 3 * TOP]
            + route_all[:, 3 * TOP :],
        ],
        axis=1,
    )
    up_rows = w_kv_up.shape[0]
    query_width = w_query.shape[1]
    (up_cols,) = arrange(
        index,
        [first_all],
        [(R, w_kv_up.shape[1])],
        [
            (
                0,
                (
                    slice((j * ratio + g) * up_rows, (j * ratio + g + 1) * up_rows),
                    slice(query_width, query_width + slim),
                ),
                0,
                lambda ref, j=j, g=g: (
                    slice(j * up_rows, (j + 1) * up_rows),
                    slice(g * slim, (g + 1) * slim),
                ),
            )
            for j in range(n_exp)
            for g in range(ratio)
        ],
    )
    token_odd = {}
    for k in range(chips - 1, -1, -1):
        token_odd[k] = swap(after(token_even[k], *token_odd.values()), "seq", 1)
    token_odd = [token_odd[k] for k in range(chips)]
    token_blocks = token_even + token_odd
    output_even = free.chips(after(w_output, *token_odd, packed_odd))
    grad_even = along.chips(after(out_grad, *token_odd))

    column = jnp.stack(
        [
            ((other * n_seq + seq) * pieces + i) // parts_per
            for i in range(pieces)
            for other in range(n_exp)
        ]
    )
    kinds = n_exp * pieces
    named = route_all[:, None, :TOP, :].astype(jnp.int32) == column[None, :, None, None]
    matched = jnp.any(named, axis=2)
    match_weight = jnp.sum(jnp.where(named, route_all[:, None, TOP:, :], 0.0), axis=2)
    earlier = (jnp.arange(count)[:, None] < jnp.arange(count)[None, :]).astype(BF)
    rank = jnp.dot(matched.astype(BF), earlier, preferred_element_type=F32).astype(jnp.int32)
    chosen = (rank[:, :, None, :] == jnp.arange(CAP, dtype=jnp.int32)[None, None, :, None]) & (
        matched[:, :, None, :]
    )
    select = chosen.astype(BF).reshape(n_seq, kinds * CAP, count)
    weighted = jnp.where(chosen, match_weight[:, :, None, :], 0.0).reshape(
        n_seq, kinds * CAP, count
    )
    slot_weight = jnp.sum(weighted, axis=2, keepdims=True)
    weighted_high = weighted.astype(BF)
    weighted_low = (weighted - weighted_high.astype(F32)).astype(BF)

    positions = jnp.concatenate(
        [(seq ^ r) * count + jnp.arange(count, dtype=jnp.int32) for r in order]
    )
    row_position, column_position = positions[None, :], positions[:, None]
    cosine_table, sine_table = rope_tables(positions, DR)
    cosine_wide = jnp.concatenate([cosine_table, cosine_table], axis=1)
    sine_wide = jnp.concatenate([-sine_table, sine_table], axis=1)
    gain_first = after(gain_first, select, slot_weight, column_position)
    normed_one, latent_all, latent_raw, query_heads, key_heads, value_heads = project(
        token_blocks,
        gain_first,
        first_all,
        down_full,
        latent_wide,
        up_cols,
        cosine_wide,
        sine_wide,
        heads,
    )
    output_even = stacked([after(x, normed_one) for x in output_even])
    result, logsum = attend(
        query_heads, key_heads, value_heads, row_position, column_position, factor
    )

    output_parts = across.corners(output_even, result, *grad_even[1:])
    (output_even,) = arrange(
        index,
        [part[2] for part in output_parts],
        [(H * DV // 2, width)],
        [
            (
                n,
                everything,
                0,
                lambda ref, j=j, at=at, x=x: (
                    slice(at, at + x.shape[0]),
                    span(ref[0] ^ j, block_rows),
                ),
            )
            for n, (j, at, x) in enumerate(output_parts)
        ],
    )
    output_odd = swap(output_even, "seq", 1)

    grad_even, grad_odd = along.pair([after(x, result) for x in grad_even])

    def give(rows):
        return lax.all_to_all(rows, "exp", split_axis=0, concat_axis=0, tiled=True)

    grad_rows = stacked([grad_even, grad_odd])
    send_cots = dispatch(select, grad_rows, slot_weight, pieces)
    received_grad = [give(rows) for rows in send_cots]

    result_even = along.chips(result)
    gathered = (gate_cols, lift_cols, drop_rows)
    result_even = [after(x, received_grad[0], *gathered) for x in result_even]
    result_blocks = result_even + [swap(x, "seq", 1) for x in result_even]
    normed_two, residual = add_norm(
        token_blocks,
        result_blocks,
        output_even,
        output_odd,
        gain_second,
    )
    inverse_two = inverse_rms(residual)
    send_rows = dispatch(select, after(normed_two, *received_grad), None, pieces)
    received = [give(after(send_rows[0], *received_grad))]


    shared_rows = after(normed_two, *send_rows)
    shared_hidden, sgate_grad, sup_grad = shared(
        shared_rows, grad_rows, gate_cols, lift_cols, drop_rows
    )
    received[0] = after(received[0], shared_hidden)
    received += [give(after(x, received[0])) for x in send_rows[1:]]

    slot_rows = n_exp * n_seq * CAP
    pairs = []
    results_back, grads_back, kept = [], [], []
    for i in range(pieces):
        rows = received[i].reshape(slot_rows, width)
        cots = received_grad[i].reshape(slot_rows, width)
        expert_result, input_grad, *saved = expert(
            rows, cots, expert_gate, expert_up, expert_down, i
        )
        grads_back.append(give(input_grad.reshape(n_exp, n_seq * CAP, width)))
        results_back.append(expert_result.reshape(n_exp, n_seq * CAP, width))
        kept.append((rows, cots, *saved))
    two_products = [(sgate_grad, gate_cols, True), (sup_grad, lift_cols, True)]
    expert_grads = expert_weights(
        after(kept[0][0], input_grad), *kept[0][1:], 0, pieces, None
    )
    gate_part, lift_part, drop_part = expert_weights(
        after(shared_rows, input_grad), grad_rows, shared_hidden, sgate_grad, sup_grad, 0, 1, None, BF
    )
    token_wide = tokens.astype(F32)
    token_inverse = inverse_rms(token_wide)
    select = after(select, *expert_grads, gate_part, lift_part, drop_part, token_inverse)
    two_odd = combine(1, [select], grads_back, two_products, BF)
    two_even = combine(0, [select], grads_back, two_products, F32)
    two_blocks = along.begin(two_even, two_odd)
    back = []
    for i in range(pieces):
        back.append(give(after(results_back[i], *(two_blocks if i == 0 else expert_grads))))
        if i:
            expert_grads = expert_weights(
                after(kept[i][0], back[0]), *kept[i][1:], i, pieces, expert_grads
            )
    results_back = back
    expert_gate_grad, expert_up_grad, expert_down_grad = expert_grads
    (own_heads,) = arrange(
        index,
        [after(result_blocks[0], *two_blocks)] + result_blocks[1:],
        [(count, H * DV)],
        [
            (
                p,
                (slice(p * count, (p + 1) * count), everything),
                0,
                lambda ref, p=p: (everything, slice(p * heads * DV, (p + 1) * heads * DV)),
            )
            for p in range(n_seq)
        ],
    )
    gate_part, lift_part, drop_part = [
        after(x[0], *two_blocks) for x in (gate_part, lift_part, drop_part)
    ]
    gate_out, lift_out, drop_out = sum_exp(gate_part, 0), sum_exp(lift_part, 0), sum_exp(drop_part, 1)
    two_grad = along.finish(
        two_blocks, *expert_grads, own_heads
    )
    residual_norm_grad, second_terms = norm_back(
        two_grad, residual, inverse_two, gain_second
    )
    residual_grad = out_grad.astype(F32) + residual_norm_grad
    residual_half = residual_grad.astype(BF)
    even_heads = dot_t(residual_half, output_even).astype(BF)
    odd_heads = dot_t(residual_half, output_odd).astype(BF)
    wide = heads * DV
    pairs = [
        jnp.stack([even_heads[:, k * wide : (k + 1) * wide], odd_heads[:, k * wide : (k + 1) * wide]])
        for k in range(chips)
    ]
    stacks = pairs
    pairs = [pairs[0]] + [along.send(pairs[k], 2 * k) for k in range(1, chips)]
    other_half = swap(jnp.stack([pair[1] for pair in pairs]), "seq", 1)
    attention_grad = jnp.concatenate(
        [jnp.stack([pair[0] for pair in pairs]), other_half], axis=0
    ).reshape(length, wide)
    mine = lax.axis_index("exp")
    out_products = [(shared_hidden, drop_rows, False)]
    out_masks = [weighted_high, weighted_low]
    out_masks = [after(mask, *stacks, *pairs[1:]) for mask in out_masks]
    out_odd = combine(1, out_masks, results_back, out_products, BF)
    out_even = combine(0, out_masks, results_back, out_products, F32)
    out_blocks = along.begin(out_even, out_odd)
    output_got = [along.send(out_blocks[k], 2 * k) for k in range(chips - 1, 0, -1)]

    query_in_grad, kv_grad, latent_part, latent_sum = attend_back(
        query_heads,
        key_heads,
        value_heads,
        result,
        after(attention_grad, *out_blocks),
        logsum,
        row_position,
        column_position,
        cosine_wide,
        -sine_wide,
        up_cols,
        latent_all,
        latent_wide,
        factor,
        columns,
    )
    one_odd, odd_sum = query_back(1, query_in_grad, first_all, normed_one, gain_first, BF)
    one_even, even_sum = query_back(0, after(query_in_grad, *output_got[:2]), first_all, normed_one, gain_first, F32)
    late = Lane("exp", 3)
    attention_parts = late.others(after(own_heads, one_even))
    column_blocks = [
        lax.dynamic_slice_in_dim(residual_half, (mine ^ j) * block_rows, block_rows, 1)
        for j in range(n_exp)
    ]
    column_blocks = [column_blocks[0]] + [
        late.send(column_blocks[j], j) for j in range(1, n_exp)
    ]
    sums = jnp.concatenate(
        [
            (odd_sum + even_sum).reshape(n_exp, n_seq, gain_rows),
            jnp.sum(second_terms, axis=0).reshape(n_exp, n_seq, gain_rows),
            latent_sum.reshape(n_exp, n_seq, latent_rows_local),
        ],
        axis=2,
    )
    many = sums.shape[2]
    turn = (seq ^ jnp.array(order))[:, None] == jnp.arange(n_seq)[None, :]
    sums = jnp.einsum("ps,esw->pew", turn.astype(F32), sums, precision=lax.Precision.HIGHEST)
    sums = jnp.pad(
        sums.reshape(n_seq, 1, n_exp * many), ((0, 0), (0, 15), (0, columns - n_exp * many))
    )
    latent_part = jnp.concatenate([latent_part.reshape(n_seq, count, columns), sums], axis=1)
    latent_part = latent_part.reshape(n_seq * (count + 16), columns)
    latent_grad = along.scatter(
        latent_part[: chips * (count + 16)], latent_part[chips * (count + 16) :]
    )
    one_blocks = along.begin(one_even, one_odd)
    one_got = [along.send(one_blocks[k], 2 * k) for k in range(chips - 1, 0, -1)]
    output_odd_part = output_weights(1, attention_parts, column_blocks, BF)
    output_even_part = output_weights(0, attention_parts, column_blocks, F32)
    output_blocks = along.begin(output_even_part, output_odd_part)
    up_part = t_dot(after(latent_all, one_odd), kv_grad).astype(BF)
    query_part = t_dot(after(normed_one, one_odd), query_in_grad).astype(BF)
    up_out = sum_exp(up_part, 0)
    query_out = sum_exp(query_part, 0)
    sums = latent_grad[count, : n_exp * many].reshape(n_exp, 1, many)
    latent_grad = latent_grad[:count]
    latent_raw_grad, _ = norm_back(
        latent_grad[:, :R], latent_raw[:count], inverse_rms(latent_raw[:count]), latent_wide
    )
    down_rows = jnp.concatenate(
        [
            latent_raw_grad,
            rotate(latent_grad[:, R : R + DR], cosine_table[:count], -sine_table[:count]),
            jnp.zeros((count, columns - R - DR), F32),
        ],
        axis=1,
    ).astype(BF)
    down_even, down_odd = free.pair(
        [after(x, *one_got, *output_blocks) for x in free.chips(down_rows)]
    )
    wide_got = [
        swap(after(output_blocks[k], down_even), "seq", 2 * k) for k in range(chips - 1, 0, -1)
    ]
    down_part = down_weights(index, normed_one, down_even, down_odd, n_exp, n_seq, gain_rows)
    down_part = jnp.concatenate(
        [
            down_part,
            jnp.pad(sums, ((0, 0), (0, 15), (0, columns - many))),
        ],
        axis=1,
    )
    down_sum = lax.dynamic_index_in_dim(down_part, mine, 0, keepdims=False)
    for j in range(1, n_exp):
        piece = lax.dynamic_index_in_dim(down_part, mine ^ j, 0, keepdims=False).astype(BF)
        down_sum = down_sum + swap(piece, "exp", j).astype(F32)
    down_out = down_sum[:gain_rows, : R + DR]
    small = down_sum[gain_rows, :many]
    first_out = small[:gain_rows] + jnp.sum(
        w_kv_down.astype(F32) * down_out, axis=1
    ) / norm_gain.astype(F32)

    output = residual + out_blocks[0]
    for block in output_got:
        output = output + after(block, *one_blocks).astype(F32)
    output = output.astype(BF)
    output_out = output_blocks[0]
    for block in wide_got:
        output_out = output_out + block.astype(F32)
    one_grad = one_blocks[0]
    for block in one_got:
        block = after(block, up_part, query_part, gate_out, lift_out, drop_out)
        one_grad = one_grad + block.astype(F32)
    down_back = dot_t(down_rows[:, : R + DR], down_full)
    token_norm_grad, _ = norm_back(
        one_grad + down_back, token_wide, token_inverse, gain_first
    )
    tokens_grad = (residual_grad + token_norm_grad).astype(BF)
    return (
        output,
        tokens_grad,
        first_out,
        query_out,
        down_out,
        small[2 * gain_rows : many],
        up_out,
        output_out,
        small[gain_rows : 2 * gain_rows],
        gate_out,
        lift_out,
        drop_out,
        expert_gate_grad,
        expert_up_grad,
        expert_down_grad,
    )


def solution(mesh):
    rows = P(("exp", "seq"), None)
    line = P(("exp", "seq"))
    grid = P("exp", "seq")
    turned = P("seq", "exp")
    part = P(("exp", "seq"), None, None)
    return jax.shard_map(
        shards,
        mesh=mesh,
        in_specs=(
            rows,
            rows,
            rows,
            line,
            grid,
            rows,
            line,
            grid,
            turned,
            line,
            grid,
            grid,
            turned,
            part,
            part,
            part,
            rows,
        ),
        out_specs=(
            rows,
            rows,
            line,
            grid,
            rows,
            line,
            grid,
            turned,
            line,
            grid,
            grid,
            turned,
            part,
            part,
            part,
        ),
        check_vma=False,
    )
```

```python
import math

import jax
import jax.numpy as jnp
from jax import lax
from jax.experimental import pallas as pl
from jax.experimental.pallas import tpu as pltpu
from jax.sharding import PartitionSpec as P

H = 16
DN = 128
DR = 64
DV = 128
R = 512
EXPERTS = 64
TOP = 6
CAP = 16


eps_norm = 1e-06
rope_base = 50000.0
BF = jnp.bfloat16
F32 = jnp.float32


def dot(a, b):
    return jnp.dot(a, b, preferred_element_type=F32)


def dot_t(a, b):
    return lax.dot_general(a, b, (((1,), (1,)), ((), ())), preferred_element_type=F32)


def t_dot(a, b):
    return lax.dot_general(a, b, (((0,), (0,)), ((), ())), preferred_element_type=F32)


def rope_tables(positions, width):
    middle = width // 2
    frequency = rope_base ** (-(jnp.arange(middle, dtype=F32) * 2.0 / width))
    angles = positions.astype(F32)[:, None] * frequency[None, :]
    return (jnp.cos(angles), jnp.sin(angles))


def rotate(values, cosine_table, sine_table):
    middle = values.shape[-1] // 2
    leading = values[..., :middle]
    trailing = values[..., middle:]
    return jnp.concatenate(
        [
            leading * cosine_table - trailing * sine_table,
            trailing * cosine_table + leading * sine_table,
        ],
        axis=-1,
    )


def silu_slope(gate_values):
    sigmoid = jax.nn.sigmoid(gate_values)
    return sigmoid * (1.0 + gate_values * (1.0 - sigmoid))


def norm_back(dy, v, inverse, gain):
    hat = v * inverse
    scaled = dy * gain
    dv = inverse * (scaled - hat * jnp.mean(scaled * hat, axis=-1, keepdims=True))
    return dv, dy * hat


def inverse_rms(v):
    return lax.rsqrt(jnp.mean(v * v, axis=-1, keepdims=True) + eps_norm)


LIMIT = 56 * 1024 * 1024
LIGHT = pl.CostEstimate(flops=0, transcendentals=0, bytes_accessed=0)
ANY = pl.BlockSpec(memory_space=pl.ANY)
SCALARS = pl.BlockSpec(memory_space=pltpu.SMEM)


def whole(shape):
    return pl.BlockSpec(shape, lambda *grid: (0,) * len(shape))


def arrange(index, blocks, outs, plan):
    def kernel(index_ref, *refs):
        sources = refs[: len(blocks)]
        targets = refs[len(blocks) :]
        for block, source, out, target in plan:
            targets[out][target(index_ref)] = sources[block][source]

    return pl.pallas_call(
        kernel,
        out_shape=[jax.ShapeDtypeStruct(s, BF) for s in outs],
        in_specs=[SCALARS] + [pl.BlockSpec(memory_space=pltpu.VMEM)] * len(blocks),
        out_specs=[pl.BlockSpec(memory_space=pltpu.VMEM)] * len(outs),
        compiler_params=pltpu.CompilerParams(vmem_limit_bytes=LIMIT),
        cost_estimate=LIGHT,
        name="arrange",
    )(index, *blocks)


def span(start, size):
    return pl.ds(pl.multiple_of(start * size, size), size)


def turned(v, cosine, sine):
    middle = v.shape[1] // 2
    return v * cosine + jnp.concatenate([v[:, middle:], v[:, :middle]], axis=1) * sine


def project(token_blocks, gain, w_first, w_down, latent_gain, w_up, cosine, sine, heads):
    count, width = token_blocks[0].shape
    chips = len(token_blocks) // 2
    half = chips * count
    wide = DN + DR
    columns = heads * wide

    def kernel(g_ref, wd_ref, lg_ref, wu_ref, c_ref, s_ref, *refs):
        tokens, w_ref = refs[: 2 * chips], refs[2 * chips]
        n_ref, l_ref, r_ref, q_ref, k_ref, v_ref, x_ref = refs[2 * chips + 1 :]
        for h in range(2):

            @pl.when(pl.program_id(0) == h)
            def _():
                for k in range(chips):
                    x_ref[k * count : (k + 1) * count] = tokens[h * chips + k][...]

        x = x_ref[...].astype(F32)
        inverse = lax.rsqrt(jnp.mean(x * x, axis=1, keepdims=True) + eps_norm)
        n_ref[...] = (x * inverse * g_ref[...]).astype(BF)
        down = dot(n_ref[...], wd_ref[...])
        raw = down[:, :R]
        r_ref[...] = raw
        inverse = lax.rsqrt(jnp.mean(raw * raw, axis=1, keepdims=True) + eps_norm)
        l_ref[...] = (raw * inverse * lg_ref[...]).astype(BF)
        query = dot(n_ref[...], w_ref[:, :columns])
        up = dot(l_ref[...], wu_ref[...]).astype(BF)
        cosine, sine = c_ref[...], s_ref[...]
        zeros = jnp.zeros((half, 256 - wide), BF)
        rope = jnp.concatenate([turned(down[:, R : R + DR], cosine, sine).astype(BF), zeros], axis=1)
        for n in range(heads):
            own = query[:, n * wide : (n + 1) * wide]
            q_ref[n, :, :DN] = own[:, :DN].astype(BF)
            q_ref[n, :, DN:] = jnp.concatenate(
                [turned(own[:, DN:], cosine, sine).astype(BF), zeros], axis=1
            )
            k_ref[n, :, :DN] = up[:, n * (DN + DV) : n * (DN + DV) + DN]
            k_ref[n, :, DN:] = rope
            v_ref[n] = up[:, n * (DN + DV) + DN : (n + 1) * (DN + DV)]

    def rows(w):
        return pl.BlockSpec((half, w), lambda i: (i, 0))

    def head_rows(w):
        return pl.BlockSpec((heads, half, w), lambda i: (0, i, 0))

    length = 2 * half
    return pl.pallas_call(
        kernel,
        grid=(2,),
        in_specs=[
            whole((1, width)),
            whole(w_down.shape),
            whole((1, R)),
            whole(w_up.shape),
            rows(DR),
            rows(DR),
        ]
        + [whole((count, width))] * (2 * chips)
        + [whole(w_first.shape)],
        out_specs=[rows(width), rows(R), rows(R), head_rows(256), head_rows(256), head_rows(DV)],
        out_shape=[
            jax.ShapeDtypeStruct((length, width), BF),
            jax.ShapeDtypeStruct((length, R), BF),
            jax.ShapeDtypeStruct((length, R), F32),
            jax.ShapeDtypeStruct((heads, length, 256), BF),
            jax.ShapeDtypeStruct((heads, length, 256), BF),
            jax.ShapeDtypeStruct((heads, length, DV), BF),
        ],
        scratch_shapes=[pltpu.VMEM((half, width), BF)],
        compiler_params=pltpu.CompilerParams(vmem_limit_bytes=LIMIT),
        cost_estimate=LIGHT,
        name="project",
    )(gain, w_down, latent_gain, w_up, cosine, sine, *token_blocks, w_first)


def query_back(base, query_grad, w_first, normed, gain, dtype):
    length, columns = query_grad.shape
    half = length // 2
    width = normed.shape[1]
    tile = 512

    def kernel(q_ref, n_ref, g_ref, w_ref, o_ref, t_ref):
        part = dot_t(q_ref[...], w_ref[:, :columns])
        o_ref[...] = part.astype(dtype)
        product = part * n_ref[...].astype(F32)
        t_ref[...] = jnp.sum(product, axis=0, keepdims=True) / g_ref[...]

    return pl.pallas_call(
        kernel,
        grid=(width // tile,),
        in_specs=[
            pl.BlockSpec((half, columns), lambda i: (base, 0)),
            pl.BlockSpec((half, tile), lambda i: (base, i)),
            pl.BlockSpec((1, tile), lambda i: (0, i)),
            pl.BlockSpec((tile, w_first.shape[1]), lambda i: (i, 0)),
        ],
        out_specs=[
            pl.BlockSpec((half, tile), lambda i: (0, i)),
            pl.BlockSpec((1, tile), lambda i: (0, i)),
        ],
        out_shape=[
            jax.ShapeDtypeStruct((half, width), dtype),
            jax.ShapeDtypeStruct((1, width), F32),
        ],
        compiler_params=pltpu.CompilerParams(vmem_limit_bytes=LIMIT),
        cost_estimate=LIGHT,
        name="query_back",
    )(query_grad, normed, gain, w_first)


def attend(query, key, value, row_position, column_position, factor):
    heads, length, _ = query.shape
    tile = 256

    def kernel(q_ref, k_ref, v_ref, row_ref, column_ref, o_ref, s_ref):
        allowed = column_ref[...] <= row_ref[...]
        for n in range(heads):
            scores = dot_t(k_ref[n], q_ref[n]) * factor
            exponent = jnp.where(allowed, jnp.exp(jnp.where(allowed, scores, -1e30)), 0.0)
            total = jnp.sum(exponent, axis=0, keepdims=True)
            probs = (exponent / total).astype(BF)
            o_ref[:, n * DV : (n + 1) * DV] = t_dot(v_ref[n], probs).T.astype(BF)
            s_ref[n : n + 1, :] = jnp.log(total)

    return pl.pallas_call(
        kernel,
        grid=(length // tile,),
        in_specs=[
            pl.BlockSpec((heads, tile, 256), lambda i: (0, i, 0)),
            whole(key.shape),
            whole(value.shape),
            pl.BlockSpec((1, tile), lambda i: (0, i)),
            whole((length, 1)),
        ],
        out_specs=[
            pl.BlockSpec((tile, heads * DV), lambda i: (i, 0)),
            pl.BlockSpec((heads, tile), lambda i: (0, i)),
        ],
        out_shape=[
            jax.ShapeDtypeStruct((length, heads * DV), BF),
            jax.ShapeDtypeStruct((heads, length), F32),
        ],
        compiler_params=pltpu.CompilerParams(vmem_limit_bytes=LIMIT),
        cost_estimate=LIGHT,
        name="attend",
    )(query, key, value, row_position, column_position)


def attend_back(query, key, value, result, result_grad, logsum, row_position, column_position, cosine, sine, w_up, latent_all, latent_gain, factor):
    heads, length, _ = query.shape
    tile = 256
    steps = length // tile
    wide = DN + DR

    def kernel(q_ref, k_ref, v_ref, o_ref, do_ref, ls_ref, row_ref, column_ref, c_ref, s_ref, wu_ref, l_ref, lg_ref, dq_ref, kv_ref, lp_ref, t_ref, dk_acc, dv_acc, kt):
        step = pl.program_id(0)

        @pl.when(step == 0)
        def _():
            dk_acc[...] = jnp.zeros_like(dk_acc)
            dv_acc[...] = jnp.zeros_like(dv_acc)
            for n in range(heads):
                kt[n] = k_ref[n].T

        allowed = column_ref[...] <= row_ref[...]
        cosine, sine = c_ref[...], s_ref[...]
        parts = []
        for n in range(heads):
            q = q_ref[n]
            grad = do_ref[:, n * DV : (n + 1) * DV]
            scores = jnp.where(allowed, dot_t(k_ref[n], q) * factor, -1e30)
            probs = jnp.exp(scores - ls_ref[n : n + 1, :])
            dv_acc[n] += dot(probs.astype(BF), grad)
            product = grad.astype(F32) * o_ref[:, n * DV : (n + 1) * DV].astype(F32)
            row_dot = jnp.sum(product.T, axis=0, keepdims=True)
            probs_grad = dot_t(v_ref[n], grad)
            score_grad = (probs * (probs_grad - row_dot) * factor).astype(BF)
            dk_acc[n] += dot(score_grad, q)
            query_grad = dot(kt[n], score_grad).T.astype(BF)
            parts.append(query_grad[:, :DN])
            parts.append(turned(query_grad[:, DN:wide].astype(F32), cosine, sine).astype(BF))
        dq_ref[...] = jnp.concatenate(parts, axis=1)

        @pl.when(step == steps - 1)
        def _():
            rope = jnp.zeros((length, DR), F32)
            for n in range(heads):
                key_grad = dk_acc[n].astype(BF)
                value_grad = dv_acc[n].astype(BF)
                base = n * (DN + DV)
                kv_ref[:, base : base + DN] = key_grad[:, :DN]
                kv_ref[:, base + DN : base + DN + DV] = value_grad
                rope = rope + key_grad[:, DN:wide].astype(F32)
            latent = dot_t(kv_ref[...], wu_ref[...])
            lp_ref[:, :R] = latent
            lp_ref[:, R:] = rope
            t_ref[...] = jnp.sum(
                latent * l_ref[...].astype(F32), axis=0, keepdims=True
            ) / lg_ref[...]

    return pl.pallas_call(
        kernel,
        grid=(steps,),
        in_specs=[
            pl.BlockSpec((heads, tile, 256), lambda i: (0, i, 0)),
            whole(key.shape),
            whole(value.shape),
            pl.BlockSpec((tile, heads * DV), lambda i: (i, 0)),
            pl.BlockSpec((tile, heads * DV), lambda i: (i, 0)),
            pl.BlockSpec((heads, tile), lambda i: (0, i)),
            pl.BlockSpec((1, tile), lambda i: (0, i)),
            whole((length, 1)),
            pl.BlockSpec((tile, DR), lambda i: (i, 0)),
            pl.BlockSpec((tile, DR), lambda i: (i, 0)),
            whole(w_up.shape),
            whole((length, R)),
            whole((1, R)),
        ],
        out_specs=[
            pl.BlockSpec((tile, heads * wide), lambda i: (i, 0)),
            whole((length, heads * (DN + DV))),
            whole((length, R + DR)),
            whole((1, R)),
        ],
        out_shape=[
            jax.ShapeDtypeStruct((length, heads * wide), BF),
            jax.ShapeDtypeStruct((length, heads * (DN + DV)), BF),
            jax.ShapeDtypeStruct((length, R + DR), F32),
            jax.ShapeDtypeStruct((1, R), F32),
        ],
        scratch_shapes=[
            pltpu.VMEM((heads, length, 256), F32),
            pltpu.VMEM((heads, length, DV), F32),
            pltpu.VMEM((heads, 256, length), BF),
        ],
        compiler_params=pltpu.CompilerParams(vmem_limit_bytes=LIMIT),
        cost_estimate=LIGHT,
        name="attend_back",
    )(query, key, value, result, result_grad, logsum, row_position, column_position, cosine, sine, w_up, latent_all, latent_gain)


def add_norm(token_blocks, blocks, w_even, w_odd, gain):
    count, width = token_blocks[0].shape
    many = len(blocks)
    chips = many // 2
    half = chips * count
    length = count * many
    depth = blocks[0].shape[1]

    def kernel(we_ref, wo_ref, g_ref, *refs):
        parts, tokens = refs[:many], refs[many : 2 * many]
        n_ref, r_ref, x_ref, a_ref = refs[2 * many :]
        for q in range(many):
            for p in range(chips):
                other = p ^ (q % chips)
                a_ref[p * count : (p + 1) * count, q * depth : (q + 1) * depth] = parts[q][
                    other * count : (other + 1) * count
                ]
        for h in range(2):

            @pl.when(pl.program_id(0) == h)
            def _():
                for k in range(chips):
                    x_ref[k * count : (k + 1) * count] = tokens[h * chips + k][...]

        middle = chips * depth
        total = dot(a_ref[:, :middle], we_ref[...]) + dot(a_ref[:, middle:], wo_ref[...])
        total = total + x_ref[...].astype(F32)
        inverse = lax.rsqrt(jnp.mean(total * total, axis=1, keepdims=True) + eps_norm)
        n_ref[...] = (total * inverse * g_ref[...]).astype(BF)

        @pl.when(pl.program_id(0) == 0)
        def _():
            r_ref[...] = total[:count]

    def source(q):
        return pl.BlockSpec((half, depth), lambda i: (i ^ (q // chips), 0))

    return pl.pallas_call(
        kernel,
        grid=(2,),
        in_specs=[whole(w_even.shape), whole(w_odd.shape), whole((1, width))]
        + [source(q) for q in range(many)]
        + [whole((count, width))] * many,
        out_specs=[pl.BlockSpec((half, width), lambda i: (i, 0)), whole((count, width))],
        out_shape=[
            jax.ShapeDtypeStruct((length, width), BF),
            jax.ShapeDtypeStruct((count, width), F32),
        ],
        scratch_shapes=[pltpu.VMEM((half, width), BF), pltpu.VMEM((half, many * depth), BF)],
        compiler_params=pltpu.CompilerParams(vmem_limit_bytes=LIMIT),
        cost_estimate=LIGHT,
        name="add_norm",
    )(w_even, w_odd, gain, *blocks, *token_blocks)


def expert(rows, cots, gate, up, down, piece):
    count, width = rows.shape
    units = gate.shape[2]
    tile = min(512, count)
    step = 256
    full = units // step
    rest = units % step
    spans = [(n * step, step) for n in range(full)] + ([(full * step, rest)] if rest else [])

    def kernel(x_ref, c_ref, gate_hbm, up_hbm, down_hbm, res_ref, in_ref, h_ref, gg_ref, ug_ref, wg, wu, wd, acc_r, acc_i, sems):
        first = pl.program_id(0) == 0

        def copies(n, start, size):
            span = pl.ds(start, size)
            return [
                pltpu.make_async_copy(gate_hbm.at[piece, :, span], wg.at[:, span], sems.at[0, n]),
                pltpu.make_async_copy(up_hbm.at[piece, :, span], wu.at[:, span], sems.at[1, n]),
                pltpu.make_async_copy(down_hbm.at[piece, span, :], wd.at[span, :], sems.at[2, n]),
            ]

        @pl.when(first)
        def _():
            for n, (start, size) in enumerate(spans):
                for copy in copies(n, start, size):
                    copy.start()

        acc_r[...] = jnp.zeros_like(acc_r)
        acc_i[...] = jnp.zeros_like(acc_i)

        def chunk(n, start, size):
            @pl.when(first)
            def _():
                for copy in copies(n, start, size):
                    copy.wait()

            span = pl.ds(start, size)
            x, c = x_ref[...], c_ref[...]
            w_gate, w_up, w_down = wg[:, span], wu[:, span], wd[span, :]
            g = dot(x, w_gate)
            u = dot(x, w_up)
            hidden_grad = dot_t(c, w_down)
            s = jax.nn.sigmoid(g)
            silu = g * s
            hidden = (silu * u).astype(BF)
            gate_grad = (hidden_grad * u * (s * (1.0 + g * (1.0 - s)))).astype(BF)
            up_grad = (hidden_grad * silu).astype(BF)
            h_ref[:, span] = hidden
            gg_ref[:, span] = gate_grad
            ug_ref[:, span] = up_grad
            acc_r[...] += dot(hidden, w_down)
            acc_i[...] += dot_t(gate_grad, w_gate) + dot_t(up_grad, w_up)

        if full:

            @pl.loop(0, full)
            def _(n):
                chunk(n, pl.multiple_of(n * step, step), step)

        if rest:
            chunk(full, full * step, rest)
        res_ref[...] = acc_r[...].astype(BF)
        in_ref[...] = acc_i[...].astype(BF)

    def block(w):
        return pl.BlockSpec((tile, w), lambda i: (i, 0))

    def array(w):
        return jax.ShapeDtypeStruct((count, w), BF)

    return pl.pallas_call(
        kernel,
        grid=(count // tile,),
        in_specs=[block(width), block(width), ANY, ANY, ANY],
        out_specs=[block(width), block(width), block(units), block(units), block(units)],
        out_shape=[array(width), array(width), array(units), array(units), array(units)],
        scratch_shapes=[
            pltpu.VMEM((width, units), BF),
            pltpu.VMEM((width, units), BF),
            pltpu.VMEM((units, width), BF),
            pltpu.VMEM((tile, width), F32),
            pltpu.VMEM((tile, width), F32),
            pltpu.SemaphoreType.DMA((3, len(spans))),
        ],
        compiler_params=pltpu.CompilerParams(vmem_limit_bytes=LIMIT),
        cost_estimate=LIGHT,
        name="expert",
    )(rows, cots, gate, up, down)


def shared(rows, cots, gate, up, down):
    count, width = rows.shape
    units = gate.shape[1]
    tile = 256

    def kernel(x_ref, c_ref, wg_ref, wu_ref, wd_ref, h_ref, gg_ref, ug_ref):
        g = dot(x_ref[...], wg_ref[...])
        u = dot(x_ref[...], wu_ref[...])
        hidden_grad = dot_t(c_ref[...], wd_ref[...])
        s = jax.nn.sigmoid(g)
        silu = g * s
        h_ref[...] = (silu * u).astype(BF)
        gg_ref[...] = (hidden_grad * u * (s * (1.0 + g * (1.0 - s)))).astype(BF)
        ug_ref[...] = (hidden_grad * silu).astype(BF)

    row = pl.BlockSpec((tile, width), lambda i: (i, 0))
    unit = pl.BlockSpec((tile, units), lambda i: (i, 0))
    return pl.pallas_call(
        kernel,
        grid=(count // tile,),
        in_specs=[row, row, whole(gate.shape), whole(up.shape), whole(down.shape)],
        out_specs=[unit] * 3,
        out_shape=[jax.ShapeDtypeStruct((count, units), BF)] * 3,
        compiler_params=pltpu.CompilerParams(vmem_limit_bytes=LIMIT),
        cost_estimate=LIGHT,
        name="shared",
    )(rows, cots, gate, up, down)


def expert_weights(rows, cots, hidden, gate_grad, up_grad, piece, pieces, earlier, dtype=F32):
    count, width = rows.shape
    units = hidden.shape[1]
    tile = 256

    def kernel(x_ref, c_ref, h_ref, gg_ref, ug_ref, *refs):
        g_ref, u_ref, d_ref = refs[-3:]
        g_ref[0] = t_dot(x_ref[...], gg_ref[...]).astype(dtype)
        u_ref[0] = t_dot(x_ref[...], ug_ref[...]).astype(dtype)
        d_ref[0] = t_dot(h_ref[...], c_ref[...]).astype(dtype)

    tall = pl.BlockSpec((1, tile, units), lambda i: (piece, i, 0))
    flat = pl.BlockSpec((1, units, tile), lambda i: (piece, 0, i))
    column = pl.BlockSpec((count, tile), lambda i: (0, i))
    kept = list(earlier or ())
    return pl.pallas_call(
        kernel,
        grid=(width // tile,),
        in_specs=[column, column] + [whole((count, units))] * 3 + [ANY] * len(kept),
        out_specs=[tall, tall, flat],
        out_shape=[
            jax.ShapeDtypeStruct((pieces, width, units), dtype),
            jax.ShapeDtypeStruct((pieces, width, units), dtype),
            jax.ShapeDtypeStruct((pieces, units, width), dtype),
        ],
        input_output_aliases={5 + n: n for n in range(len(kept))},
        compiler_params=pltpu.CompilerParams(vmem_limit_bytes=LIMIT),
        cost_estimate=LIGHT,
        name="expert_weights",
    )(rows, cots, hidden, gate_grad, up_grad, *kept)


def dispatch(select, rows, slot_weight, pieces):
    blocks, slots, count = select.shape
    width = rows.shape[1]
    others = slots // pieces // CAP

    def kernel(m_ref, x_ref, *refs):
        got = dot(m_ref[0], x_ref[...])
        if slot_weight is not None:
            got = got * refs[0][0]
        got = got.astype(BF)
        for i in range(pieces):
            for j in range(others):
                start = (i * others + j) * CAP
                refs[-pieces + i][j] = got[start : start + CAP]

    weights = [] if slot_weight is None else [slot_weight]
    out = pl.BlockSpec((others, CAP, width), lambda b: (0, b, 0))
    return pl.pallas_call(
        kernel,
        grid=(blocks,),
        in_specs=[
            pl.BlockSpec((1, slots, count), lambda b: (b, 0, 0)),
            pl.BlockSpec((count, width), lambda b: (b, 0)),
        ]
        + [pl.BlockSpec((1, slots, 1), lambda b: (b, 0, 0))] * len(weights),
        out_specs=[out] * pieces,
        out_shape=[jax.ShapeDtypeStruct((others, blocks * CAP, width), BF)] * pieces,
        compiler_params=pltpu.CompilerParams(vmem_limit_bytes=LIMIT),
        cost_estimate=LIGHT,
        name="dispatch",
    )(select, rows, *weights)


def down_weights(index, normed, down_even, down_odd, others, n_seq, gain_rows):
    length, _ = normed.shape
    half, columns = down_even.shape
    per = 128 // gain_rows

    def kernel(index_ref, n_ref, e_ref, d_ref, o_ref, part):
        part[...] = t_dot(n_ref[:half], e_ref[...]) + t_dot(n_ref[half:], d_ref[...])
        o_ref[0] = part[span(index_ref[1] % per, gain_rows)]

    return pl.pallas_call(
        kernel,
        grid_spec=pltpu.PrefetchScalarGridSpec(
            num_scalar_prefetch=1,
            grid=(others,),
            in_specs=[
                pl.BlockSpec(
                    (length, 128), lambda i, ref: (0, (i * n_seq + ref[1]) * gain_rows // 128)
                ),
                pl.BlockSpec((half, columns), lambda i, ref: (0, 0)),
                pl.BlockSpec((half, columns), lambda i, ref: (0, 0)),
            ],
            out_specs=pl.BlockSpec((1, gain_rows, columns), lambda i, ref: (i, 0, 0)),
            scratch_shapes=[pltpu.VMEM((128, columns), F32)],
        ),
        out_shape=jax.ShapeDtypeStruct((others, gain_rows, columns), F32),
        compiler_params=pltpu.CompilerParams(vmem_limit_bytes=LIMIT),
        cost_estimate=LIGHT,
        name="down_weights",
    )(index, normed, down_even, down_odd)


def output_weights(base, heads, columns, dtype):
    count, width = heads[0].shape
    wide = columns[0].shape[1]
    half = width // 2
    tile = 256
    many = len(heads)

    def kernel(*refs):
        total = 0.0
        for j in range(many):
            total = total + t_dot(refs[j][...], refs[many + j][...])
        refs[-1][...] = total.astype(dtype)

    return pl.pallas_call(
        kernel,
        grid=(half // tile,),
        in_specs=[pl.BlockSpec((count, tile), lambda i: (0, base * (half // tile) + i))] * many
        + [whole((count, wide))] * many,
        out_specs=pl.BlockSpec((tile, wide), lambda i: (i, 0)),
        out_shape=jax.ShapeDtypeStruct((half, wide), dtype),
        compiler_params=pltpu.CompilerParams(vmem_limit_bytes=LIMIT),
        cost_estimate=LIGHT,
        name="output_weights",
    )(*heads, *columns)


def combine(base, masks, returned, products, dtype):
    half = masks[0].shape[0] // 2
    slots, count = masks[0].shape[1:]
    pieces = len(returned)
    others, _, width = returned[0].shape
    many = len(masks)

    tile = 512

    def kernel(*refs):
        mask_refs, row_refs = refs[:many], refs[many : many + pieces]
        rest, out_ref = refs[many + pieces : -1], refs[-1]
        total = 0.0
        for n, (_, _, flipped) in enumerate(products):
            total = total + (dot_t if flipped else dot)(rest[2 * n][...], rest[2 * n + 1][...])
        for b in range(half):
            rows = jnp.concatenate(
                [
                    row_refs[i][j, b * CAP : (b + 1) * CAP]
                    for i in range(pieces)
                    for j in range(others)
                ],
                axis=0,
            )
            block = total[b * count : (b + 1) * count]
            for mask_ref in mask_refs:
                block = block + t_dot(mask_ref[b], rows)
            out_ref[b * count : (b + 1) * count] = block.astype(dtype)

    factors = []
    specs = []
    for left, right, flipped in products:
        factors += [left, right]
        specs.append(pl.BlockSpec((half * count, left.shape[1]), lambda t: (base, 0)))
        if flipped:
            specs.append(pl.BlockSpec((tile, right.shape[1]), lambda t: (t, 0)))
        else:
            specs.append(pl.BlockSpec((right.shape[0], tile), lambda t: (0, t)))
    return pl.pallas_call(
        kernel,
        grid=(width // tile,),
        in_specs=[pl.BlockSpec((half, slots, count), lambda t: (base, 0, 0))] * many
        + [pl.BlockSpec((others, half * CAP, tile), lambda t: (0, base, t))] * pieces
        + specs,
        out_specs=pl.BlockSpec((half * count, tile), lambda t: (0, t)),
        out_shape=jax.ShapeDtypeStruct((half * count, width), dtype),
        compiler_params=pltpu.CompilerParams(vmem_limit_bytes=LIMIT),
        cost_estimate=LIGHT,
        name="combine",
    )(*masks, *returned, *factors)


def swap(x, axis, mask):
    n = lax.axis_size(axis)
    return lax.ppermute(x, axis, [(i, i ^ mask) for i in range(n)])


def after(x, *earlier):
    return lax.optimization_barrier((x, *earlier))[0]


class Lane:
    def __init__(self, axis, depth):
        self.axis = axis
        self.depth = depth
        self.sent = []

    def send(self, x, mask):
        if len(self.sent) >= self.depth:
            x = after(x, self.sent[-self.depth])
        got = swap(x, self.axis, mask)
        self.sent.append(got)
        return got

    def chips(self, x):
        chips = lax.axis_size("seq") // 2
        return [x] + [self.send(x, 2 * k) for k in range(1, chips)]

    def group(self, x):
        return self.pair(self.chips(x))

    def pair(self, evens):
        rows, columns = evens[0].shape
        everything = slice(None)
        (even,) = arrange(
            jnp.zeros((1,), jnp.int32),
            evens,
            [(rows * len(evens), columns)],
            [
                (k, everything, 0, lambda ref, k=k: (slice(k * rows, (k + 1) * rows), everything))
                for k in range(len(evens))
            ],
        )
        return even, swap(even, "seq", 1)

    def scatter(self, even, odd):
        return self.finish(self.begin(even, odd))

    def begin(self, even, odd):
        chips = lax.axis_size("seq") // 2
        rows = even.shape[0] // chips
        got = swap(odd.astype(BF), "seq", 1)
        blocks = [
            even[k * rows : (k + 1) * rows] + got[k * rows : (k + 1) * rows].astype(F32)
            for k in range(chips)
        ]
        return blocks[:1] + [block.astype(BF) for block in blocks[1:]]

    def finish(self, blocks, *gates):
        got = [self.send(blocks[k], 2 * k) for k in range(1, len(blocks))]
        total = blocks[0]
        for block in got:
            total = total + after(block, *gates).astype(F32)
        return total

    def corners(self, x, *gates):
        if lax.axis_size("exp") != 4:
            return [(j, 0, y) for j, y in enumerate(self.others(x))]
        middle = x.shape[0] // 2
        one, two = self.send(x, 1), self.send(x, 2)
        return [
            (0, 0, x),
            (1, 0, one),
            (2, 0, two),
            (3, 0, self.send(after(two[:middle], *gates), 1)),
            (3, middle, self.send(after(one[middle:], *gates), 2)),
        ]

    def others(self, x):
        return [x] + [self.send(x, j) for j in range(1, lax.axis_size("exp"))]

def relative_order(count):
    chips = count // 2
    return [2 * k for k in range(chips)] + [2 * k + 1 for k in range(chips)]


def sum_exp(x, axis):
    return lax.psum_scatter(x.astype(BF), "exp", scatter_dimension=axis, tiled=True).astype(F32)


def shards(
    tokens,
    routes,
    route_weights,
    norm_gain,
    w_query,
    w_kv_down,
    latent_gain,
    w_kv_up,
    w_output,
    ffn_gain,
    shared_gate,
    shared_up,
    shared_down,
    expert_gate,
    expert_up,
    expert_down,
    out_grad,
):
    count, width = tokens.shape
    n_seq = lax.axis_size("seq")
    n_exp = lax.axis_size("exp")
    seq = lax.axis_index("seq")
    order = relative_order(n_seq)
    chips = n_seq // 2
    heads = H // n_seq
    length = count * n_seq
    half = length // 2
    pieces = expert_gate.shape[0]
    parts_per = pieces * n_seq * n_exp // EXPERTS
    factor = 1.0 / math.sqrt(DN + DR)
    gain_rows = norm_gain.shape[0]
    latent_rows_local = latent_gain.shape[0]
    along = Lane("seq", 3)
    across = Lane("exp", 3)
    free = Lane("seq", 3)

    index = jnp.stack([lax.axis_index("exp"), seq]).astype(jnp.int32)
    ratio = w_query.shape[0] // w_kv_up.shape[0]
    slim = w_kv_up.shape[1] // ratio
    columns = w_kv_down.shape[1]
    high = lax.reduce_precision(route_weights, 8, 7)
    middle = lax.reduce_precision(route_weights - high, 8, 7)
    low = route_weights - high - middle
    route_pack = jnp.concatenate([routes.astype(F32), high, middle, low], axis=1).astype(BF).T
    lines = route_pack.shape[0] // 4
    gains = jnp.concatenate([norm_gain, ffn_gain, latent_gain])
    packed = jnp.concatenate(
        [
            w_kv_down,
            jnp.pad(gains, (0, columns - gains.shape[0]))[None, :],
            jnp.pad(
                route_pack.reshape(4, lines, count).transpose(1, 0, 2).reshape(lines, 4 * count),
                ((0, 15 - lines), (0, columns - 4 * count)),
            ),
        ],
        axis=0,
    )
    packed_even = jnp.stack(free.chips(packed))
    token_even = along.chips(tokens)
    first_all = lax.all_gather(
        jnp.concatenate(
            [
                w_query,
                jnp.concatenate(
                    [w_kv_up[:, g * slim : (g + 1) * slim] for g in range(ratio)], axis=0
                ),
            ],
            axis=1,
        ),
        "exp",
        axis=0,
        tiled=True,
    )
    packed_parts = across.others(packed_even)
    packed_even = jnp.stack(packed_parts)
    packed_odd = swap(packed_even, "seq", 1)
    token_odd = []
    for x in token_even:
        token_odd.append(swap(after(x, *token_odd), "seq", 1))
    token_blocks = token_even + token_odd
    output_even = along.chips(after(w_output, *token_odd, packed_odd))
    early = packed_parts[-1]
    gate_cols = lax.all_gather(after(shared_gate, early), "exp", axis=0, tiled=True)
    lift_cols = lax.all_gather(after(shared_up, early), "exp", axis=0, tiled=True)
    drop_rows = lax.all_gather(after(shared_down, early), "exp", axis=1, tiled=True)
    grad_even = along.chips(out_grad)

    everything = slice(None)
    block_rows = width // n_exp
    plan = []
    for h in range(2):
        for j in range(n_exp):
            for k in range(chips):

                def where(ref, h=h, j=j, k=k):
                    return (ref[0] ^ j) * n_seq + (ref[1] ^ (2 * k + h))

                plan.append(
                    (
                        h,
                        (j, k, slice(0, gain_rows)),
                        0,
                        lambda ref, where=where: (span(where(ref), gain_rows), everything),
                    )
                )
                plan.append(
                    (
                        h,
                        (j, k, slice(gain_rows, gain_rows + 16)),
                        1,
                        lambda ref, where=where: (where(ref),),
                    )
                )
    down_full, extra_all = arrange(
        index,
        [packed_even, packed_odd],
        [(width, columns), (n_exp * n_seq, 16, columns)],
        plan,
    )
    gain_first = extra_all[:, 0, :gain_rows].reshape(1, width).astype(F32)
    gain_second = extra_all[:, 0, gain_rows : 2 * gain_rows].reshape(1, width).astype(F32)
    latent_wide = (
        extra_all[:, 0, 2 * gain_rows : 2 * gain_rows + latent_rows_local]
        .reshape(1, R)
        .astype(F32)
    )
    route_all = jnp.concatenate(
        [packed_even[0, :, gain_rows + 1 :], packed_odd[0, :, gain_rows + 1 :]], axis=0
    )[:, :lines, : 4 * count]
    route_all = route_all.reshape(n_seq, lines, 4, count).transpose(0, 2, 1, 3)
    route_all = route_all.reshape(n_seq, 4 * lines, count).astype(F32)
    route_all = jnp.concatenate(
        [
            route_all[:, :TOP],
            route_all[:, TOP : 2 * TOP]
            + route_all[:, 2 * TOP : 3 * TOP]
            + route_all[:, 3 * TOP :],
        ],
        axis=1,
    )
    up_rows = w_kv_up.shape[0]
    query_width = w_query.shape[1]
    (up_cols,) = arrange(
        index,
        [first_all],
        [(R, w_kv_up.shape[1])],
        [
            (
                0,
                (
                    slice((j * ratio + g) * up_rows, (j * ratio + g + 1) * up_rows),
                    slice(query_width, query_width + slim),
                ),
                0,
                lambda ref, j=j, g=g: (
                    slice(j * up_rows, (j + 1) * up_rows),
                    slice(g * slim, (g + 1) * slim),
                ),
            )
            for j in range(n_exp)
            for g in range(ratio)
        ],
    )
    positions = jnp.concatenate(
        [(seq ^ r) * count + jnp.arange(count, dtype=jnp.int32) for r in order]
    )
    row_position, column_position = positions[None, :], positions[:, None]
    cosine_table, sine_table = rope_tables(positions, DR)
    cosine_wide = jnp.concatenate([cosine_table, cosine_table], axis=1)
    sine_wide = jnp.concatenate([-sine_table, sine_table], axis=1)
    normed_one, latent_all, latent_raw, query_heads, key_heads, value_heads = project(
        token_blocks,
        gain_first,
        first_all,
        down_full,
        latent_wide,
        up_cols,
        cosine_wide,
        sine_wide,
        heads,
    )
    output_even = jnp.concatenate([after(x, normed_one) for x in output_even], axis=0)
    result, logsum = attend(
        query_heads, key_heads, value_heads, row_position, column_position, factor
    )

    output_parts = across.corners(output_even, result, *grad_even[1:])
    result_even = along.chips(result)
    (output_even,) = arrange(
        index,
        [part[2] for part in output_parts],
        [(H * DV // 2, width)],
        [
            (
                n,
                everything,
                0,
                lambda ref, j=j, at=at, x=x: (
                    slice(at, at + x.shape[0]),
                    span(ref[0] ^ j, block_rows),
                ),
            )
            for n, (j, at, x) in enumerate(output_parts)
        ],
    )
    output_odd = swap(output_even, "seq", 1)

    grad_even, grad_odd = along.pair([after(x, result) for x in grad_even])

    column = jnp.stack(
        [
            ((other * n_seq + seq) * pieces + i) // parts_per
            for i in range(pieces)
            for other in range(n_exp)
        ]
    )
    kinds = n_exp * pieces
    named = route_all[:, None, :TOP, :].astype(jnp.int32) == column[None, :, None, None]
    matched = jnp.any(named, axis=2)
    match_weight = jnp.sum(jnp.where(named, route_all[:, None, TOP:, :], 0.0), axis=2)
    earlier = (jnp.arange(count)[:, None] < jnp.arange(count)[None, :]).astype(BF)
    rank = jnp.dot(matched.astype(BF), earlier, preferred_element_type=F32).astype(jnp.int32)
    chosen = (rank[:, :, None, :] == jnp.arange(CAP, dtype=jnp.int32)[None, None, :, None]) & (
        matched[:, :, None, :]
    )
    select = chosen.astype(BF).reshape(n_seq, kinds * CAP, count)
    weighted = jnp.where(chosen, match_weight[:, :, None, :], 0.0).reshape(
        n_seq, kinds * CAP, count
    )
    slot_weight = jnp.sum(weighted, axis=2, keepdims=True)
    weighted_high = weighted.astype(BF)
    weighted_low = (weighted - weighted_high.astype(F32)).astype(BF)

    def give(rows):
        return lax.all_to_all(rows, "exp", split_axis=0, concat_axis=0, tiled=True)

    (grad_rows,) = arrange(
        index,
        [grad_even, grad_odd],
        [(length, width)],
        [
            (h, everything, 0, lambda ref, h=h: (slice(h * half, (h + 1) * half), everything))
            for h in range(2)
        ],
    )
    send_cots = dispatch(select, grad_rows, slot_weight, pieces)
    received_grad = [give(send_cots[0])]
    received_grad += [give(after(rows, *result_even[1:])) for rows in send_cots[1:]]

    gathered = (gate_cols, lift_cols, drop_rows)
    result_even = [after(x, *send_cots, *gathered) for x in result_even]
    result_blocks = result_even + [swap(x, "seq", 1) for x in result_even]
    normed_two, residual = add_norm(
        token_blocks,
        [after(result_blocks[0], received_grad[0])] + result_blocks[1:],
        output_even,
        output_odd,
        gain_second,
    )
    inverse_two = inverse_rms(residual)
    send_rows = dispatch(select, normed_two, None, pieces)
    received = [give(after(send_rows[0], *received_grad))]


    shared_rows = after(normed_two, *send_rows)
    shared_hidden, sgate_grad, sup_grad = shared(
        shared_rows, grad_rows, gate_cols, lift_cols, drop_rows
    )
    received[0] = after(received[0], shared_hidden)
    received += [give(after(rows, received[0])) for rows in send_rows[1:]]

    slot_rows = n_exp * n_seq * CAP
    pairs = []
    results_back, grads_back, kept = [], [], []
    for i in range(pieces):
        rows = received[i].reshape(slot_rows, width)
        cots = received_grad[i].reshape(slot_rows, width)
        expert_result, input_grad, *saved = expert(
            rows, cots, expert_gate, expert_up, expert_down, i
        )
        grads_back.append(give(input_grad.reshape(n_exp, n_seq * CAP, width)))
        results_back.append(expert_result.reshape(n_exp, n_seq * CAP, width))
        kept.append((rows, cots, *saved))
    two_products = [(sgate_grad, gate_cols, True), (sup_grad, lift_cols, True)]
    expert_grads = expert_weights(
        after(kept[0][0], input_grad), *kept[0][1:], 0, pieces, None
    )
    gate_part, lift_part, drop_part = expert_weights(
        after(shared_rows, input_grad), grad_rows, shared_hidden, sgate_grad, sup_grad, 0, 1, None, BF
    )
    token_wide = tokens.astype(F32)
    token_inverse = inverse_rms(token_wide)
    select = after(select, *expert_grads, gate_part, lift_part, drop_part, token_inverse)
    two_odd = combine(1, [select], grads_back, two_products, BF)
    two_even = combine(0, [select], grads_back, two_products, F32)
    two_blocks = along.begin(two_even, two_odd)
    back = []
    for i in range(pieces):
        back.append(give(after(results_back[i], *(two_blocks if i == 0 else expert_grads))))
        if i:
            expert_grads = expert_weights(
                after(kept[i][0], back[0]), *kept[i][1:], i, pieces, expert_grads
            )
    results_back = back
    expert_gate_grad, expert_up_grad, expert_down_grad = expert_grads
    (own_heads,) = arrange(
        index,
        [after(result_blocks[0], *two_blocks)] + result_blocks[1:],
        [(count, H * DV)],
        [
            (
                p,
                (slice(p * count, (p + 1) * count), everything),
                0,
                lambda ref, p=p: (everything, slice(p * heads * DV, (p + 1) * heads * DV)),
            )
            for p in range(n_seq)
        ],
    )
    two_grad = along.finish(two_blocks, *expert_grads, own_heads)
    gate_part, lift_part, drop_part = [
        after(x[0], *two_blocks) for x in (gate_part, lift_part, drop_part)
    ]
    gate_out, lift_out, drop_out = sum_exp(gate_part, 0), sum_exp(lift_part, 0), sum_exp(drop_part, 1)

    residual_norm_grad, second_terms = norm_back(
        two_grad, residual, inverse_two, gain_second
    )
    residual_grad = out_grad.astype(F32) + residual_norm_grad
    residual_half = residual_grad.astype(BF)
    even_heads = dot_t(residual_half, output_even).astype(BF)
    odd_heads = dot_t(residual_half, output_odd).astype(BF)
    wide = heads * DV
    pairs = [
        jnp.stack([even_heads[:, k * wide : (k + 1) * wide], odd_heads[:, k * wide : (k + 1) * wide]])
        for k in range(chips)
    ]
    stacks = pairs
    pairs = [pairs[0]] + [along.send(pairs[k], 2 * k) for k in range(1, chips)]
    other_half = swap(jnp.stack([pair[1] for pair in pairs]), "seq", 1)
    attention_grad = jnp.concatenate(
        [jnp.stack([pair[0] for pair in pairs]), other_half], axis=0
    ).reshape(length, wide)
    out_products = [(shared_hidden, drop_rows, False)]
    out_masks = [weighted_high, weighted_low]
    out_masks = [after(mask, *stacks, *pairs[1:]) for mask in out_masks]
    out_odd = combine(1, out_masks, results_back, out_products, BF)
    out_even = combine(0, out_masks, results_back, out_products, F32)
    out_blocks = along.begin(out_even, out_odd)
    output_got = [along.send(out_blocks[k], 2 * k) for k in range(chips - 1, 0, -1)]

    query_in_grad, kv_grad, latent_part, latent_sum = attend_back(
        query_heads,
        key_heads,
        value_heads,
        result,
        after(attention_grad, *out_blocks),
        logsum,
        row_position,
        column_position,
        cosine_wide,
        -sine_wide,
        up_cols,
        latent_all,
        latent_wide,
        factor,
    )
    one_odd, odd_sum = query_back(1, query_in_grad, first_all, normed_one, gain_first, BF)
    one_even, even_sum = query_back(0, after(query_in_grad, *output_got[:2]), first_all, normed_one, gain_first, F32)
    mine = lax.axis_index("exp")
    late = Lane("exp", 3)
    attention_parts = late.others(after(own_heads, one_even))
    column_blocks = [
        lax.dynamic_slice_in_dim(residual_half, (mine ^ j) * block_rows, block_rows, 1)
        for j in range(n_exp)
    ]
    column_blocks = [column_blocks[0]] + [
        late.send(column_blocks[j], j) for j in range(1, n_exp)
    ]
    sums = jnp.concatenate(
        [
            (odd_sum + even_sum).reshape(n_exp, n_seq, gain_rows),
            jnp.sum(second_terms, axis=0).reshape(n_exp, n_seq, gain_rows),
            latent_sum.reshape(n_exp, n_seq, latent_rows_local),
        ],
        axis=2,
    )
    many = sums.shape[2]
    turn = (seq ^ jnp.array(order))[:, None] == jnp.arange(n_seq)[None, :]
    sums = jnp.einsum("ps,esw->pew", turn.astype(F32), sums, precision=lax.Precision.HIGHEST)
    sums = jnp.pad(
        sums.reshape(n_seq, 1, n_exp * many), ((0, 0), (0, 15), (0, columns - n_exp * many))
    )
    latent_part = jnp.concatenate([latent_part.reshape(n_seq, count, columns), sums], axis=1)
    latent_part = latent_part.reshape(n_seq * (count + 16), columns)
    latent_grad = along.scatter(
        latent_part[: chips * (count + 16)], latent_part[chips * (count + 16) :]
    )
    one_blocks = along.begin(one_even, one_odd)
    one_got = [along.send(one_blocks[k], 2 * k) for k in range(chips - 1, 0, -1)]
    output_odd_part = output_weights(1, attention_parts, column_blocks, BF)
    output_even_part = output_weights(0, attention_parts, column_blocks, F32)
    output_blocks = along.begin(output_even_part, output_odd_part)
    up_part = t_dot(after(latent_all, one_odd), kv_grad).astype(BF)
    query_part = t_dot(after(normed_one, one_odd), query_in_grad).astype(BF)
    up_out = sum_exp(up_part, 0)
    query_out = sum_exp(query_part, 0)
    sums = latent_grad[count, : n_exp * many].reshape(n_exp, 1, many)
    latent_grad = latent_grad[:count]
    latent_raw_grad, _ = norm_back(
        latent_grad[:, :R], latent_raw[:count], inverse_rms(latent_raw[:count]), latent_wide
    )
    down_rows = jnp.concatenate(
        [
            latent_raw_grad,
            rotate(latent_grad[:, R:], cosine_table[:count], -sine_table[:count]),
        ],
        axis=1,
    ).astype(BF)
    down_even, down_odd = free.pair(
        [after(x, *one_got, *output_blocks) for x in free.chips(down_rows)]
    )
    wide_got = [
        swap(after(output_blocks[k], down_even), "seq", 2 * k) for k in range(chips - 1, 0, -1)
    ]
    down_part = down_weights(index, normed_one, down_even, down_odd, n_exp, n_seq, gain_rows)
    down_part = jnp.concatenate(
        [
            down_part,
            jnp.pad(sums, ((0, 0), (0, 15), (0, columns - many))),
        ],
        axis=1,
    )
    down_sum = lax.dynamic_index_in_dim(down_part, mine, 0, keepdims=False)
    for j in range(1, n_exp):
        piece = lax.dynamic_index_in_dim(down_part, mine ^ j, 0, keepdims=False).astype(BF)
        down_sum = down_sum + swap(piece, "exp", j).astype(F32)
    down_out = down_sum[:gain_rows]
    small = down_sum[gain_rows, :many]
    first_out = small[:gain_rows] + jnp.sum(
        w_kv_down.astype(F32) * down_out, axis=1
    ) / norm_gain.astype(F32)

    output = residual + out_blocks[0]
    for block in output_got:
        output = output + after(block, *one_blocks).astype(F32)
    output = output.astype(BF)
    output_out = output_blocks[0]
    for block in wide_got:
        output_out = output_out + block.astype(F32)
    one_grad = one_blocks[0]
    for block in one_got:
        block = after(block, up_part, query_part, gate_out, lift_out, drop_out)
        one_grad = one_grad + block.astype(F32)
    down_back = dot_t(down_rows, down_full)
    token_norm_grad, _ = norm_back(
        one_grad + down_back, token_wide, token_inverse, gain_first
    )
    tokens_grad = (residual_grad + token_norm_grad).astype(BF)
    return (
        output,
        tokens_grad,
        first_out,
        query_out,
        down_out,
        small[2 * gain_rows : many],
        up_out,
        output_out,
        small[gain_rows : 2 * gain_rows],
        gate_out,
        lift_out,
        drop_out,
        expert_gate_grad,
        expert_up_grad,
        expert_down_grad,
    )


def solution(mesh):
    rows = P(("exp", "seq"), None)
    line = P(("exp", "seq"))
    grid = P("exp", "seq")
    turned = P("seq", "exp")
    part = P(("exp", "seq"), None, None)
    return jax.shard_map(
        shards,
        mesh=mesh,
        in_specs=(
            rows,
            rows,
            rows,
            line,
            grid,
            rows,
            line,
            grid,
            turned,
            line,
            grid,
            grid,
            turned,
            part,
            part,
            part,
            rows,
        ),
        out_specs=(
            rows,
            rows,
            line,
            grid,
            rows,
            line,
            grid,
            turned,
            line,
            grid,
            grid,
            turned,
            part,
            part,
            part,
        ),
        check_vma=False,
    )
```
